256 devices in a mesh: seq: 32 (over x, z), mp: 8 (over y, core).
Axes of the slice: x: 4, y: 4, z: 8, core: 2. Of those that a mesh axis runs over, the one named last changes fastest.
Arguments:
- prompt_hidden: bfloat16 [1024, 4096], P('seq', 'mp'), may hold values from -6 to 6
- recompute_hidden: bfloat16 [1024, 4096], P('seq', 'mp'), may hold values from -6 to 6
- key_cache: bfloat16 [32, 1024, 1024], P('seq', None, 'mp')
- value_cache: bfloat16 [32, 1024, 1024], P('seq', None, 'mp'), may hold values from -6 to 6
- norm_gain: float32 [4096], replicated, may hold values from 0.1 to 1.9
- w_query: bfloat16 [4096, 4096], P(None, 'mp'), may hold values from -0.09375 to 0.09375
- key_weight: bfloat16 [4096, 1024], P(None, 'mp'), may hold values from -0.09375 to 0.09375
- value_weight: bfloat16 [4096, 1024], P(None, 'mp'), may hold values from -0.09375 to 0.09375
- w_out: bfloat16 [4096, 4096], P('mp'), may hold values from -0.375 to 0.375
- passage_owner: int32 [32], replicated, may hold values from 0 to 31
- prompt_slot: int32 [32], replicated, may hold values from 0 to 31, each once
- prompt_length: int32 [32], replicated, may hold values from 1 to 32, 768 in all
- recompute_count: int32 [32], replicated, may hold values from 1 to 32, 768 in all
- recompute_index: int32 [32, 32], replicated, may hold values from 0 to 1023, as said below
Outputs:
- prompt_out: bfloat16 [1024, 4096], P('seq', 'mp')
- recompute_out: bfloat16 [1024, 4096], P('seq', 'mp')
The draws below stay inside these ranges and needn't reach their ends.
Inputs may be any that keep to these rules, and one draw needn't show every extreme that they name: `recompute_index`: within each row the 32 entries are distinct positions of the passage. `prompt_slot`: each request appears once. `passage_owner`: A request's passages stand in its context in the order of their indices.
All inputs are finite; a program needn't handle non-finite values.
Results may differ from the reference program's by a relative error of at most 0.015.
Values may be sent and summed in bfloat16 or wider, within the bound.
A program may use at most 128 MiB of HBM per device.

```python
import math
import jax
import jax.numpy as jnp
import numpy as np
from jax import lax

MODEL_WIDTH = 4096
QUERY_HEADS = 32
KEY_VALUE_HEADS = 8
HEAD_SIZE = 128
PASSAGE_TOKENS = 1024
R_MAX = 32
PROMPT_TOKENS = 32
SLOTS = 32
PASSAGE_COUNT = 32
PROMPT_ROWS = 1024
RECOMPUTE_ROWS = 1024
N_SEQ = 32


def draw_key_cache(key, part):
    drawn_sample = jax.random.normal(key, (PASSAGE_COUNT, PASSAGE_TOKENS, KEY_VALUE_HEADS * HEAD_SIZE), jnp.float32)
    return drawn_sample.astype(jnp.bfloat16)


def draw_recompute_index(key, part):
    split_keys = jax.random.split(jax.random.fold_in(key, 21), PASSAGE_COUNT)
    shuffled = jax.vmap(lambda subkey: jax.random.permutation(subkey, PASSAGE_TOKENS))(split_keys).astype(jnp.int32)
    row_index = jnp.arange(PASSAGE_COUNT, dtype=jnp.int32)
    target = jnp.where(row_index == 0, PASSAGE_TOKENS - 1, jnp.where(row_index == 1, 0, shuffled[:, 0]))
    where_at = jnp.argmax(shuffled == target[:, None], axis=1).astype(jnp.int32)
    column = jnp.arange(PASSAGE_TOKENS, dtype=jnp.int32)[None, :]
    swapped = jnp.where(column == 0, target[:, None], jnp.where(column == where_at[:, None], shuffled[:, 0:1], shuffled))
    return swapped[:, :R_MAX].astype(jnp.int32)


def set_ends(drawn, key, least, top_value):
    index_at = [jax.random.randint(jax.random.fold_in(key, axis), (), 0, length) for axis, length in enumerate(drawn.shape)]
    main_axis = drawn.shape.index(max(drawn.shape))
    neighbour = index_at[:main_axis] + [(index_at[main_axis] + 1) % drawn.shape[main_axis]] + index_at[main_axis + 1:]
    return drawn.at[tuple(index_at)].set(least).at[tuple(neighbour)].set(top_value)


def levels(stream_key, dims, cuts, smallest, top_value):
    level, own = 1.0, jax.random.fold_in(stream_key, 6)
    for dim, shards_of in cuts:
        draws = jnp.exp(jax.random.uniform(jax.random.fold_in(own, dim), (shards_of,), jnp.float32, smallest / len(cuts), top_value / len(cuts)))
        level = level * jnp.repeat(draws, dims[dim] // shards_of).reshape([-1 if axis == dim else 1 for axis in range(len(dims))])
    return level


def cumulative_ranks(number_of, skew):
    loads = [(1 << 20) // math.isqrt(standing ** skew) + 1 for standing in range(1, number_of + 1)]
    scale = 1 + sum(loads) // (1 << 30)
    return np.cumsum(np.array([max(1, weight // scale) for weight in loads]))


def ranked_ids(stream_key, extent, count, lean):
    grid = cumulative_ranks(count, lean)
    ticket = jax.random.randint(jax.random.fold_in(stream_key, 1), extent, 0, int(grid[count - 1]))
    rank = jnp.searchsorted(jnp.asarray(grid, jnp.int32), ticket, side="right")
    return jax.random.permutation(jax.random.fold_in(stream_key, 2), count)[rank].astype(jnp.int32)


def length_profile(count, total, reach, lean):
    portions = [(1 << 20) // math.isqrt(grade ** lean) + 1 for grade in range(2, count + 1)]
    spare, holding = total - reach - (count - 1), [1] * (count - 1)
    while spare > 0:
        movable = [i for i in range(count - 1) if holding[i] < reach]
        mass, remaining = sum([portions[i] for i in movable]), spare
        for i in movable:
            more = min(reach - holding[i], max(1, remaining * portions[i] // mass), spare)
            holding[i] = holding[i] + more
            spare = spare - more
    return np.array([reach] + holding)


def uneven(own_key, number_of, total, limit, slope):
    if number_of == 2:
        one = jax.random.randint(own_key, (), max(1, total - limit), min(limit, total - 1) + 1)
        return jnp.stack([one, total - one])
    tallies = jnp.asarray(length_profile(number_of, total, limit, slope), jnp.int32)
    pairs = (number_of - 1) // 2
    donor, receiver = tallies[1:1 + 2 * pairs:2], tallies[2:2 + 2 * pairs:2]
    margin = jnp.minimum(donor - 1, limit - receiver)
    passed = jax.random.randint(jax.random.fold_in(own_key, 1), (pairs,), 0, 1 << 20) % (margin + 1)
    tallies = tallies.at[1:1 + 2 * pairs:2].set(donor - passed).at[2:2 + 2 * pairs:2].set(receiver + passed)
    return tallies[jax.random.permutation(jax.random.fold_in(own_key, 2), number_of)]


def centred(rng, shape, deviation, reach, shards=(), kind=jnp.bfloat16):
    values = jax.random.normal(rng, shape, jnp.float32) * deviation
    if len(shards) > 0:
        values = levels(rng, shape, shards, -0.22, 0.18) * values
    return jnp.clip(values, min=-reach, max=reach).astype(kind)


def setup_inputs(seed: int = 0) -> dict:
    seeds = jax.random.split(jax.random.key(seed), 15)
    prompt_hidden = centred(seeds[0], (PROMPT_ROWS, MODEL_WIDTH), 1.0, 6.0, ((0, 32), (1, 8)))
    recompute_hidden = centred(seeds[1], (RECOMPUTE_ROWS, MODEL_WIDTH), 1.0, 6.0, ((0, 32), (1, 8)))
    key_cache = draw_key_cache(jax.random.fold_in(seeds[14], 71), 0)
    value_cache = centred(seeds[3], (PASSAGE_COUNT, PASSAGE_TOKENS, KEY_VALUE_HEADS * HEAD_SIZE), 1.0, 6.0, ((0, 32), (2, 8)))
    norm_gain = jnp.clip(1.0 + 0.18 * jax.random.normal(seeds[4], (MODEL_WIDTH,), jnp.float32), 0.1, 1.9)
    w_query = centred(seeds[5], (MODEL_WIDTH, QUERY_HEADS * HEAD_SIZE), MODEL_WIDTH ** -0.5, 0.09375, ((1, 8),))
    key_weight = centred(seeds[6], (MODEL_WIDTH, KEY_VALUE_HEADS * HEAD_SIZE), MODEL_WIDTH ** -0.5, 0.09375, ((1, 8),))
    value_weight = centred(seeds[7], (MODEL_WIDTH, KEY_VALUE_HEADS * HEAD_SIZE), MODEL_WIDTH ** -0.5, 0.09375, ((1, 8),))
    w_out = centred(seeds[8], (QUERY_HEADS * HEAD_SIZE, MODEL_WIDTH), (QUERY_HEADS * HEAD_SIZE // 16) ** -0.5, 0.375, ((0, 8),))
    passage_owner = set_ends(ranked_ids(seeds[9], (PASSAGE_COUNT,), SLOTS, 2), jax.random.fold_in(seeds[9], 3), 0, SLOTS - 1).astype(jnp.int32)
    prompt_slot = jax.random.permutation(seeds[10], SLOTS).astype(jnp.int32)
    prompt_length = uneven(seeds[11], SLOTS, 3 * SLOTS * PROMPT_TOKENS // 4, PROMPT_TOKENS, 0).astype(jnp.int32)
    recompute_count = uneven(seeds[12], PASSAGE_COUNT, 3 * PASSAGE_COUNT * R_MAX // 4, R_MAX, 0).astype(jnp.int32)
    recompute_index = draw_recompute_index(jax.random.fold_in(seeds[14], 71), 0)
    return dict(prompt_hidden=prompt_hidden, recompute_hidden=recompute_hidden, key_cache=key_cache, value_cache=value_cache, norm_gain=norm_gain, w_query=w_query, key_weight=key_weight, value_weight=value_weight, w_out=w_out, passage_owner=passage_owner, prompt_slot=prompt_slot, prompt_length=prompt_length, recompute_count=recompute_count, recompute_index=recompute_index)


NEGATIVE_FLOOR = -1e+30

def layout(passage_owner, prompt_slot, prompt_length, recompute_count, recompute_index, passage_length, prompt_rows):
    seq_count = passage_owner.shape[0]
    recompute_rows = recompute_index.shape[1]
    indices = jnp.arange(seq_count, dtype=jnp.int32)
    same_owner = passage_owner[:, None] == passage_owner[None, :]
    passage_rank = lax.optimization_barrier(jnp.sum(jnp.where(same_owner & (indices[None, :] < indices[:, None]), 1, 0), axis=1)).astype(jnp.int32)
    held_count = lax.optimization_barrier(jnp.sum(jnp.where(passage_owner[None, :] == prompt_slot[:, None], 1, 0), axis=1)).astype(jnp.int32)
    prompt_index = jnp.arange(prompt_rows, dtype=jnp.int32)
    slot_index = jnp.arange(recompute_rows, dtype=jnp.int32)
    token_index = jnp.arange(passage_length, dtype=jnp.int32)
    prompt_req = jnp.broadcast_to(prompt_slot[:, None], (seq_count, prompt_rows))
    prompt_pos = held_count[:, None] * passage_length + prompt_index[None, :]
    prompt_live = jnp.broadcast_to(prompt_index[None, :] < prompt_length[:, None], (seq_count, prompt_rows))
    recompute_req = jnp.broadcast_to(passage_owner[:, None], (seq_count, recompute_rows))
    recompute_pos = passage_rank[:, None] * passage_length + recompute_index
    recompute_live = jnp.broadcast_to(slot_index[None, :] < recompute_count[:, None], (seq_count, recompute_rows))
    cached_req = jnp.broadcast_to(passage_owner[:, None], (seq_count, passage_length))
    cached_pos = passage_rank[:, None] * passage_length + token_index[None, :]
    cached_live = jnp.ones((seq_count, passage_length), dtype=bool)
    query_req = jnp.concatenate([prompt_req, recompute_req], axis=1).astype(jnp.int32)
    query_pos = jnp.concatenate([prompt_pos, recompute_pos], axis=1).astype(jnp.int32)
    query_live = jnp.concatenate([prompt_live, recompute_live], axis=1)
    key_req = jnp.concatenate([cached_req, prompt_req], axis=1).astype(jnp.int32)
    key_pos = jnp.concatenate([cached_pos, prompt_pos], axis=1).astype(jnp.int32)
    key_live = jnp.concatenate([cached_live, prompt_live], axis=1)
    return (query_req, query_pos, query_live, key_req, key_pos, key_live, passage_rank)

def apply_rotation(vectors, positions):
    half_width = vectors.shape[-1] // 2
    exponent = jnp.arange(half_width).astype(jnp.float32) * (2.0 / vectors.shape[-1])
    frequency = jnp.exp(-exponent * math.log(500000.0))
    angles = positions.astype(jnp.float32)[:, None] * frequency[None, :]
    cosines = jnp.cos(angles)[:, None, :]
    sines = jnp.sin(angles)[:, None, :]
    leading = vectors[..., :half_width]
    trailing = vectors[..., half_width:]
    return jnp.concatenate([leading * cosines - trailing * sines, trailing * cosines + leading * sines], axis=-1)

def normalize(rows_in, norm_gain):
    values = rows_in.astype(jnp.float32)
    inverse_rms = lax.rsqrt(lax.optimization_barrier(jnp.mean(values * values, axis=-1, keepdims=True)) + 1e-05)
    return (values * inverse_rms * norm_gain.astype(jnp.float32)).astype(jnp.bfloat16)

def merge_parts(earlier, later):
    highest = jnp.maximum(earlier[1], later[1])
    earlier_scale = jnp.exp(earlier[1] - highest)
    later_scale = jnp.exp(later[1] - highest)
    accumulated = earlier[0] * earlier_scale[..., None] + later[0] * later_scale[..., None]
    return (accumulated, highest, earlier[2] * earlier_scale + later[2] * later_scale)

def reference(prompt_hidden, recompute_hidden, key_cache, value_cache, norm_gain, w_query, key_weight, value_weight, w_out, passage_owner, prompt_slot, prompt_length, recompute_count, recompute_index):
    query_row_stack = PROMPT_TOKENS + R_MAX
    key_row_stack = PASSAGE_TOKENS + PROMPT_TOKENS
    queries_per_group = QUERY_HEADS // KEY_VALUE_HEADS
    query_req, query_pos, query_live, key_req, key_pos, key_live, passage_rank = layout(passage_owner, prompt_slot, prompt_length, recompute_count, recompute_index, PASSAGE_TOKENS, PROMPT_TOKENS)
    hidden_rows = jnp.concatenate([prompt_hidden.reshape(N_SEQ, PROMPT_TOKENS, MODEL_WIDTH), recompute_hidden.reshape(N_SEQ, R_MAX, MODEL_WIDTH)], axis=1).reshape(N_SEQ * query_row_stack, MODEL_WIDTH)
    normalized_hidden = normalize(hidden_rows, norm_gain)
    flattened_position = query_pos.reshape(-1)
    query_vectors = apply_rotation(jnp.dot(normalized_hidden, w_query, preferred_element_type=jnp.float32).reshape(-1, QUERY_HEADS, HEAD_SIZE), flattened_position).astype(jnp.bfloat16)
    newest_keys = apply_rotation(jnp.dot(normalized_hidden, key_weight, preferred_element_type=jnp.float32).reshape(-1, KEY_VALUE_HEADS, HEAD_SIZE), flattened_position).astype(jnp.bfloat16).reshape(N_SEQ, query_row_stack, KEY_VALUE_HEADS * HEAD_SIZE)
    newest_values = jnp.dot(normalized_hidden, value_weight, preferred_element_type=jnp.float32).astype(jnp.bfloat16).reshape(N_SEQ, query_row_stack, KEY_VALUE_HEADS * HEAD_SIZE)
    position_shift = jnp.repeat(passage_rank * PASSAGE_TOKENS, PASSAGE_TOKENS).astype(jnp.int32)
    shifted_keys = apply_rotation(key_cache.astype(jnp.float32).reshape(N_SEQ * PASSAGE_TOKENS, KEY_VALUE_HEADS, HEAD_SIZE), position_shift).astype(jnp.bfloat16).reshape(N_SEQ, PASSAGE_TOKENS, KEY_VALUE_HEADS * HEAD_SIZE)
    slot_index = jnp.arange(R_MAX, dtype=jnp.int32)
    chosen = (recompute_index[:, :, None] == jnp.arange(PASSAGE_TOKENS, dtype=jnp.int32)[None, None, :]) & (slot_index[None, :, None] < recompute_count[:, None, None])
    replaced = jnp.any(chosen, axis=1)[:, :, None]
    chosen_float = chosen.astype(jnp.float32)
    placed_keys = jnp.einsum('crt,crf->ctf', chosen_float, newest_keys[:, PROMPT_TOKENS:].astype(jnp.float32)).astype(jnp.bfloat16)
    placed_values = jnp.einsum('crt,crf->ctf', chosen_float, newest_values[:, PROMPT_TOKENS:].astype(jnp.float32)).astype(jnp.bfloat16)
    passage_key_rows = jnp.where(replaced, placed_keys, shifted_keys)
    passage_value_rows = jnp.where(replaced, placed_values, value_cache)
    joined_keys = jnp.concatenate([passage_key_rows, newest_keys[:, :PROMPT_TOKENS]], axis=1).astype(jnp.float32).reshape(N_SEQ, key_row_stack, KEY_VALUE_HEADS, HEAD_SIZE)
    joined_values = jnp.concatenate([passage_value_rows, newest_values[:, :PROMPT_TOKENS]], axis=1).astype(jnp.float32).reshape(N_SEQ, key_row_stack, KEY_VALUE_HEADS, HEAD_SIZE)
    query_block_list = query_vectors.astype(jnp.float32).reshape(N_SEQ, query_row_stack, KEY_VALUE_HEADS, queries_per_group, HEAD_SIZE)
    score_scale = 1.0 / math.sqrt(HEAD_SIZE)

    def block_attention(inputs):
        block_queries, block_req, block_pos, block_live = inputs

        def visit(running, visited):
            keys_in, values_in, visit_req, visit_pos, visit_live = visited
            visible = (block_req[:, None] == visit_req[None, :]) & (visit_pos[None, :] <= block_pos[:, None]) & visit_live[None, :]

            def compute(current):
                scores = jnp.einsum('qhgd,khd->qhgk', block_queries, keys_in) * score_scale
                visible_mask = visible[:, None, None, :]
                scores = jnp.where(visible_mask, scores, NEGATIVE_FLOOR)
                maxima = lax.optimization_barrier(jnp.max(scores, axis=-1))
                weights = jnp.where(visible_mask, jnp.exp(scores - maxima[..., None]), 0.0)
                totals = lax.optimization_barrier(jnp.sum(weights, axis=-1))
                rounded = lax.optimization_barrier(weights.astype(jnp.bfloat16)).astype(jnp.float32)
                accumulated = jnp.einsum('qhgk,khd->qhgd', rounded, values_in)
                return merge_parts(current, (accumulated, maxima, totals))
            return (lax.cond(jnp.any(visible), compute, lambda current: current, running), None)
        starting_state = (jnp.zeros((query_row_stack, KEY_VALUE_HEADS, queries_per_group, HEAD_SIZE), jnp.float32), jnp.full((query_row_stack, KEY_VALUE_HEADS, queries_per_group), NEGATIVE_FLOOR, jnp.float32), jnp.zeros((query_row_stack, KEY_VALUE_HEADS, queries_per_group), jnp.float32))
        final, _ = lax.scan(visit, starting_state, (joined_keys, joined_values, key_req, key_pos, key_live))
        accumulated, maxima, totals = final
        safe_totals = jnp.where(totals > 0, totals, 1.0)
        result = jnp.where(block_live[:, None, None, None], accumulated / safe_totals[..., None], 0.0)
        return result.reshape(query_row_stack, QUERY_HEADS * HEAD_SIZE).astype(jnp.bfloat16)
    attention = lax.map(block_attention, (query_block_list, query_req, query_pos, query_live))
    projected = jnp.dot(attention.reshape(-1, QUERY_HEADS * HEAD_SIZE), w_out, preferred_element_type=jnp.float32).astype(jnp.bfloat16).reshape(N_SEQ, query_row_stack, MODEL_WIDTH)
    return (projected[:, :PROMPT_TOKENS].reshape(N_SEQ * PROMPT_TOKENS, MODEL_WIDTH), projected[:, PROMPT_TOKENS:].reshape(N_SEQ * R_MAX, MODEL_WIDTH))
```

```python
import functools
import math

import jax
import jax.numpy as jnp
from jax import lax
from jax.experimental import pallas as pl
from jax.experimental.pallas import tpu as pltpu
from jax.sharding import PartitionSpec as P

HEAD_SIZE = 128
NEGATIVE_FLOOR = -1e30


def apply_rotation(vectors, positions):
    half_width = vectors.shape[-1] // 2
    exponent = jnp.arange(half_width).astype(jnp.float32) * (2.0 / vectors.shape[-1])
    frequency = jnp.exp(-exponent * math.log(500000.0))
    angles = positions.astype(jnp.float32)[:, None] * frequency[None, :]
    cosines = jnp.cos(angles)[:, None, :]
    sines = jnp.sin(angles)[:, None, :]
    leading = vectors[..., :half_width]
    trailing = vectors[..., half_width:]
    return jnp.concatenate(
        [leading * cosines - trailing * sines, trailing * cosines + leading * sines], axis=-1
    )


def normalize(rows_in, norm_gain):
    values = rows_in.astype(jnp.float32)
    inverse_rms = lax.rsqrt(jnp.mean(values * values, axis=-1, keepdims=True) + 1e-05)
    return (values * inverse_rms * norm_gain).astype(jnp.bfloat16)


def passage_kernel(flags_ref, q_ref, k_ref, v_ref, lim_ref, acc_ref, st_ref):
    b = pl.program_id(0)
    flag = flags_ref[b]
    rows = q_ref.shape[1]
    keys = k_ref.shape[0]

    @pl.when(flag == 0)
    def _():
        acc_ref[...] = jnp.zeros_like(acc_ref)
        sub = lax.broadcasted_iota(jnp.int32, st_ref.shape, 1)
        st_ref[...] = jnp.where(sub == 0, NEGATIVE_FLOOR, 0.0).astype(jnp.float32)

    @pl.when(flag > 0)
    def _():
        scores = lax.dot_general(
            q_ref[0], k_ref[...], (((1,), (1,)), ((), ())), preferred_element_type=jnp.float32
        ) * (1.0 / math.sqrt(HEAD_SIZE))
        limit = jnp.where(flag == 2, lim_ref[...], keys - 1)
        token = lax.broadcasted_iota(jnp.int32, (rows, keys), 1)
        scores = jnp.where(token <= limit, scores, NEGATIVE_FLOOR)
        maxima = jnp.max(scores, axis=1, keepdims=True)
        weights = jnp.exp(scores - maxima)
        totals = jnp.sum(weights, axis=1, keepdims=True)
        acc_ref[0] = jnp.dot(
            weights.astype(jnp.bfloat16), v_ref[...], preferred_element_type=jnp.float32
        ).astype(acc_ref.dtype)
        m_row = jnp.transpose(jnp.broadcast_to(maxima, (rows, rows)))[0:8]
        l_row = jnp.transpose(jnp.broadcast_to(totals, (rows, rows)))[0:8]
        sub = lax.broadcasted_iota(jnp.int32, (8, rows), 0)
        st_ref[0] = jnp.where(sub == 0, m_row, jnp.where(sub == 1, l_row, 0.0))


def passage_attention(flags, q_blocks, keys, values, lim):
    nb, rows, _ = q_blocks.shape
    n_keys = keys.shape[0]
    grid_spec = pltpu.PrefetchScalarGridSpec(
        num_scalar_prefetch=1,
        grid=(nb,),
        in_specs=[
            pl.BlockSpec((1, rows, HEAD_SIZE), lambda b, f: (b, 0, 0)),
            pl.BlockSpec((n_keys, HEAD_SIZE), lambda b, f: (0, 0)),
            pl.BlockSpec((n_keys, HEAD_SIZE), lambda b, f: (0, 0)),
            pl.BlockSpec((rows, 1), lambda b, f: (0, 0)),
        ],
        out_specs=[
            pl.BlockSpec((1, rows, HEAD_SIZE), lambda b, f: (b, 0, 0)),
            pl.BlockSpec((1, 8, rows), lambda b, f: (b, 0, 0)),
        ],
    )
    return pl.pallas_call(
        passage_kernel,
        grid_spec=grid_spec,
        out_shape=[
            jax.ShapeDtypeStruct((nb, rows, HEAD_SIZE), jnp.bfloat16),
            jax.ShapeDtypeStruct((nb, 8, rows), jnp.float32),
        ],
    )(flags, q_blocks, keys, values, lim)


def local(
    prompt_hidden,
    recompute_hidden,
    key_cache,
    value_cache,
    norm_gain,
    w_query,
    key_weight,
    value_weight,
    w_out,
    passage_owner,
    prompt_slot,
    prompt_length,
    recompute_count,
    recompute_index,
):
    prompt_rows = prompt_hidden.shape[0]
    recompute_rows = recompute_hidden.shape[0]
    query_rows = prompt_rows + recompute_rows
    passage_length = key_cache.shape[1]
    local_heads = w_query.shape[1] // HEAD_SIZE
    n_seq = passage_owner.shape[0]
    me = lax.axis_index("seq")
    scale = 1.0 / math.sqrt(HEAD_SIZE)

    seq_ids = jnp.arange(n_seq, dtype=jnp.int32)
    same_owner = passage_owner[:, None] == passage_owner[None, :]
    passage_rank = jnp.sum(
        jnp.where(same_owner & (seq_ids[None, :] < seq_ids[:, None]), 1, 0), axis=1
    ).astype(jnp.int32)
    held_count = jnp.sum(
        jnp.where(passage_owner[None, :] == prompt_slot[:, None], 1, 0), axis=1
    ).astype(jnp.int32)
    own_rank = passage_rank[me]
    own_owner = passage_owner[me]
    own_held = held_count[me]
    own_index = lax.dynamic_index_in_dim(recompute_index, me, 0, keepdims=False)
    own_length = prompt_length[me]
    own_count = recompute_count[me]

    prompt_pos = own_held * passage_length + jnp.arange(prompt_rows, dtype=jnp.int32)
    recompute_pos = own_rank * passage_length + own_index
    own_pos = jnp.concatenate([prompt_pos, recompute_pos])
    own_live = jnp.concatenate(
        [
            jnp.arange(prompt_rows, dtype=jnp.int32) < own_length,
            jnp.arange(recompute_rows, dtype=jnp.int32) < own_count,
        ]
    )

    rows_local = jnp.concatenate([prompt_hidden, recompute_hidden], axis=0)
    full_rows = lax.all_gather(rows_local, "mp", axis=1, tiled=True)
    normalized_hidden = normalize(full_rows, norm_gain)
    queries = (
        apply_rotation(
            jnp.dot(normalized_hidden, w_query, preferred_element_type=jnp.float32).reshape(
                query_rows, local_heads, HEAD_SIZE
            ),
            own_pos,
        )
        .astype(jnp.bfloat16)
    )
    fresh_keys = (
        apply_rotation(
            jnp.dot(normalized_hidden, key_weight, preferred_element_type=jnp.float32).reshape(
                query_rows, 1, HEAD_SIZE
            ),
            own_pos,
        )
        .astype(jnp.bfloat16)
        .reshape(query_rows, HEAD_SIZE)
    )
    fresh_values = jnp.dot(
        normalized_hidden, value_weight, preferred_element_type=jnp.float32
    ).astype(jnp.bfloat16)

    position_shift = jnp.full((passage_length,), own_rank * passage_length, jnp.int32)
    shifted_keys = (
        apply_rotation(
            key_cache[0].astype(jnp.float32).reshape(passage_length, 1, HEAD_SIZE),
            position_shift,
        )
        .astype(jnp.bfloat16)
        .reshape(passage_length, HEAD_SIZE)
    )
    chosen = (own_index[:, None] == jnp.arange(passage_length, dtype=jnp.int32)[None, :]) & (
        jnp.arange(recompute_rows, dtype=jnp.int32)[:, None] < own_count
    )
    replaced = jnp.any(chosen, axis=0)[:, None]
    fresh_pair = jnp.concatenate([fresh_keys[prompt_rows:], fresh_values[prompt_rows:]], axis=1)
    placed = lax.dot_general(
        chosen.astype(jnp.bfloat16),
        fresh_pair,
        (((0,), (0,)), ((), ())),
        preferred_element_type=jnp.float32,
    ).astype(jnp.bfloat16)
    passage_keys = jnp.where(replaced, placed[:, :HEAD_SIZE], shifted_keys)
    passage_values = jnp.where(replaced, placed[:, HEAD_SIZE:], value_cache[0])

    all_queries = lax.all_gather(queries, "seq", axis=0, tiled=False)
    q_blocks = all_queries.reshape(n_seq * 2, prompt_rows * local_heads, HEAD_SIZE)
    prompt_flag = jnp.where(prompt_slot == own_owner, 1, 0)
    recompute_flag = jnp.where(
        seq_ids == me, 2, jnp.where((passage_owner == own_owner) & (seq_ids > me), 1, 0)
    )
    flags = jnp.stack([prompt_flag, recompute_flag], axis=1).reshape(-1).astype(jnp.int32)
    lim = jnp.repeat(own_index, local_heads).reshape(-1, 1).astype(jnp.int32)
    acc, stats = passage_attention(flags, q_blocks, passage_keys, passage_values, lim)

    acc = acc.reshape(n_seq, query_rows, local_heads * HEAD_SIZE)
    stats = stats[:, 0:2].reshape(n_seq, 2, 2, prompt_rows * local_heads)
    acc_back = lax.all_to_all(acc, "seq", 0, 0, tiled=True)
    stats_back = lax.all_to_all(stats, "seq", 0, 0, tiled=True)
    part_max = jnp.transpose(stats_back[:, :, 0], (0, 1, 2)).reshape(n_seq, query_rows, local_heads)
    part_tot = stats_back[:, :, 1].reshape(n_seq, query_rows, local_heads)
    part_acc = acc_back.reshape(n_seq, query_rows, local_heads, HEAD_SIZE).astype(jnp.float32)

    pq = queries[:prompt_rows].astype(jnp.float32)
    pk = fresh_keys[:prompt_rows].astype(jnp.float32)
    pv = fresh_values[:prompt_rows].astype(jnp.float32)
    ps = jnp.einsum("qhd,kd->qhk", pq, pk) * scale
    jj = jnp.arange(prompt_rows, dtype=jnp.int32)
    pvis = (jj[None, :] <= jj[:, None]) & (jj[None, :] < own_length)
    ps = jnp.where(pvis[:, None, :], ps, NEGATIVE_FLOOR)
    pmax = jnp.max(ps, axis=-1)
    pw = jnp.where(pvis[:, None, :], jnp.exp(ps - pmax[..., None]), 0.0)
    ptot = jnp.sum(pw, axis=-1)
    pacc = jnp.einsum("qhk,kd->qhd", pw.astype(jnp.bfloat16).astype(jnp.float32), pv)
    loc_max = jnp.concatenate(
        [pmax, jnp.full((recompute_rows, local_heads), NEGATIVE_FLOOR, jnp.float32)]
    )
    loc_tot = jnp.concatenate([ptot, jnp.zeros((recompute_rows, local_heads), jnp.float32)])
    loc_acc = jnp.concatenate(
        [pacc, jnp.zeros((recompute_rows, local_heads, HEAD_SIZE), jnp.float32)]
    )

    highest = jnp.maximum(jnp.max(part_max, axis=0), loc_max)
    part_scale = jnp.exp(part_max - highest[None])
    loc_scale = jnp.exp(loc_max - highest)
    accumulated = jnp.sum(part_acc * part_scale[..., None], axis=0) + loc_acc * loc_scale[..., None]
    totals = jnp.sum(part_tot * part_scale, axis=0) + loc_tot * loc_scale
    safe_totals = jnp.where(totals > 0, totals, 1.0)
    attention = jnp.where(
        own_live[:, None, None], accumulated / safe_totals[..., None], 0.0
    ).astype(jnp.bfloat16).reshape(query_rows, local_heads * HEAD_SIZE)
    projected = jnp.dot(attention, w_out, preferred_element_type=jnp.float32)
    combined = lax.psum_scatter(projected, "mp", scatter_dimension=1, tiled=True).astype(
        jnp.bfloat16
    )
    return (combined[:prompt_rows], combined[prompt_rows:])


def solution(mesh):
    return jax.shard_map(
        local,
        mesh=mesh,
        in_specs=(
            P("seq", "mp"),
            P("seq", "mp"),
            P("seq", None, "mp"),
            P("seq", None, "mp"),
            P(),
            P(None, "mp"),
            P(None, "mp"),
            P(None, "mp"),
            P("mp", None),
            P(),
            P(),
            P(),
            P(),
            P(),
        ),
        out_specs=(P("seq", "mp"), P("seq", "mp")),
        check_vma=False,
    )
```

```python
import functools
import math

import jax
import jax.numpy as jnp
from jax import lax
from jax.experimental import pallas as pl
from jax.experimental.pallas import tpu as pltpu
from jax.sharding import PartitionSpec as P

HEAD_SIZE = 128
NEGATIVE_FLOOR = -1e30


def apply_rotation(vectors, positions):
    half_width = vectors.shape[-1] // 2
    exponent = jnp.arange(half_width).astype(jnp.float32) * (2.0 / vectors.shape[-1])
    frequency = jnp.exp(-exponent * math.log(500000.0))
    angles = positions.astype(jnp.float32)[:, None] * frequency[None, :]
    cosines = jnp.cos(angles)[:, None, :]
    sines = jnp.sin(angles)[:, None, :]
    leading = vectors[..., :half_width]
    trailing = vectors[..., half_width:]
    return jnp.concatenate(
        [leading * cosines - trailing * sines, trailing * cosines + leading * sines], axis=-1
    )


def normalize(rows_in, norm_gain):
    values = rows_in.astype(jnp.float32)
    inverse_rms = lax.rsqrt(jnp.mean(values * values, axis=-1, keepdims=True) + 1e-05)
    return (values * inverse_rms * norm_gain).astype(jnp.bfloat16)


MESH = pl.DeviceIdType.MESH


def passage_kernel(flags_ref, q_ref, k_ref, v_ref, lim_ref, acc_ref, st_ref):
    nb, rows, _ = q_ref.shape
    keys = k_ref.shape[0]
    token = lax.broadcasted_iota(jnp.int32, (rows, keys), 1)
    sub = lax.broadcasted_iota(jnp.int32, (8, rows), 0)

    def body(b, carry):
        flag = flags_ref[b]

        @pl.when(flag == 0)
        def _():
            acc_ref[b] = jnp.zeros((rows, HEAD_SIZE), acc_ref.dtype)
            st_ref[b] = jnp.where(sub == 0, NEGATIVE_FLOOR, 0.0).astype(jnp.float32)

        @pl.when(flag > 0)
        def _():
            scores = lax.dot_general(
                q_ref[b], k_ref[...], (((1,), (1,)), ((), ())), preferred_element_type=jnp.float32
            ) * (1.0 / math.sqrt(HEAD_SIZE))
            limit = jnp.where(flag == 2, lim_ref[...], keys - 1)
            scores = jnp.where(token <= limit, scores, NEGATIVE_FLOOR)
            maxima = jnp.max(scores, axis=1, keepdims=True)
            weights = jnp.exp(scores - maxima)
            totals = jnp.sum(weights, axis=1, keepdims=True)
            acc_ref[b] = jnp.dot(
                weights.astype(jnp.bfloat16), v_ref[...], preferred_element_type=jnp.float32
            ).astype(acc_ref.dtype)
            m_row = jnp.transpose(jnp.broadcast_to(maxima, (rows, rows)))[0:8]
            l_row = jnp.transpose(jnp.broadcast_to(totals, (rows, rows)))[0:8]
            st_ref[b] = jnp.where(sub == 0, m_row, jnp.where(sub == 1, l_row, 0.0))

        return carry

    lax.fori_loop(0, nb, body, 0)


def passage_attention(flags, q_blocks, keys, values, lim):
    nb, rows, _ = q_blocks.shape
    vmem = pl.BlockSpec(memory_space=pltpu.VMEM)
    return pl.pallas_call(
        passage_kernel,
        in_specs=[pl.BlockSpec(memory_space=pltpu.SMEM), vmem, vmem, vmem, vmem],
        out_specs=[vmem, vmem],
        out_shape=[
            jax.ShapeDtypeStruct((nb, rows, HEAD_SIZE), jnp.bfloat16),
            jax.ShapeDtypeStruct((nb, 8, rows), jnp.float32),
        ],
    )(flags, q_blocks, keys, values, lim)


def exchange_kernel(n, gather, *refs):
    count = len(refs) // 2 - 1
    ins, outs = refs[:count], refs[count : 2 * count]
    send_sem, recv_sem, local_sem = refs[2 * count :]
    me = lax.axis_index("seq")
    mp = lax.axis_index("mp")
    barrier = pltpu.get_barrier_semaphore()
    for k in range(1, n):
        peer = lax.rem(me + k, n)
        pl.semaphore_signal(barrier, inc=1, device_id=(peer, mp), device_id_type=MESH)
    pl.semaphore_wait(barrier, n - 1)
    copies = []
    for a in range(count):
        for k in range(1, n):
            peer = lax.rem(me + k, n)
            src = ins[a] if gather else ins[a].at[peer]
            c = pltpu.make_async_remote_copy(
                src_ref=src,
                dst_ref=outs[a].at[me],
                send_sem=send_sem.at[a, k],
                recv_sem=recv_sem.at[a, k],
                device_id=(peer, mp),
                device_id_type=MESH,
            )
            c.start()
            copies.append(c)
    locals_ = []
    for a in range(count):
        src = ins[a] if gather else ins[a].at[me]
        c = pltpu.make_async_copy(src, outs[a].at[me], local_sem.at[a])
        c.start()
        locals_.append(c)
    for c in copies:
        c.wait()
    for c in locals_:
        c.wait()


def exchange(arrays, n, gather, collective_id):
    count = len(arrays)
    vmem = pl.BlockSpec(memory_space=pltpu.VMEM)
    out_shape = [
        jax.ShapeDtypeStruct(((n,) + x.shape) if gather else x.shape, x.dtype) for x in arrays
    ]
    return pl.pallas_call(
        functools.partial(exchange_kernel, n, gather),
        in_specs=[vmem] * count,
        out_specs=[vmem] * count,
        out_shape=out_shape,
        scratch_shapes=[
            pltpu.SemaphoreType.DMA((count, n)),
            pltpu.SemaphoreType.DMA((count, n)),
            pltpu.SemaphoreType.DMA((count,)),
        ],
        compiler_params=pltpu.CompilerParams(collective_id=collective_id, has_side_effects=True),
    )(*arrays)


def local(
    prompt_hidden,
    recompute_hidden,
    key_cache,
    value_cache,
    norm_gain,
    w_query,
    key_weight,
    value_weight,
    w_out,
    passage_owner,
    prompt_slot,
    prompt_length,
    recompute_count,
    recompute_index,
):
    prompt_rows = prompt_hidden.shape[0]
    recompute_rows = recompute_hidden.shape[0]
    query_rows = prompt_rows + recompute_rows
    passage_length = key_cache.shape[1]
    local_heads = w_query.shape[1] // HEAD_SIZE
    n_seq = passage_owner.shape[0]
    me = lax.axis_index("seq")
    scale = 1.0 / math.sqrt(HEAD_SIZE)

    seq_ids = jnp.arange(n_seq, dtype=jnp.int32)
    same_owner = passage_owner[:, None] == passage_owner[None, :]
    passage_rank = jnp.sum(
        jnp.where(same_owner & (seq_ids[None, :] < seq_ids[:, None]), 1, 0), axis=1
    ).astype(jnp.int32)
    held_count = jnp.sum(
        jnp.where(passage_owner[None, :] == prompt_slot[:, None], 1, 0), axis=1
    ).astype(jnp.int32)
    own_rank = passage_rank[me]
    own_owner = passage_owner[me]
    own_held = held_count[me]
    own_index = lax.dynamic_index_in_dim(recompute_index, me, 0, keepdims=False)
    own_length = prompt_length[me]
    own_count = recompute_count[me]

    prompt_pos = own_held * passage_length + jnp.arange(prompt_rows, dtype=jnp.int32)
    recompute_pos = own_rank * passage_length + own_index
    own_pos = jnp.concatenate([prompt_pos, recompute_pos])
    own_live = jnp.concatenate(
        [
            jnp.arange(prompt_rows, dtype=jnp.int32) < own_length,
            jnp.arange(recompute_rows, dtype=jnp.int32) < own_count,
        ]
    )

    rows_local = jnp.concatenate([prompt_hidden, recompute_hidden], axis=0)
    full_rows = lax.all_gather(rows_local, "mp", axis=1, tiled=True)
    normalized_hidden = normalize(full_rows, norm_gain)
    queries = (
        apply_rotation(
            jnp.dot(normalized_hidden, w_query, preferred_element_type=jnp.float32).reshape(
                query_rows, local_heads, HEAD_SIZE
            ),
            own_pos,
        )
        .astype(jnp.bfloat16)
    )
    fresh_keys = (
        apply_rotation(
            jnp.dot(normalized_hidden, key_weight, preferred_element_type=jnp.float32).reshape(
                query_rows, 1, HEAD_SIZE
            ),
            own_pos,
        )
        .astype(jnp.bfloat16)
        .reshape(query_rows, HEAD_SIZE)
    )
    fresh_values = jnp.dot(
        normalized_hidden, value_weight, preferred_element_type=jnp.float32
    ).astype(jnp.bfloat16)

    position_shift = jnp.full((passage_length,), own_rank * passage_length, jnp.int32)
    shifted_keys = (
        apply_rotation(
            key_cache[0].astype(jnp.float32).reshape(passage_length, 1, HEAD_SIZE),
            position_shift,
        )
        .astype(jnp.bfloat16)
        .reshape(passage_length, HEAD_SIZE)
    )
    chosen = (own_index[:, None] == jnp.arange(passage_length, dtype=jnp.int32)[None, :]) & (
        jnp.arange(recompute_rows, dtype=jnp.int32)[:, None] < own_count
    )
    replaced = jnp.any(chosen, axis=0)[:, None]
    fresh_pair = jnp.concatenate([fresh_keys[prompt_rows:], fresh_values[prompt_rows:]], axis=1)
    placed = lax.dot_general(
        chosen.astype(jnp.bfloat16),
        fresh_pair,
        (((0,), (0,)), ((), ())),
        preferred_element_type=jnp.float32,
    ).astype(jnp.bfloat16)
    passage_keys = jnp.where(replaced, placed[:, :HEAD_SIZE], shifted_keys)
    passage_values = jnp.where(replaced, placed[:, HEAD_SIZE:], value_cache[0])

    (all_queries,) = exchange(
        [queries.reshape(2, prompt_rows * local_heads, HEAD_SIZE)], n_seq, True, 0
    )
    q_blocks = all_queries.reshape(n_seq * 2, prompt_rows * local_heads, HEAD_SIZE)
    prompt_flag = jnp.where(prompt_slot == own_owner, 1, 0)
    recompute_flag = jnp.where(
        seq_ids == me, 2, jnp.where((passage_owner == own_owner) & (seq_ids > me), 1, 0)
    )
    flags = jnp.stack([prompt_flag, recompute_flag], axis=1).reshape(-1).astype(jnp.int32)
    lim = jnp.repeat(own_index, local_heads).reshape(-1, 1).astype(jnp.int32)
    acc, stats = passage_attention(flags, q_blocks, passage_keys, passage_values, lim)

    acc_back, stats_back = exchange(
        [
            acc.reshape(n_seq, 2, prompt_rows * local_heads, HEAD_SIZE),
            stats.reshape(n_seq, 2, 8, prompt_rows * local_heads),
        ],
        n_seq,
        False,
        1,
    )
    part_max = stats_back[:, :, 0].reshape(n_seq, query_rows, local_heads)
    part_tot = stats_back[:, :, 1].reshape(n_seq, query_rows, local_heads)
    part_acc = acc_back.reshape(n_seq, query_rows, local_heads, HEAD_SIZE).astype(jnp.float32)

    pq = queries[:prompt_rows].astype(jnp.float32)
    pk = fresh_keys[:prompt_rows].astype(jnp.float32)
    pv = fresh_values[:prompt_rows].astype(jnp.float32)
    ps = jnp.einsum("qhd,kd->qhk", pq, pk) * scale
    jj = jnp.arange(prompt_rows, dtype=jnp.int32)
    pvis = (jj[None, :] <= jj[:, None]) & (jj[None, :] < own_length)
    ps = jnp.where(pvis[:, None, :], ps, NEGATIVE_FLOOR)
    pmax = jnp.max(ps, axis=-1)
    pw = jnp.where(pvis[:, None, :], jnp.exp(ps - pmax[..., None]), 0.0)
    ptot = jnp.sum(pw, axis=-1)
    pacc = jnp.einsum("qhk,kd->qhd", pw.astype(jnp.bfloat16).astype(jnp.float32), pv)
    loc_max = jnp.concatenate(
        [pmax, jnp.full((recompute_rows, local_heads), NEGATIVE_FLOOR, jnp.float32)]
    )
    loc_tot = jnp.concatenate([ptot, jnp.zeros((recompute_rows, local_heads), jnp.float32)])
    loc_acc = jnp.concatenate(
        [pacc, jnp.zeros((recompute_rows, local_heads, HEAD_SIZE), jnp.float32)]
    )

    highest = jnp.maximum(jnp.max(part_max, axis=0), loc_max)
    part_scale = jnp.exp(part_max - highest[None])
    loc_scale = jnp.exp(loc_max - highest)
    accumulated = jnp.sum(part_acc * part_scale[..., None], axis=0) + loc_acc * loc_scale[..., None]
    totals = jnp.sum(part_tot * part_scale, axis=0) + loc_tot * loc_scale
    safe_totals = jnp.where(totals > 0, totals, 1.0)
    attention = jnp.where(
        own_live[:, None, None], accumulated / safe_totals[..., None], 0.0
    ).astype(jnp.bfloat16).reshape(query_rows, local_heads * HEAD_SIZE)
    projected = jnp.dot(attention, w_out, preferred_element_type=jnp.float32)
    combined = lax.psum_scatter(projected, "mp", scatter_dimension=1, tiled=True).astype(
        jnp.bfloat16
    )
    return (combined[:prompt_rows], combined[prompt_rows:])


def solution(mesh):
    return jax.shard_map(
        local,
        mesh=mesh,
        in_specs=(
            P("seq", "mp"),
            P("seq", "mp"),
            P("seq", None, "mp"),
            P("seq", None, "mp"),
            P(),
            P(None, "mp"),
            P(None, "mp"),
            P(None, "mp"),
            P("mp", None),
            P(),
            P(),
            P(),
            P(),
            P(),
        ),
        out_specs=(P("seq", "mp"), P("seq", "mp")),
        check_vma=False,
    )
```

```python
import functools
import math

import jax
import jax.numpy as jnp
from jax import lax
from jax.experimental import pallas as pl
from jax.experimental.pallas import tpu as pltpu
from jax.sharding import PartitionSpec as P

HEAD_SIZE = 128
NEGATIVE_FLOOR = -1e30


def apply_rotation(vectors, positions):
    half_width = vectors.shape[-1] // 2
    exponent = jnp.arange(half_width).astype(jnp.float32) * (2.0 / vectors.shape[-1])
    frequency = jnp.exp(-exponent * math.log(500000.0))
    angles = positions.astype(jnp.float32)[:, None] * frequency[None, :]
    cosines = jnp.cos(angles)[:, None, :]
    sines = jnp.sin(angles)[:, None, :]
    leading = vectors[..., :half_width]
    trailing = vectors[..., half_width:]
    return jnp.concatenate(
        [leading * cosines - trailing * sines, trailing * cosines + leading * sines], axis=-1
    )


def normalize(rows_in, norm_gain):
    values = rows_in.astype(jnp.float32)
    inverse_rms = lax.rsqrt(jnp.mean(values * values, axis=-1, keepdims=True) + 1e-05)
    return (values * inverse_rms * norm_gain).astype(jnp.bfloat16)


MESH = pl.DeviceIdType.MESH


def passage_kernel(flags_ref, q_ref, k_ref, v_ref, lim_ref, acc_ref, st_ref):
    nb, rows, _ = q_ref.shape
    keys = k_ref.shape[0]
    token = lax.broadcasted_iota(jnp.int32, (rows, keys), 1)
    sub = lax.broadcasted_iota(jnp.int32, (8, rows), 0)

    def body(b, carry):
        flag = flags_ref[b]

        @pl.when(flag == 0)
        def _():
            acc_ref[b] = jnp.zeros((rows, HEAD_SIZE), acc_ref.dtype)
            st_ref[b] = jnp.where(sub == 0, NEGATIVE_FLOOR, 0.0).astype(jnp.float32)

        @pl.when(flag > 0)
        def _():
            scores = lax.dot_general(
                q_ref[b], k_ref[...], (((1,), (1,)), ((), ())), preferred_element_type=jnp.float32
            ) * (1.0 / math.sqrt(HEAD_SIZE))
            limit = jnp.where(flag == 2, lim_ref[...], keys - 1)
            scores = jnp.where(token <= limit, scores, NEGATIVE_FLOOR)
            maxima = jnp.max(scores, axis=1, keepdims=True)
            weights = jnp.exp(scores - maxima)
            totals = jnp.sum(weights, axis=1, keepdims=True)
            acc_ref[b] = jnp.dot(
                weights.astype(jnp.bfloat16), v_ref[...], preferred_element_type=jnp.float32
            ).astype(acc_ref.dtype)
            m_row = jnp.transpose(jnp.broadcast_to(maxima, (rows, rows)))[0:8]
            l_row = jnp.transpose(jnp.broadcast_to(totals, (rows, rows)))[0:8]
            st_ref[b] = jnp.where(sub == 0, m_row, jnp.where(sub == 1, l_row, 0.0))

        return carry

    lax.fori_loop(0, nb, body, 0)


def passage_attention(flags, q_blocks, keys, values, lim):
    nb, rows, _ = q_blocks.shape
    vmem = pl.BlockSpec(memory_space=pltpu.VMEM)
    return pl.pallas_call(
        passage_kernel,
        in_specs=[pl.BlockSpec(memory_space=pltpu.SMEM), vmem, vmem, vmem, vmem],
        out_specs=[vmem, vmem],
        out_shape=[
            jax.ShapeDtypeStruct((nb, rows, HEAD_SIZE), jnp.bfloat16),
            jax.ShapeDtypeStruct((nb, 8, rows), jnp.float32),
        ],
    )(flags, q_blocks, keys, values, lim)


def exchange_kernel(n, gather, *refs):
    count = len(refs) // 2 - 1
    ins, outs = refs[:count], refs[count : 2 * count]
    send_sem, recv_sem, local_sem = refs[2 * count :]
    me = lax.axis_index("seq")
    mp = lax.axis_index("mp")
    barrier = pltpu.get_barrier_semaphore()
    for k in range(1, n):
        peer = lax.rem(me + k, n)
        pl.semaphore_signal(barrier, inc=1, device_id=(peer, mp), device_id_type=MESH)
    pl.semaphore_wait(barrier, n - 1)
    copies = []
    for a in range(count):
        for k in range(1, n):
            peer = lax.rem(me + k, n)
            src = ins[a] if gather else ins[a].at[peer]
            c = pltpu.make_async_remote_copy(
                src_ref=src,
                dst_ref=outs[a].at[me],
                send_sem=send_sem.at[a, k],
                recv_sem=recv_sem.at[a, k],
                device_id=(peer, mp),
                device_id_type=MESH,
            )
            c.start()
            copies.append(c)
    locals_ = []
    for a in range(count):
        src = ins[a] if gather else ins[a].at[me]
        c = pltpu.make_async_copy(src, outs[a].at[me], local_sem.at[a])
        c.start()
        locals_.append(c)
    for c in copies:
        c.wait()
    for c in locals_:
        c.wait()


def exchange(arrays, n, gather, collective_id):
    count = len(arrays)
    vmem = pl.BlockSpec(memory_space=pltpu.VMEM)
    out_shape = [
        jax.ShapeDtypeStruct(((n,) + x.shape) if gather else x.shape, x.dtype) for x in arrays
    ]
    return pl.pallas_call(
        functools.partial(exchange_kernel, n, gather),
        in_specs=[vmem] * count,
        out_specs=[vmem] * count,
        out_shape=out_shape,
        scratch_shapes=[
            pltpu.SemaphoreType.DMA((count, n)),
            pltpu.SemaphoreType.DMA((count, n)),
            pltpu.SemaphoreType.DMA((count,)),
        ],
        compiler_params=pltpu.CompilerParams(collective_id=collective_id, has_side_effects=True),
    )(*arrays)


def local(
    prompt_hidden,
    recompute_hidden,
    key_cache,
    value_cache,
    norm_gain,
    w_query,
    key_weight,
    value_weight,
    w_out,
    passage_owner,
    prompt_slot,
    prompt_length,
    recompute_count,
    recompute_index,
):
    prompt_rows = prompt_hidden.shape[0]
    recompute_rows = recompute_hidden.shape[0]
    query_rows = prompt_rows + recompute_rows
    passage_length = key_cache.shape[1]
    local_heads = w_query.shape[1] // HEAD_SIZE
    n_seq = passage_owner.shape[0]
    me = lax.axis_index("seq")
    scale = 1.0 / math.sqrt(HEAD_SIZE)

    seq_ids = jnp.arange(n_seq, dtype=jnp.int32)
    same_owner = passage_owner[:, None] == passage_owner[None, :]
    passage_rank = jnp.sum(
        jnp.where(same_owner & (seq_ids[None, :] < seq_ids[:, None]), 1, 0), axis=1
    ).astype(jnp.int32)
    held_count = jnp.sum(
        jnp.where(passage_owner[None, :] == prompt_slot[:, None], 1, 0), axis=1
    ).astype(jnp.int32)
    own_rank = passage_rank[me]
    own_owner = passage_owner[me]
    own_held = held_count[me]
    own_index = lax.dynamic_index_in_dim(recompute_index, me, 0, keepdims=False)
    own_length = prompt_length[me]
    own_count = recompute_count[me]

    prompt_pos = own_held * passage_length + jnp.arange(prompt_rows, dtype=jnp.int32)
    recompute_pos = own_rank * passage_length + own_index
    own_pos = jnp.concatenate([prompt_pos, recompute_pos])
    own_live = jnp.concatenate(
        [
            jnp.arange(prompt_rows, dtype=jnp.int32) < own_length,
            jnp.arange(recompute_rows, dtype=jnp.int32) < own_count,
        ]
    )

    rows_local = jnp.concatenate([prompt_hidden, recompute_hidden], axis=0)
    n_mp = w_out.shape[1] // rows_local.shape[1]
    gathered = lax.all_to_all(
        jnp.broadcast_to(rows_local[None], (n_mp,) + rows_local.shape), "mp", 0, 0, tiled=True
    )
    full_rows = jnp.transpose(gathered, (1, 0, 2)).reshape(query_rows, -1)
    normalized_hidden = normalize(full_rows, norm_gain)
    queries = (
        apply_rotation(
            jnp.dot(normalized_hidden, w_query, preferred_element_type=jnp.float32).reshape(
                query_rows, local_heads, HEAD_SIZE
            ),
            own_pos,
        )
        .astype(jnp.bfloat16)
    )
    fresh_keys = (
        apply_rotation(
            jnp.dot(normalized_hidden, key_weight, preferred_element_type=jnp.float32).reshape(
                query_rows, 1, HEAD_SIZE
            ),
            own_pos,
        )
        .astype(jnp.bfloat16)
        .reshape(query_rows, HEAD_SIZE)
    )
    fresh_values = jnp.dot(
        normalized_hidden, value_weight, preferred_element_type=jnp.float32
    ).astype(jnp.bfloat16)

    position_shift = jnp.full((passage_length,), own_rank * passage_length, jnp.int32)
    shifted_keys = (
        apply_rotation(
            key_cache[0].astype(jnp.float32).reshape(passage_length, 1, HEAD_SIZE),
            position_shift,
        )
        .astype(jnp.bfloat16)
        .reshape(passage_length, HEAD_SIZE)
    )
    chosen = (own_index[:, None] == jnp.arange(passage_length, dtype=jnp.int32)[None, :]) & (
        jnp.arange(recompute_rows, dtype=jnp.int32)[:, None] < own_count
    )
    replaced = jnp.any(chosen, axis=0)[:, None]
    fresh_pair = jnp.concatenate([fresh_keys[prompt_rows:], fresh_values[prompt_rows:]], axis=1)
    placed = lax.dot_general(
        chosen.astype(jnp.bfloat16),
        fresh_pair,
        (((0,), (0,)), ((), ())),
        preferred_element_type=jnp.float32,
    ).astype(jnp.bfloat16)
    passage_keys = jnp.where(replaced, placed[:, :HEAD_SIZE], shifted_keys)
    passage_values = jnp.where(replaced, placed[:, HEAD_SIZE:], value_cache[0])

    own_blocks = queries.reshape(1, 2, prompt_rows * local_heads, HEAD_SIZE)
    all_queries = lax.all_to_all(
        jnp.broadcast_to(own_blocks, (n_seq,) + own_blocks.shape[1:]), "seq", 0, 0, tiled=True
    )
    q_blocks = all_queries.reshape(n_seq * 2, prompt_rows * local_heads, HEAD_SIZE)
    prompt_flag = jnp.where(prompt_slot == own_owner, 1, 0)
    recompute_flag = jnp.where(
        seq_ids == me, 2, jnp.where((passage_owner == own_owner) & (seq_ids > me), 1, 0)
    )
    flags = jnp.stack([prompt_flag, recompute_flag], axis=1).reshape(-1).astype(jnp.int32)
    lim = jnp.repeat(own_index, local_heads).reshape(-1, 1).astype(jnp.int32)
    acc, stats = passage_attention(flags, q_blocks, passage_keys, passage_values, lim)

    acc_back = lax.all_to_all(
        acc.reshape(n_seq, 2, prompt_rows * local_heads, HEAD_SIZE), "seq", 0, 0, tiled=True
    )
    stats_back = lax.all_to_all(
        stats[:, 0:2].reshape(n_seq, 2, 2, prompt_rows * local_heads), "seq", 0, 0, tiled=True
    )
    part_max = stats_back[:, :, 0].reshape(n_seq, query_rows, local_heads)
    part_tot = stats_back[:, :, 1].reshape(n_seq, query_rows, local_heads)
    part_acc = acc_back.reshape(n_seq, query_rows, local_heads, HEAD_SIZE).astype(jnp.float32)

    pq = queries[:prompt_rows].astype(jnp.float32)
    pk = fresh_keys[:prompt_rows].astype(jnp.float32)
    pv = fresh_values[:prompt_rows].astype(jnp.float32)
    ps = jnp.einsum("qhd,kd->qhk", pq, pk) * scale
    jj = jnp.arange(prompt_rows, dtype=jnp.int32)
    pvis = (jj[None, :] <= jj[:, None]) & (jj[None, :] < own_length)
    ps = jnp.where(pvis[:, None, :], ps, NEGATIVE_FLOOR)
    pmax = jnp.max(ps, axis=-1)
    pw = jnp.where(pvis[:, None, :], jnp.exp(ps - pmax[..., None]), 0.0)
    ptot = jnp.sum(pw, axis=-1)
    pacc = jnp.einsum("qhk,kd->qhd", pw.astype(jnp.bfloat16).astype(jnp.float32), pv)
    loc_max = jnp.concatenate(
        [pmax, jnp.full((recompute_rows, local_heads), NEGATIVE_FLOOR, jnp.float32)]
    )
    loc_tot = jnp.concatenate([ptot, jnp.zeros((recompute_rows, local_heads), jnp.float32)])
    loc_acc = jnp.concatenate(
        [pacc, jnp.zeros((recompute_rows, local_heads, HEAD_SIZE), jnp.float32)]
    )

    highest = jnp.maximum(jnp.max(part_max, axis=0), loc_max)
    part_scale = jnp.exp(part_max - highest[None])
    loc_scale = jnp.exp(loc_max - highest)
    accumulated = jnp.sum(part_acc * part_scale[..., None], axis=0) + loc_acc * loc_scale[..., None]
    totals = jnp.sum(part_tot * part_scale, axis=0) + loc_tot * loc_scale
    safe_totals = jnp.where(totals > 0, totals, 1.0)
    attention = jnp.where(
        own_live[:, None, None], accumulated / safe_totals[..., None], 0.0
    ).astype(jnp.bfloat16).reshape(query_rows, local_heads * HEAD_SIZE)
    projected = jnp.dot(attention, w_out, preferred_element_type=jnp.float32)
    pieces = jnp.transpose(projected.reshape(query_rows, n_mp, -1), (1, 0, 2))
    combined = jnp.sum(lax.all_to_all(pieces, "mp", 0, 0, tiled=True), axis=0).astype(jnp.bfloat16)
    return (combined[:prompt_rows], combined[prompt_rows:])


def solution(mesh):
    return jax.shard_map(
        local,
        mesh=mesh,
        in_specs=(
            P("seq", "mp"),
            P("seq", "mp"),
            P("seq", None, "mp"),
            P("seq", None, "mp"),
            P(),
            P(None, "mp"),
            P(None, "mp"),
            P(None, "mp"),
            P("mp", None),
            P(),
            P(),
            P(),
            P(),
            P(),
        ),
        out_specs=(P("seq", "mp"), P("seq", "mp")),
        check_vma=False,
    )
```

```python
import functools
import math

import jax
import jax.numpy as jnp
from jax import lax
from jax.experimental import pallas as pl
from jax.experimental.pallas import tpu as pltpu
from jax.sharding import PartitionSpec as P

HEAD_SIZE = 128
NEGATIVE_FLOOR = -1e30


def apply_rotation(vectors, positions):
    half_width = vectors.shape[-1] // 2
    exponent = jnp.arange(half_width).astype(jnp.float32) * (2.0 / vectors.shape[-1])
    frequency = jnp.exp(-exponent * math.log(500000.0))
    angles = positions.astype(jnp.float32)[:, None] * frequency[None, :]
    cosines = jnp.cos(angles)[:, None, :]
    sines = jnp.sin(angles)[:, None, :]
    leading = vectors[..., :half_width]
    trailing = vectors[..., half_width:]
    return jnp.concatenate(
        [leading * cosines - trailing * sines, trailing * cosines + leading * sines], axis=-1
    )


def normalize(rows_in, norm_gain):
    values = rows_in.astype(jnp.float32)
    inverse_rms = lax.rsqrt(jnp.mean(values * values, axis=-1, keepdims=True) + 1e-05)
    return (values * inverse_rms * norm_gain).astype(jnp.bfloat16)


MESH = pl.DeviceIdType.MESH


def passage_kernel(flags_ref, q_ref, k_ref, v_ref, lim_ref, out_ref):
    nb, rows, _ = q_ref.shape
    keys = k_ref.shape[0]
    token = lax.broadcasted_iota(jnp.int32, (rows, keys), 1)
    sub = lax.broadcasted_iota(jnp.int32, (16, rows), 0)

    def split(m_row, l_row):
        m_hi = m_row.astype(jnp.bfloat16).astype(jnp.float32)
        l_hi = l_row.astype(jnp.bfloat16).astype(jnp.float32)
        st = jnp.where(
            sub == 0,
            m_row,
            jnp.where(
                sub == 1,
                m_row - m_hi,
                jnp.where(sub == 2, l_row, jnp.where(sub == 3, l_row - l_hi, 0.0)),
            ),
        )
        return st.astype(jnp.bfloat16)

    def body(b, carry):
        flag = flags_ref[b]

        @pl.when(flag == 0)
        def _():
            out_ref[b, 0:rows] = jnp.zeros((rows, HEAD_SIZE), out_ref.dtype)
            floor = jnp.full((16, rows), NEGATIVE_FLOOR, jnp.float32)
            out_ref[b, rows:] = split(floor, jnp.zeros((16, rows), jnp.float32))

        @pl.when(flag > 0)
        def _():
            scores = lax.dot_general(
                q_ref[b], k_ref[...], (((1,), (1,)), ((), ())), preferred_element_type=jnp.float32
            ) * (1.0 / math.sqrt(HEAD_SIZE))
            limit = jnp.where(flag == 2, lim_ref[...], keys - 1)
            scores = jnp.where(token <= limit, scores, NEGATIVE_FLOOR)
            maxima = jnp.max(scores, axis=1, keepdims=True)
            weights = jnp.exp(scores - maxima)
            totals = jnp.sum(weights, axis=1, keepdims=True)
            out_ref[b, 0:rows] = jnp.dot(
                weights.astype(jnp.bfloat16), v_ref[...], preferred_element_type=jnp.float32
            ).astype(out_ref.dtype)
            m_row = jnp.transpose(jnp.broadcast_to(maxima, (rows, rows)))[0:16]
            l_row = jnp.transpose(jnp.broadcast_to(totals, (rows, rows)))[0:16]
            out_ref[b, rows:] = split(m_row, l_row)

        return carry

    lax.fori_loop(0, nb, body, 0)


def passage_attention(flags, q_blocks, keys, values, lim):
    nb, rows, _ = q_blocks.shape
    vmem = pl.BlockSpec(memory_space=pltpu.VMEM)
    return pl.pallas_call(
        passage_kernel,
        in_specs=[pl.BlockSpec(memory_space=pltpu.SMEM), vmem, vmem, vmem, vmem],
        out_specs=vmem,
        out_shape=jax.ShapeDtypeStruct((nb, rows + 16, HEAD_SIZE), jnp.bfloat16),
    )(flags, q_blocks, keys, values, lim)


def mp_gather_kernel(n, x_ref, y_ref, send_sem, recv_sem, local_sem):
    me = lax.axis_index("mp")
    row = lax.axis_index("seq")
    width = x_ref.shape[1]
    barrier = pltpu.get_barrier_semaphore()
    for k in range(1, n):
        peer = lax.rem(me + k, n)
        pl.semaphore_signal(barrier, inc=1, device_id=(row, peer), device_id_type=MESH)
    pl.semaphore_wait(barrier, n - 1)
    cols = pl.ds(pl.multiple_of(me * width, width), width)
    copies = []
    for k in range(1, n):
        peer = lax.rem(me + k, n)
        c = pltpu.make_async_remote_copy(
            src_ref=x_ref,
            dst_ref=y_ref.at[:, cols],
            send_sem=send_sem.at[k],
            recv_sem=recv_sem.at[k],
            device_id=(row, peer),
            device_id_type=MESH,
        )
        c.start()
        copies.append(c)
    own = pltpu.make_async_copy(x_ref, y_ref.at[:, cols], local_sem)
    own.start()
    for c in copies:
        c.wait()
    own.wait()


def mp_gather(x, n):
    vmem = pl.BlockSpec(memory_space=pltpu.VMEM)
    return pl.pallas_call(
        functools.partial(mp_gather_kernel, n),
        in_specs=[vmem],
        out_specs=vmem,
        out_shape=jax.ShapeDtypeStruct((x.shape[0], x.shape[1] * n), x.dtype),
        scratch_shapes=[
            pltpu.SemaphoreType.DMA((n,)),
            pltpu.SemaphoreType.DMA((n,)),
            pltpu.SemaphoreType.DMA(()),
        ],
        compiler_params=pltpu.CompilerParams(collective_id=0, has_side_effects=True),
    )(x)


def mp_scatter_kernel(n, x_ref, y_ref, send_sem, recv_sem, local_sem):
    me = lax.axis_index("mp")
    row = lax.axis_index("seq")
    width = y_ref.shape[2]
    barrier = pltpu.get_barrier_semaphore()
    for k in range(1, n):
        peer = lax.rem(me + k, n)
        pl.semaphore_signal(barrier, inc=1, device_id=(row, peer), device_id_type=MESH)
    pl.semaphore_wait(barrier, n - 1)
    copies = []
    for k in range(1, n):
        peer = lax.rem(me + k, n)
        c = pltpu.make_async_remote_copy(
            src_ref=x_ref.at[:, pl.ds(pl.multiple_of(peer * width, width), width)],
            dst_ref=y_ref.at[me],
            send_sem=send_sem.at[k],
            recv_sem=recv_sem.at[k],
            device_id=(row, peer),
            device_id_type=MESH,
        )
        c.start()
        copies.append(c)
    own = pltpu.make_async_copy(
        x_ref.at[:, pl.ds(pl.multiple_of(me * width, width), width)], y_ref.at[me], local_sem
    )
    own.start()
    for c in copies:
        c.wait()
    own.wait()


def mp_scatter(x, n):
    vmem = pl.BlockSpec(memory_space=pltpu.VMEM)
    return pl.pallas_call(
        functools.partial(mp_scatter_kernel, n),
        in_specs=[vmem],
        out_specs=vmem,
        out_shape=jax.ShapeDtypeStruct((n, x.shape[0], x.shape[1] // n), x.dtype),
        scratch_shapes=[
            pltpu.SemaphoreType.DMA((n,)),
            pltpu.SemaphoreType.DMA((n,)),
            pltpu.SemaphoreType.DMA(()),
        ],
        compiler_params=pltpu.CompilerParams(collective_id=1, has_side_effects=True),
    )(x)


def local(
    prompt_hidden,
    recompute_hidden,
    key_cache,
    value_cache,
    norm_gain,
    w_query,
    key_weight,
    value_weight,
    w_out,
    passage_owner,
    prompt_slot,
    prompt_length,
    recompute_count,
    recompute_index,
):
    prompt_rows = prompt_hidden.shape[0]
    recompute_rows = recompute_hidden.shape[0]
    query_rows = prompt_rows + recompute_rows
    passage_length = key_cache.shape[1]
    local_heads = w_query.shape[1] // HEAD_SIZE
    n_seq = passage_owner.shape[0]
    me = lax.axis_index("seq")
    scale = 1.0 / math.sqrt(HEAD_SIZE)

    seq_ids = jnp.arange(n_seq, dtype=jnp.int32)
    same_owner = passage_owner[:, None] == passage_owner[None, :]
    passage_rank = jnp.sum(
        jnp.where(same_owner & (seq_ids[None, :] < seq_ids[:, None]), 1, 0), axis=1
    ).astype(jnp.int32)
    held_count = jnp.sum(
        jnp.where(passage_owner[None, :] == prompt_slot[:, None], 1, 0), axis=1
    ).astype(jnp.int32)
    own_rank = passage_rank[me]
    own_owner = passage_owner[me]
    own_held = held_count[me]
    own_index = lax.dynamic_index_in_dim(recompute_index, me, 0, keepdims=False)
    own_length = prompt_length[me]
    own_count = recompute_count[me]

    prompt_pos = own_held * passage_length + jnp.arange(prompt_rows, dtype=jnp.int32)
    recompute_pos = own_rank * passage_length + own_index
    own_pos = jnp.concatenate([prompt_pos, recompute_pos])
    own_live = jnp.concatenate(
        [
            jnp.arange(prompt_rows, dtype=jnp.int32) < own_length,
            jnp.arange(recompute_rows, dtype=jnp.int32) < own_count,
        ]
    )

    rows_local = jnp.concatenate([prompt_hidden, recompute_hidden], axis=0)
    n_mp = w_out.shape[1] // rows_local.shape[1]
    full_rows = mp_gather(rows_local, n_mp)
    normalized_hidden = normalize(full_rows, norm_gain)
    queries = (
        apply_rotation(
            jnp.dot(normalized_hidden, w_query, preferred_element_type=jnp.float32).reshape(
                query_rows, local_heads, HEAD_SIZE
            ),
            own_pos,
        )
        .astype(jnp.bfloat16)
    )
    fresh_keys = (
        apply_rotation(
            jnp.dot(normalized_hidden, key_weight, preferred_element_type=jnp.float32).reshape(
                query_rows, 1, HEAD_SIZE
            ),
            own_pos,
        )
        .astype(jnp.bfloat16)
        .reshape(query_rows, HEAD_SIZE)
    )
    fresh_values = jnp.dot(
        normalized_hidden, value_weight, preferred_element_type=jnp.float32
    ).astype(jnp.bfloat16)

    position_shift = jnp.full((passage_length,), own_rank * passage_length, jnp.int32)
    shifted_keys = (
        apply_rotation(
            key_cache[0].astype(jnp.float32).reshape(passage_length, 1, HEAD_SIZE),
            position_shift,
        )
        .astype(jnp.bfloat16)
        .reshape(passage_length, HEAD_SIZE)
    )
    chosen = (own_index[:, None] == jnp.arange(passage_length, dtype=jnp.int32)[None, :]) & (
        jnp.arange(recompute_rows, dtype=jnp.int32)[:, None] < own_count
    )
    replaced = jnp.any(chosen, axis=0)[:, None]
    fresh_pair = jnp.concatenate([fresh_keys[prompt_rows:], fresh_values[prompt_rows:]], axis=1)
    placed = lax.dot_general(
        chosen.astype(jnp.bfloat16),
        fresh_pair,
        (((0,), (0,)), ((), ())),
        preferred_element_type=jnp.float32,
    ).astype(jnp.bfloat16)
    passage_keys = jnp.where(replaced, placed[:, :HEAD_SIZE], shifted_keys)
    passage_values = jnp.where(replaced, placed[:, HEAD_SIZE:], value_cache[0])

    own_blocks = queries.reshape(1, 2, prompt_rows * local_heads, HEAD_SIZE)
    all_queries = lax.all_to_all(
        jnp.broadcast_to(own_blocks, (n_seq,) + own_blocks.shape[1:]), "seq", 0, 0, tiled=True
    )
    q_blocks = all_queries.reshape(n_seq * 2, prompt_rows * local_heads, HEAD_SIZE)
    prompt_flag = jnp.where(prompt_slot == own_owner, 1, 0)
    recompute_flag = jnp.where(
        seq_ids == me, 2, jnp.where((passage_owner == own_owner) & (seq_ids > me), 1, 0)
    )
    flags = jnp.stack([prompt_flag, recompute_flag], axis=1).reshape(-1).astype(jnp.int32)
    lim = jnp.repeat(own_index, local_heads).reshape(-1, 1).astype(jnp.int32)
    packed = passage_attention(flags, q_blocks, passage_keys, passage_values, lim)
    block_rows = packed.shape[1]

    back = lax.all_to_all(
        packed.reshape(n_seq, 2, block_rows, HEAD_SIZE), "seq", 0, 0, tiled=True
    )
    rows128 = prompt_rows * local_heads
    stats_back = back[:, :, rows128 : rows128 + 4].astype(jnp.float32)
    part_max = (stats_back[:, :, 0] + stats_back[:, :, 1]).reshape(n_seq, query_rows, local_heads)
    part_tot = (stats_back[:, :, 2] + stats_back[:, :, 3]).reshape(n_seq, query_rows, local_heads)
    part_acc = (
        back[:, :, :rows128].reshape(n_seq, query_rows, local_heads, HEAD_SIZE).astype(jnp.float32)
    )

    pq = queries[:prompt_rows].astype(jnp.float32)
    pk = fresh_keys[:prompt_rows].astype(jnp.float32)
    pv = fresh_values[:prompt_rows].astype(jnp.float32)
    ps = jnp.einsum("qhd,kd->qhk", pq, pk) * scale
    jj = jnp.arange(prompt_rows, dtype=jnp.int32)
    pvis = (jj[None, :] <= jj[:, None]) & (jj[None, :] < own_length)
    ps = jnp.where(pvis[:, None, :], ps, NEGATIVE_FLOOR)
    pmax = jnp.max(ps, axis=-1)
    pw = jnp.where(pvis[:, None, :], jnp.exp(ps - pmax[..., None]), 0.0)
    ptot = jnp.sum(pw, axis=-1)
    pacc = jnp.einsum("qhk,kd->qhd", pw.astype(jnp.bfloat16).astype(jnp.float32), pv)
    loc_max = jnp.concatenate(
        [pmax, jnp.full((recompute_rows, local_heads), NEGATIVE_FLOOR, jnp.float32)]
    )
    loc_tot = jnp.concatenate([ptot, jnp.zeros((recompute_rows, local_heads), jnp.float32)])
    loc_acc = jnp.concatenate(
        [pacc, jnp.zeros((recompute_rows, local_heads, HEAD_SIZE), jnp.float32)]
    )

    highest = jnp.maximum(jnp.max(part_max, axis=0), loc_max)
    part_scale = jnp.exp(part_max - highest[None])
    loc_scale = jnp.exp(loc_max - highest)
    accumulated = jnp.sum(part_acc * part_scale[..., None], axis=0) + loc_acc * loc_scale[..., None]
    totals = jnp.sum(part_tot * part_scale, axis=0) + loc_tot * loc_scale
    safe_totals = jnp.where(totals > 0, totals, 1.0)
    attention = jnp.where(
        own_live[:, None, None], accumulated / safe_totals[..., None], 0.0
    ).astype(jnp.bfloat16).reshape(query_rows, local_heads * HEAD_SIZE)
    projected = jnp.dot(attention, w_out, preferred_element_type=jnp.float32)
    combined = jnp.sum(mp_scatter(projected, n_mp), axis=0).astype(jnp.bfloat16)
    return (combined[:prompt_rows], combined[prompt_rows:])


def solution(mesh):
    return jax.shard_map(
        local,
        mesh=mesh,
        in_specs=(
            P("seq", "mp"),
            P("seq", "mp"),
            P("seq", None, "mp"),
            P("seq", None, "mp"),
            P(),
            P(None, "mp"),
            P(None, "mp"),
            P(None, "mp"),
            P("mp", None),
            P(),
            P(),
            P(),
            P(),
            P(),
        ),
        out_specs=(P("seq", "mp"), P("seq", "mp")),
        check_vma=False,
    )
```

```python
import functools
import math

import jax
import jax.numpy as jnp
from jax import lax
from jax.experimental import pallas as pl
from jax.experimental.pallas import tpu as pltpu
from jax.sharding import PartitionSpec as P

HEAD_SIZE = 128
NEGATIVE_FLOOR = -1e30


def apply_rotation(vectors, positions):
    half_width = vectors.shape[-1] // 2
    exponent = jnp.arange(half_width).astype(jnp.float32) * (2.0 / vectors.shape[-1])
    frequency = jnp.exp(-exponent * math.log(500000.0))
    angles = positions.astype(jnp.float32)[:, None] * frequency[None, :]
    cosines = jnp.cos(angles)[:, None, :]
    sines = jnp.sin(angles)[:, None, :]
    leading = vectors[..., :half_width]
    trailing = vectors[..., half_width:]
    return jnp.concatenate(
        [leading * cosines - trailing * sines, trailing * cosines + leading * sines], axis=-1
    )


def normalize(rows_in, norm_gain):
    values = rows_in.astype(jnp.float32)
    inverse_rms = lax.rsqrt(jnp.mean(values * values, axis=-1, keepdims=True) + 1e-05)
    return (values * inverse_rms * norm_gain).astype(jnp.bfloat16)


MESH = pl.DeviceIdType.MESH


def passage_kernel(nx, nz, flags_ref, q_ref, k_ref, v_ref, lim_ref, out_ref):
    nb, rows, _ = q_ref.shape
    keys = k_ref.shape[0]
    token = lax.broadcasted_iota(jnp.int32, (rows, keys), 1)
    sub = lax.broadcasted_iota(jnp.int32, (16, rows), 0)

    def split(m_row, l_row):
        m_hi = m_row.astype(jnp.bfloat16).astype(jnp.float32)
        l_hi = l_row.astype(jnp.bfloat16).astype(jnp.float32)
        st = jnp.where(
            sub == 0,
            m_row,
            jnp.where(
                sub == 1,
                m_row - m_hi,
                jnp.where(sub == 2, l_row, jnp.where(sub == 3, l_row - l_hi, 0.0)),
            ),
        )
        return st.astype(jnp.bfloat16)

    def body(b, carry):
        flag = flags_ref[b]

        @pl.when(flag == 0)
        def _():
            out_ref[b, 0:rows] = jnp.zeros((rows, HEAD_SIZE), out_ref.dtype)
            floor = jnp.full((16, rows), NEGATIVE_FLOOR, jnp.float32)
            out_ref[b, rows:] = split(floor, jnp.zeros((16, rows), jnp.float32))

        @pl.when(flag > 0)
        def _():
            d = b // 2
            stored = ((d % nz) * nx + d // nz) * 2 + b % 2
            scores = lax.dot_general(
                q_ref[stored], k_ref[...], (((1,), (1,)), ((), ())), preferred_element_type=jnp.float32
            ) * (1.0 / math.sqrt(HEAD_SIZE))
            limit = jnp.where(flag == 2, lim_ref[...], keys - 1)
            scores = jnp.where(token <= limit, scores, NEGATIVE_FLOOR)
            maxima = jnp.max(scores, axis=1, keepdims=True)
            weights = jnp.exp(scores - maxima)
            totals = jnp.sum(weights, axis=1, keepdims=True)
            out_ref[b, 0:rows] = jnp.dot(
                weights.astype(jnp.bfloat16), v_ref[...], preferred_element_type=jnp.float32
            ).astype(out_ref.dtype)
            m_row = jnp.transpose(jnp.broadcast_to(maxima, (rows, rows)))[0:16]
            l_row = jnp.transpose(jnp.broadcast_to(totals, (rows, rows)))[0:16]
            out_ref[b, rows:] = split(m_row, l_row)

        return carry

    lax.fori_loop(0, nb, body, 0)


def passage_attention(nx, nz, flags, q_blocks, keys, values, lim):
    nb, rows, _ = q_blocks.shape
    vmem = pl.BlockSpec(memory_space=pltpu.VMEM)
    return pl.pallas_call(
        functools.partial(passage_kernel, nx, nz),
        in_specs=[pl.BlockSpec(memory_space=pltpu.SMEM), vmem, vmem, vmem, vmem],
        out_specs=vmem,
        out_shape=jax.ShapeDtypeStruct((nb, rows + 16, HEAD_SIZE), jnp.bfloat16),
    )(flags, q_blocks, keys, values, lim)


def mp_gather_kernel(n, x_ref, y_ref, send_sem, recv_sem, local_sem):
    me = lax.axis_index("mp")
    row = lax.axis_index("seq")
    width = x_ref.shape[1]
    barrier = pltpu.get_barrier_semaphore()
    for k in range(1, n):
        peer = lax.rem(me + k, n)
        pl.semaphore_signal(barrier, inc=1, device_id=(row, peer), device_id_type=MESH)
    pl.semaphore_wait(barrier, n - 1)
    cols = pl.ds(pl.multiple_of(me * width, width), width)
    copies = []
    for k in range(1, n):
        peer = lax.rem(me + k, n)
        c = pltpu.make_async_remote_copy(
            src_ref=x_ref,
            dst_ref=y_ref.at[:, cols],
            send_sem=send_sem.at[k],
            recv_sem=recv_sem.at[k],
            device_id=(row, peer),
            device_id_type=MESH,
        )
        c.start()
        copies.append(c)
    own = pltpu.make_async_copy(x_ref, y_ref.at[:, cols], local_sem)
    own.start()
    for c in copies:
        c.wait()
    own.wait()


def mp_gather(x, n):
    vmem = pl.BlockSpec(memory_space=pltpu.VMEM)
    return pl.pallas_call(
        functools.partial(mp_gather_kernel, n),
        in_specs=[vmem],
        out_specs=vmem,
        out_shape=jax.ShapeDtypeStruct((x.shape[0], x.shape[1] * n), x.dtype),
        scratch_shapes=[
            pltpu.SemaphoreType.DMA((n,)),
            pltpu.SemaphoreType.DMA((n,)),
            pltpu.SemaphoreType.DMA(()),
        ],
        compiler_params=pltpu.CompilerParams(collective_id=0, has_side_effects=True),
    )(x)


def mp_scatter_kernel(n, x_ref, y_ref, send_sem, recv_sem, local_sem):
    me = lax.axis_index("mp")
    row = lax.axis_index("seq")
    width = y_ref.shape[2]
    barrier = pltpu.get_barrier_semaphore()
    for k in range(1, n):
        peer = lax.rem(me + k, n)
        pl.semaphore_signal(barrier, inc=1, device_id=(row, peer), device_id_type=MESH)
    pl.semaphore_wait(barrier, n - 1)
    copies = []
    for k in range(1, n):
        peer = lax.rem(me + k, n)
        c = pltpu.make_async_remote_copy(
            src_ref=x_ref.at[:, pl.ds(pl.multiple_of(peer * width, width), width)],
            dst_ref=y_ref.at[me],
            send_sem=send_sem.at[k],
            recv_sem=recv_sem.at[k],
            device_id=(row, peer),
            device_id_type=MESH,
        )
        c.start()
        copies.append(c)
    own = pltpu.make_async_copy(
        x_ref.at[:, pl.ds(pl.multiple_of(me * width, width), width)], y_ref.at[me], local_sem
    )
    own.start()
    for c in copies:
        c.wait()
    own.wait()


def mp_scatter(x, n):
    vmem = pl.BlockSpec(memory_space=pltpu.VMEM)
    return pl.pallas_call(
        functools.partial(mp_scatter_kernel, n),
        in_specs=[vmem],
        out_specs=vmem,
        out_shape=jax.ShapeDtypeStruct((n, x.shape[0], x.shape[1] // n), x.dtype),
        scratch_shapes=[
            pltpu.SemaphoreType.DMA((n,)),
            pltpu.SemaphoreType.DMA((n,)),
            pltpu.SemaphoreType.DMA(()),
        ],
        compiler_params=pltpu.CompilerParams(collective_id=1, has_side_effects=True),
    )(x)


def relay_gather_kernel(nx, nz, x_ref, y_ref, sx_send, sx_recv, zp_send, zp_recv, zm_send, zm_recv, own_sem):
    me = lax.axis_index("seq")
    mp = lax.axis_index("mp")
    x = me // nz
    z = me % nz
    up = lax.rem(z + 1, nz)
    down = lax.rem(z + nz - 1, nz)
    barrier = pltpu.get_barrier_semaphore()
    peers = [(lax.rem(x + k, nx) * nz + z, mp) for k in range(1, nx)]
    peers += [(x * nz + up, mp), (x * nz + down, mp)]
    for p in peers:
        pl.semaphore_signal(barrier, inc=1, device_id=p, device_id_type=MESH)
    pl.semaphore_wait(barrier, len(peers))

    slot = z * nx + x
    first = []
    for k in range(1, nx):
        c = pltpu.make_async_remote_copy(
            src_ref=x_ref,
            dst_ref=y_ref.at[slot],
            send_sem=sx_send.at[k],
            recv_sem=sx_recv.at[k],
            device_id=peers[k - 1],
            device_id_type=MESH,
        )
        c.start()
        first.append(c)
    own = pltpu.make_async_copy(x_ref, y_ref.at[slot], own_sem)
    own.start()
    for c in first:
        c.wait()
    own.wait()

    plus_steps = nz // 2
    minus_steps = nz - 1 - plus_steps
    sent = []
    for t in range(1, plus_steps + 1):
        step = []
        column = lax.rem(z - (t - 1) + nz, nz)
        bundle = pl.ds(pl.multiple_of(column * nx, nx), nx)
        c = pltpu.make_async_remote_copy(
            src_ref=y_ref.at[bundle],
            dst_ref=y_ref.at[bundle],
            send_sem=zp_send.at[t],
            recv_sem=zp_recv.at[t],
            device_id=(x * nz + up, mp),
            device_id_type=MESH,
        )
        c.start()
        step.append(c)
        if t <= minus_steps:
            column = lax.rem(z + (t - 1), nz)
            bundle = pl.ds(pl.multiple_of(column * nx, nx), nx)
            c = pltpu.make_async_remote_copy(
                src_ref=y_ref.at[bundle],
                dst_ref=y_ref.at[bundle],
                send_sem=zm_send.at[t],
                recv_sem=zm_recv.at[t],
                device_id=(x * nz + down, mp),
                device_id_type=MESH,
            )
            c.start()
            step.append(c)
        for c in step:
            c.wait_recv()
        sent += step
    for c in sent:
        c.wait_send()


def relay_gather(x, nx, nz):
    vmem = pl.BlockSpec(memory_space=pltpu.VMEM)
    plus_steps = nz // 2
    minus_steps = nz - 1 - plus_steps
    return pl.pallas_call(
        functools.partial(relay_gather_kernel, nx, nz),
        in_specs=[vmem],
        out_specs=vmem,
        out_shape=jax.ShapeDtypeStruct((nx * nz,) + x.shape, x.dtype),
        scratch_shapes=[
            pltpu.SemaphoreType.DMA((nx,)),
            pltpu.SemaphoreType.DMA((nx,)),
            pltpu.SemaphoreType.DMA((plus_steps + 1,)),
            pltpu.SemaphoreType.DMA((plus_steps + 1,)),
            pltpu.SemaphoreType.DMA((minus_steps + 1,)),
            pltpu.SemaphoreType.DMA((minus_steps + 1,)),
            pltpu.SemaphoreType.DMA(()),
        ],
        compiler_params=pltpu.CompilerParams(collective_id=2, has_side_effects=True),
    )(x)


def local(
    prompt_hidden,
    recompute_hidden,
    key_cache,
    value_cache,
    norm_gain,
    w_query,
    key_weight,
    value_weight,
    w_out,
    passage_owner,
    prompt_slot,
    prompt_length,
    recompute_count,
    recompute_index,
):
    prompt_rows = prompt_hidden.shape[0]
    recompute_rows = recompute_hidden.shape[0]
    query_rows = prompt_rows + recompute_rows
    passage_length = key_cache.shape[1]
    local_heads = w_query.shape[1] // HEAD_SIZE
    n_seq = passage_owner.shape[0]
    me = lax.axis_index("seq")
    scale = 1.0 / math.sqrt(HEAD_SIZE)

    seq_ids = jnp.arange(n_seq, dtype=jnp.int32)
    same_owner = passage_owner[:, None] == passage_owner[None, :]
    passage_rank = jnp.sum(
        jnp.where(same_owner & (seq_ids[None, :] < seq_ids[:, None]), 1, 0), axis=1
    ).astype(jnp.int32)
    held_count = jnp.sum(
        jnp.where(passage_owner[None, :] == prompt_slot[:, None], 1, 0), axis=1
    ).astype(jnp.int32)
    own_rank = passage_rank[me]
    own_owner = passage_owner[me]
    own_held = held_count[me]
    own_index = lax.dynamic_index_in_dim(recompute_index, me, 0, keepdims=False)
    own_length = prompt_length[me]
    own_count = recompute_count[me]

    prompt_pos = own_held * passage_length + jnp.arange(prompt_rows, dtype=jnp.int32)
    recompute_pos = own_rank * passage_length + own_index
    own_pos = jnp.concatenate([prompt_pos, recompute_pos])
    own_live = jnp.concatenate(
        [
            jnp.arange(prompt_rows, dtype=jnp.int32) < own_length,
            jnp.arange(recompute_rows, dtype=jnp.int32) < own_count,
        ]
    )

    rows_local = jnp.concatenate([prompt_hidden, recompute_hidden], axis=0)
    n_mp = w_out.shape[1] // rows_local.shape[1]
    full_rows = mp_gather(rows_local, n_mp)
    normalized_hidden = normalize(full_rows, norm_gain)
    queries = (
        apply_rotation(
            jnp.dot(normalized_hidden, w_query, preferred_element_type=jnp.float32).reshape(
                query_rows, local_heads, HEAD_SIZE
            ),
            own_pos,
        )
        .astype(jnp.bfloat16)
    )
    fresh_keys = (
        apply_rotation(
            jnp.dot(normalized_hidden, key_weight, preferred_element_type=jnp.float32).reshape(
                query_rows, 1, HEAD_SIZE
            ),
            own_pos,
        )
        .astype(jnp.bfloat16)
        .reshape(query_rows, HEAD_SIZE)
    )
    fresh_values = jnp.dot(
        normalized_hidden, value_weight, preferred_element_type=jnp.float32
    ).astype(jnp.bfloat16)

    position_shift = jnp.full((passage_length,), own_rank * passage_length, jnp.int32)
    shifted_keys = (
        apply_rotation(
            key_cache[0].astype(jnp.float32).reshape(passage_length, 1, HEAD_SIZE),
            position_shift,
        )
        .astype(jnp.bfloat16)
        .reshape(passage_length, HEAD_SIZE)
    )
    chosen = (own_index[:, None] == jnp.arange(passage_length, dtype=jnp.int32)[None, :]) & (
        jnp.arange(recompute_rows, dtype=jnp.int32)[:, None] < own_count
    )
    replaced = jnp.any(chosen, axis=0)[:, None]
    fresh_pair = jnp.concatenate([fresh_keys[prompt_rows:], fresh_values[prompt_rows:]], axis=1)
    placed = lax.dot_general(
        chosen.astype(jnp.bfloat16),
        fresh_pair,
        (((0,), (0,)), ((), ())),
        preferred_element_type=jnp.float32,
    ).astype(jnp.bfloat16)
    passage_keys = jnp.where(replaced, placed[:, :HEAD_SIZE], shifted_keys)
    passage_values = jnp.where(replaced, placed[:, HEAD_SIZE:], value_cache[0])

    nx, nz = SEQ_SHAPE
    all_queries = relay_gather(
        queries.reshape(2, prompt_rows * local_heads, HEAD_SIZE), nx, nz
    )
    q_blocks = all_queries.reshape(n_seq * 2, prompt_rows * local_heads, HEAD_SIZE)
    prompt_flag = jnp.where(prompt_slot == own_owner, 1, 0)
    recompute_flag = jnp.where(
        seq_ids == me, 2, jnp.where((passage_owner == own_owner) & (seq_ids > me), 1, 0)
    )
    flags = jnp.stack([prompt_flag, recompute_flag], axis=1).reshape(-1).astype(jnp.int32)
    lim = jnp.repeat(own_index, local_heads).reshape(-1, 1).astype(jnp.int32)
    packed = passage_attention(nx, nz, flags, q_blocks, passage_keys, passage_values, lim)
    block_rows = packed.shape[1]

    back = lax.all_to_all(
        packed.reshape(n_seq, 2, block_rows, HEAD_SIZE), "seq", 0, 0, tiled=True
    )
    rows128 = prompt_rows * local_heads
    stats_back = back[:, :, rows128 : rows128 + 4].astype(jnp.float32)
    part_max = (stats_back[:, :, 0] + stats_back[:, :, 1]).reshape(n_seq, query_rows, local_heads)
    part_tot = (stats_back[:, :, 2] + stats_back[:, :, 3]).reshape(n_seq, query_rows, local_heads)
    part_acc = (
        back[:, :, :rows128].reshape(n_seq, query_rows, local_heads, HEAD_SIZE).astype(jnp.float32)
    )

    pq = queries[:prompt_rows].astype(jnp.float32)
    pk = fresh_keys[:prompt_rows].astype(jnp.float32)
    pv = fresh_values[:prompt_rows].astype(jnp.float32)
    ps = jnp.einsum("qhd,kd->qhk", pq, pk) * scale
    jj = jnp.arange(prompt_rows, dtype=jnp.int32)
    pvis = (jj[None, :] <= jj[:, None]) & (jj[None, :] < own_length)
    ps = jnp.where(pvis[:, None, :], ps, NEGATIVE_FLOOR)
    pmax = jnp.max(ps, axis=-1)
    pw = jnp.where(pvis[:, None, :], jnp.exp(ps - pmax[..., None]), 0.0)
    ptot = jnp.sum(pw, axis=-1)
    pacc = jnp.einsum("qhk,kd->qhd", pw.astype(jnp.bfloat16).astype(jnp.float32), pv)
    loc_max = jnp.concatenate(
        [pmax, jnp.full((recompute_rows, local_heads), NEGATIVE_FLOOR, jnp.float32)]
    )
    loc_tot = jnp.concatenate([ptot, jnp.zeros((recompute_rows, local_heads), jnp.float32)])
    loc_acc = jnp.concatenate(
        [pacc, jnp.zeros((recompute_rows, local_heads, HEAD_SIZE), jnp.float32)]
    )

    highest = jnp.maximum(jnp.max(part_max, axis=0), loc_max)
    part_scale = jnp.exp(part_max - highest[None])
    loc_scale = jnp.exp(loc_max - highest)
    accumulated = jnp.sum(part_acc * part_scale[..., None], axis=0) + loc_acc * loc_scale[..., None]
    totals = jnp.sum(part_tot * part_scale, axis=0) + loc_tot * loc_scale
    safe_totals = jnp.where(totals > 0, totals, 1.0)
    attention = jnp.where(
        own_live[:, None, None], accumulated / safe_totals[..., None], 0.0
    ).astype(jnp.bfloat16).reshape(query_rows, local_heads * HEAD_SIZE)
    projected = jnp.dot(attention, w_out, preferred_element_type=jnp.float32)
    combined = jnp.sum(mp_scatter(projected, n_mp), axis=0).astype(jnp.bfloat16)
    return (combined[:prompt_rows], combined[prompt_rows:])


def solution(mesh):
    global SEQ_SHAPE
    sizes = dict(zip(mesh.axis_names, mesh.devices.shape))
    seq_devices = mesh.devices.reshape(sizes["seq"], sizes["mp"])[:, 0]
    xs = sorted({d.coords[0] for d in seq_devices})
    SEQ_SHAPE = (len(xs), sizes["seq"] // len(xs))
    return jax.shard_map(
        local,
        mesh=mesh,
        in_specs=(
            P("seq", "mp"),
            P("seq", "mp"),
            P("seq", None, "mp"),
            P("seq", None, "mp"),
            P(),
            P(None, "mp"),
            P(None, "mp"),
            P(None, "mp"),
            P("mp", None),
            P(),
            P(),
            P(),
            P(),
            P(),
        ),
        out_specs=(P("seq", "mp"), P("seq", "mp")),
        check_vma=False,
    )
```

```python
import functools
import math

import jax
import jax.numpy as jnp
from jax import lax
from jax.experimental import pallas as pl
from jax.experimental.pallas import tpu as pltpu
from jax.sharding import PartitionSpec as P

HEAD_SIZE = 128
NEGATIVE_FLOOR = -1e30


def apply_rotation(vectors, positions):
    half_width = vectors.shape[-1] // 2
    exponent = jnp.arange(half_width).astype(jnp.float32) * (2.0 / vectors.shape[-1])
    frequency = jnp.exp(-exponent * math.log(500000.0))
    angles = positions.astype(jnp.float32)[:, None] * frequency[None, :]
    cosines = jnp.cos(angles)[:, None, :]
    sines = jnp.sin(angles)[:, None, :]
    leading = vectors[..., :half_width]
    trailing = vectors[..., half_width:]
    return jnp.concatenate(
        [leading * cosines - trailing * sines, trailing * cosines + leading * sines], axis=-1
    )


def normalize(rows_in, norm_gain):
    values = rows_in.astype(jnp.float32)
    inverse_rms = lax.rsqrt(jnp.mean(values * values, axis=-1, keepdims=True) + 1e-05)
    return (values * inverse_rms * norm_gain).astype(jnp.bfloat16)


MESH = pl.DeviceIdType.MESH


def passage_kernel(nx, nz, flags_ref, q_ref, k_ref, v_ref, lim_ref, out_ref):
    nb, rows, _ = q_ref.shape
    keys = k_ref.shape[0]
    token = lax.broadcasted_iota(jnp.int32, (rows, keys), 1)
    sub = lax.broadcasted_iota(jnp.int32, (16, rows), 0)

    def split(m_row, l_row):
        m_hi = m_row.astype(jnp.bfloat16).astype(jnp.float32)
        l_hi = l_row.astype(jnp.bfloat16).astype(jnp.float32)
        st = jnp.where(
            sub == 0,
            m_row,
            jnp.where(
                sub == 1,
                m_row - m_hi,
                jnp.where(sub == 2, l_row, jnp.where(sub == 3, l_row - l_hi, 0.0)),
            ),
        )
        return st.astype(jnp.bfloat16)

    def body(b, carry):
        flag = flags_ref[b]

        @pl.when(flag == 0)
        def _():
            out_ref[b, 0:rows] = jnp.zeros((rows, HEAD_SIZE), out_ref.dtype)
            floor = jnp.full((16, rows), NEGATIVE_FLOOR, jnp.float32)
            out_ref[b, rows:] = split(floor, jnp.zeros((16, rows), jnp.float32))

        @pl.when(flag > 0)
        def _():
            d = b // 2
            stored = ((d % nz) * nx + d // nz) * 2 + b % 2
            scores = lax.dot_general(
                q_ref[stored], k_ref[...], (((1,), (1,)), ((), ())), preferred_element_type=jnp.float32
            ) * (1.0 / math.sqrt(HEAD_SIZE))
            limit = jnp.where(flag == 2, lim_ref[...], keys - 1)
            scores = jnp.where(token <= limit, scores, NEGATIVE_FLOOR)
            maxima = jnp.max(scores, axis=1, keepdims=True)
            weights = jnp.exp(scores - maxima)
            totals = jnp.sum(weights, axis=1, keepdims=True)
            out_ref[b, 0:rows] = jnp.dot(
                weights.astype(jnp.bfloat16), v_ref[...], preferred_element_type=jnp.float32
            ).astype(out_ref.dtype)
            m_row = jnp.transpose(jnp.broadcast_to(maxima, (rows, rows)))[0:16]
            l_row = jnp.transpose(jnp.broadcast_to(totals, (rows, rows)))[0:16]
            out_ref[b, rows:] = split(m_row, l_row)

        return carry

    lax.fori_loop(0, nb, body, 0)


def passage_attention(nx, nz, flags, q_blocks, keys, values, lim):
    nb, rows, _ = q_blocks.shape
    vmem = pl.BlockSpec(memory_space=pltpu.VMEM)
    return pl.pallas_call(
        functools.partial(passage_kernel, nx, nz),
        in_specs=[pl.BlockSpec(memory_space=pltpu.SMEM), vmem, vmem, vmem, vmem],
        out_specs=vmem,
        out_shape=jax.ShapeDtypeStruct((nb, rows + 16, HEAD_SIZE), jnp.bfloat16),
    )(flags, q_blocks, keys, values, lim)


def mp_gather_kernel(n, x_ref, y_ref, send_sem, recv_sem, local_sem):
    me = lax.axis_index("mp")
    row = lax.axis_index("seq")
    width = x_ref.shape[1]
    barrier = pltpu.get_barrier_semaphore()
    for k in range(1, n):
        peer = lax.rem(me + k, n)
        pl.semaphore_signal(barrier, inc=1, device_id=(row, peer), device_id_type=MESH)
    pl.semaphore_wait(barrier, n - 1)
    cols = pl.ds(pl.multiple_of(me * width, width), width)
    copies = []
    for k in range(1, n):
        peer = lax.rem(me + k, n)
        c = pltpu.make_async_remote_copy(
            src_ref=x_ref,
            dst_ref=y_ref.at[:, cols],
            send_sem=send_sem.at[k],
            recv_sem=recv_sem.at[k],
            device_id=(row, peer),
            device_id_type=MESH,
        )
        c.start()
        copies.append(c)
    own = pltpu.make_async_copy(x_ref, y_ref.at[:, cols], local_sem)
    own.start()
    for c in copies:
        c.wait()
    own.wait()


def mp_gather(x, n):
    vmem = pl.BlockSpec(memory_space=pltpu.VMEM)
    return pl.pallas_call(
        functools.partial(mp_gather_kernel, n),
        in_specs=[vmem],
        out_specs=vmem,
        out_shape=jax.ShapeDtypeStruct((x.shape[0], x.shape[1] * n), x.dtype),
        scratch_shapes=[
            pltpu.SemaphoreType.DMA((n,)),
            pltpu.SemaphoreType.DMA((n,)),
            pltpu.SemaphoreType.DMA(()),
        ],
        compiler_params=pltpu.CompilerParams(collective_id=0, has_side_effects=True),
    )(x)


def mp_scatter_kernel(n, x_ref, y_ref, send_sem, recv_sem, local_sem):
    me = lax.axis_index("mp")
    row = lax.axis_index("seq")
    width = y_ref.shape[2]
    barrier = pltpu.get_barrier_semaphore()
    for k in range(1, n):
        peer = lax.rem(me + k, n)
        pl.semaphore_signal(barrier, inc=1, device_id=(row, peer), device_id_type=MESH)
    pl.semaphore_wait(barrier, n - 1)
    copies = []
    for k in range(1, n):
        peer = lax.rem(me + k, n)
        c = pltpu.make_async_remote_copy(
            src_ref=x_ref.at[:, pl.ds(pl.multiple_of(peer * width, width), width)],
            dst_ref=y_ref.at[me],
            send_sem=send_sem.at[k],
            recv_sem=recv_sem.at[k],
            device_id=(row, peer),
            device_id_type=MESH,
        )
        c.start()
        copies.append(c)
    own = pltpu.make_async_copy(
        x_ref.at[:, pl.ds(pl.multiple_of(me * width, width), width)], y_ref.at[me], local_sem
    )
    own.start()
    for c in copies:
        c.wait()
    own.wait()


def mp_scatter(x, n):
    vmem = pl.BlockSpec(memory_space=pltpu.VMEM)
    return pl.pallas_call(
        functools.partial(mp_scatter_kernel, n),
        in_specs=[vmem],
        out_specs=vmem,
        out_shape=jax.ShapeDtypeStruct((n, x.shape[0], x.shape[1] // n), x.dtype),
        scratch_shapes=[
            pltpu.SemaphoreType.DMA((n,)),
            pltpu.SemaphoreType.DMA((n,)),
            pltpu.SemaphoreType.DMA(()),
        ],
        compiler_params=pltpu.CompilerParams(collective_id=1, has_side_effects=True),
    )(x)


def relay_gather_kernel(nx, nz, x_ref, y_ref, sx_send, sx_recv, zp_send, zp_recv, zm_send, zm_recv, own_sem):
    me = lax.axis_index("seq")
    mp = lax.axis_index("mp")
    x = me // nz
    z = me % nz
    up = lax.rem(z + 1, nz)
    down = lax.rem(z + nz - 1, nz)
    barrier = pltpu.get_barrier_semaphore()
    peers = [(lax.rem(x + k, nx) * nz + z, mp) for k in range(1, nx)]
    peers += [(x * nz + up, mp), (x * nz + down, mp)]
    for p in peers:
        pl.semaphore_signal(barrier, inc=1, device_id=p, device_id_type=MESH)
    pl.semaphore_wait(barrier, len(peers))

    slot = z * nx + x
    first = []
    for k in range(1, nx):
        c = pltpu.make_async_remote_copy(
            src_ref=x_ref,
            dst_ref=y_ref.at[slot],
            send_sem=sx_send.at[k],
            recv_sem=sx_recv.at[k],
            device_id=peers[k - 1],
            device_id_type=MESH,
        )
        c.start()
        first.append(c)
    own = pltpu.make_async_copy(x_ref, y_ref.at[slot], own_sem)
    own.start()
    for c in first:
        c.wait()
    own.wait()

    steps = nz // 2
    half = nx // 2
    last = {}
    sent = []
    for t in range(1, steps + 1):
        for i in range(nx):
            for sign, send_sem, recv_sem, target in (
                (1, zp_send, zp_recv, up),
                (-1, zm_send, zm_recv, down),
            ):
                if t == steps and (i < half) != (sign == 1):
                    continue
                if t > 1:
                    last[(sign, i)].wait_recv()
                column = lax.rem(z - sign * (t - 1) + nz, nz)
                c = pltpu.make_async_remote_copy(
                    src_ref=y_ref.at[column * nx + i],
                    dst_ref=y_ref.at[column * nx + i],
                    send_sem=send_sem.at[t, i],
                    recv_sem=recv_sem.at[t, i],
                    device_id=(x * nz + target, mp),
                    device_id_type=MESH,
                )
                c.start()
                last[(sign, i)] = c
                sent.append(c)
    for c in last.values():
        c.wait_recv()
    for c in sent:
        c.wait_send()


def relay_gather(x, nx, nz):
    vmem = pl.BlockSpec(memory_space=pltpu.VMEM)
    steps = nz // 2
    return pl.pallas_call(
        functools.partial(relay_gather_kernel, nx, nz),
        in_specs=[vmem],
        out_specs=vmem,
        out_shape=jax.ShapeDtypeStruct((nx * nz,) + x.shape, x.dtype),
        scratch_shapes=[
            pltpu.SemaphoreType.DMA((nx,)),
            pltpu.SemaphoreType.DMA((nx,)),
            pltpu.SemaphoreType.DMA((steps + 1, nx)),
            pltpu.SemaphoreType.DMA((steps + 1, nx)),
            pltpu.SemaphoreType.DMA((steps + 1, nx)),
            pltpu.SemaphoreType.DMA((steps + 1, nx)),
            pltpu.SemaphoreType.DMA(()),
        ],
        compiler_params=pltpu.CompilerParams(collective_id=2, has_side_effects=True),
    )(x)


def local(
    prompt_hidden,
    recompute_hidden,
    key_cache,
    value_cache,
    norm_gain,
    w_query,
    key_weight,
    value_weight,
    w_out,
    passage_owner,
    prompt_slot,
    prompt_length,
    recompute_count,
    recompute_index,
):
    prompt_rows = prompt_hidden.shape[0]
    recompute_rows = recompute_hidden.shape[0]
    query_rows = prompt_rows + recompute_rows
    passage_length = key_cache.shape[1]
    local_heads = w_query.shape[1] // HEAD_SIZE
    n_seq = passage_owner.shape[0]
    me = lax.axis_index("seq")
    scale = 1.0 / math.sqrt(HEAD_SIZE)

    seq_ids = jnp.arange(n_seq, dtype=jnp.int32)
    same_owner = passage_owner[:, None] == passage_owner[None, :]
    passage_rank = jnp.sum(
        jnp.where(same_owner & (seq_ids[None, :] < seq_ids[:, None]), 1, 0), axis=1
    ).astype(jnp.int32)
    held_count = jnp.sum(
        jnp.where(passage_owner[None, :] == prompt_slot[:, None], 1, 0), axis=1
    ).astype(jnp.int32)
    own_rank = passage_rank[me]
    own_owner = passage_owner[me]
    own_held = held_count[me]
    own_index = lax.dynamic_index_in_dim(recompute_index, me, 0, keepdims=False)
    own_length = prompt_length[me]
    own_count = recompute_count[me]

    prompt_pos = own_held * passage_length + jnp.arange(prompt_rows, dtype=jnp.int32)
    recompute_pos = own_rank * passage_length + own_index
    own_pos = jnp.concatenate([prompt_pos, recompute_pos])
    own_live = jnp.concatenate(
        [
            jnp.arange(prompt_rows, dtype=jnp.int32) < own_length,
            jnp.arange(recompute_rows, dtype=jnp.int32) < own_count,
        ]
    )

    rows_local = jnp.concatenate([prompt_hidden, recompute_hidden], axis=0)
    n_mp = w_out.shape[1] // rows_local.shape[1]
    full_rows = mp_gather(rows_local, n_mp)
    normalized_hidden = normalize(full_rows, norm_gain)
    queries = (
        apply_rotation(
            jnp.dot(normalized_hidden, w_query, preferred_element_type=jnp.float32).reshape(
                query_rows, local_heads, HEAD_SIZE
            ),
            own_pos,
        )
        .astype(jnp.bfloat16)
    )
    fresh_keys = (
        apply_rotation(
            jnp.dot(normalized_hidden, key_weight, preferred_element_type=jnp.float32).reshape(
                query_rows, 1, HEAD_SIZE
            ),
            own_pos,
        )
        .astype(jnp.bfloat16)
        .reshape(query_rows, HEAD_SIZE)
    )
    fresh_values = jnp.dot(
        normalized_hidden, value_weight, preferred_element_type=jnp.float32
    ).astype(jnp.bfloat16)

    position_shift = jnp.full((passage_length,), own_rank * passage_length, jnp.int32)
    shifted_keys = (
        apply_rotation(
            key_cache[0].astype(jnp.float32).reshape(passage_length, 1, HEAD_SIZE),
            position_shift,
        )
        .astype(jnp.bfloat16)
        .reshape(passage_length, HEAD_SIZE)
    )
    chosen = (own_index[:, None] == jnp.arange(passage_length, dtype=jnp.int32)[None, :]) & (
        jnp.arange(recompute_rows, dtype=jnp.int32)[:, None] < own_count
    )
    replaced = jnp.any(chosen, axis=0)[:, None]
    fresh_pair = jnp.concatenate([fresh_keys[prompt_rows:], fresh_values[prompt_rows:]], axis=1)
    placed = lax.dot_general(
        chosen.astype(jnp.bfloat16),
        fresh_pair,
        (((0,), (0,)), ((), ())),
        preferred_element_type=jnp.float32,
    ).astype(jnp.bfloat16)
    passage_keys = jnp.where(replaced, placed[:, :HEAD_SIZE], shifted_keys)
    passage_values = jnp.where(replaced, placed[:, HEAD_SIZE:], value_cache[0])

    nx, nz = SEQ_SHAPE
    all_queries = relay_gather(
        queries.reshape(2, prompt_rows * local_heads, HEAD_SIZE), nx, nz
    )
    q_blocks = all_queries.reshape(n_seq * 2, prompt_rows * local_heads, HEAD_SIZE)
    prompt_flag = jnp.where(prompt_slot == own_owner, 1, 0)
    recompute_flag = jnp.where(
        seq_ids == me, 2, jnp.where((passage_owner == own_owner) & (seq_ids > me), 1, 0)
    )
    flags = jnp.stack([prompt_flag, recompute_flag], axis=1).reshape(-1).astype(jnp.int32)
    lim = jnp.repeat(own_index, local_heads).reshape(-1, 1).astype(jnp.int32)
    packed = passage_attention(nx, nz, flags, q_blocks, passage_keys, passage_values, lim)
    block_rows = packed.shape[1]

    back = lax.all_to_all(
        packed.reshape(n_seq, 2, block_rows, HEAD_SIZE), "seq", 0, 0, tiled=True
    )
    rows128 = prompt_rows * local_heads
    stats_back = back[:, :, rows128 : rows128 + 4].astype(jnp.float32)
    part_max = (stats_back[:, :, 0] + stats_back[:, :, 1]).reshape(n_seq, query_rows, local_heads)
    part_tot = (stats_back[:, :, 2] + stats_back[:, :, 3]).reshape(n_seq, query_rows, local_heads)
    part_acc = (
        back[:, :, :rows128].reshape(n_seq, query_rows, local_heads, HEAD_SIZE).astype(jnp.float32)
    )

    pq = queries[:prompt_rows].astype(jnp.float32)
    pk = fresh_keys[:prompt_rows].astype(jnp.float32)
    pv = fresh_values[:prompt_rows].astype(jnp.float32)
    ps = jnp.einsum("qhd,kd->qhk", pq, pk) * scale
    jj = jnp.arange(prompt_rows, dtype=jnp.int32)
    pvis = (jj[None, :] <= jj[:, None]) & (jj[None, :] < own_length)
    ps = jnp.where(pvis[:, None, :], ps, NEGATIVE_FLOOR)
    pmax = jnp.max(ps, axis=-1)
    pw = jnp.where(pvis[:, None, :], jnp.exp(ps - pmax[..., None]), 0.0)
    ptot = jnp.sum(pw, axis=-1)
    pacc = jnp.einsum("qhk,kd->qhd", pw.astype(jnp.bfloat16).astype(jnp.float32), pv)
    loc_max = jnp.concatenate(
        [pmax, jnp.full((recompute_rows, local_heads), NEGATIVE_FLOOR, jnp.float32)]
    )
    loc_tot = jnp.concatenate([ptot, jnp.zeros((recompute_rows, local_heads), jnp.float32)])
    loc_acc = jnp.concatenate(
        [pacc, jnp.zeros((recompute_rows, local_heads, HEAD_SIZE), jnp.float32)]
    )

    highest = jnp.maximum(jnp.max(part_max, axis=0), loc_max)
    part_scale = jnp.exp(part_max - highest[None])
    loc_scale = jnp.exp(loc_max - highest)
    accumulated = jnp.sum(part_acc * part_scale[..., None], axis=0) + loc_acc * loc_scale[..., None]
    totals = jnp.sum(part_tot * part_scale, axis=0) + loc_tot * loc_scale
    safe_totals = jnp.where(totals > 0, totals, 1.0)
    attention = jnp.where(
        own_live[:, None, None], accumulated / safe_totals[..., None], 0.0
    ).astype(jnp.bfloat16).reshape(query_rows, local_heads * HEAD_SIZE)
    projected = jnp.dot(attention, w_out, preferred_element_type=jnp.float32)
    combined = jnp.sum(mp_scatter(projected, n_mp), axis=0).astype(jnp.bfloat16)
    return (combined[:prompt_rows], combined[prompt_rows:])


def solution(mesh):
    global SEQ_SHAPE
    sizes = dict(zip(mesh.axis_names, mesh.devices.shape))
    seq_devices = mesh.devices.reshape(sizes["seq"], sizes["mp"])[:, 0]
    xs = sorted({d.coords[0] for d in seq_devices})
    SEQ_SHAPE = (len(xs), sizes["seq"] // len(xs))
    return jax.shard_map(
        local,
        mesh=mesh,
        in_specs=(
            P("seq", "mp"),
            P("seq", "mp"),
            P("seq", None, "mp"),
            P("seq", None, "mp"),
            P(),
            P(None, "mp"),
            P(None, "mp"),
            P(None, "mp"),
            P("mp", None),
            P(),
            P(),
            P(),
            P(),
            P(),
        ),
        out_specs=(P("seq", "mp"), P("seq", "mp")),
        check_vma=False,
    )
```

```python
import functools
import math

import jax
import jax.numpy as jnp
from jax import lax
from jax.experimental import pallas as pl
from jax.experimental.pallas import tpu as pltpu
from jax.sharding import PartitionSpec as P

HEAD_SIZE = 128
NEGATIVE_FLOOR = -1e30


def apply_rotation(vectors, positions):
    half_width = vectors.shape[-1] // 2
    exponent = jnp.arange(half_width).astype(jnp.float32) * (2.0 / vectors.shape[-1])
    frequency = jnp.exp(-exponent * math.log(500000.0))
    angles = positions.astype(jnp.float32)[:, None] * frequency[None, :]
    cosines = jnp.cos(angles)[:, None, :]
    sines = jnp.sin(angles)[:, None, :]
    leading = vectors[..., :half_width]
    trailing = vectors[..., half_width:]
    return jnp.concatenate(
        [leading * cosines - trailing * sines, trailing * cosines + leading * sines], axis=-1
    )


def normalize(rows_in, norm_gain):
    values = rows_in.astype(jnp.float32)
    inverse_rms = lax.rsqrt(jnp.mean(values * values, axis=-1, keepdims=True) + 1e-05)
    return (values * inverse_rms * norm_gain).astype(jnp.bfloat16)


MESH = pl.DeviceIdType.MESH


def passage_kernel(nx, nz, flags_ref, q_ref, k_ref, v_ref, lim_ref, out_ref):
    nb, rows, _ = q_ref.shape
    keys = k_ref.shape[0]
    token = lax.broadcasted_iota(jnp.int32, (rows, keys), 1)
    sub = lax.broadcasted_iota(jnp.int32, (16, rows), 0)

    def split(m_row, l_row):
        m_hi = m_row.astype(jnp.bfloat16).astype(jnp.float32)
        l_hi = l_row.astype(jnp.bfloat16).astype(jnp.float32)
        st = jnp.where(
            sub == 0,
            m_row,
            jnp.where(
                sub == 1,
                m_row - m_hi,
                jnp.where(sub == 2, l_row, jnp.where(sub == 3, l_row - l_hi, 0.0)),
            ),
        )
        return st.astype(jnp.bfloat16)

    def body(b, carry):
        flag = flags_ref[b]

        @pl.when(flag == 0)
        def _():
            out_ref[b, 0:rows] = jnp.zeros((rows, HEAD_SIZE), out_ref.dtype)
            floor = jnp.full((16, rows), NEGATIVE_FLOOR, jnp.float32)
            out_ref[b, rows:] = split(floor, jnp.zeros((16, rows), jnp.float32))

        @pl.when(flag > 0)
        def _():
            d = b // 2
            stored = ((d % nz) * nx + d // nz) * 2 + b % 2
            scores = lax.dot_general(
                q_ref[stored], k_ref[...], (((1,), (1,)), ((), ())), preferred_element_type=jnp.float32
            ) * (1.0 / math.sqrt(HEAD_SIZE))
            limit = jnp.where(flag == 2, lim_ref[...], keys - 1)
            scores = jnp.where(token <= limit, scores, NEGATIVE_FLOOR)
            maxima = jnp.max(scores, axis=1, keepdims=True)
            weights = jnp.exp(scores - maxima)
            totals = jnp.sum(weights, axis=1, keepdims=True)
            out_ref[b, 0:rows] = jnp.dot(
                weights.astype(jnp.bfloat16), v_ref[...], preferred_element_type=jnp.float32
            ).astype(out_ref.dtype)
            m_row = jnp.transpose(jnp.broadcast_to(maxima, (rows, rows)))[0:16]
            l_row = jnp.transpose(jnp.broadcast_to(totals, (rows, rows)))[0:16]
            out_ref[b, rows:] = split(m_row, l_row)

        return carry

    lax.fori_loop(0, nb, body, 0)


def passage_attention(nx, nz, flags, q_blocks, keys, values, lim):
    nb, rows, _ = q_blocks.shape
    vmem = pl.BlockSpec(memory_space=pltpu.VMEM)
    return pl.pallas_call(
        functools.partial(passage_kernel, nx, nz),
        in_specs=[pl.BlockSpec(memory_space=pltpu.SMEM), vmem, vmem, vmem, vmem],
        out_specs=vmem,
        out_shape=jax.ShapeDtypeStruct((nb, rows + 16, HEAD_SIZE), jnp.bfloat16),
    )(flags, q_blocks, keys, values, lim)


def mp_gather_kernel(n, x_ref, y_ref, send_sem, recv_sem, local_sem):
    me = lax.axis_index("mp")
    row = lax.axis_index("seq")
    width = x_ref.shape[1]
    barrier = pltpu.get_barrier_semaphore()
    for k in range(1, n):
        peer = lax.rem(me + k, n)
        pl.semaphore_signal(barrier, inc=1, device_id=(row, peer), device_id_type=MESH)
    pl.semaphore_wait(barrier, n - 1)
    cols = pl.ds(pl.multiple_of(me * width, width), width)
    copies = []
    for k in range(1, n):
        peer = lax.rem(me + k, n)
        c = pltpu.make_async_remote_copy(
            src_ref=x_ref,
            dst_ref=y_ref.at[:, cols],
            send_sem=send_sem.at[k],
            recv_sem=recv_sem.at[k],
            device_id=(row, peer),
            device_id_type=MESH,
        )
        c.start()
        copies.append(c)
    own = pltpu.make_async_copy(x_ref, y_ref.at[:, cols], local_sem)
    own.start()
    for c in copies:
        c.wait()
    own.wait()


def mp_gather(x, n):
    vmem = pl.BlockSpec(memory_space=pltpu.VMEM)
    return pl.pallas_call(
        functools.partial(mp_gather_kernel, n),
        in_specs=[vmem],
        out_specs=vmem,
        out_shape=jax.ShapeDtypeStruct((x.shape[0], x.shape[1] * n), x.dtype),
        scratch_shapes=[
            pltpu.SemaphoreType.DMA((n,)),
            pltpu.SemaphoreType.DMA((n,)),
            pltpu.SemaphoreType.DMA(()),
        ],
        compiler_params=pltpu.CompilerParams(collective_id=0, has_side_effects=True),
    )(x)


def mp_scatter_kernel(n, x_ref, y_ref, send_sem, recv_sem, local_sem):
    me = lax.axis_index("mp")
    row = lax.axis_index("seq")
    width = y_ref.shape[2]
    barrier = pltpu.get_barrier_semaphore()
    for k in range(1, n):
        peer = lax.rem(me + k, n)
        pl.semaphore_signal(barrier, inc=1, device_id=(row, peer), device_id_type=MESH)
    pl.semaphore_wait(barrier, n - 1)
    copies = []
    for k in range(1, n):
        peer = lax.rem(me + k, n)
        c = pltpu.make_async_remote_copy(
            src_ref=x_ref.at[:, pl.ds(pl.multiple_of(peer * width, width), width)],
            dst_ref=y_ref.at[me],
            send_sem=send_sem.at[k],
            recv_sem=recv_sem.at[k],
            device_id=(row, peer),
            device_id_type=MESH,
        )
        c.start()
        copies.append(c)
    own = pltpu.make_async_copy(
        x_ref.at[:, pl.ds(pl.multiple_of(me * width, width), width)], y_ref.at[me], local_sem
    )
    own.start()
    for c in copies:
        c.wait()
    own.wait()


def mp_scatter(x, n):
    vmem = pl.BlockSpec(memory_space=pltpu.VMEM)
    return pl.pallas_call(
        functools.partial(mp_scatter_kernel, n),
        in_specs=[vmem],
        out_specs=vmem,
        out_shape=jax.ShapeDtypeStruct((n, x.shape[0], x.shape[1] // n), x.dtype),
        scratch_shapes=[
            pltpu.SemaphoreType.DMA((n,)),
            pltpu.SemaphoreType.DMA((n,)),
            pltpu.SemaphoreType.DMA(()),
        ],
        compiler_params=pltpu.CompilerParams(collective_id=1, has_side_effects=True),
    )(x)


def relay_gather_kernel(nx, nz, x_ref, y_ref, sx_send, sx_recv, zp_send, zp_recv, zm_send, zm_recv, own_sem):
    me = lax.axis_index("seq")
    mp = lax.axis_index("mp")
    x = me // nz
    z = me % nz
    up = lax.rem(z + 1, nz)
    down = lax.rem(z + nz - 1, nz)
    barrier = pltpu.get_barrier_semaphore()
    peers = [(lax.rem(x + k, nx) * nz + z, mp) for k in range(1, nx)]
    peers += [(x * nz + up, mp), (x * nz + down, mp)]
    for p in peers:
        pl.semaphore_signal(barrier, inc=1, device_id=p, device_id_type=MESH)
    pl.semaphore_wait(barrier, len(peers))

    slot = z * nx + x
    first = []
    for k in range(1, nx):
        c = pltpu.make_async_remote_copy(
            src_ref=x_ref,
            dst_ref=y_ref.at[slot],
            send_sem=sx_send.at[k],
            recv_sem=sx_recv.at[k],
            device_id=peers[k - 1],
            device_id_type=MESH,
        )
        c.start()
        first.append(c)
    own = pltpu.make_async_copy(x_ref, y_ref.at[slot], own_sem)
    own.start()
    for c in first:
        c.wait()
    own.wait()

    steps = nz // 2
    half = nx // 2
    last = {}
    sent = []
    for t in range(1, steps + 1):
        for i in range(nx):
            for sign, send_sem, recv_sem, target in (
                (1, zp_send, zp_recv, up),
                (-1, zm_send, zm_recv, down),
            ):
                if t == steps and (i < half) != (sign == 1):
                    continue
                if t > 1:
                    last[(sign, i)].wait_recv()
                column = lax.rem(z - sign * (t - 1) + nz, nz)
                c = pltpu.make_async_remote_copy(
                    src_ref=y_ref.at[column * nx + i],
                    dst_ref=y_ref.at[column * nx + i],
                    send_sem=send_sem.at[t, i],
                    recv_sem=recv_sem.at[t, i],
                    device_id=(x * nz + target, mp),
                    device_id_type=MESH,
                )
                c.start()
                last[(sign, i)] = c
                sent.append(c)
    for c in last.values():
        c.wait_recv()
    for c in sent:
        c.wait_send()


def relay_gather(x, nx, nz):
    vmem = pl.BlockSpec(memory_space=pltpu.VMEM)
    steps = nz // 2
    return pl.pallas_call(
        functools.partial(relay_gather_kernel, nx, nz),
        in_specs=[vmem],
        out_specs=vmem,
        out_shape=jax.ShapeDtypeStruct((nx * nz,) + x.shape, x.dtype),
        scratch_shapes=[
            pltpu.SemaphoreType.DMA((nx,)),
            pltpu.SemaphoreType.DMA((nx,)),
            pltpu.SemaphoreType.DMA((steps + 1, nx)),
            pltpu.SemaphoreType.DMA((steps + 1, nx)),
            pltpu.SemaphoreType.DMA((steps + 1, nx)),
            pltpu.SemaphoreType.DMA((steps + 1, nx)),
            pltpu.SemaphoreType.DMA(()),
        ],
        compiler_params=pltpu.CompilerParams(collective_id=2, has_side_effects=True),
    )(x)


def merge_piece(a, b, rows):
    af = a.astype(jnp.float32)
    bf = b.astype(jnp.float32)
    m1 = af[rows : rows + 1] + af[rows + 1 : rows + 2]
    l1 = af[rows + 2 : rows + 3] + af[rows + 3 : rows + 4]
    m2 = bf[rows : rows + 1] + bf[rows + 1 : rows + 2]
    l2 = bf[rows + 2 : rows + 3] + bf[rows + 3 : rows + 4]
    top = jnp.maximum(m1, m2)
    s1 = jnp.exp(m1 - top)
    s2 = jnp.exp(m2 - top)
    total = l1 * s1 + l2 * s2
    c1 = jnp.transpose(jnp.broadcast_to(s1, (rows, rows)))
    c2 = jnp.transpose(jnp.broadcast_to(s2, (rows, rows)))
    acc = af[0:rows] * c1 + bf[0:rows] * c2
    sub = lax.broadcasted_iota(jnp.int32, (16, rows), 0)
    top_hi = top.astype(jnp.bfloat16).astype(jnp.float32)
    tot_hi = total.astype(jnp.bfloat16).astype(jnp.float32)
    st = jnp.where(
        sub == 0,
        top,
        jnp.where(
            sub == 1, top - top_hi, jnp.where(sub == 2, total, jnp.where(sub == 3, total - tot_hi, 0.0))
        ),
    )
    return acc.astype(jnp.bfloat16), st.astype(jnp.bfloat16)


def relay_reduce_kernel(
    nx, nz, x_ref, y_ref, rp, rm, bp, bm, col, sp_send, sp_recv, sm_send, sm_recv, sx_send, sx_recv
):
    me = lax.axis_index("seq")
    mp = lax.axis_index("mp")
    x = me // nz
    z = me % nz
    up = lax.rem(z + 1, nz)
    down = lax.rem(z + nz - 1, nz)
    rows = x_ref.shape[2] - 16
    barrier = pltpu.get_barrier_semaphore()
    peers = [(lax.rem(x + k, nx) * nz + z, mp) for k in range(1, nx)]
    peers += [(x * nz + up, mp), (x * nz + down, mp)]
    for p in peers:
        pl.semaphore_signal(barrier, inc=1, device_id=p, device_id_type=MESH)
    pl.semaphore_wait(barrier, len(peers))

    def merge_into(dst, first, second):
        for h in range(2):
            acc, st = merge_piece(first[h], second[h], rows)
            dst[h, 0:rows] = acc
            dst[h, rows:] = st

    steps = nz // 2
    half = nx // 2
    last = {}
    sent = []
    dirs = ((1, rp, bp, sp_send, sp_recv, up), (-1, rm, bm, sm_send, sm_recv, down))
    for t in range(1, steps + 1):
        for i in range(nx):
            for sign, recv_buf, send_buf, send_sem, recv_sem, target in dirs:
                if t == 1 and (i < half) != (sign == 1):
                    continue
                column = lax.rem(z + sign * (steps + 1 - t) + nz, nz)
                own = x_ref.at[i * nz + column]
                if (sign, i) in last:
                    last[(sign, i)].wait_recv()
                    merge_into(send_buf.at[t, i], own, recv_buf.at[t - 1, i])
                    src = send_buf.at[t, i]
                else:
                    src = own
                c = pltpu.make_async_remote_copy(
                    src_ref=src,
                    dst_ref=recv_buf.at[t, i],
                    send_sem=send_sem.at[t, i],
                    recv_sem=recv_sem.at[t, i],
                    device_id=(x * nz + target, mp),
                    device_id_type=MESH,
                )
                c.start()
                last[(sign, i)] = c
                sent.append(c)

    mine = []
    for i in range(nx):
        last[(1, i)].wait_recv()
        last[(-1, i)].wait_recv()
        merge_into(col.at[i], x_ref.at[i * nz + z], rp.at[steps, i])
        merge_into(col.at[i], col.at[i], rm.at[steps, i])
    for k in range(1, nx):
        target = lax.rem(x + k, nx)
        c = pltpu.make_async_remote_copy(
            src_ref=col.at[target],
            dst_ref=y_ref.at[x],
            send_sem=sx_send.at[k],
            recv_sem=sx_recv.at[k],
            device_id=(target * nz + z, mp),
            device_id_type=MESH,
        )
        c.start()
        mine.append(c)
    y_ref[x] = col[x]
    for c in sent:
        c.wait_send()
    for c in mine:
        c.wait()


def relay_reduce(parts, nx, nz):
    vmem = pl.BlockSpec(memory_space=pltpu.VMEM)
    steps = nz // 2
    piece = parts.shape[1:]
    return pl.pallas_call(
        functools.partial(relay_reduce_kernel, nx, nz),
        in_specs=[vmem],
        out_specs=vmem,
        out_shape=jax.ShapeDtypeStruct((nx,) + piece, parts.dtype),
        scratch_shapes=[
            pltpu.VMEM((steps + 1, nx) + piece, parts.dtype),
            pltpu.VMEM((steps + 1, nx) + piece, parts.dtype),
            pltpu.VMEM((steps + 1, nx) + piece, parts.dtype),
            pltpu.VMEM((steps + 1, nx) + piece, parts.dtype),
            pltpu.VMEM((nx,) + piece, parts.dtype),
            pltpu.SemaphoreType.DMA((steps + 1, nx)),
            pltpu.SemaphoreType.DMA((steps + 1, nx)),
            pltpu.SemaphoreType.DMA((steps + 1, nx)),
            pltpu.SemaphoreType.DMA((steps + 1, nx)),
            pltpu.SemaphoreType.DMA((nx,)),
            pltpu.SemaphoreType.DMA((nx,)),
        ],
        compiler_params=pltpu.CompilerParams(collective_id=3, has_side_effects=True),
    )(parts)


def local(
    prompt_hidden,
    recompute_hidden,
    key_cache,
    value_cache,
    norm_gain,
    w_query,
    key_weight,
    value_weight,
    w_out,
    passage_owner,
    prompt_slot,
    prompt_length,
    recompute_count,
    recompute_index,
):
    prompt_rows = prompt_hidden.shape[0]
    recompute_rows = recompute_hidden.shape[0]
    query_rows = prompt_rows + recompute_rows
    passage_length = key_cache.shape[1]
    local_heads = w_query.shape[1] // HEAD_SIZE
    n_seq = passage_owner.shape[0]
    me = lax.axis_index("seq")
    scale = 1.0 / math.sqrt(HEAD_SIZE)

    seq_ids = jnp.arange(n_seq, dtype=jnp.int32)
    same_owner = passage_owner[:, None] == passage_owner[None, :]
    passage_rank = jnp.sum(
        jnp.where(same_owner & (seq_ids[None, :] < seq_ids[:, None]), 1, 0), axis=1
    ).astype(jnp.int32)
    held_count = jnp.sum(
        jnp.where(passage_owner[None, :] == prompt_slot[:, None], 1, 0), axis=1
    ).astype(jnp.int32)
    own_rank = passage_rank[me]
    own_owner = passage_owner[me]
    own_held = held_count[me]
    own_index = lax.dynamic_index_in_dim(recompute_index, me, 0, keepdims=False)
    own_length = prompt_length[me]
    own_count = recompute_count[me]

    prompt_pos = own_held * passage_length + jnp.arange(prompt_rows, dtype=jnp.int32)
    recompute_pos = own_rank * passage_length + own_index
    own_pos = jnp.concatenate([prompt_pos, recompute_pos])
    own_live = jnp.concatenate(
        [
            jnp.arange(prompt_rows, dtype=jnp.int32) < own_length,
            jnp.arange(recompute_rows, dtype=jnp.int32) < own_count,
        ]
    )

    rows_local = jnp.concatenate([prompt_hidden, recompute_hidden], axis=0)
    n_mp = w_out.shape[1] // rows_local.shape[1]
    full_rows = mp_gather(rows_local, n_mp)
    normalized_hidden = normalize(full_rows, norm_gain)
    queries = (
        apply_rotation(
            jnp.dot(normalized_hidden, w_query, preferred_element_type=jnp.float32).reshape(
                query_rows, local_heads, HEAD_SIZE
            ),
            own_pos,
        )
        .astype(jnp.bfloat16)
    )
    fresh_keys = (
        apply_rotation(
            jnp.dot(normalized_hidden, key_weight, preferred_element_type=jnp.float32).reshape(
                query_rows, 1, HEAD_SIZE
            ),
            own_pos,
        )
        .astype(jnp.bfloat16)
        .reshape(query_rows, HEAD_SIZE)
    )
    fresh_values = jnp.dot(
        normalized_hidden, value_weight, preferred_element_type=jnp.float32
    ).astype(jnp.bfloat16)

    position_shift = jnp.full((passage_length,), own_rank * passage_length, jnp.int32)
    shifted_keys = (
        apply_rotation(
            key_cache[0].astype(jnp.float32).reshape(passage_length, 1, HEAD_SIZE),
            position_shift,
        )
        .astype(jnp.bfloat16)
        .reshape(passage_length, HEAD_SIZE)
    )
    chosen = (own_index[:, None] == jnp.arange(passage_length, dtype=jnp.int32)[None, :]) & (
        jnp.arange(recompute_rows, dtype=jnp.int32)[:, None] < own_count
    )
    replaced = jnp.any(chosen, axis=0)[:, None]
    fresh_pair = jnp.concatenate([fresh_keys[prompt_rows:], fresh_values[prompt_rows:]], axis=1)
    placed = lax.dot_general(
        chosen.astype(jnp.bfloat16),
        fresh_pair,
        (((0,), (0,)), ((), ())),
        preferred_element_type=jnp.float32,
    ).astype(jnp.bfloat16)
    passage_keys = jnp.where(replaced, placed[:, :HEAD_SIZE], shifted_keys)
    passage_values = jnp.where(replaced, placed[:, HEAD_SIZE:], value_cache[0])

    nx, nz = SEQ_SHAPE
    all_queries = relay_gather(
        queries.reshape(2, prompt_rows * local_heads, HEAD_SIZE), nx, nz
    )
    q_blocks = all_queries.reshape(n_seq * 2, prompt_rows * local_heads, HEAD_SIZE)
    prompt_flag = jnp.where(prompt_slot == own_owner, 1, 0)
    recompute_flag = jnp.where(
        seq_ids == me, 2, jnp.where((passage_owner == own_owner) & (seq_ids > me), 1, 0)
    )
    flags = jnp.stack([prompt_flag, recompute_flag], axis=1).reshape(-1).astype(jnp.int32)
    lim = jnp.repeat(own_index, local_heads).reshape(-1, 1).astype(jnp.int32)
    packed = passage_attention(nx, nz, flags, q_blocks, passage_keys, passage_values, lim)
    block_rows = packed.shape[1]

    back = relay_reduce(packed.reshape(n_seq, 2, block_rows, HEAD_SIZE), nx, nz)
    n_parts = back.shape[0]
    rows128 = prompt_rows * local_heads
    stats_back = back[:, :, rows128 : rows128 + 4].astype(jnp.float32)
    part_max = (stats_back[:, :, 0] + stats_back[:, :, 1]).reshape(n_parts, query_rows, local_heads)
    part_tot = (stats_back[:, :, 2] + stats_back[:, :, 3]).reshape(n_parts, query_rows, local_heads)
    part_acc = (
        back[:, :, :rows128].reshape(n_parts, query_rows, local_heads, HEAD_SIZE).astype(jnp.float32)
    )

    pq = queries[:prompt_rows].astype(jnp.float32)
    pk = fresh_keys[:prompt_rows].astype(jnp.float32)
    pv = fresh_values[:prompt_rows].astype(jnp.float32)
    ps = jnp.einsum("qhd,kd->qhk", pq, pk) * scale
    jj = jnp.arange(prompt_rows, dtype=jnp.int32)
    pvis = (jj[None, :] <= jj[:, None]) & (jj[None, :] < own_length)
    ps = jnp.where(pvis[:, None, :], ps, NEGATIVE_FLOOR)
    pmax = jnp.max(ps, axis=-1)
    pw = jnp.where(pvis[:, None, :], jnp.exp(ps - pmax[..., None]), 0.0)
    ptot = jnp.sum(pw, axis=-1)
    pacc = jnp.einsum("qhk,kd->qhd", pw.astype(jnp.bfloat16).astype(jnp.float32), pv)
    loc_max = jnp.concatenate(
        [pmax, jnp.full((recompute_rows, local_heads), NEGATIVE_FLOOR, jnp.float32)]
    )
    loc_tot = jnp.concatenate([ptot, jnp.zeros((recompute_rows, local_heads), jnp.float32)])
    loc_acc = jnp.concatenate(
        [pacc, jnp.zeros((recompute_rows, local_heads, HEAD_SIZE), jnp.float32)]
    )

    highest = jnp.maximum(jnp.max(part_max, axis=0), loc_max)
    part_scale = jnp.exp(part_max - highest[None])
    loc_scale = jnp.exp(loc_max - highest)
    accumulated = jnp.sum(part_acc * part_scale[..., None], axis=0) + loc_acc * loc_scale[..., None]
    totals = jnp.sum(part_tot * part_scale, axis=0) + loc_tot * loc_scale
    safe_totals = jnp.where(totals > 0, totals, 1.0)
    attention = jnp.where(
        own_live[:, None, None], accumulated / safe_totals[..., None], 0.0
    ).astype(jnp.bfloat16).reshape(query_rows, local_heads * HEAD_SIZE)
    projected = jnp.dot(attention, w_out, preferred_element_type=jnp.float32)
    combined = jnp.sum(mp_scatter(projected, n_mp), axis=0).astype(jnp.bfloat16)
    return (combined[:prompt_rows], combined[prompt_rows:])


def solution(mesh):
    global SEQ_SHAPE
    sizes = dict(zip(mesh.axis_names, mesh.devices.shape))
    seq_devices = mesh.devices.reshape(sizes["seq"], sizes["mp"])[:, 0]
    xs = sorted({d.coords[0] for d in seq_devices})
    SEQ_SHAPE = (len(xs), sizes["seq"] // len(xs))
    return jax.shard_map(
        local,
        mesh=mesh,
        in_specs=(
            P("seq", "mp"),
            P("seq", "mp"),
            P("seq", None, "mp"),
            P("seq", None, "mp"),
            P(),
            P(None, "mp"),
            P(None, "mp"),
            P(None, "mp"),
            P("mp", None),
            P(),
            P(),
            P(),
            P(),
            P(),
        ),
        out_specs=(P("seq", "mp"), P("seq", "mp")),
        check_vma=False,
    )
```

```python
import functools
import math

import jax
import jax.numpy as jnp
from jax import lax
from jax.experimental import pallas as pl
from jax.experimental.pallas import tpu as pltpu
from jax.sharding import PartitionSpec as P

HEAD_SIZE = 128
NEGATIVE_FLOOR = -1e30


def apply_rotation(vectors, positions):
    half_width = vectors.shape[-1] // 2
    exponent = jnp.arange(half_width).astype(jnp.float32) * (2.0 / vectors.shape[-1])
    frequency = jnp.exp(-exponent * math.log(500000.0))
    angles = positions.astype(jnp.float32)[:, None] * frequency[None, :]
    cosines = jnp.cos(angles)[:, None, :]
    sines = jnp.sin(angles)[:, None, :]
    leading = vectors[..., :half_width]
    trailing = vectors[..., half_width:]
    return jnp.concatenate(
        [leading * cosines - trailing * sines, trailing * cosines + leading * sines], axis=-1
    )


def normalize(rows_in, norm_gain):
    values = rows_in.astype(jnp.float32)
    inverse_rms = lax.rsqrt(jnp.mean(values * values, axis=-1, keepdims=True) + 1e-05)
    return (values * inverse_rms * norm_gain).astype(jnp.bfloat16)


MESH = pl.DeviceIdType.MESH


def passage_kernel(nx, nz, flags_ref, q_ref, k_ref, v_ref, lim_ref, out_ref):
    nb, rows, _ = q_ref.shape
    keys = k_ref.shape[0]
    token = lax.broadcasted_iota(jnp.int32, (rows, keys), 1)
    sub = lax.broadcasted_iota(jnp.int32, (16, rows), 0)

    def split(m_row, l_row):
        m_hi = m_row.astype(jnp.bfloat16).astype(jnp.float32)
        l_hi = l_row.astype(jnp.bfloat16).astype(jnp.float32)
        st = jnp.where(
            sub == 0,
            m_row,
            jnp.where(
                sub == 1,
                m_row - m_hi,
                jnp.where(sub == 2, l_row, jnp.where(sub == 3, l_row - l_hi, 0.0)),
            ),
        )
        return st.astype(jnp.bfloat16)

    def body(b, carry):
        flag = flags_ref[b]

        @pl.when(flag == 0)
        def _():
            out_ref[b, 0:rows] = jnp.zeros((rows, HEAD_SIZE), out_ref.dtype)
            floor = jnp.full((16, rows), NEGATIVE_FLOOR, jnp.float32)
            out_ref[b, rows:] = split(floor, jnp.zeros((16, rows), jnp.float32))

        @pl.when(flag > 0)
        def _():
            d = b // 2
            stored = ((d % nz) * nx + d // nz) * 2 + b % 2
            scores = lax.dot_general(
                q_ref[stored], k_ref[...], (((1,), (1,)), ((), ())), preferred_element_type=jnp.float32
            ) * (1.0 / math.sqrt(HEAD_SIZE))
            limit = jnp.where(flag == 2, lim_ref[...], keys - 1)
            scores = jnp.where(token <= limit, scores, NEGATIVE_FLOOR)
            maxima = jnp.max(scores, axis=1, keepdims=True)
            weights = jnp.exp(scores - maxima)
            totals = jnp.sum(weights, axis=1, keepdims=True)
            out_ref[b, 0:rows] = jnp.dot(
                weights.astype(jnp.bfloat16), v_ref[...], preferred_element_type=jnp.float32
            ).astype(out_ref.dtype)
            m_row = jnp.transpose(jnp.broadcast_to(maxima, (rows, rows)))[0:16]
            l_row = jnp.transpose(jnp.broadcast_to(totals, (rows, rows)))[0:16]
            out_ref[b, rows:] = split(m_row, l_row)

        return carry

    lax.fori_loop(0, nb, body, 0)


def passage_attention(nx, nz, flags, q_blocks, keys, values, lim):
    nb, rows, _ = q_blocks.shape
    vmem = pl.BlockSpec(memory_space=pltpu.VMEM)
    return pl.pallas_call(
        functools.partial(passage_kernel, nx, nz),
        in_specs=[pl.BlockSpec(memory_space=pltpu.SMEM), vmem, vmem, vmem, vmem],
        out_specs=vmem,
        out_shape=jax.ShapeDtypeStruct((nb, rows + 16, HEAD_SIZE), jnp.bfloat16),
    )(flags, q_blocks, keys, values, lim)


def mp_gather_kernel(n, x_ref, y_ref, send_sem, recv_sem, local_sem):
    me = lax.axis_index("mp")
    row = lax.axis_index("seq")
    width = x_ref.shape[1]
    barrier = pltpu.get_barrier_semaphore()
    for k in range(1, n):
        peer = lax.rem(me + k, n)
        pl.semaphore_signal(barrier, inc=1, device_id=(row, peer), device_id_type=MESH)
    pl.semaphore_wait(barrier, n - 1)
    cols = pl.ds(pl.multiple_of(me * width, width), width)
    copies = []
    for k in range(1, n):
        peer = lax.rem(me + k, n)
        c = pltpu.make_async_remote_copy(
            src_ref=x_ref,
            dst_ref=y_ref.at[:, cols],
            send_sem=send_sem.at[k],
            recv_sem=recv_sem.at[k],
            device_id=(row, peer),
            device_id_type=MESH,
        )
        c.start()
        copies.append(c)
    own = pltpu.make_async_copy(x_ref, y_ref.at[:, cols], local_sem)
    own.start()
    for c in copies:
        c.wait()
    own.wait()


def mp_gather(x, n):
    vmem = pl.BlockSpec(memory_space=pltpu.VMEM)
    return pl.pallas_call(
        functools.partial(mp_gather_kernel, n),
        in_specs=[vmem],
        out_specs=vmem,
        out_shape=jax.ShapeDtypeStruct((x.shape[0], x.shape[1] * n), x.dtype),
        scratch_shapes=[
            pltpu.SemaphoreType.DMA((n,)),
            pltpu.SemaphoreType.DMA((n,)),
            pltpu.SemaphoreType.DMA(()),
        ],
        compiler_params=pltpu.CompilerParams(collective_id=0, has_side_effects=True),
    )(x)


def mp_scatter_kernel(n, x_ref, y_ref, send_sem, recv_sem, local_sem):
    me = lax.axis_index("mp")
    row = lax.axis_index("seq")
    width = y_ref.shape[2]
    barrier = pltpu.get_barrier_semaphore()
    for k in range(1, n):
        peer = lax.rem(me + k, n)
        pl.semaphore_signal(barrier, inc=1, device_id=(row, peer), device_id_type=MESH)
    pl.semaphore_wait(barrier, n - 1)
    copies = []
    for k in range(1, n):
        peer = lax.rem(me + k, n)
        c = pltpu.make_async_remote_copy(
            src_ref=x_ref.at[:, pl.ds(pl.multiple_of(peer * width, width), width)],
            dst_ref=y_ref.at[me],
            send_sem=send_sem.at[k],
            recv_sem=recv_sem.at[k],
            device_id=(row, peer),
            device_id_type=MESH,
        )
        c.start()
        copies.append(c)
    own = pltpu.make_async_copy(
        x_ref.at[:, pl.ds(pl.multiple_of(me * width, width), width)], y_ref.at[me], local_sem
    )
    own.start()
    for c in copies:
        c.wait()
    own.wait()


def mp_scatter(x, n):
    vmem = pl.BlockSpec(memory_space=pltpu.VMEM)
    return pl.pallas_call(
        functools.partial(mp_scatter_kernel, n),
        in_specs=[vmem],
        out_specs=vmem,
        out_shape=jax.ShapeDtypeStruct((n, x.shape[0], x.shape[1] // n), x.dtype),
        scratch_shapes=[
            pltpu.SemaphoreType.DMA((n,)),
            pltpu.SemaphoreType.DMA((n,)),
            pltpu.SemaphoreType.DMA(()),
        ],
        compiler_params=pltpu.CompilerParams(collective_id=1, has_side_effects=True),
    )(x)


def relay_gather_kernel(nx, nz, x_ref, y_ref, sx_send, sx_recv, zp_send, zp_recv, zm_send, zm_recv, own_sem):
    me = lax.axis_index("seq")
    mp = lax.axis_index("mp")
    x = me // nz
    z = me % nz
    up = lax.rem(z + 1, nz)
    down = lax.rem(z + nz - 1, nz)
    barrier = pltpu.get_barrier_semaphore()
    peers = [(lax.rem(x + k, nx) * nz + z, mp) for k in range(1, nx)]
    peers += [(x * nz + up, mp), (x * nz + down, mp)]
    for p in peers:
        pl.semaphore_signal(barrier, inc=1, device_id=p, device_id_type=MESH)
    pl.semaphore_wait(barrier, len(peers))

    slot = z * nx + x
    first = []
    for k in range(1, nx):
        c = pltpu.make_async_remote_copy(
            src_ref=x_ref,
            dst_ref=y_ref.at[slot],
            send_sem=sx_send.at[k],
            recv_sem=sx_recv.at[k],
            device_id=peers[k - 1],
            device_id_type=MESH,
        )
        c.start()
        first.append(c)
    own = pltpu.make_async_copy(x_ref, y_ref.at[slot], own_sem)
    own.start()
    for c in first:
        c.wait()
    own.wait()

    steps = nz // 2
    half = nx // 2
    last = {}
    sent = []
    for t in range(1, steps + 1):
        for i in range(nx):
            for sign, send_sem, recv_sem, target in (
                (1, zp_send, zp_recv, up),
                (-1, zm_send, zm_recv, down),
            ):
                if t == steps and (i < half) != (sign == 1):
                    continue
                if t > 1:
                    last[(sign, i)].wait_recv()
                column = lax.rem(z - sign * (t - 1) + nz, nz)
                c = pltpu.make_async_remote_copy(
                    src_ref=y_ref.at[column * nx + i],
                    dst_ref=y_ref.at[column * nx + i],
                    send_sem=send_sem.at[t, i],
                    recv_sem=recv_sem.at[t, i],
                    device_id=(x * nz + target, mp),
                    device_id_type=MESH,
                )
                c.start()
                last[(sign, i)] = c
                sent.append(c)
    for c in last.values():
        c.wait_recv()
    for c in sent:
        c.wait_send()


def relay_gather(x, nx, nz):
    vmem = pl.BlockSpec(memory_space=pltpu.VMEM)
    steps = nz // 2
    return pl.pallas_call(
        functools.partial(relay_gather_kernel, nx, nz),
        in_specs=[vmem],
        out_specs=vmem,
        out_shape=jax.ShapeDtypeStruct((nx * nz,) + x.shape, x.dtype),
        scratch_shapes=[
            pltpu.SemaphoreType.DMA((nx,)),
            pltpu.SemaphoreType.DMA((nx,)),
            pltpu.SemaphoreType.DMA((steps + 1, nx)),
            pltpu.SemaphoreType.DMA((steps + 1, nx)),
            pltpu.SemaphoreType.DMA((steps + 1, nx)),
            pltpu.SemaphoreType.DMA((steps + 1, nx)),
            pltpu.SemaphoreType.DMA(()),
        ],
        compiler_params=pltpu.CompilerParams(collective_id=2, has_side_effects=True),
    )(x)


def merge_piece(a, b, rows):
    af = a.astype(jnp.float32)
    bf = b.astype(jnp.float32)
    m1 = af[rows : rows + 1] + af[rows + 1 : rows + 2]
    l1 = af[rows + 2 : rows + 3] + af[rows + 3 : rows + 4]
    m2 = bf[rows : rows + 1] + bf[rows + 1 : rows + 2]
    l2 = bf[rows + 2 : rows + 3] + bf[rows + 3 : rows + 4]
    top = jnp.maximum(m1, m2)
    s1 = jnp.exp(m1 - top)
    s2 = jnp.exp(m2 - top)
    total = l1 * s1 + l2 * s2
    c1 = jnp.transpose(jnp.broadcast_to(s1, (rows, rows)))
    c2 = jnp.transpose(jnp.broadcast_to(s2, (rows, rows)))
    acc = af[0:rows] * c1 + bf[0:rows] * c2
    sub = lax.broadcasted_iota(jnp.int32, (16, rows), 0)
    top_hi = top.astype(jnp.bfloat16).astype(jnp.float32)
    tot_hi = total.astype(jnp.bfloat16).astype(jnp.float32)
    st = jnp.where(
        sub == 0,
        top,
        jnp.where(
            sub == 1, top - top_hi, jnp.where(sub == 2, total, jnp.where(sub == 3, total - tot_hi, 0.0))
        ),
    )
    return acc.astype(jnp.bfloat16), st.astype(jnp.bfloat16)


def relay_reduce_kernel(
    nx, nz, x_ref, y_ref, rp, rm, bp, bm, col, sp_send, sp_recv, sm_send, sm_recv, sx_send, sx_recv
):
    me = lax.axis_index("seq")
    mp = lax.axis_index("mp")
    x = me // nz
    z = me % nz
    up = lax.rem(z + 1, nz)
    down = lax.rem(z + nz - 1, nz)
    rows = x_ref.shape[2] - 16
    barrier = pltpu.get_barrier_semaphore()
    peers = [(lax.rem(x + k, nx) * nz + z, mp) for k in range(1, nx)]
    peers += [(x * nz + up, mp), (x * nz + down, mp)]
    for p in peers:
        pl.semaphore_signal(barrier, inc=1, device_id=p, device_id_type=MESH)
    pl.semaphore_wait(barrier, len(peers))

    def merge_into(dst, first, second):
        for h in range(2):
            acc, st = merge_piece(first[h], second[h], rows)
            dst[h, 0:rows] = acc
            dst[h, rows:] = st

    steps = nz // 2
    half = nx // 2
    last = {}
    sent = []
    dirs = ((1, rp, bp, sp_send, sp_recv, up), (-1, rm, bm, sm_send, sm_recv, down))
    for t in range(1, steps + 1):
        for i in range(nx):
            for sign, recv_buf, send_buf, send_sem, recv_sem, target in dirs:
                if t == 1 and (i < half) != (sign == 1):
                    continue
                column = lax.rem(z + sign * (steps + 1 - t) + nz, nz)
                own = x_ref.at[i * nz + column]
                if (sign, i) in last:
                    last[(sign, i)].wait_recv()
                    merge_into(send_buf.at[t, i], own, recv_buf.at[t - 1, i])
                    src = send_buf.at[t, i]
                else:
                    src = own
                c = pltpu.make_async_remote_copy(
                    src_ref=src,
                    dst_ref=recv_buf.at[t, i],
                    send_sem=send_sem.at[t, i],
                    recv_sem=recv_sem.at[t, i],
                    device_id=(x * nz + target, mp),
                    device_id_type=MESH,
                )
                c.start()
                last[(sign, i)] = c
                sent.append(c)

    mine = []
    for i in range(nx):
        last[(1, i)].wait_recv()
        last[(-1, i)].wait_recv()
        merge_into(col.at[i], x_ref.at[i * nz + z], rp.at[steps, i])
        merge_into(col.at[i], col.at[i], rm.at[steps, i])
    for k in range(1, nx):
        target = lax.rem(x + k, nx)
        c = pltpu.make_async_remote_copy(
            src_ref=col.at[target],
            dst_ref=y_ref.at[x],
            send_sem=sx_send.at[k],
            recv_sem=sx_recv.at[k],
            device_id=(target * nz + z, mp),
            device_id_type=MESH,
        )
        c.start()
        mine.append(c)
    y_ref[x] = col[x]
    for c in sent:
        c.wait_send()
    for c in mine:
        c.wait()


def relay_reduce(parts, nx, nz):
    vmem = pl.BlockSpec(memory_space=pltpu.VMEM)
    steps = nz // 2
    piece = parts.shape[1:]
    return pl.pallas_call(
        functools.partial(relay_reduce_kernel, nx, nz),
        in_specs=[vmem],
        out_specs=vmem,
        out_shape=jax.ShapeDtypeStruct((nx,) + piece, parts.dtype),
        scratch_shapes=[
            pltpu.VMEM((steps + 1, nx) + piece, parts.dtype),
            pltpu.VMEM((steps + 1, nx) + piece, parts.dtype),
            pltpu.VMEM((steps + 1, nx) + piece, parts.dtype),
            pltpu.VMEM((steps + 1, nx) + piece, parts.dtype),
            pltpu.VMEM((nx,) + piece, parts.dtype),
            pltpu.SemaphoreType.DMA((steps + 1, nx)),
            pltpu.SemaphoreType.DMA((steps + 1, nx)),
            pltpu.SemaphoreType.DMA((steps + 1, nx)),
            pltpu.SemaphoreType.DMA((steps + 1, nx)),
            pltpu.SemaphoreType.DMA((nx,)),
            pltpu.SemaphoreType.DMA((nx,)),
        ],
        compiler_params=pltpu.CompilerParams(collective_id=3, has_side_effects=True),
    )(parts)


def local(
    prompt_hidden,
    recompute_hidden,
    key_cache,
    value_cache,
    norm_gain,
    w_query,
    key_weight,
    value_weight,
    w_out,
    passage_owner,
    prompt_slot,
    prompt_length,
    recompute_count,
    recompute_index,
):
    prompt_rows = prompt_hidden.shape[0]
    recompute_rows = recompute_hidden.shape[0]
    query_rows = prompt_rows + recompute_rows
    passage_length = key_cache.shape[1]
    local_heads = w_query.shape[1] // HEAD_SIZE
    n_seq = passage_owner.shape[0]
    me = lax.axis_index("seq")
    scale = 1.0 / math.sqrt(HEAD_SIZE)

    seq_ids = jnp.arange(n_seq, dtype=jnp.int32)
    same_owner = passage_owner[:, None] == passage_owner[None, :]
    passage_rank = jnp.sum(
        jnp.where(same_owner & (seq_ids[None, :] < seq_ids[:, None]), 1, 0), axis=1
    ).astype(jnp.int32)
    held_count = jnp.sum(
        jnp.where(passage_owner[None, :] == prompt_slot[:, None], 1, 0), axis=1
    ).astype(jnp.int32)
    own_rank = passage_rank[me]
    own_owner = passage_owner[me]
    own_held = held_count[me]
    own_index = lax.dynamic_index_in_dim(recompute_index, me, 0, keepdims=False)
    own_length = prompt_length[me]
    own_count = recompute_count[me]

    prompt_pos = own_held * passage_length + jnp.arange(prompt_rows, dtype=jnp.int32)
    recompute_pos = own_rank * passage_length + own_index
    own_pos = jnp.concatenate([prompt_pos, recompute_pos])
    own_live = jnp.concatenate(
        [
            jnp.arange(prompt_rows, dtype=jnp.int32) < own_length,
            jnp.arange(recompute_rows, dtype=jnp.int32) < own_count,
        ]
    )

    rows_local = jnp.concatenate([prompt_hidden, recompute_hidden], axis=0)
    n_mp = w_out.shape[1] // rows_local.shape[1]
    full_rows = mp_gather(rows_local, n_mp)
    normalized_hidden = normalize(full_rows, norm_gain)
    queries = (
        apply_rotation(
            jnp.dot(normalized_hidden, w_query, preferred_element_type=jnp.float32).reshape(
                query_rows, local_heads, HEAD_SIZE
            ),
            own_pos,
        )
        .astype(jnp.bfloat16)
    )
    fresh_keys = (
        apply_rotation(
            jnp.dot(normalized_hidden, key_weight, preferred_element_type=jnp.float32).reshape(
                query_rows, 1, HEAD_SIZE
            ),
            own_pos,
        )
        .astype(jnp.bfloat16)
        .reshape(query_rows, HEAD_SIZE)
    )
    fresh_values = jnp.dot(
        normalized_hidden, value_weight, preferred_element_type=jnp.float32
    ).astype(jnp.bfloat16)

    position_shift = jnp.full((passage_length,), own_rank * passage_length, jnp.int32)
    shifted_keys = (
        apply_rotation(
            key_cache[0].astype(jnp.float32).reshape(passage_length, 1, HEAD_SIZE),
            position_shift,
        )
        .astype(jnp.bfloat16)
        .reshape(passage_length, HEAD_SIZE)
    )
    chosen = (own_index[:, None] == jnp.arange(passage_length, dtype=jnp.int32)[None, :]) & (
        jnp.arange(recompute_rows, dtype=jnp.int32)[:, None] < own_count
    )
    replaced = jnp.any(chosen, axis=0)[:, None]
    fresh_pair = jnp.concatenate([fresh_keys[prompt_rows:], fresh_values[prompt_rows:]], axis=1)
    placed = lax.dot_general(
        chosen.astype(jnp.bfloat16),
        fresh_pair,
        (((0,), (0,)), ((), ())),
        preferred_element_type=jnp.float32,
    ).astype(jnp.bfloat16)
    passage_keys = jnp.where(replaced, placed[:, :HEAD_SIZE], shifted_keys)
    passage_values = jnp.where(replaced, placed[:, HEAD_SIZE:], value_cache[0])

    nx, nz = SEQ_SHAPE
    all_queries = relay_gather(
        queries.reshape(2, prompt_rows * local_heads, HEAD_SIZE), nx, nz
    )
    q_blocks = all_queries.reshape(n_seq * 2, prompt_rows * local_heads, HEAD_SIZE)
    prompt_flag = jnp.where(prompt_slot == own_owner, 1, 0)
    recompute_flag = jnp.where(
        seq_ids == me, 2, jnp.where((passage_owner == own_owner) & (seq_ids > me), 1, 0)
    )
    flags = jnp.stack([prompt_flag, recompute_flag], axis=1).reshape(-1).astype(jnp.int32)
    lim = jnp.repeat(own_index, local_heads).reshape(-1, 1).astype(jnp.int32)
    packed = passage_attention(nx, nz, flags, q_blocks, passage_keys, passage_values, lim)
    block_rows = packed.shape[1]

    back = relay_reduce(packed.reshape(n_seq, 2, block_rows, HEAD_SIZE), nx, nz)
    n_parts = back.shape[0]
    rows128 = prompt_rows * local_heads
    stats_back = back[:, :, rows128 : rows128 + 4].astype(jnp.float32)
    part_max = (stats_back[:, :, 0] + stats_back[:, :, 1]).reshape(n_parts, query_rows, local_heads)
    part_tot = (stats_back[:, :, 2] + stats_back[:, :, 3]).reshape(n_parts, query_rows, local_heads)
    part_acc = (
        back[:, :, :rows128].reshape(n_parts, query_rows, local_heads, HEAD_SIZE).astype(jnp.float32)
    )

    pq = queries[:prompt_rows].astype(jnp.float32)
    pk = fresh_keys[:prompt_rows].astype(jnp.float32)
    pv = fresh_values[:prompt_rows].astype(jnp.float32)
    ps = jnp.einsum("qhd,kd->qhk", pq, pk) * scale
    jj = jnp.arange(prompt_rows, dtype=jnp.int32)
    pvis = (jj[None, :] <= jj[:, None]) & (jj[None, :] < own_length)
    ps = jnp.where(pvis[:, None, :], ps, NEGATIVE_FLOOR)
    pmax = jnp.max(ps, axis=-1)
    pw = jnp.where(pvis[:, None, :], jnp.exp(ps - pmax[..., None]), 0.0)
    ptot = jnp.sum(pw, axis=-1)
    pacc = jnp.einsum("qhk,kd->qhd", pw.astype(jnp.bfloat16).astype(jnp.float32), pv)
    loc_max = jnp.concatenate(
        [pmax, jnp.full((recompute_rows, local_heads), NEGATIVE_FLOOR, jnp.float32)]
    )
    loc_tot = jnp.concatenate([ptot, jnp.zeros((recompute_rows, local_heads), jnp.float32)])
    loc_acc = jnp.concatenate(
        [pacc, jnp.zeros((recompute_rows, local_heads, HEAD_SIZE), jnp.float32)]
    )

    highest = jnp.maximum(jnp.max(part_max, axis=0), loc_max)
    part_scale = jnp.exp(part_max - highest[None])
    loc_scale = jnp.exp(loc_max - highest)
    accumulated = jnp.sum(part_acc * part_scale[..., None], axis=0) + loc_acc * loc_scale[..., None]
    totals = jnp.sum(part_tot * part_scale, axis=0) + loc_tot * loc_scale
    safe_totals = jnp.where(totals > 0, totals, 1.0)
    attention = jnp.where(
        own_live[:, None, None], accumulated / safe_totals[..., None], 0.0
    ).astype(jnp.bfloat16).reshape(query_rows, local_heads * HEAD_SIZE)
    projected = jnp.dot(attention, w_out, preferred_element_type=jnp.float32)
    shares = mp_scatter(projected.astype(jnp.bfloat16), n_mp)
    combined = jnp.sum(shares.astype(jnp.float32), axis=0).astype(jnp.bfloat16)
    return (combined[:prompt_rows], combined[prompt_rows:])


def solution(mesh):
    global SEQ_SHAPE
    sizes = dict(zip(mesh.axis_names, mesh.devices.shape))
    seq_devices = mesh.devices.reshape(sizes["seq"], sizes["mp"])[:, 0]
    xs = sorted({d.coords[0] for d in seq_devices})
    SEQ_SHAPE = (len(xs), sizes["seq"] // len(xs))
    return jax.shard_map(
        local,
        mesh=mesh,
        in_specs=(
            P("seq", "mp"),
            P("seq", "mp"),
            P("seq", None, "mp"),
            P("seq", None, "mp"),
            P(),
            P(None, "mp"),
            P(None, "mp"),
            P(None, "mp"),
            P("mp", None),
            P(),
            P(),
            P(),
            P(),
            P(),
        ),
        out_specs=(P("seq", "mp"), P("seq", "mp")),
        check_vma=False,
    )
```

```python
import functools
import math

import jax
import jax.numpy as jnp
from jax import lax
from jax.experimental import pallas as pl
from jax.experimental.pallas import tpu as pltpu
from jax.sharding import PartitionSpec as P

HEAD_SIZE = 128
NEGATIVE_FLOOR = -1e30


def apply_rotation(vectors, positions):
    half_width = vectors.shape[-1] // 2
    exponent = jnp.arange(half_width).astype(jnp.float32) * (2.0 / vectors.shape[-1])
    frequency = jnp.exp(-exponent * math.log(500000.0))
    angles = positions.astype(jnp.float32)[:, None] * frequency[None, :]
    cosines = jnp.cos(angles)[:, None, :]
    sines = jnp.sin(angles)[:, None, :]
    leading = vectors[..., :half_width]
    trailing = vectors[..., half_width:]
    return jnp.concatenate(
        [leading * cosines - trailing * sines, trailing * cosines + leading * sines], axis=-1
    )


def normalize(rows_in, norm_gain):
    values = rows_in.astype(jnp.float32)
    inverse_rms = lax.rsqrt(jnp.mean(values * values, axis=-1, keepdims=True) + 1e-05)
    return (values * inverse_rms * norm_gain).astype(jnp.bfloat16)


MESH = pl.DeviceIdType.MESH


def passage_kernel(nx, nz, flags_ref, q_ref, k_ref, v_ref, lim_ref, out_ref):
    nb, rows, _ = q_ref.shape
    keys = k_ref.shape[0]
    token = lax.broadcasted_iota(jnp.int32, (rows, keys), 1)
    sub = lax.broadcasted_iota(jnp.int32, (16, rows), 0)

    def split(m_row, l_row):
        m_hi = m_row.astype(jnp.bfloat16).astype(jnp.float32)
        l_hi = l_row.astype(jnp.bfloat16).astype(jnp.float32)
        st = jnp.where(
            sub == 0,
            m_row,
            jnp.where(
                sub == 1,
                m_row - m_hi,
                jnp.where(sub == 2, l_row, jnp.where(sub == 3, l_row - l_hi, 0.0)),
            ),
        )
        return st.astype(jnp.bfloat16)

    def body(b, carry):
        flag = flags_ref[b]

        @pl.when(flag == 0)
        def _():
            out_ref[b, 0:rows] = jnp.zeros((rows, HEAD_SIZE), out_ref.dtype)
            floor = jnp.full((16, rows), NEGATIVE_FLOOR, jnp.float32)
            out_ref[b, rows:] = split(floor, jnp.zeros((16, rows), jnp.float32))

        @pl.when(flag > 0)
        def _():
            d = b // 2
            stored = ((d % nz) * nx + d // nz) * 2 + b % 2
            scores = lax.dot_general(
                q_ref[stored], k_ref[...], (((1,), (1,)), ((), ())), preferred_element_type=jnp.float32
            ) * (1.0 / math.sqrt(HEAD_SIZE))
            limit = jnp.where(flag == 2, lim_ref[...], keys - 1)
            scores = jnp.where(token <= limit, scores, NEGATIVE_FLOOR)
            maxima = jnp.max(scores, axis=1, keepdims=True)
            weights = jnp.exp(scores - maxima)
            totals = jnp.sum(weights, axis=1, keepdims=True)
            out_ref[b, 0:rows] = jnp.dot(
                weights.astype(jnp.bfloat16), v_ref[...], preferred_element_type=jnp.float32
            ).astype(out_ref.dtype)
            m_row = jnp.transpose(jnp.broadcast_to(maxima, (rows, rows)))[0:16]
            l_row = jnp.transpose(jnp.broadcast_to(totals, (rows, rows)))[0:16]
            out_ref[b, rows:] = split(m_row, l_row)

        return carry

    lax.fori_loop(0, nb, body, 0)


def passage_attention(nx, nz, flags, q_blocks, keys, values, lim):
    nb, rows, _ = q_blocks.shape
    vmem = pl.BlockSpec(memory_space=pltpu.VMEM)
    return pl.pallas_call(
        functools.partial(passage_kernel, nx, nz),
        in_specs=[pl.BlockSpec(memory_space=pltpu.SMEM), vmem, vmem, vmem, vmem],
        out_specs=vmem,
        out_shape=jax.ShapeDtypeStruct((nb, rows + 16, HEAD_SIZE), jnp.bfloat16),
    )(flags, q_blocks, keys, values, lim)


def mp_gather_kernel(n, x_ref, y_ref, send_sem, recv_sem, local_sem):
    me = lax.axis_index("mp")
    row = lax.axis_index("seq")
    width = x_ref.shape[1]
    barrier = pltpu.get_barrier_semaphore()
    for k in range(1, n):
        peer = lax.rem(me + k, n)
        pl.semaphore_signal(barrier, inc=1, device_id=(row, peer), device_id_type=MESH)
    pl.semaphore_wait(barrier, n - 1)
    cols = pl.ds(pl.multiple_of(me * width, width), width)
    copies = []
    for k in range(1, n):
        peer = lax.rem(me + k, n)
        c = pltpu.make_async_remote_copy(
            src_ref=x_ref,
            dst_ref=y_ref.at[:, cols],
            send_sem=send_sem.at[k],
            recv_sem=recv_sem.at[k],
            device_id=(row, peer),
            device_id_type=MESH,
        )
        c.start()
        copies.append(c)
    own = pltpu.make_async_copy(x_ref, y_ref.at[:, cols], local_sem)
    own.start()
    for c in copies:
        c.wait()
    own.wait()


def mp_gather(x, n):
    vmem = pl.BlockSpec(memory_space=pltpu.VMEM)
    return pl.pallas_call(
        functools.partial(mp_gather_kernel, n),
        in_specs=[vmem],
        out_specs=vmem,
        out_shape=jax.ShapeDtypeStruct((x.shape[0], x.shape[1] * n), x.dtype),
        scratch_shapes=[
            pltpu.SemaphoreType.DMA((n,)),
            pltpu.SemaphoreType.DMA((n,)),
            pltpu.SemaphoreType.DMA(()),
        ],
        compiler_params=pltpu.CompilerParams(collective_id=0, has_side_effects=True),
    )(x)


def mp_scatter_kernel(n, x_ref, y_ref, send_sem, recv_sem, local_sem):
    me = lax.axis_index("mp")
    row = lax.axis_index("seq")
    width = y_ref.shape[2]
    barrier = pltpu.get_barrier_semaphore()
    for k in range(1, n):
        peer = lax.rem(me + k, n)
        pl.semaphore_signal(barrier, inc=1, device_id=(row, peer), device_id_type=MESH)
    pl.semaphore_wait(barrier, n - 1)
    copies = []
    for k in range(1, n):
        peer = lax.rem(me + k, n)
        c = pltpu.make_async_remote_copy(
            src_ref=x_ref.at[:, pl.ds(pl.multiple_of(peer * width, width), width)],
            dst_ref=y_ref.at[me],
            send_sem=send_sem.at[k],
            recv_sem=recv_sem.at[k],
            device_id=(row, peer),
            device_id_type=MESH,
        )
        c.start()
        copies.append(c)
    own = pltpu.make_async_copy(
        x_ref.at[:, pl.ds(pl.multiple_of(me * width, width), width)], y_ref.at[me], local_sem
    )
    own.start()
    for c in copies:
        c.wait()
    own.wait()


def mp_scatter(x, n):
    vmem = pl.BlockSpec(memory_space=pltpu.VMEM)
    return pl.pallas_call(
        functools.partial(mp_scatter_kernel, n),
        in_specs=[vmem],
        out_specs=vmem,
        out_shape=jax.ShapeDtypeStruct((n, x.shape[0], x.shape[1] // n), x.dtype),
        scratch_shapes=[
            pltpu.SemaphoreType.DMA((n,)),
            pltpu.SemaphoreType.DMA((n,)),
            pltpu.SemaphoreType.DMA(()),
        ],
        compiler_params=pltpu.CompilerParams(collective_id=1, has_side_effects=True),
    )(x)


def relay_gather_kernel(nx, nz, x_ref, y_ref, *sems):
    (sx_send, sx_recv, zp_send, zp_recv, zm_send, zm_recv, own_sem,
     bp_send, bp_recv, bm_send, bm_recv, xp_send, xp_recv, xm_send, xm_recv,
     fp_send, fp_recv, fm_send, fm_recv) = sems
    me = lax.axis_index("seq")
    mp = lax.axis_index("mp")
    x = me // nz
    z = me % nz
    up = lax.rem(z + 1, nz)
    down = lax.rem(z + nz - 1, nz)
    right = lax.rem(x + 1, nx)
    left = lax.rem(x + nx - 1, nx)
    barrier = pltpu.get_barrier_semaphore()
    peers = [(lax.rem(x + k, nx) * nz + z, mp) for k in range(1, nx)]
    peers += [(x * nz + up, mp), (x * nz + down, mp)]
    for p in peers:
        pl.semaphore_signal(barrier, inc=1, device_id=p, device_id_type=MESH)
    pl.semaphore_wait(barrier, len(peers))

    def copy(src, dst, send_sem, recv_sem, device):
        c = pltpu.make_async_remote_copy(
            src_ref=src,
            dst_ref=dst,
            send_sem=send_sem,
            recv_sem=recv_sem,
            device_id=device,
            device_id_type=MESH,
        )
        c.start()
        return c

    sent = []
    slot = z * nx + x
    first = [
        copy(x_ref.at[0], y_ref.at[slot, 0], sx_send.at[k], sx_recv.at[k], peers[k - 1])
        for k in range(1, nx)
    ]
    own = pltpu.make_async_copy(x_ref, y_ref.at[slot], own_sem)
    own.start()

    def x_out(column):
        a = copy(
            y_ref.at[column * nx + x, 1], y_ref.at[column * nx + x, 1],
            xp_send.at[column], xp_recv.at[column], (right * nz + z, mp),
        )
        b = copy(
            y_ref.at[column * nx + x, 1], y_ref.at[column * nx + x, 1],
            xm_send.at[column], xm_recv.at[column], (left * nz + z, mp),
        )
        return [a, b]

    own.wait()
    steps = nz // 2
    half = nx // 2
    zlast = {}
    blast = {}
    xcopies = {}
    for c in first:
        c.wait()
    for t in range(1, steps + 1):
        for sign, send_sem, recv_sem, target, count in (
            (1, bp_send, bp_recv, up, steps),
            (-1, bm_send, bm_recv, down, nz - 1 - steps),
        ):
            if t > count:
                continue
            if t > 1:
                blast[sign].wait_recv()
            column = lax.rem(z - sign * (t - 1) + nz, nz)
            if t > 1:
                xcopies[(sign, t - 1)] = x_out(column)
            elif sign == 1:
                xcopies[(0, 0)] = x_out(column)
            blast[sign] = copy(
                y_ref.at[column * nx + x, 1], y_ref.at[column * nx + x, 1],
                send_sem.at[t], recv_sem.at[t], (x * nz + target, mp),
            )
            sent.append(blast[sign])
        for i in range(nx):
            for sign, send_sem, recv_sem, target in (
                (1, zp_send, zp_recv, up),
                (-1, zm_send, zm_recv, down),
            ):
                if t == steps and (i < half) != (sign == 1):
                    continue
                if t > 1:
                    zlast[(sign, i)].wait_recv()
                column = lax.rem(z - sign * (t - 1) + nz, nz)
                zlast[(sign, i)] = copy(
                    y_ref.at[column * nx + i, 0], y_ref.at[column * nx + i, 0],
                    send_sem.at[t, i], recv_sem.at[t, i], (x * nz + target, mp),
                )
                sent.append(zlast[(sign, i)])
    for sign, count in ((1, steps), (-1, nz - 1 - steps)):
        blast[sign].wait_recv()
        column = lax.rem(z - sign * count + nz, nz)
        xcopies[(sign, count)] = x_out(column)
    order = [(0, 0)] + [(s, t) for t in range(1, steps + 1) for s in (1, -1) if (s, t) in xcopies]
    forwards = []
    for key in order:
        sign, t = key
        column = lax.rem(z - sign * t + nz, nz)
        from_left, from_right = xcopies[key]
        from_left.wait_recv()
        from_right.wait_recv()
        sent += xcopies[key]
    for zc in range(nz):
        if zc < nz // 2:
            forwards.append(
                copy(
                    y_ref.at[zc * nx + left, 1], y_ref.at[zc * nx + left, 1],
                    fp_send.at[zc], fp_recv.at[zc], (right * nz + z, mp),
                )
            )
        else:
            forwards.append(
                copy(
                    y_ref.at[zc * nx + right, 1], y_ref.at[zc * nx + right, 1],
                    fm_send.at[zc], fm_recv.at[zc], (left * nz + z, mp),
                )
            )
    for c in zlast.values():
        c.wait_recv()
    for c in forwards:
        c.wait_recv()
    for c in sent:
        c.wait_send()
    for c in forwards:
        c.wait_send()


def relay_gather(x, nx, nz):
    assert nx == 4 and nz % 2 == 0
    vmem = pl.BlockSpec(memory_space=pltpu.VMEM)
    steps = nz // 2
    dma = pltpu.SemaphoreType.DMA
    return pl.pallas_call(
        functools.partial(relay_gather_kernel, nx, nz),
        in_specs=[vmem],
        out_specs=vmem,
        out_shape=jax.ShapeDtypeStruct((nx * nz,) + x.shape, x.dtype),
        scratch_shapes=[
            dma((nx,)), dma((nx,)),
            dma((steps + 1, nx)), dma((steps + 1, nx)), dma((steps + 1, nx)), dma((steps + 1, nx)),
            dma(()),
            dma((steps + 1,)), dma((steps + 1,)), dma((steps + 1,)), dma((steps + 1,)),
            dma((nz,)), dma((nz,)), dma((nz,)), dma((nz,)),
            dma((nz,)), dma((nz,)), dma((nz,)), dma((nz,)),
        ],
        compiler_params=pltpu.CompilerParams(collective_id=2, has_side_effects=True),
    )(x)


def merge_piece(a, b, rows):
    af = a.astype(jnp.float32)
    bf = b.astype(jnp.float32)
    m1 = af[rows : rows + 1] + af[rows + 1 : rows + 2]
    l1 = af[rows + 2 : rows + 3] + af[rows + 3 : rows + 4]
    m2 = bf[rows : rows + 1] + bf[rows + 1 : rows + 2]
    l2 = bf[rows + 2 : rows + 3] + bf[rows + 3 : rows + 4]
    top = jnp.maximum(m1, m2)
    s1 = jnp.exp(m1 - top)
    s2 = jnp.exp(m2 - top)
    total = l1 * s1 + l2 * s2
    c1 = jnp.transpose(jnp.broadcast_to(s1, (rows, rows)))
    c2 = jnp.transpose(jnp.broadcast_to(s2, (rows, rows)))
    acc = af[0:rows] * c1 + bf[0:rows] * c2
    sub = lax.broadcasted_iota(jnp.int32, (16, rows), 0)
    top_hi = top.astype(jnp.bfloat16).astype(jnp.float32)
    tot_hi = total.astype(jnp.bfloat16).astype(jnp.float32)
    st = jnp.where(
        sub == 0,
        top,
        jnp.where(
            sub == 1, top - top_hi, jnp.where(sub == 2, total, jnp.where(sub == 3, total - tot_hi, 0.0))
        ),
    )
    return acc.astype(jnp.bfloat16), st.astype(jnp.bfloat16)


def relay_reduce_kernel(
    nx, nz, x_ref, y_ref, rp, rm, bp, bm, col, sp_send, sp_recv, sm_send, sm_recv, sx_send, sx_recv
):
    me = lax.axis_index("seq")
    mp = lax.axis_index("mp")
    x = me // nz
    z = me % nz
    up = lax.rem(z + 1, nz)
    down = lax.rem(z + nz - 1, nz)
    rows = x_ref.shape[2] - 16
    barrier = pltpu.get_barrier_semaphore()
    peers = [(lax.rem(x + k, nx) * nz + z, mp) for k in range(1, nx)]
    peers += [(x * nz + up, mp), (x * nz + down, mp)]
    for p in peers:
        pl.semaphore_signal(barrier, inc=1, device_id=p, device_id_type=MESH)
    pl.semaphore_wait(barrier, len(peers))

    def merge_into(dst, first, second):
        for h in range(2):
            acc, st = merge_piece(first[h], second[h], rows)
            dst[h, 0:rows] = acc
            dst[h, rows:] = st

    steps = nz // 2
    half = nx // 2
    last = {}
    sent = []
    dirs = ((1, rp, bp, sp_send, sp_recv, up), (-1, rm, bm, sm_send, sm_recv, down))
    for t in range(1, steps + 1):
        for i in range(nx):
            for sign, recv_buf, send_buf, send_sem, recv_sem, target in dirs:
                if t == 1 and (i < half) != (sign == 1):
                    continue
                column = lax.rem(z + sign * (steps + 1 - t) + nz, nz)
                own = x_ref.at[i * nz + column]
                if (sign, i) in last:
                    last[(sign, i)].wait_recv()
                    merge_into(send_buf.at[t, i], own, recv_buf.at[t - 1, i])
                    src = send_buf.at[t, i]
                else:
                    src = own
                c = pltpu.make_async_remote_copy(
                    src_ref=src,
                    dst_ref=recv_buf.at[t, i],
                    send_sem=send_sem.at[t, i],
                    recv_sem=recv_sem.at[t, i],
                    device_id=(x * nz + target, mp),
                    device_id_type=MESH,
                )
                c.start()
                last[(sign, i)] = c
                sent.append(c)

    mine = []
    for i in range(nx):
        last[(1, i)].wait_recv()
        last[(-1, i)].wait_recv()
        merge_into(col.at[i], x_ref.at[i * nz + z], rp.at[steps, i])
        merge_into(col.at[i], col.at[i], rm.at[steps, i])
    for k in range(1, nx):
        target = lax.rem(x + k, nx)
        c = pltpu.make_async_remote_copy(
            src_ref=col.at[target],
            dst_ref=y_ref.at[x],
            send_sem=sx_send.at[k],
            recv_sem=sx_recv.at[k],
            device_id=(target * nz + z, mp),
            device_id_type=MESH,
        )
        c.start()
        mine.append(c)
    y_ref[x] = col[x]
    for c in sent:
        c.wait_send()
    for c in mine:
        c.wait()


def relay_reduce(parts, nx, nz):
    vmem = pl.BlockSpec(memory_space=pltpu.VMEM)
    steps = nz // 2
    piece = parts.shape[1:]
    return pl.pallas_call(
        functools.partial(relay_reduce_kernel, nx, nz),
        in_specs=[vmem],
        out_specs=vmem,
        out_shape=jax.ShapeDtypeStruct((nx,) + piece, parts.dtype),
        scratch_shapes=[
            pltpu.VMEM((steps + 1, nx) + piece, parts.dtype),
            pltpu.VMEM((steps + 1, nx) + piece, parts.dtype),
            pltpu.VMEM((steps + 1, nx) + piece, parts.dtype),
            pltpu.VMEM((steps + 1, nx) + piece, parts.dtype),
            pltpu.VMEM((nx,) + piece, parts.dtype),
            pltpu.SemaphoreType.DMA((steps + 1, nx)),
            pltpu.SemaphoreType.DMA((steps + 1, nx)),
            pltpu.SemaphoreType.DMA((steps + 1, nx)),
            pltpu.SemaphoreType.DMA((steps + 1, nx)),
            pltpu.SemaphoreType.DMA((nx,)),
            pltpu.SemaphoreType.DMA((nx,)),
        ],
        compiler_params=pltpu.CompilerParams(collective_id=3, has_side_effects=True),
    )(parts)


def local(
    prompt_hidden,
    recompute_hidden,
    key_cache,
    value_cache,
    norm_gain,
    w_query,
    key_weight,
    value_weight,
    w_out,
    passage_owner,
    prompt_slot,
    prompt_length,
    recompute_count,
    recompute_index,
):
    prompt_rows = prompt_hidden.shape[0]
    recompute_rows = recompute_hidden.shape[0]
    query_rows = prompt_rows + recompute_rows
    passage_length = key_cache.shape[1]
    local_heads = w_query.shape[1] // HEAD_SIZE
    n_seq = passage_owner.shape[0]
    me = lax.axis_index("seq")
    scale = 1.0 / math.sqrt(HEAD_SIZE)

    seq_ids = jnp.arange(n_seq, dtype=jnp.int32)
    same_owner = passage_owner[:, None] == passage_owner[None, :]
    passage_rank = jnp.sum(
        jnp.where(same_owner & (seq_ids[None, :] < seq_ids[:, None]), 1, 0), axis=1
    ).astype(jnp.int32)
    held_count = jnp.sum(
        jnp.where(passage_owner[None, :] == prompt_slot[:, None], 1, 0), axis=1
    ).astype(jnp.int32)
    own_rank = passage_rank[me]
    own_owner = passage_owner[me]
    own_held = held_count[me]
    own_index = lax.dynamic_index_in_dim(recompute_index, me, 0, keepdims=False)
    own_length = prompt_length[me]
    own_count = recompute_count[me]

    prompt_pos = own_held * passage_length + jnp.arange(prompt_rows, dtype=jnp.int32)
    recompute_pos = own_rank * passage_length + own_index
    own_pos = jnp.concatenate([prompt_pos, recompute_pos])
    own_live = jnp.concatenate(
        [
            jnp.arange(prompt_rows, dtype=jnp.int32) < own_length,
            jnp.arange(recompute_rows, dtype=jnp.int32) < own_count,
        ]
    )

    rows_local = jnp.concatenate([prompt_hidden, recompute_hidden], axis=0)
    n_mp = w_out.shape[1] // rows_local.shape[1]
    full_rows = mp_gather(rows_local, n_mp)
    normalized_hidden = normalize(full_rows, norm_gain)
    queries = (
        apply_rotation(
            jnp.dot(normalized_hidden, w_query, preferred_element_type=jnp.float32).reshape(
                query_rows, local_heads, HEAD_SIZE
            ),
            own_pos,
        )
        .astype(jnp.bfloat16)
    )
    fresh_keys = (
        apply_rotation(
            jnp.dot(normalized_hidden, key_weight, preferred_element_type=jnp.float32).reshape(
                query_rows, 1, HEAD_SIZE
            ),
            own_pos,
        )
        .astype(jnp.bfloat16)
        .reshape(query_rows, HEAD_SIZE)
    )
    fresh_values = jnp.dot(
        normalized_hidden, value_weight, preferred_element_type=jnp.float32
    ).astype(jnp.bfloat16)

    position_shift = jnp.full((passage_length,), own_rank * passage_length, jnp.int32)
    shifted_keys = (
        apply_rotation(
            key_cache[0].astype(jnp.float32).reshape(passage_length, 1, HEAD_SIZE),
            position_shift,
        )
        .astype(jnp.bfloat16)
        .reshape(passage_length, HEAD_SIZE)
    )
    chosen = (own_index[:, None] == jnp.arange(passage_length, dtype=jnp.int32)[None, :]) & (
        jnp.arange(recompute_rows, dtype=jnp.int32)[:, None] < own_count
    )
    replaced = jnp.any(chosen, axis=0)[:, None]
    fresh_pair = jnp.concatenate([fresh_keys[prompt_rows:], fresh_values[prompt_rows:]], axis=1)
    placed = lax.dot_general(
        chosen.astype(jnp.bfloat16),
        fresh_pair,
        (((0,), (0,)), ((), ())),
        preferred_element_type=jnp.float32,
    ).astype(jnp.bfloat16)
    passage_keys = jnp.where(replaced, placed[:, :HEAD_SIZE], shifted_keys)
    passage_values = jnp.where(replaced, placed[:, HEAD_SIZE:], value_cache[0])

    nx, nz = SEQ_SHAPE
    all_queries = relay_gather(
        queries.reshape(2, prompt_rows * local_heads, HEAD_SIZE), nx, nz
    )
    q_blocks = all_queries.reshape(n_seq * 2, prompt_rows * local_heads, HEAD_SIZE)
    prompt_flag = jnp.where(prompt_slot == own_owner, 1, 0)
    recompute_flag = jnp.where(
        seq_ids == me, 2, jnp.where((passage_owner == own_owner) & (seq_ids > me), 1, 0)
    )
    flags = jnp.stack([prompt_flag, recompute_flag], axis=1).reshape(-1).astype(jnp.int32)
    lim = jnp.repeat(own_index, local_heads).reshape(-1, 1).astype(jnp.int32)
    packed = passage_attention(nx, nz, flags, q_blocks, passage_keys, passage_values, lim)
    block_rows = packed.shape[1]

    back = relay_reduce(packed.reshape(n_seq, 2, block_rows, HEAD_SIZE), nx, nz)
    n_parts = back.shape[0]
    rows128 = prompt_rows * local_heads
    stats_back = back[:, :, rows128 : rows128 + 4].astype(jnp.float32)
    part_max = (stats_back[:, :, 0] + stats_back[:, :, 1]).reshape(n_parts, query_rows, local_heads)
    part_tot = (stats_back[:, :, 2] + stats_back[:, :, 3]).reshape(n_parts, query_rows, local_heads)
    part_acc = (
        back[:, :, :rows128].reshape(n_parts, query_rows, local_heads, HEAD_SIZE).astype(jnp.float32)
    )

    pq = queries[:prompt_rows].astype(jnp.float32)
    pk = fresh_keys[:prompt_rows].astype(jnp.float32)
    pv = fresh_values[:prompt_rows].astype(jnp.float32)
    ps = jnp.einsum("qhd,kd->qhk", pq, pk) * scale
    jj = jnp.arange(prompt_rows, dtype=jnp.int32)
    pvis = (jj[None, :] <= jj[:, None]) & (jj[None, :] < own_length)
    ps = jnp.where(pvis[:, None, :], ps, NEGATIVE_FLOOR)
    pmax = jnp.max(ps, axis=-1)
    pw = jnp.where(pvis[:, None, :], jnp.exp(ps - pmax[..., None]), 0.0)
    ptot = jnp.sum(pw, axis=-1)
    pacc = jnp.einsum("qhk,kd->qhd", pw.astype(jnp.bfloat16).astype(jnp.float32), pv)
    loc_max = jnp.concatenate(
        [pmax, jnp.full((recompute_rows, local_heads), NEGATIVE_FLOOR, jnp.float32)]
    )
    loc_tot = jnp.concatenate([ptot, jnp.zeros((recompute_rows, local_heads), jnp.float32)])
    loc_acc = jnp.concatenate(
        [pacc, jnp.zeros((recompute_rows, local_heads, HEAD_SIZE), jnp.float32)]
    )

    highest = jnp.maximum(jnp.max(part_max, axis=0), loc_max)
    part_scale = jnp.exp(part_max - highest[None])
    loc_scale = jnp.exp(loc_max - highest)
    accumulated = jnp.sum(part_acc * part_scale[..., None], axis=0) + loc_acc * loc_scale[..., None]
    totals = jnp.sum(part_tot * part_scale, axis=0) + loc_tot * loc_scale
    safe_totals = jnp.where(totals > 0, totals, 1.0)
    attention = jnp.where(
        own_live[:, None, None], accumulated / safe_totals[..., None], 0.0
    ).astype(jnp.bfloat16).reshape(query_rows, local_heads * HEAD_SIZE)
    projected = jnp.dot(attention, w_out, preferred_element_type=jnp.float32)
    shares = mp_scatter(projected.astype(jnp.bfloat16), n_mp)
    combined = jnp.sum(shares.astype(jnp.float32), axis=0).astype(jnp.bfloat16)
    return (combined[:prompt_rows], combined[prompt_rows:])


def solution(mesh):
    global SEQ_SHAPE
    sizes = dict(zip(mesh.axis_names, mesh.devices.shape))
    seq_devices = mesh.devices.reshape(sizes["seq"], sizes["mp"])[:, 0]
    xs = sorted({d.coords[0] for d in seq_devices})
    SEQ_SHAPE = (len(xs), sizes["seq"] // len(xs))
    return jax.shard_map(
        local,
        mesh=mesh,
        in_specs=(
            P("seq", "mp"),
            P("seq", "mp"),
            P("seq", None, "mp"),
            P("seq", None, "mp"),
            P(),
            P(None, "mp"),
            P(None, "mp"),
            P(None, "mp"),
            P("mp", None),
            P(),
            P(),
            P(),
            P(),
            P(),
        ),
        out_specs=(P("seq", "mp"), P("seq", "mp")),
        check_vma=False,
    )
```

```python
import functools
import math

import jax
import jax.numpy as jnp
from jax import lax
from jax.experimental import pallas as pl
from jax.experimental.pallas import tpu as pltpu
from jax.sharding import PartitionSpec as P

HEAD_SIZE = 128
NEGATIVE_FLOOR = -1e30


def apply_rotation(vectors, positions):
    half_width = vectors.shape[-1] // 2
    exponent = jnp.arange(half_width).astype(jnp.float32) * (2.0 / vectors.shape[-1])
    frequency = jnp.exp(-exponent * math.log(500000.0))
    angles = positions.astype(jnp.float32)[:, None] * frequency[None, :]
    cosines = jnp.cos(angles)[:, None, :]
    sines = jnp.sin(angles)[:, None, :]
    leading = vectors[..., :half_width]
    trailing = vectors[..., half_width:]
    return jnp.concatenate(
        [leading * cosines - trailing * sines, trailing * cosines + leading * sines], axis=-1
    )


def normalize(rows_in, norm_gain):
    values = rows_in.astype(jnp.float32)
    inverse_rms = lax.rsqrt(jnp.mean(values * values, axis=-1, keepdims=True) + 1e-05)
    return (values * inverse_rms * norm_gain).astype(jnp.bfloat16)


MESH = pl.DeviceIdType.MESH


def passage_kernel(nx, nz, flags_ref, q_ref, k_ref, v_ref, lim_ref, out_ref):
    nb, rows, _ = q_ref.shape
    keys = k_ref.shape[0]
    token = lax.broadcasted_iota(jnp.int32, (rows, keys), 1)
    sub = lax.broadcasted_iota(jnp.int32, (16, rows), 0)

    def split(m_row, l_row):
        m_hi = m_row.astype(jnp.bfloat16).astype(jnp.float32)
        l_hi = l_row.astype(jnp.bfloat16).astype(jnp.float32)
        st = jnp.where(
            sub == 0,
            m_row,
            jnp.where(
                sub == 1,
                m_row - m_hi,
                jnp.where(sub == 2, l_row, jnp.where(sub == 3, l_row - l_hi, 0.0)),
            ),
        )
        return st.astype(jnp.bfloat16)

    out_ref[:, 0:rows] = jnp.zeros((nb, rows, HEAD_SIZE), out_ref.dtype)
    floor = jnp.full((16, rows), NEGATIVE_FLOOR, jnp.float32)
    empty = split(floor, jnp.zeros((16, rows), jnp.float32))
    out_ref[:, rows:] = jnp.broadcast_to(empty[None], (nb, 16, rows))

    def attend(b, masked):
        d = b // 2
        stored = ((d % nz) * nx + d // nz) * 2 + b % 2
        scores = lax.dot_general(
            q_ref[stored], k_ref[...], (((1,), (1,)), ((), ())), preferred_element_type=jnp.float32
        ) * (1.0 / math.sqrt(HEAD_SIZE))
        if masked:
            scores = jnp.where(token <= lim_ref[...], scores, NEGATIVE_FLOOR)
        maxima = jnp.max(scores, axis=1, keepdims=True)
        weights = jnp.exp(scores - maxima)
        totals = jnp.sum(weights, axis=1, keepdims=True)
        out_ref[b, 0:rows] = jnp.dot(
            weights.astype(jnp.bfloat16), v_ref[...], preferred_element_type=jnp.float32
        ).astype(out_ref.dtype)
        m_row = jnp.transpose(jnp.broadcast_to(maxima, (rows, rows)))[0:16]
        l_row = jnp.transpose(jnp.broadcast_to(totals, (rows, rows)))[0:16]
        out_ref[b, rows:] = split(m_row, l_row)

    def body(b, carry):
        flag = flags_ref[b]

        @pl.when(flag == 1)
        def _():
            attend(b, False)

        @pl.when(flag == 2)
        def _():
            attend(b, True)

        return carry

    lax.fori_loop(0, nb, body, 0)


def passage_attention(nx, nz, flags, q_blocks, keys, values, lim):
    nb, rows, _ = q_blocks.shape
    vmem = pl.BlockSpec(memory_space=pltpu.VMEM)
    return pl.pallas_call(
        functools.partial(passage_kernel, nx, nz),
        in_specs=[pl.BlockSpec(memory_space=pltpu.SMEM), vmem, vmem, vmem, vmem],
        out_specs=vmem,
        out_shape=jax.ShapeDtypeStruct((nb, rows + 16, HEAD_SIZE), jnp.bfloat16),
    )(flags, q_blocks, keys, values, lim)


def mp_gather_kernel(n, x_ref, y_ref, send_sem, recv_sem, local_sem):
    me = lax.axis_index("mp")
    row = lax.axis_index("seq")
    width = x_ref.shape[1]
    barrier = pltpu.get_barrier_semaphore()
    for k in range(1, n):
        peer = lax.rem(me + k, n)
        pl.semaphore_signal(barrier, inc=1, device_id=(row, peer), device_id_type=MESH)
    pl.semaphore_wait(barrier, n - 1)
    cols = pl.ds(pl.multiple_of(me * width, width), width)
    copies = []
    for k in range(1, n):
        peer = lax.rem(me + k, n)
        c = pltpu.make_async_remote_copy(
            src_ref=x_ref,
            dst_ref=y_ref.at[:, cols],
            send_sem=send_sem.at[k],
            recv_sem=recv_sem.at[k],
            device_id=(row, peer),
            device_id_type=MESH,
        )
        c.start()
        copies.append(c)
    own = pltpu.make_async_copy(x_ref, y_ref.at[:, cols], local_sem)
    own.start()
    for c in copies:
        c.wait()
    own.wait()


def mp_gather(x, n):
    vmem = pl.BlockSpec(memory_space=pltpu.VMEM)
    return pl.pallas_call(
        functools.partial(mp_gather_kernel, n),
        in_specs=[vmem],
        out_specs=vmem,
        out_shape=jax.ShapeDtypeStruct((x.shape[0], x.shape[1] * n), x.dtype),
        scratch_shapes=[
            pltpu.SemaphoreType.DMA((n,)),
            pltpu.SemaphoreType.DMA((n,)),
            pltpu.SemaphoreType.DMA(()),
        ],
        compiler_params=pltpu.CompilerParams(collective_id=0, has_side_effects=True),
    )(x)


def mp_scatter_kernel(n, x_ref, y_ref, send_sem, recv_sem, local_sem):
    me = lax.axis_index("mp")
    row = lax.axis_index("seq")
    width = y_ref.shape[2]
    barrier = pltpu.get_barrier_semaphore()
    for k in range(1, n):
        peer = lax.rem(me + k, n)
        pl.semaphore_signal(barrier, inc=1, device_id=(row, peer), device_id_type=MESH)
    pl.semaphore_wait(barrier, n - 1)
    copies = []
    for k in range(1, n):
        peer = lax.rem(me + k, n)
        c = pltpu.make_async_remote_copy(
            src_ref=x_ref.at[:, pl.ds(pl.multiple_of(peer * width, width), width)],
            dst_ref=y_ref.at[me],
            send_sem=send_sem.at[k],
            recv_sem=recv_sem.at[k],
            device_id=(row, peer),
            device_id_type=MESH,
        )
        c.start()
        copies.append(c)
    own = pltpu.make_async_copy(
        x_ref.at[:, pl.ds(pl.multiple_of(me * width, width), width)], y_ref.at[me], local_sem
    )
    own.start()
    for c in copies:
        c.wait()
    own.wait()


def mp_scatter(x, n):
    vmem = pl.BlockSpec(memory_space=pltpu.VMEM)
    return pl.pallas_call(
        functools.partial(mp_scatter_kernel, n),
        in_specs=[vmem],
        out_specs=vmem,
        out_shape=jax.ShapeDtypeStruct((n, x.shape[0], x.shape[1] // n), x.dtype),
        scratch_shapes=[
            pltpu.SemaphoreType.DMA((n,)),
            pltpu.SemaphoreType.DMA((n,)),
            pltpu.SemaphoreType.DMA(()),
        ],
        compiler_params=pltpu.CompilerParams(collective_id=1, has_side_effects=True),
    )(x)


def relay_gather_kernel(nx, nz, x_ref, y_ref, *sems):
    (sx_send, sx_recv, zp_send, zp_recv, zm_send, zm_recv, own_sem,
     bp_send, bp_recv, bm_send, bm_recv, xp_send, xp_recv, xm_send, xm_recv,
     fp_send, fp_recv, fm_send, fm_recv) = sems
    me = lax.axis_index("seq")
    mp = lax.axis_index("mp")
    x = me // nz
    z = me % nz
    up = lax.rem(z + 1, nz)
    down = lax.rem(z + nz - 1, nz)
    right = lax.rem(x + 1, nx)
    left = lax.rem(x + nx - 1, nx)
    barrier = pltpu.get_barrier_semaphore()
    peers = [(lax.rem(x + k, nx) * nz + z, mp) for k in range(1, nx)]
    peers += [(x * nz + up, mp), (x * nz + down, mp)]
    for p in peers:
        pl.semaphore_signal(barrier, inc=1, device_id=p, device_id_type=MESH)
    pl.semaphore_wait(barrier, len(peers))

    def copy(src, dst, send_sem, recv_sem, device):
        c = pltpu.make_async_remote_copy(
            src_ref=src,
            dst_ref=dst,
            send_sem=send_sem,
            recv_sem=recv_sem,
            device_id=device,
            device_id_type=MESH,
        )
        c.start()
        return c

    sent = []
    slot = z * nx + x
    first = [
        copy(x_ref.at[0], y_ref.at[slot, 0], sx_send.at[k], sx_recv.at[k], peers[k - 1])
        for k in range(1, nx)
    ]
    own = pltpu.make_async_copy(x_ref, y_ref.at[slot], own_sem)
    own.start()

    def x_out(column):
        a = copy(
            y_ref.at[column * nx + x, 1], y_ref.at[column * nx + x, 1],
            xp_send.at[column], xp_recv.at[column], (right * nz + z, mp),
        )
        b = copy(
            y_ref.at[column * nx + x, 1], y_ref.at[column * nx + x, 1],
            xm_send.at[column], xm_recv.at[column], (left * nz + z, mp),
        )
        return [a, b]

    own.wait()
    steps = nz // 2
    half = nx // 2
    zlast = {}
    blast = {}
    xcopies = {}
    for c in first:
        c.wait()
    for t in range(1, steps + 1):
        for sign, send_sem, recv_sem, target, count in (
            (1, bp_send, bp_recv, up, steps),
            (-1, bm_send, bm_recv, down, nz - 1 - steps),
        ):
            if t > count:
                continue
            if t > 1:
                blast[sign].wait_recv()
            column = lax.rem(z - sign * (t - 1) + nz, nz)
            if t > 1:
                xcopies[(sign, t - 1)] = x_out(column)
            elif sign == 1:
                xcopies[(0, 0)] = x_out(column)
            blast[sign] = copy(
                y_ref.at[column * nx + x, 1], y_ref.at[column * nx + x, 1],
                send_sem.at[t], recv_sem.at[t], (x * nz + target, mp),
            )
            sent.append(blast[sign])
        for i in range(nx):
            for sign, send_sem, recv_sem, target in (
                (1, zp_send, zp_recv, up),
                (-1, zm_send, zm_recv, down),
            ):
                if t == steps and (i < half) != (sign == 1):
                    continue
                if t > 1:
                    zlast[(sign, i)].wait_recv()
                column = lax.rem(z - sign * (t - 1) + nz, nz)
                zlast[(sign, i)] = copy(
                    y_ref.at[column * nx + i, 0], y_ref.at[column * nx + i, 0],
                    send_sem.at[t, i], recv_sem.at[t, i], (x * nz + target, mp),
                )
                sent.append(zlast[(sign, i)])
    for sign, count in ((1, steps), (-1, nz - 1 - steps)):
        blast[sign].wait_recv()
        column = lax.rem(z - sign * count + nz, nz)
        xcopies[(sign, count)] = x_out(column)
    order = [(0, 0)] + [(s, t) for t in range(1, steps + 1) for s in (1, -1) if (s, t) in xcopies]
    forwards = []
    for key in order:
        sign, t = key
        column = lax.rem(z - sign * t + nz, nz)
        from_left, from_right = xcopies[key]
        from_left.wait_recv()
        from_right.wait_recv()
        sent += xcopies[key]
    for zc in range(nz):
        if zc < nz // 2:
            forwards.append(
                copy(
                    y_ref.at[zc * nx + left, 1], y_ref.at[zc * nx + left, 1],
                    fp_send.at[zc], fp_recv.at[zc], (right * nz + z, mp),
                )
            )
        else:
            forwards.append(
                copy(
                    y_ref.at[zc * nx + right, 1], y_ref.at[zc * nx + right, 1],
                    fm_send.at[zc], fm_recv.at[zc], (left * nz + z, mp),
                )
            )
    for c in zlast.values():
        c.wait_recv()
    for c in forwards:
        c.wait_recv()
    for c in sent:
        c.wait_send()
    for c in forwards:
        c.wait_send()


def relay_gather(x, nx, nz):
    assert nx == 4 and nz % 2 == 0
    vmem = pl.BlockSpec(memory_space=pltpu.VMEM)
    steps = nz // 2
    dma = pltpu.SemaphoreType.DMA
    return pl.pallas_call(
        functools.partial(relay_gather_kernel, nx, nz),
        in_specs=[vmem],
        out_specs=vmem,
        out_shape=jax.ShapeDtypeStruct((nx * nz,) + x.shape, x.dtype),
        scratch_shapes=[
            dma((nx,)), dma((nx,)),
            dma((steps + 1, nx)), dma((steps + 1, nx)), dma((steps + 1, nx)), dma((steps + 1, nx)),
            dma(()),
            dma((steps + 1,)), dma((steps + 1,)), dma((steps + 1,)), dma((steps + 1,)),
            dma((nz,)), dma((nz,)), dma((nz,)), dma((nz,)),
            dma((nz,)), dma((nz,)), dma((nz,)), dma((nz,)),
        ],
        compiler_params=pltpu.CompilerParams(collective_id=2, has_side_effects=True),
    )(x)


def merge_piece(a, b, rows):
    af = a.astype(jnp.float32)
    bf = b.astype(jnp.float32)
    m1 = af[rows : rows + 1] + af[rows + 1 : rows + 2]
    l1 = af[rows + 2 : rows + 3] + af[rows + 3 : rows + 4]
    m2 = bf[rows : rows + 1] + bf[rows + 1 : rows + 2]
    l2 = bf[rows + 2 : rows + 3] + bf[rows + 3 : rows + 4]
    top = jnp.maximum(m1, m2)
    s1 = jnp.exp(m1 - top)
    s2 = jnp.exp(m2 - top)
    total = l1 * s1 + l2 * s2
    c1 = jnp.transpose(jnp.broadcast_to(s1, (rows, rows)))
    c2 = jnp.transpose(jnp.broadcast_to(s2, (rows, rows)))
    acc = af[0:rows] * c1 + bf[0:rows] * c2
    sub = lax.broadcasted_iota(jnp.int32, (16, rows), 0)
    top_hi = top.astype(jnp.bfloat16).astype(jnp.float32)
    tot_hi = total.astype(jnp.bfloat16).astype(jnp.float32)
    st = jnp.where(
        sub == 0,
        top,
        jnp.where(
            sub == 1, top - top_hi, jnp.where(sub == 2, total, jnp.where(sub == 3, total - tot_hi, 0.0))
        ),
    )
    return acc.astype(jnp.bfloat16), st.astype(jnp.bfloat16)


def relay_reduce_kernel(
    nx, nz, x_ref, y_ref, rp, rm, bp, bm, col, sp_send, sp_recv, sm_send, sm_recv, sx_send, sx_recv
):
    me = lax.axis_index("seq")
    mp = lax.axis_index("mp")
    x = me // nz
    z = me % nz
    up = lax.rem(z + 1, nz)
    down = lax.rem(z + nz - 1, nz)
    rows = x_ref.shape[2] - 16
    barrier = pltpu.get_barrier_semaphore()
    peers = [(lax.rem(x + k, nx) * nz + z, mp) for k in range(1, nx)]
    peers += [(x * nz + up, mp), (x * nz + down, mp)]
    for p in peers:
        pl.semaphore_signal(barrier, inc=1, device_id=p, device_id_type=MESH)
    pl.semaphore_wait(barrier, len(peers))

    def merge_into(dst, first, second):
        for h in range(2):
            acc, st = merge_piece(first[h], second[h], rows)
            dst[h, 0:rows] = acc
            dst[h, rows:] = st

    steps = nz // 2
    half = nx // 2
    last = {}
    sent = []
    dirs = ((1, rp, bp, sp_send, sp_recv, up), (-1, rm, bm, sm_send, sm_recv, down))
    for t in range(1, steps + 1):
        for i in range(nx):
            for sign, recv_buf, send_buf, send_sem, recv_sem, target in dirs:
                if t == 1 and (i < half) != (sign == 1):
                    continue
                column = lax.rem(z + sign * (steps + 1 - t) + nz, nz)
                own = x_ref.at[i * nz + column]
                if (sign, i) in last:
                    last[(sign, i)].wait_recv()
                    merge_into(send_buf.at[t, i], own, recv_buf.at[t - 1, i])
                    src = send_buf.at[t, i]
                else:
                    src = own
                c = pltpu.make_async_remote_copy(
                    src_ref=src,
                    dst_ref=recv_buf.at[t, i],
                    send_sem=send_sem.at[t, i],
                    recv_sem=recv_sem.at[t, i],
                    device_id=(x * nz + target, mp),
                    device_id_type=MESH,
                )
                c.start()
                last[(sign, i)] = c
                sent.append(c)

    mine = []
    for i in range(nx):
        last[(1, i)].wait_recv()
        last[(-1, i)].wait_recv()
        merge_into(col.at[i], x_ref.at[i * nz + z], rp.at[steps, i])
        merge_into(col.at[i], col.at[i], rm.at[steps, i])
    for k in range(1, nx):
        target = lax.rem(x + k, nx)
        c = pltpu.make_async_remote_copy(
            src_ref=col.at[target],
            dst_ref=y_ref.at[x],
            send_sem=sx_send.at[k],
            recv_sem=sx_recv.at[k],
            device_id=(target * nz + z, mp),
            device_id_type=MESH,
        )
        c.start()
        mine.append(c)
    y_ref[x] = col[x]
    for c in sent:
        c.wait_send()
    for c in mine:
        c.wait()


def relay_reduce(parts, nx, nz):
    vmem = pl.BlockSpec(memory_space=pltpu.VMEM)
    steps = nz // 2
    piece = parts.shape[1:]
    return pl.pallas_call(
        functools.partial(relay_reduce_kernel, nx, nz),
        in_specs=[vmem],
        out_specs=vmem,
        out_shape=jax.ShapeDtypeStruct((nx,) + piece, parts.dtype),
        scratch_shapes=[
            pltpu.VMEM((steps + 1, nx) + piece, parts.dtype),
            pltpu.VMEM((steps + 1, nx) + piece, parts.dtype),
            pltpu.VMEM((steps + 1, nx) + piece, parts.dtype),
            pltpu.VMEM((steps + 1, nx) + piece, parts.dtype),
            pltpu.VMEM((nx,) + piece, parts.dtype),
            pltpu.SemaphoreType.DMA((steps + 1, nx)),
            pltpu.SemaphoreType.DMA((steps + 1, nx)),
            pltpu.SemaphoreType.DMA((steps + 1, nx)),
            pltpu.SemaphoreType.DMA((steps + 1, nx)),
            pltpu.SemaphoreType.DMA((nx,)),
            pltpu.SemaphoreType.DMA((nx,)),
        ],
        compiler_params=pltpu.CompilerParams(collective_id=3, has_side_effects=True),
    )(parts)


def local(
    prompt_hidden,
    recompute_hidden,
    key_cache,
    value_cache,
    norm_gain,
    w_query,
    key_weight,
    value_weight,
    w_out,
    passage_owner,
    prompt_slot,
    prompt_length,
    recompute_count,
    recompute_index,
):
    prompt_rows = prompt_hidden.shape[0]
    recompute_rows = recompute_hidden.shape[0]
    query_rows = prompt_rows + recompute_rows
    passage_length = key_cache.shape[1]
    local_heads = w_query.shape[1] // HEAD_SIZE
    n_seq = passage_owner.shape[0]
    me = lax.axis_index("seq")
    scale = 1.0 / math.sqrt(HEAD_SIZE)

    seq_ids = jnp.arange(n_seq, dtype=jnp.int32)
    same_owner = passage_owner[:, None] == passage_owner[None, :]
    passage_rank = jnp.sum(
        jnp.where(same_owner & (seq_ids[None, :] < seq_ids[:, None]), 1, 0), axis=1
    ).astype(jnp.int32)
    held_count = jnp.sum(
        jnp.where(passage_owner[None, :] == prompt_slot[:, None], 1, 0), axis=1
    ).astype(jnp.int32)
    own_rank = passage_rank[me]
    own_owner = passage_owner[me]
    own_held = held_count[me]
    own_index = lax.dynamic_index_in_dim(recompute_index, me, 0, keepdims=False)
    own_length = prompt_length[me]
    own_count = recompute_count[me]

    prompt_pos = own_held * passage_length + jnp.arange(prompt_rows, dtype=jnp.int32)
    recompute_pos = own_rank * passage_length + own_index
    own_pos = jnp.concatenate([prompt_pos, recompute_pos])
    own_live = jnp.concatenate(
        [
            jnp.arange(prompt_rows, dtype=jnp.int32) < own_length,
            jnp.arange(recompute_rows, dtype=jnp.int32) < own_count,
        ]
    )

    rows_local = jnp.concatenate([prompt_hidden, recompute_hidden], axis=0)
    n_mp = w_out.shape[1] // rows_local.shape[1]
    full_rows = mp_gather(rows_local, n_mp)
    normalized_hidden = normalize(full_rows, norm_gain)
    queries = (
        apply_rotation(
            jnp.dot(normalized_hidden, w_query, preferred_element_type=jnp.float32).reshape(
                query_rows, local_heads, HEAD_SIZE
            ),
            own_pos,
        )
        .astype(jnp.bfloat16)
    )
    fresh_keys = (
        apply_rotation(
            jnp.dot(normalized_hidden, key_weight, preferred_element_type=jnp.float32).reshape(
                query_rows, 1, HEAD_SIZE
            ),
            own_pos,
        )
        .astype(jnp.bfloat16)
        .reshape(query_rows, HEAD_SIZE)
    )
    fresh_values = jnp.dot(
        normalized_hidden, value_weight, preferred_element_type=jnp.float32
    ).astype(jnp.bfloat16)

    position_shift = jnp.full((passage_length,), own_rank * passage_length, jnp.int32)
    shifted_keys = (
        apply_rotation(
            key_cache[0].astype(jnp.float32).reshape(passage_length, 1, HEAD_SIZE),
            position_shift,
        )
        .astype(jnp.bfloat16)
        .reshape(passage_length, HEAD_SIZE)
    )
    chosen = (own_index[:, None] == jnp.arange(passage_length, dtype=jnp.int32)[None, :]) & (
        jnp.arange(recompute_rows, dtype=jnp.int32)[:, None] < own_count
    )
    replaced = jnp.any(chosen, axis=0)[:, None]
    fresh_pair = jnp.concatenate([fresh_keys[prompt_rows:], fresh_values[prompt_rows:]], axis=1)
    placed = lax.dot_general(
        chosen.astype(jnp.bfloat16),
        fresh_pair,
        (((0,), (0,)), ((), ())),
        preferred_element_type=jnp.float32,
    ).astype(jnp.bfloat16)
    passage_keys = jnp.where(replaced, placed[:, :HEAD_SIZE], shifted_keys)
    passage_values = jnp.where(replaced, placed[:, HEAD_SIZE:], value_cache[0])

    nx, nz = SEQ_SHAPE
    all_queries = relay_gather(
        queries.reshape(2, prompt_rows * local_heads, HEAD_SIZE), nx, nz
    )
    q_blocks = all_queries.reshape(n_seq * 2, prompt_rows * local_heads, HEAD_SIZE)
    prompt_flag = jnp.where(prompt_slot == own_owner, 1, 0)
    recompute_flag = jnp.where(
        seq_ids == me, 2, jnp.where((passage_owner == own_owner) & (seq_ids > me), 1, 0)
    )
    flags = jnp.stack([prompt_flag, recompute_flag], axis=1).reshape(-1).astype(jnp.int32)
    lim = jnp.repeat(own_index, local_heads).reshape(-1, 1).astype(jnp.int32)
    packed = passage_attention(nx, nz, flags, q_blocks, passage_keys, passage_values, lim)
    block_rows = packed.shape[1]

    back = relay_reduce(packed.reshape(n_seq, 2, block_rows, HEAD_SIZE), nx, nz)
    n_parts = back.shape[0]
    rows128 = prompt_rows * local_heads
    stats_back = back[:, :, rows128 : rows128 + 4].astype(jnp.float32)
    part_max = (stats_back[:, :, 0] + stats_back[:, :, 1]).reshape(n_parts, query_rows, local_heads)
    part_tot = (stats_back[:, :, 2] + stats_back[:, :, 3]).reshape(n_parts, query_rows, local_heads)
    part_acc = (
        back[:, :, :rows128].reshape(n_parts, query_rows, local_heads, HEAD_SIZE).astype(jnp.float32)
    )

    pq = queries[:prompt_rows].astype(jnp.float32)
    pk = fresh_keys[:prompt_rows].astype(jnp.float32)
    pv = fresh_values[:prompt_rows].astype(jnp.float32)
    ps = jnp.einsum("qhd,kd->qhk", pq, pk) * scale
    jj = jnp.arange(prompt_rows, dtype=jnp.int32)
    pvis = (jj[None, :] <= jj[:, None]) & (jj[None, :] < own_length)
    ps = jnp.where(pvis[:, None, :], ps, NEGATIVE_FLOOR)
    pmax = jnp.max(ps, axis=-1)
    pw = jnp.where(pvis[:, None, :], jnp.exp(ps - pmax[..., None]), 0.0)
    ptot = jnp.sum(pw, axis=-1)
    pacc = jnp.einsum("qhk,kd->qhd", pw.astype(jnp.bfloat16).astype(jnp.float32), pv)
    loc_max = jnp.concatenate(
        [pmax, jnp.full((recompute_rows, local_heads), NEGATIVE_FLOOR, jnp.float32)]
    )
    loc_tot = jnp.concatenate([ptot, jnp.zeros((recompute_rows, local_heads), jnp.float32)])
    loc_acc = jnp.concatenate(
        [pacc, jnp.zeros((recompute_rows, local_heads, HEAD_SIZE), jnp.float32)]
    )

    highest = jnp.maximum(jnp.max(part_max, axis=0), loc_max)
    part_scale = jnp.exp(part_max - highest[None])
    loc_scale = jnp.exp(loc_max - highest)
    accumulated = jnp.sum(part_acc * part_scale[..., None], axis=0) + loc_acc * loc_scale[..., None]
    totals = jnp.sum(part_tot * part_scale, axis=0) + loc_tot * loc_scale
    safe_totals = jnp.where(totals > 0, totals, 1.0)
    attention = jnp.where(
        own_live[:, None, None], accumulated / safe_totals[..., None], 0.0
    ).astype(jnp.bfloat16).reshape(query_rows, local_heads * HEAD_SIZE)
    projected = jnp.dot(attention, w_out, preferred_element_type=jnp.float32)
    shares = mp_scatter(projected.astype(jnp.bfloat16), n_mp)
    combined = jnp.sum(shares.astype(jnp.float32), axis=0).astype(jnp.bfloat16)
    return (combined[:prompt_rows], combined[prompt_rows:])


def solution(mesh):
    global SEQ_SHAPE
    sizes = dict(zip(mesh.axis_names, mesh.devices.shape))
    seq_devices = mesh.devices.reshape(sizes["seq"], sizes["mp"])[:, 0]
    xs = sorted({d.coords[0] for d in seq_devices})
    SEQ_SHAPE = (len(xs), sizes["seq"] // len(xs))
    return jax.shard_map(
        local,
        mesh=mesh,
        in_specs=(
            P("seq", "mp"),
            P("seq", "mp"),
            P("seq", None, "mp"),
            P("seq", None, "mp"),
            P(),
            P(None, "mp"),
            P(None, "mp"),
            P(None, "mp"),
            P("mp", None),
            P(),
            P(),
            P(),
            P(),
            P(),
        ),
        out_specs=(P("seq", "mp"), P("seq", "mp")),
        check_vma=False,
    )
```

```python
import functools
import math

import jax
import jax.numpy as jnp
from jax import lax
from jax.experimental import pallas as pl
from jax.experimental.pallas import tpu as pltpu
from jax.sharding import PartitionSpec as P

HEAD_SIZE = 128
NEGATIVE_FLOOR = -1e30


def apply_rotation(vectors, positions):
    half_width = vectors.shape[-1] // 2
    exponent = jnp.arange(half_width).astype(jnp.float32) * (2.0 / vectors.shape[-1])
    frequency = jnp.exp(-exponent * math.log(500000.0))
    angles = positions.astype(jnp.float32)[:, None] * frequency[None, :]
    cosines = jnp.cos(angles)[:, None, :]
    sines = jnp.sin(angles)[:, None, :]
    leading = vectors[..., :half_width]
    trailing = vectors[..., half_width:]
    return jnp.concatenate(
        [leading * cosines - trailing * sines, trailing * cosines + leading * sines], axis=-1
    )


def normalize(rows_in, norm_gain):
    values = rows_in.astype(jnp.float32)
    inverse_rms = lax.rsqrt(jnp.mean(values * values, axis=-1, keepdims=True) + 1e-05)
    return (values * inverse_rms * norm_gain).astype(jnp.bfloat16)


MESH = pl.DeviceIdType.MESH


def passage_kernel(nx, nz, flags_ref, q_ref, k_ref, v_ref, lim_ref, out_ref):
    nb, rows, _ = q_ref.shape
    keys = k_ref.shape[0]
    token = lax.broadcasted_iota(jnp.int32, (rows, keys), 1)
    sub = lax.broadcasted_iota(jnp.int32, (16, rows), 0)

    def split(m_row, l_row):
        m_hi = m_row.astype(jnp.bfloat16).astype(jnp.float32)
        l_hi = l_row.astype(jnp.bfloat16).astype(jnp.float32)
        st = jnp.where(
            sub == 0,
            m_row,
            jnp.where(
                sub == 1,
                m_row - m_hi,
                jnp.where(sub == 2, l_row, jnp.where(sub == 3, l_row - l_hi, 0.0)),
            ),
        )
        return st.astype(jnp.bfloat16)

    out_ref[:, 0:rows] = jnp.zeros((nb, rows, HEAD_SIZE), out_ref.dtype)
    floor = jnp.full((16, rows), NEGATIVE_FLOOR, jnp.float32)
    empty = split(floor, jnp.zeros((16, rows), jnp.float32))
    out_ref[:, rows:] = jnp.broadcast_to(empty[None], (nb, 16, rows))

    def attend(b, masked):
        d = b // 2
        stored = ((d % nz) * nx + d // nz) * 2 + b % 2
        scores = lax.dot_general(
            q_ref[stored], k_ref[...], (((1,), (1,)), ((), ())), preferred_element_type=jnp.float32
        ) * (1.0 / math.sqrt(HEAD_SIZE))
        if masked:
            scores = jnp.where(token <= lim_ref[...], scores, NEGATIVE_FLOOR)
        maxima = jnp.max(scores, axis=1, keepdims=True)
        weights = jnp.exp(scores - maxima)
        totals = jnp.sum(weights, axis=1, keepdims=True)
        out_ref[b, 0:rows] = jnp.dot(
            weights.astype(jnp.bfloat16), v_ref[...], preferred_element_type=jnp.float32
        ).astype(out_ref.dtype)
        m_row = jnp.transpose(jnp.broadcast_to(maxima, (rows, rows)))[0:16]
        l_row = jnp.transpose(jnp.broadcast_to(totals, (rows, rows)))[0:16]
        out_ref[b, rows:] = split(m_row, l_row)

    def body(b, carry):
        flag = flags_ref[b % 2, b // 2]

        @pl.when(flag == 1)
        def _():
            attend(b, False)

        @pl.when(flag == 2)
        def _():
            attend(b, True)

        return carry

    lax.fori_loop(0, nb, body, 0)


def passage_attention(nx, nz, flags, q_blocks, keys, values, lim):
    nb, rows, _ = q_blocks.shape
    vmem = pl.BlockSpec(memory_space=pltpu.VMEM)
    return pl.pallas_call(
        functools.partial(passage_kernel, nx, nz),
        in_specs=[pl.BlockSpec(memory_space=pltpu.SMEM), vmem, vmem, vmem, vmem],
        out_specs=vmem,
        out_shape=jax.ShapeDtypeStruct((nb, rows + 16, HEAD_SIZE), jnp.bfloat16),
    )(flags, q_blocks, keys, values, lim)


def mp_gather_kernel(n, span, p_ref, r_ref, owner_ref, slot_ref, plen_ref, count_ref, index_ref,
                     y_ref, meta_ref, send_sem, recv_sem, local_sem):
    me = lax.axis_index("mp")
    row = lax.axis_index("seq")
    rows, width = p_ref.shape
    barrier = pltpu.get_barrier_semaphore()
    for k in range(1, n):
        peer = lax.rem(me + k, n)
        pl.semaphore_signal(barrier, inc=1, device_id=(row, peer), device_id_type=MESH)
    pl.semaphore_wait(barrier, n - 1)
    cols = pl.ds(pl.multiple_of(me * width, width), width)
    copies = []
    for k in range(1, n):
        peer = lax.rem(me + k, n)
        for part, src in enumerate((p_ref, r_ref)):
            c = pltpu.make_async_remote_copy(
                src_ref=src,
                dst_ref=y_ref.at[pl.ds(part * rows, rows), cols],
                send_sem=send_sem.at[part, k],
                recv_sem=recv_sem.at[part, k],
                device_id=(row, peer),
                device_id_type=MESH,
            )
            c.start()
            copies.append(c)
    own = [
        pltpu.make_async_copy(src, y_ref.at[pl.ds(part * rows, rows), cols], local_sem.at[part])
        for part, src in enumerate((p_ref, r_ref))
    ]
    for c in own:
        c.start()

    f32 = jnp.float32
    owner = owner_ref[...].astype(f32)
    slot = slot_ref[...].astype(f32)
    lane = lax.broadcasted_iota(jnp.int32, owner.shape, 1)
    mine = lane == row

    def pick(v):
        return jnp.sum(jnp.where(mine, v, 0.0), axis=1, keepdims=True)

    own_owner = pick(owner)
    own_slot = pick(slot)
    rank = jnp.sum(jnp.where((owner == own_owner) & (lane < row), 1.0, 0.0), axis=1, keepdims=True)
    held = jnp.sum(jnp.where(owner == own_slot, 1.0, 0.0), axis=1, keepdims=True)
    length = pick(plen_ref[...].astype(f32))
    count = pick(count_ref[...].astype(f32))
    index = index_ref[pl.ds(row, 1), :].astype(f32)
    lanef = lane.astype(f32)
    quantities = [
        held * span + lanef,
        rank * span + index,
        jnp.where(lanef < length, 1.0, 0.0),
        jnp.where(lanef < count, 1.0, 0.0),
        jnp.where(slot == own_owner, 1.0, 0.0),
        jnp.where(mine, 2.0, jnp.where((owner == own_owner) & (lane > row), 1.0, 0.0)),
        index,
        rank * span + 0.0 * lanef,
    ]
    for q, value in enumerate(quantities):
        meta_ref[q : q + 1, :] = value.astype(jnp.int32)

    for c in copies:
        c.wait()
    for c in own:
        c.wait()


def mp_gather(prompt_part, recompute_part, owner, slot, plen, count, index, n, span):
    vmem = pl.BlockSpec(memory_space=pltpu.VMEM)
    rows, width = prompt_part.shape
    small = [v.reshape(1, -1) for v in (owner, slot, plen, count)]
    return pl.pallas_call(
        functools.partial(mp_gather_kernel, n, span),
        in_specs=[vmem] * 7,
        out_specs=[vmem, vmem],
        out_shape=[
            jax.ShapeDtypeStruct((2 * rows, width * n), prompt_part.dtype),
            jax.ShapeDtypeStruct((8, owner.shape[0]), jnp.int32),
        ],
        scratch_shapes=[
            pltpu.SemaphoreType.DMA((2, n)),
            pltpu.SemaphoreType.DMA((2, n)),
            pltpu.SemaphoreType.DMA((2,)),
        ],
        compiler_params=pltpu.CompilerParams(collective_id=0, has_side_effects=True),
    )(prompt_part, recompute_part, *small, index)


def mp_scatter_kernel(n, x_ref, y_ref, send_sem, recv_sem, local_sem):
    me = lax.axis_index("mp")
    row = lax.axis_index("seq")
    width = y_ref.shape[2]
    barrier = pltpu.get_barrier_semaphore()
    for k in range(1, n):
        peer = lax.rem(me + k, n)
        pl.semaphore_signal(barrier, inc=1, device_id=(row, peer), device_id_type=MESH)
    pl.semaphore_wait(barrier, n - 1)
    copies = []
    for k in range(1, n):
        peer = lax.rem(me + k, n)
        c = pltpu.make_async_remote_copy(
            src_ref=x_ref.at[:, pl.ds(pl.multiple_of(peer * width, width), width)],
            dst_ref=y_ref.at[me],
            send_sem=send_sem.at[k],
            recv_sem=recv_sem.at[k],
            device_id=(row, peer),
            device_id_type=MESH,
        )
        c.start()
        copies.append(c)
    own = pltpu.make_async_copy(
        x_ref.at[:, pl.ds(pl.multiple_of(me * width, width), width)], y_ref.at[me], local_sem
    )
    own.start()
    for c in copies:
        c.wait()
    own.wait()


def mp_scatter(x, n):
    vmem = pl.BlockSpec(memory_space=pltpu.VMEM)
    return pl.pallas_call(
        functools.partial(mp_scatter_kernel, n),
        in_specs=[vmem],
        out_specs=vmem,
        out_shape=jax.ShapeDtypeStruct((n, x.shape[0], x.shape[1] // n), x.dtype),
        scratch_shapes=[
            pltpu.SemaphoreType.DMA((n,)),
            pltpu.SemaphoreType.DMA((n,)),
            pltpu.SemaphoreType.DMA(()),
        ],
        compiler_params=pltpu.CompilerParams(collective_id=1, has_side_effects=True),
    )(x)


def relay_gather_kernel(nx, nz, x_ref, y_ref, *sems):
    (sx_send, sx_recv, zp_send, zp_recv, zm_send, zm_recv, own_sem,
     bp_send, bp_recv, bm_send, bm_recv, xp_send, xp_recv, xm_send, xm_recv,
     fp_send, fp_recv, fm_send, fm_recv) = sems
    me = lax.axis_index("seq")
    mp = lax.axis_index("mp")
    x = me // nz
    z = me % nz
    up = lax.rem(z + 1, nz)
    down = lax.rem(z + nz - 1, nz)
    right = lax.rem(x + 1, nx)
    left = lax.rem(x + nx - 1, nx)
    barrier = pltpu.get_barrier_semaphore()
    peers = [(lax.rem(x + k, nx) * nz + z, mp) for k in range(1, nx)]
    peers += [(x * nz + up, mp), (x * nz + down, mp)]
    for p in peers:
        pl.semaphore_signal(barrier, inc=1, device_id=p, device_id_type=MESH)
    pl.semaphore_wait(barrier, len(peers))

    def copy(src, dst, send_sem, recv_sem, device):
        c = pltpu.make_async_remote_copy(
            src_ref=src,
            dst_ref=dst,
            send_sem=send_sem,
            recv_sem=recv_sem,
            device_id=device,
            device_id_type=MESH,
        )
        c.start()
        return c

    sent = []
    slot = z * nx + x
    first = [
        copy(x_ref.at[0], y_ref.at[slot, 0], sx_send.at[k], sx_recv.at[k], peers[k - 1])
        for k in range(1, nx)
    ]
    own = pltpu.make_async_copy(x_ref, y_ref.at[slot], own_sem)
    own.start()

    def x_out(column):
        a = copy(
            y_ref.at[column * nx + x, 1], y_ref.at[column * nx + x, 1],
            xp_send.at[column], xp_recv.at[column], (right * nz + z, mp),
        )
        b = copy(
            y_ref.at[column * nx + x, 1], y_ref.at[column * nx + x, 1],
            xm_send.at[column], xm_recv.at[column], (left * nz + z, mp),
        )
        return [a, b]

    own.wait()
    steps = nz // 2
    half = nx // 2
    zlast = {}
    blast = {}
    xcopies = {}
    for c in first:
        c.wait()
    for t in range(1, steps + 1):
        for sign, send_sem, recv_sem, target, count in (
            (1, bp_send, bp_recv, up, steps),
            (-1, bm_send, bm_recv, down, nz - 1 - steps),
        ):
            if t > count:
                continue
            if t > 1:
                blast[sign].wait_recv()
            column = lax.rem(z - sign * (t - 1) + nz, nz)
            if t > 1:
                xcopies[(sign, t - 1)] = x_out(column)
            elif sign == 1:
                xcopies[(0, 0)] = x_out(column)
            blast[sign] = copy(
                y_ref.at[column * nx + x, 1], y_ref.at[column * nx + x, 1],
                send_sem.at[t], recv_sem.at[t], (x * nz + target, mp),
            )
            sent.append(blast[sign])
        for i in range(nx):
            for sign, send_sem, recv_sem, target in (
                (1, zp_send, zp_recv, up),
                (-1, zm_send, zm_recv, down),
            ):
                if t == steps and (i < half) != (sign == 1):
                    continue
                if t > 1:
                    zlast[(sign, i)].wait_recv()
                column = lax.rem(z - sign * (t - 1) + nz, nz)
                zlast[(sign, i)] = copy(
                    y_ref.at[column * nx + i, 0], y_ref.at[column * nx + i, 0],
                    send_sem.at[t, i], recv_sem.at[t, i], (x * nz + target, mp),
                )
                sent.append(zlast[(sign, i)])
    for sign, count in ((1, steps), (-1, nz - 1 - steps)):
        blast[sign].wait_recv()
        column = lax.rem(z - sign * count + nz, nz)
        xcopies[(sign, count)] = x_out(column)
    order = [(0, 0)] + [(s, t) for t in range(1, steps + 1) for s in (1, -1) if (s, t) in xcopies]
    forwards = []
    for key in order:
        sign, t = key
        column = lax.rem(z - sign * t + nz, nz)
        from_left, from_right = xcopies[key]
        from_left.wait_recv()
        from_right.wait_recv()
        sent += xcopies[key]
    for zc in range(nz):
        if zc < nz // 2:
            forwards.append(
                copy(
                    y_ref.at[zc * nx + left, 1], y_ref.at[zc * nx + left, 1],
                    fp_send.at[zc], fp_recv.at[zc], (right * nz + z, mp),
                )
            )
        else:
            forwards.append(
                copy(
                    y_ref.at[zc * nx + right, 1], y_ref.at[zc * nx + right, 1],
                    fm_send.at[zc], fm_recv.at[zc], (left * nz + z, mp),
                )
            )
    for c in zlast.values():
        c.wait_recv()
    for c in forwards:
        c.wait_recv()
    for c in sent:
        c.wait_send()
    for c in forwards:
        c.wait_send()


def relay_gather(x, nx, nz):
    assert nx == 4 and nz % 2 == 0
    vmem = pl.BlockSpec(memory_space=pltpu.VMEM)
    steps = nz // 2
    dma = pltpu.SemaphoreType.DMA
    return pl.pallas_call(
        functools.partial(relay_gather_kernel, nx, nz),
        in_specs=[vmem],
        out_specs=vmem,
        out_shape=jax.ShapeDtypeStruct((nx * nz,) + x.shape, x.dtype),
        scratch_shapes=[
            dma((nx,)), dma((nx,)),
            dma((steps + 1, nx)), dma((steps + 1, nx)), dma((steps + 1, nx)), dma((steps + 1, nx)),
            dma(()),
            dma((steps + 1,)), dma((steps + 1,)), dma((steps + 1,)), dma((steps + 1,)),
            dma((nz,)), dma((nz,)), dma((nz,)), dma((nz,)),
            dma((nz,)), dma((nz,)), dma((nz,)), dma((nz,)),
        ],
        compiler_params=pltpu.CompilerParams(collective_id=2, has_side_effects=True),
    )(x)


def merge_piece(a, b, rows):
    af = a.astype(jnp.float32)
    bf = b.astype(jnp.float32)
    m1 = af[rows : rows + 1] + af[rows + 1 : rows + 2]
    l1 = af[rows + 2 : rows + 3] + af[rows + 3 : rows + 4]
    m2 = bf[rows : rows + 1] + bf[rows + 1 : rows + 2]
    l2 = bf[rows + 2 : rows + 3] + bf[rows + 3 : rows + 4]
    top = jnp.maximum(m1, m2)
    s1 = jnp.exp(m1 - top)
    s2 = jnp.exp(m2 - top)
    total = l1 * s1 + l2 * s2
    c1 = jnp.transpose(jnp.broadcast_to(s1, (rows, rows)))
    c2 = jnp.transpose(jnp.broadcast_to(s2, (rows, rows)))
    acc = af[0:rows] * c1 + bf[0:rows] * c2
    sub = lax.broadcasted_iota(jnp.int32, (16, rows), 0)
    top_hi = top.astype(jnp.bfloat16).astype(jnp.float32)
    tot_hi = total.astype(jnp.bfloat16).astype(jnp.float32)
    st = jnp.where(
        sub == 0,
        top,
        jnp.where(
            sub == 1, top - top_hi, jnp.where(sub == 2, total, jnp.where(sub == 3, total - tot_hi, 0.0))
        ),
    )
    return acc.astype(jnp.bfloat16), st.astype(jnp.bfloat16)


def relay_reduce_kernel(
    nx, nz, x_ref, y_ref, rp, rm, bp, bm, col, sp_send, sp_recv, sm_send, sm_recv, sx_send, sx_recv
):
    me = lax.axis_index("seq")
    mp = lax.axis_index("mp")
    x = me // nz
    z = me % nz
    up = lax.rem(z + 1, nz)
    down = lax.rem(z + nz - 1, nz)
    rows = x_ref.shape[2] - 16
    barrier = pltpu.get_barrier_semaphore()
    peers = [(lax.rem(x + k, nx) * nz + z, mp) for k in range(1, nx)]
    peers += [(x * nz + up, mp), (x * nz + down, mp)]
    for p in peers:
        pl.semaphore_signal(barrier, inc=1, device_id=p, device_id_type=MESH)
    pl.semaphore_wait(barrier, len(peers))

    def merge_into(dst, first, second):
        for h in range(2):
            acc, st = merge_piece(first[h], second[h], rows)
            dst[h, 0:rows] = acc
            dst[h, rows:] = st

    steps = nz // 2
    half = nx // 2
    last = {}
    sent = []
    dirs = ((1, rp, bp, sp_send, sp_recv, up), (-1, rm, bm, sm_send, sm_recv, down))
    for t in range(1, steps + 1):
        for i in range(nx):
            for sign, recv_buf, send_buf, send_sem, recv_sem, target in dirs:
                if t == 1 and (i < half) != (sign == 1):
                    continue
                column = lax.rem(z + sign * (steps + 1 - t) + nz, nz)
                own = x_ref.at[i * nz + column]
                if (sign, i) in last:
                    last[(sign, i)].wait_recv()
                    merge_into(send_buf.at[t, i], own, recv_buf.at[t - 1, i])
                    src = send_buf.at[t, i]
                else:
                    src = own
                c = pltpu.make_async_remote_copy(
                    src_ref=src,
                    dst_ref=recv_buf.at[t, i],
                    send_sem=send_sem.at[t, i],
                    recv_sem=recv_sem.at[t, i],
                    device_id=(x * nz + target, mp),
                    device_id_type=MESH,
                )
                c.start()
                last[(sign, i)] = c
                sent.append(c)

    mine = []
    for i in range(nx):
        last[(1, i)].wait_recv()
        last[(-1, i)].wait_recv()
        merge_into(col.at[i], x_ref.at[i * nz + z], rp.at[steps, i])
        merge_into(col.at[i], col.at[i], rm.at[steps, i])
    for k in range(1, nx):
        target = lax.rem(x + k, nx)
        c = pltpu.make_async_remote_copy(
            src_ref=col.at[target],
            dst_ref=y_ref.at[x],
            send_sem=sx_send.at[k],
            recv_sem=sx_recv.at[k],
            device_id=(target * nz + z, mp),
            device_id_type=MESH,
        )
        c.start()
        mine.append(c)
    y_ref[x] = col[x]
    for c in sent:
        c.wait_send()
    for c in mine:
        c.wait()


def relay_reduce(parts, nx, nz):
    vmem = pl.BlockSpec(memory_space=pltpu.VMEM)
    steps = nz // 2
    piece = parts.shape[1:]
    return pl.pallas_call(
        functools.partial(relay_reduce_kernel, nx, nz),
        in_specs=[vmem],
        out_specs=vmem,
        out_shape=jax.ShapeDtypeStruct((nx,) + piece, parts.dtype),
        scratch_shapes=[
            pltpu.VMEM((steps + 1, nx) + piece, parts.dtype),
            pltpu.VMEM((steps + 1, nx) + piece, parts.dtype),
            pltpu.VMEM((steps + 1, nx) + piece, parts.dtype),
            pltpu.VMEM((steps + 1, nx) + piece, parts.dtype),
            pltpu.VMEM((nx,) + piece, parts.dtype),
            pltpu.SemaphoreType.DMA((steps + 1, nx)),
            pltpu.SemaphoreType.DMA((steps + 1, nx)),
            pltpu.SemaphoreType.DMA((steps + 1, nx)),
            pltpu.SemaphoreType.DMA((steps + 1, nx)),
            pltpu.SemaphoreType.DMA((nx,)),
            pltpu.SemaphoreType.DMA((nx,)),
        ],
        compiler_params=pltpu.CompilerParams(collective_id=3, has_side_effects=True),
    )(parts)


def local(
    prompt_hidden,
    recompute_hidden,
    key_cache,
    value_cache,
    norm_gain,
    w_query,
    key_weight,
    value_weight,
    w_out,
    passage_owner,
    prompt_slot,
    prompt_length,
    recompute_count,
    recompute_index,
):
    prompt_rows = prompt_hidden.shape[0]
    recompute_rows = recompute_hidden.shape[0]
    query_rows = prompt_rows + recompute_rows
    passage_length = key_cache.shape[1]
    local_heads = w_query.shape[1] // HEAD_SIZE
    n_seq = passage_owner.shape[0]
    me = lax.axis_index("seq")
    scale = 1.0 / math.sqrt(HEAD_SIZE)

    n_mp = w_out.shape[1] // prompt_hidden.shape[1]
    full_rows, meta = mp_gather(
        prompt_hidden, recompute_hidden, passage_owner, prompt_slot, prompt_length,
        recompute_count, recompute_index, n_mp, passage_length,
    )
    own_pos = jnp.concatenate([meta[0], meta[1]])
    own_live = jnp.concatenate([meta[2], meta[3]]) > 0
    own_index = meta[6]
    own_shift = meta[7, 0]
    prompt_live = meta[2] > 0
    recompute_live = meta[3] > 0
    normalized_hidden = normalize(full_rows, norm_gain)
    queries = (
        apply_rotation(
            jnp.dot(normalized_hidden, w_query, preferred_element_type=jnp.float32).reshape(
                query_rows, local_heads, HEAD_SIZE
            ),
            own_pos,
        )
        .astype(jnp.bfloat16)
    )
    fresh_keys = (
        apply_rotation(
            jnp.dot(normalized_hidden, key_weight, preferred_element_type=jnp.float32).reshape(
                query_rows, 1, HEAD_SIZE
            ),
            own_pos,
        )
        .astype(jnp.bfloat16)
        .reshape(query_rows, HEAD_SIZE)
    )
    fresh_values = jnp.dot(
        normalized_hidden, value_weight, preferred_element_type=jnp.float32
    ).astype(jnp.bfloat16)

    position_shift = jnp.full((passage_length,), own_shift, jnp.int32)
    shifted_keys = (
        apply_rotation(
            key_cache[0].astype(jnp.float32).reshape(passage_length, 1, HEAD_SIZE),
            position_shift,
        )
        .astype(jnp.bfloat16)
        .reshape(passage_length, HEAD_SIZE)
    )
    chosen = (own_index[:, None] == jnp.arange(passage_length, dtype=jnp.int32)[None, :]) & (
        recompute_live[:, None]
    )
    replaced = jnp.any(chosen, axis=0)[:, None]
    fresh_pair = jnp.concatenate([fresh_keys[prompt_rows:], fresh_values[prompt_rows:]], axis=1)
    placed = lax.dot_general(
        chosen.astype(jnp.bfloat16),
        fresh_pair,
        (((0,), (0,)), ((), ())),
        preferred_element_type=jnp.float32,
    ).astype(jnp.bfloat16)
    passage_keys = jnp.where(replaced, placed[:, :HEAD_SIZE], shifted_keys)
    passage_values = jnp.where(replaced, placed[:, HEAD_SIZE:], value_cache[0])

    nx, nz = SEQ_SHAPE
    all_queries = relay_gather(
        queries.reshape(2, prompt_rows * local_heads, HEAD_SIZE), nx, nz
    )
    q_blocks = all_queries.reshape(n_seq * 2, prompt_rows * local_heads, HEAD_SIZE)
    lim = jnp.repeat(own_index, local_heads).reshape(-1, 1).astype(jnp.int32)
    packed = passage_attention(nx, nz, meta[4:6], q_blocks, passage_keys, passage_values, lim)
    block_rows = packed.shape[1]

    back = relay_reduce(packed.reshape(n_seq, 2, block_rows, HEAD_SIZE), nx, nz)
    n_parts = back.shape[0]
    rows128 = prompt_rows * local_heads
    stats_back = back[:, :, rows128 : rows128 + 4].astype(jnp.float32)
    part_max = (stats_back[:, :, 0] + stats_back[:, :, 1]).reshape(n_parts, query_rows, local_heads)
    part_tot = (stats_back[:, :, 2] + stats_back[:, :, 3]).reshape(n_parts, query_rows, local_heads)
    part_acc = (
        back[:, :, :rows128].reshape(n_parts, query_rows, local_heads, HEAD_SIZE).astype(jnp.float32)
    )

    pq = queries[:prompt_rows].astype(jnp.float32)
    pk = fresh_keys[:prompt_rows].astype(jnp.float32)
    pv = fresh_values[:prompt_rows].astype(jnp.float32)
    ps = jnp.einsum("qhd,kd->qhk", pq, pk) * scale
    jj = jnp.arange(prompt_rows, dtype=jnp.int32)
    pvis = (jj[None, :] <= jj[:, None]) & prompt_live[None, :]
    ps = jnp.where(pvis[:, None, :], ps, NEGATIVE_FLOOR)
    pmax = jnp.max(ps, axis=-1)
    pw = jnp.where(pvis[:, None, :], jnp.exp(ps - pmax[..., None]), 0.0)
    ptot = jnp.sum(pw, axis=-1)
    pacc = jnp.einsum("qhk,kd->qhd", pw.astype(jnp.bfloat16).astype(jnp.float32), pv)
    loc_max = jnp.concatenate(
        [pmax, jnp.full((recompute_rows, local_heads), NEGATIVE_FLOOR, jnp.float32)]
    )
    loc_tot = jnp.concatenate([ptot, jnp.zeros((recompute_rows, local_heads), jnp.float32)])
    loc_acc = jnp.concatenate(
        [pacc, jnp.zeros((recompute_rows, local_heads, HEAD_SIZE), jnp.float32)]
    )

    highest = jnp.maximum(jnp.max(part_max, axis=0), loc_max)
    part_scale = jnp.exp(part_max - highest[None])
    loc_scale = jnp.exp(loc_max - highest)
    accumulated = jnp.sum(part_acc * part_scale[..., None], axis=0) + loc_acc * loc_scale[..., None]
    totals = jnp.sum(part_tot * part_scale, axis=0) + loc_tot * loc_scale
    safe_totals = jnp.where(totals > 0, totals, 1.0)
    attention = jnp.where(
        own_live[:, None, None], accumulated / safe_totals[..., None], 0.0
    ).astype(jnp.bfloat16).reshape(query_rows, local_heads * HEAD_SIZE)
    projected = jnp.dot(attention, w_out, preferred_element_type=jnp.float32)
    shares = mp_scatter(projected.astype(jnp.bfloat16), n_mp)
    combined = jnp.sum(shares.astype(jnp.float32), axis=0).astype(jnp.bfloat16)
    return (combined[:prompt_rows], combined[prompt_rows:])


def solution(mesh):
    global SEQ_SHAPE
    sizes = dict(zip(mesh.axis_names, mesh.devices.shape))
    seq_devices = mesh.devices.reshape(sizes["seq"], sizes["mp"])[:, 0]
    xs = sorted({d.coords[0] for d in seq_devices})
    SEQ_SHAPE = (len(xs), sizes["seq"] // len(xs))
    return jax.shard_map(
        local,
        mesh=mesh,
        in_specs=(
            P("seq", "mp"),
            P("seq", "mp"),
            P("seq", None, "mp"),
            P("seq", None, "mp"),
            P(),
            P(None, "mp"),
            P(None, "mp"),
            P(None, "mp"),
            P("mp", None),
            P(),
            P(),
            P(),
            P(),
            P(),
        ),
        out_specs=(P("seq", "mp"), P("seq", "mp")),
        check_vma=False,
    )
```

```python
import functools
import math

import jax
import jax.numpy as jnp
from jax import lax
from jax.experimental import pallas as pl
from jax.experimental.pallas import tpu as pltpu
from jax.sharding import PartitionSpec as P

HEAD_SIZE = 128
NEGATIVE_FLOOR = -1e30


def apply_rotation(vectors, positions):
    half_width = vectors.shape[-1] // 2
    exponent = jnp.arange(half_width).astype(jnp.float32) * (2.0 / vectors.shape[-1])
    frequency = jnp.exp(-exponent * math.log(500000.0))
    angles = positions.astype(jnp.float32)[:, None] * frequency[None, :]
    cosines = jnp.cos(angles)[:, None, :]
    sines = jnp.sin(angles)[:, None, :]
    leading = vectors[..., :half_width]
    trailing = vectors[..., half_width:]
    return jnp.concatenate(
        [leading * cosines - trailing * sines, trailing * cosines + leading * sines], axis=-1
    )


def normalize(rows_in, norm_gain):
    values = rows_in.astype(jnp.float32)
    inverse_rms = lax.rsqrt(jnp.mean(values * values, axis=-1, keepdims=True) + 1e-05)
    return (values * inverse_rms * norm_gain).astype(jnp.bfloat16)


MESH = pl.DeviceIdType.MESH


def passage_kernel(nx, nz, flags_ref, q_ref, k_ref, v_ref, lim_ref, out_ref):
    nb, rows, _ = q_ref.shape
    keys = k_ref.shape[0]
    token = lax.broadcasted_iota(jnp.int32, (rows, keys), 1)
    sub = lax.broadcasted_iota(jnp.int32, (16, rows), 0)

    def split(m_row, l_row):
        m_hi = m_row.astype(jnp.bfloat16).astype(jnp.float32)
        l_hi = l_row.astype(jnp.bfloat16).astype(jnp.float32)
        st = jnp.where(
            sub == 0,
            m_row,
            jnp.where(
                sub == 1,
                m_row - m_hi,
                jnp.where(sub == 2, l_row, jnp.where(sub == 3, l_row - l_hi, 0.0)),
            ),
        )
        return st.astype(jnp.bfloat16)

    out_ref[:, 0:rows] = jnp.zeros((nb, rows, HEAD_SIZE), out_ref.dtype)
    floor = jnp.full((16, rows), NEGATIVE_FLOOR, jnp.float32)
    empty = split(floor, jnp.zeros((16, rows), jnp.float32))
    out_ref[:, rows:] = jnp.broadcast_to(empty[None], (nb, 16, rows))

    def attend(b, masked):
        d = b // 2
        stored = ((d % nz) * nx + d // nz) * 2 + b % 2
        scores = lax.dot_general(
            q_ref[stored], k_ref[...], (((1,), (1,)), ((), ())), preferred_element_type=jnp.float32
        ) * (1.0 / math.sqrt(HEAD_SIZE))
        if masked:
            scores = jnp.where(token <= lim_ref[...], scores, NEGATIVE_FLOOR)
        maxima = jnp.max(scores, axis=1, keepdims=True)
        weights = jnp.exp(scores - maxima)
        totals = jnp.sum(weights, axis=1, keepdims=True)
        out_ref[b, 0:rows] = jnp.dot(
            weights.astype(jnp.bfloat16), v_ref[...], preferred_element_type=jnp.float32
        ).astype(out_ref.dtype)
        m_row = jnp.transpose(jnp.broadcast_to(maxima, (rows, rows)))[0:16]
        l_row = jnp.transpose(jnp.broadcast_to(totals, (rows, rows)))[0:16]
        out_ref[b, rows:] = split(m_row, l_row)

    def body(b, carry):
        flag = flags_ref[4 + b % 2, b // 2]

        @pl.when(flag == 1)
        def _():
            attend(b, False)

        @pl.when(flag == 2)
        def _():
            attend(b, True)

        return carry

    lax.fori_loop(0, nb, body, 0)


def passage_attention(nx, nz, flags, q_blocks, keys, values, lim):
    nb, rows, _ = q_blocks.shape
    vmem = pl.BlockSpec(memory_space=pltpu.VMEM)
    return pl.pallas_call(
        functools.partial(passage_kernel, nx, nz),
        in_specs=[pl.BlockSpec(memory_space=pltpu.SMEM), vmem, vmem, vmem, vmem],
        out_specs=vmem,
        out_shape=jax.ShapeDtypeStruct((nb, rows + 16, HEAD_SIZE), jnp.bfloat16),
    )(flags, q_blocks, keys, values, lim)


def mp_gather_kernel(n, span, p_ref, r_ref, owner_ref, slot_ref, plen_ref, count_ref, index_ref,
                     y_ref, meta_ref, lim_ref, send_sem, recv_sem, local_sem):
    me = lax.axis_index("mp")
    row = lax.axis_index("seq")
    rows, width = p_ref.shape
    barrier = pltpu.get_barrier_semaphore()
    for k in range(1, n):
        peer = lax.rem(me + k, n)
        pl.semaphore_signal(barrier, inc=1, device_id=(row, peer), device_id_type=MESH)
    pl.semaphore_wait(barrier, n - 1)
    cols = pl.ds(pl.multiple_of(me * width, width), width)
    copies = []
    for k in range(1, n):
        peer = lax.rem(me + k, n)
        for part, src in enumerate((p_ref, r_ref)):
            c = pltpu.make_async_remote_copy(
                src_ref=src,
                dst_ref=y_ref.at[pl.ds(part * rows, rows), cols],
                send_sem=send_sem.at[part, k],
                recv_sem=recv_sem.at[part, k],
                device_id=(row, peer),
                device_id_type=MESH,
            )
            c.start()
            copies.append(c)
    own = [
        pltpu.make_async_copy(src, y_ref.at[pl.ds(part * rows, rows), cols], local_sem.at[part])
        for part, src in enumerate((p_ref, r_ref))
    ]
    for c in own:
        c.start()

    f32 = jnp.float32
    owner = owner_ref[...].astype(f32)
    slot = slot_ref[...].astype(f32)
    lane = lax.broadcasted_iota(jnp.int32, owner.shape, 1)
    mine = lane == row

    def pick(v):
        return jnp.sum(jnp.where(mine, v, 0.0), axis=1, keepdims=True)

    own_owner = pick(owner)
    own_slot = pick(slot)
    rank = jnp.sum(jnp.where((owner == own_owner) & (lane < row), 1.0, 0.0), axis=1, keepdims=True)
    held = jnp.sum(jnp.where(owner == own_slot, 1.0, 0.0), axis=1, keepdims=True)
    length = pick(plen_ref[...].astype(f32))
    count = pick(count_ref[...].astype(f32))
    index = index_ref[pl.ds(row, 1), :].astype(f32)
    lanef = lane.astype(f32)
    quantities = [
        held * span + lanef,
        rank * span + index,
        jnp.where(lanef < length, 1.0, 0.0),
        jnp.where(lanef < count, 1.0, 0.0),
        jnp.where(slot == own_owner, 1.0, 0.0),
        jnp.where(mine, 2.0, jnp.where((owner == own_owner) & (lane > row), 1.0, 0.0)),
        index,
        rank * span + 0.0 * lanef,
    ]
    for q, value in enumerate(quantities):
        meta_ref[q : q + 1, :] = value.astype(jnp.int32)
    heads = lim_ref.shape[0] // index.shape[1]
    wide = jnp.broadcast_to(index, (lim_ref.shape[0], index.shape[1]))
    which = lax.broadcasted_iota(jnp.int32, wide.shape, 0) // heads
    pick_lane = lax.broadcasted_iota(jnp.int32, wide.shape, 1)
    lim_ref[...] = jnp.sum(jnp.where(which == pick_lane, wide, 0.0), axis=1, keepdims=True).astype(jnp.int32)

    for c in copies:
        c.wait()
    for c in own:
        c.wait()


def mp_gather(prompt_part, recompute_part, owner, slot, plen, count, index, n, span, heads):
    vmem = pl.BlockSpec(memory_space=pltpu.VMEM)
    rows, width = prompt_part.shape
    small = [v.reshape(1, -1) for v in (owner, slot, plen, count)]
    return pl.pallas_call(
        functools.partial(mp_gather_kernel, n, span),
        in_specs=[vmem] * 7,
        out_specs=[vmem, vmem, vmem],
        out_shape=[
            jax.ShapeDtypeStruct((2 * rows, width * n), prompt_part.dtype),
            jax.ShapeDtypeStruct((8, owner.shape[0]), jnp.int32),
            jax.ShapeDtypeStruct((index.shape[1] * heads, 1), jnp.int32),
        ],
        scratch_shapes=[
            pltpu.SemaphoreType.DMA((2, n)),
            pltpu.SemaphoreType.DMA((2, n)),
            pltpu.SemaphoreType.DMA((2,)),
        ],
        compiler_params=pltpu.CompilerParams(collective_id=0, has_side_effects=True),
    )(prompt_part, recompute_part, *small, index)


def mp_scatter_kernel(n, x_ref, y_ref, send_sem, recv_sem, local_sem):
    me = lax.axis_index("mp")
    row = lax.axis_index("seq")
    width = y_ref.shape[2]
    barrier = pltpu.get_barrier_semaphore()
    for k in range(1, n):
        peer = lax.rem(me + k, n)
        pl.semaphore_signal(barrier, inc=1, device_id=(row, peer), device_id_type=MESH)
    pl.semaphore_wait(barrier, n - 1)
    copies = []
    for k in range(1, n):
        peer = lax.rem(me + k, n)
        c = pltpu.make_async_remote_copy(
            src_ref=x_ref.at[:, pl.ds(pl.multiple_of(peer * width, width), width)],
            dst_ref=y_ref.at[me],
            send_sem=send_sem.at[k],
            recv_sem=recv_sem.at[k],
            device_id=(row, peer),
            device_id_type=MESH,
        )
        c.start()
        copies.append(c)
    own = pltpu.make_async_copy(
        x_ref.at[:, pl.ds(pl.multiple_of(me * width, width), width)], y_ref.at[me], local_sem
    )
    own.start()
    for c in copies:
        c.wait()
    own.wait()


def mp_scatter(x, n):
    vmem = pl.BlockSpec(memory_space=pltpu.VMEM)
    return pl.pallas_call(
        functools.partial(mp_scatter_kernel, n),
        in_specs=[vmem],
        out_specs=vmem,
        out_shape=jax.ShapeDtypeStruct((n, x.shape[0], x.shape[1] // n), x.dtype),
        scratch_shapes=[
            pltpu.SemaphoreType.DMA((n,)),
            pltpu.SemaphoreType.DMA((n,)),
            pltpu.SemaphoreType.DMA(()),
        ],
        compiler_params=pltpu.CompilerParams(collective_id=1, has_side_effects=True),
    )(x)


def relay_gather_kernel(nx, nz, x_ref, y_ref, *sems):
    (sx_send, sx_recv, zp_send, zp_recv, zm_send, zm_recv, own_sem,
     bp_send, bp_recv, bm_send, bm_recv, xp_send, xp_recv, xm_send, xm_recv,
     fp_send, fp_recv, fm_send, fm_recv) = sems
    me = lax.axis_index("seq")
    mp = lax.axis_index("mp")
    x = me // nz
    z = me % nz
    up = lax.rem(z + 1, nz)
    down = lax.rem(z + nz - 1, nz)
    right = lax.rem(x + 1, nx)
    left = lax.rem(x + nx - 1, nx)
    barrier = pltpu.get_barrier_semaphore()
    peers = [(lax.rem(x + k, nx) * nz + z, mp) for k in range(1, nx)]
    peers += [(x * nz + up, mp), (x * nz + down, mp)]
    for p in peers:
        pl.semaphore_signal(barrier, inc=1, device_id=p, device_id_type=MESH)
    pl.semaphore_wait(barrier, len(peers))

    def copy(src, dst, send_sem, recv_sem, device):
        c = pltpu.make_async_remote_copy(
            src_ref=src,
            dst_ref=dst,
            send_sem=send_sem,
            recv_sem=recv_sem,
            device_id=device,
            device_id_type=MESH,
        )
        c.start()
        return c

    sent = []
    slot = z * nx + x
    first = [
        copy(x_ref.at[0], y_ref.at[slot, 0], sx_send.at[k], sx_recv.at[k], peers[k - 1])
        for k in range(1, nx)
    ]
    own = pltpu.make_async_copy(x_ref, y_ref.at[slot], own_sem)
    own.start()

    def x_out(column):
        a = copy(
            y_ref.at[column * nx + x, 1], y_ref.at[column * nx + x, 1],
            xp_send.at[column], xp_recv.at[column], (right * nz + z, mp),
        )
        b = copy(
            y_ref.at[column * nx + x, 1], y_ref.at[column * nx + x, 1],
            xm_send.at[column], xm_recv.at[column], (left * nz + z, mp),
        )
        return [a, b]

    own.wait()
    steps = nz // 2
    half = nx // 2
    zlast = {}
    blast = {}
    xcopies = {}
    for c in first:
        c.wait()
    for t in range(1, steps + 1):
        for sign, send_sem, recv_sem, target, count in (
            (1, bp_send, bp_recv, up, steps),
            (-1, bm_send, bm_recv, down, nz - 1 - steps),
        ):
            if t > count:
                continue
            if t > 1:
                blast[sign].wait_recv()
            column = lax.rem(z - sign * (t - 1) + nz, nz)
            if t > 1:
                xcopies[(sign, t - 1)] = x_out(column)
            elif sign == 1:
                xcopies[(0, 0)] = x_out(column)
            blast[sign] = copy(
                y_ref.at[column * nx + x, 1], y_ref.at[column * nx + x, 1],
                send_sem.at[t], recv_sem.at[t], (x * nz + target, mp),
            )
            sent.append(blast[sign])
        for i in range(nx):
            for sign, send_sem, recv_sem, target in (
                (1, zp_send, zp_recv, up),
                (-1, zm_send, zm_recv, down),
            ):
                if t == steps and (i < half) != (sign == 1):
                    continue
                if t > 1:
                    zlast[(sign, i)].wait_recv()
                column = lax.rem(z - sign * (t - 1) + nz, nz)
                zlast[(sign, i)] = copy(
                    y_ref.at[column * nx + i, 0], y_ref.at[column * nx + i, 0],
                    send_sem.at[t, i], recv_sem.at[t, i], (x * nz + target, mp),
                )
                sent.append(zlast[(sign, i)])
    for sign, count in ((1, steps), (-1, nz - 1 - steps)):
        blast[sign].wait_recv()
        column = lax.rem(z - sign * count + nz, nz)
        xcopies[(sign, count)] = x_out(column)
    order = [(0, 0)] + [(s, t) for t in range(1, steps + 1) for s in (1, -1) if (s, t) in xcopies]
    forwards = []
    for key in order:
        sign, t = key
        column = lax.rem(z - sign * t + nz, nz)
        from_left, from_right = xcopies[key]
        from_left.wait_recv()
        from_right.wait_recv()
        sent += xcopies[key]
    for zc in range(nz):
        if zc < nz // 2:
            forwards.append(
                copy(
                    y_ref.at[zc * nx + left, 1], y_ref.at[zc * nx + left, 1],
                    fp_send.at[zc], fp_recv.at[zc], (right * nz + z, mp),
                )
            )
        else:
            forwards.append(
                copy(
                    y_ref.at[zc * nx + right, 1], y_ref.at[zc * nx + right, 1],
                    fm_send.at[zc], fm_recv.at[zc], (left * nz + z, mp),
                )
            )
    for c in zlast.values():
        c.wait_recv()
    for c in forwards:
        c.wait_recv()
    for c in sent:
        c.wait_send()
    for c in forwards:
        c.wait_send()


def relay_gather(x, nx, nz):
    assert nx == 4 and nz % 2 == 0
    vmem = pl.BlockSpec(memory_space=pltpu.VMEM)
    steps = nz // 2
    dma = pltpu.SemaphoreType.DMA
    return pl.pallas_call(
        functools.partial(relay_gather_kernel, nx, nz),
        in_specs=[vmem],
        out_specs=vmem,
        out_shape=jax.ShapeDtypeStruct((nx * nz,) + x.shape, x.dtype),
        scratch_shapes=[
            dma((nx,)), dma((nx,)),
            dma((steps + 1, nx)), dma((steps + 1, nx)), dma((steps + 1, nx)), dma((steps + 1, nx)),
            dma(()),
            dma((steps + 1,)), dma((steps + 1,)), dma((steps + 1,)), dma((steps + 1,)),
            dma((nz,)), dma((nz,)), dma((nz,)), dma((nz,)),
            dma((nz,)), dma((nz,)), dma((nz,)), dma((nz,)),
        ],
        compiler_params=pltpu.CompilerParams(collective_id=2, has_side_effects=True),
    )(x)


def merge_piece(a, b, rows):
    af = a.astype(jnp.float32)
    bf = b.astype(jnp.float32)
    m1 = af[rows : rows + 1] + af[rows + 1 : rows + 2]
    l1 = af[rows + 2 : rows + 3] + af[rows + 3 : rows + 4]
    m2 = bf[rows : rows + 1] + bf[rows + 1 : rows + 2]
    l2 = bf[rows + 2 : rows + 3] + bf[rows + 3 : rows + 4]
    top = jnp.maximum(m1, m2)
    s1 = jnp.exp(m1 - top)
    s2 = jnp.exp(m2 - top)
    total = l1 * s1 + l2 * s2
    c1 = jnp.transpose(jnp.broadcast_to(s1, (rows, rows)))
    c2 = jnp.transpose(jnp.broadcast_to(s2, (rows, rows)))
    acc = af[0:rows] * c1 + bf[0:rows] * c2
    sub = lax.broadcasted_iota(jnp.int32, (16, rows), 0)
    top_hi = top.astype(jnp.bfloat16).astype(jnp.float32)
    tot_hi = total.astype(jnp.bfloat16).astype(jnp.float32)
    st = jnp.where(
        sub == 0,
        top,
        jnp.where(
            sub == 1, top - top_hi, jnp.where(sub == 2, total, jnp.where(sub == 3, total - tot_hi, 0.0))
        ),
    )
    return acc.astype(jnp.bfloat16), st.astype(jnp.bfloat16)


def relay_reduce_kernel(
    nx, nz, x_ref, y_ref, rp, rm, bp, bm, col, sp_send, sp_recv, sm_send, sm_recv, sx_send, sx_recv
):
    me = lax.axis_index("seq")
    mp = lax.axis_index("mp")
    x = me // nz
    z = me % nz
    up = lax.rem(z + 1, nz)
    down = lax.rem(z + nz - 1, nz)
    rows = x_ref.shape[2] - 16
    barrier = pltpu.get_barrier_semaphore()
    peers = [(lax.rem(x + k, nx) * nz + z, mp) for k in range(1, nx)]
    peers += [(x * nz + up, mp), (x * nz + down, mp)]
    for p in peers:
        pl.semaphore_signal(barrier, inc=1, device_id=p, device_id_type=MESH)
    pl.semaphore_wait(barrier, len(peers))

    def merge_into(dst, first, second):
        for h in range(2):
            acc, st = merge_piece(first[h], second[h], rows)
            dst[h, 0:rows] = acc
            dst[h, rows:] = st

    steps = nz // 2
    half = nx // 2
    last = {}
    sent = []
    dirs = ((1, rp, bp, sp_send, sp_recv, up), (-1, rm, bm, sm_send, sm_recv, down))
    for t in range(1, steps + 1):
        for i in range(nx):
            for sign, recv_buf, send_buf, send_sem, recv_sem, target in dirs:
                if t == 1 and (i < half) != (sign == 1):
                    continue
                column = lax.rem(z + sign * (steps + 1 - t) + nz, nz)
                own = x_ref.at[i * nz + column]
                if (sign, i) in last:
                    last[(sign, i)].wait_recv()
                    merge_into(send_buf.at[t, i], own, recv_buf.at[t - 1, i])
                    src = send_buf.at[t, i]
                else:
                    src = own
                c = pltpu.make_async_remote_copy(
                    src_ref=src,
                    dst_ref=recv_buf.at[t, i],
                    send_sem=send_sem.at[t, i],
                    recv_sem=recv_sem.at[t, i],
                    device_id=(x * nz + target, mp),
                    device_id_type=MESH,
                )
                c.start()
                last[(sign, i)] = c
                sent.append(c)

    mine = []
    for i in range(nx):
        last[(1, i)].wait_recv()
        last[(-1, i)].wait_recv()
        merge_into(col.at[i], x_ref.at[i * nz + z], rp.at[steps, i])
        merge_into(col.at[i], col.at[i], rm.at[steps, i])
    for k in range(1, nx):
        target = lax.rem(x + k, nx)
        c = pltpu.make_async_remote_copy(
            src_ref=col.at[target],
            dst_ref=y_ref.at[x],
            send_sem=sx_send.at[k],
            recv_sem=sx_recv.at[k],
            device_id=(target * nz + z, mp),
            device_id_type=MESH,
        )
        c.start()
        mine.append(c)
    y_ref[x] = col[x]
    for c in sent:
        c.wait_send()
    for c in mine:
        c.wait()


def relay_reduce(parts, nx, nz):
    vmem = pl.BlockSpec(memory_space=pltpu.VMEM)
    steps = nz // 2
    piece = parts.shape[1:]
    return pl.pallas_call(
        functools.partial(relay_reduce_kernel, nx, nz),
        in_specs=[vmem],
        out_specs=vmem,
        out_shape=jax.ShapeDtypeStruct((nx,) + piece, parts.dtype),
        scratch_shapes=[
            pltpu.VMEM((steps + 1, nx) + piece, parts.dtype),
            pltpu.VMEM((steps + 1, nx) + piece, parts.dtype),
            pltpu.VMEM((steps + 1, nx) + piece, parts.dtype),
            pltpu.VMEM((steps + 1, nx) + piece, parts.dtype),
            pltpu.VMEM((nx,) + piece, parts.dtype),
            pltpu.SemaphoreType.DMA((steps + 1, nx)),
            pltpu.SemaphoreType.DMA((steps + 1, nx)),
            pltpu.SemaphoreType.DMA((steps + 1, nx)),
            pltpu.SemaphoreType.DMA((steps + 1, nx)),
            pltpu.SemaphoreType.DMA((nx,)),
            pltpu.SemaphoreType.DMA((nx,)),
        ],
        compiler_params=pltpu.CompilerParams(collective_id=3, has_side_effects=True),
    )(parts)


def local(
    prompt_hidden,
    recompute_hidden,
    key_cache,
    value_cache,
    norm_gain,
    w_query,
    key_weight,
    value_weight,
    w_out,
    passage_owner,
    prompt_slot,
    prompt_length,
    recompute_count,
    recompute_index,
):
    prompt_rows = prompt_hidden.shape[0]
    recompute_rows = recompute_hidden.shape[0]
    query_rows = prompt_rows + recompute_rows
    passage_length = key_cache.shape[1]
    local_heads = w_query.shape[1] // HEAD_SIZE
    n_seq = passage_owner.shape[0]
    me = lax.axis_index("seq")
    scale = 1.0 / math.sqrt(HEAD_SIZE)

    n_mp = w_out.shape[1] // prompt_hidden.shape[1]
    full_rows, meta, lim = mp_gather(
        prompt_hidden, recompute_hidden, passage_owner, prompt_slot, prompt_length,
        recompute_count, recompute_index, n_mp, passage_length, local_heads,
    )
    own_pos = jnp.concatenate([meta[0], meta[1]])
    own_live = jnp.concatenate([meta[2], meta[3]]) > 0
    own_index = meta[6]
    own_shift = meta[7, 0]
    prompt_live = meta[2] > 0
    recompute_live = meta[3] > 0
    normalized_hidden = normalize(full_rows, norm_gain)
    queries = (
        apply_rotation(
            jnp.dot(normalized_hidden, w_query, preferred_element_type=jnp.float32).reshape(
                query_rows, local_heads, HEAD_SIZE
            ),
            own_pos,
        )
        .astype(jnp.bfloat16)
    )
    fresh_keys = (
        apply_rotation(
            jnp.dot(normalized_hidden, key_weight, preferred_element_type=jnp.float32).reshape(
                query_rows, 1, HEAD_SIZE
            ),
            own_pos,
        )
        .astype(jnp.bfloat16)
        .reshape(query_rows, HEAD_SIZE)
    )
    fresh_values = jnp.dot(
        normalized_hidden, value_weight, preferred_element_type=jnp.float32
    ).astype(jnp.bfloat16)

    position_shift = jnp.full((passage_length,), own_shift, jnp.int32)
    shifted_keys = (
        apply_rotation(
            key_cache[0].astype(jnp.float32).reshape(passage_length, 1, HEAD_SIZE),
            position_shift,
        )
        .astype(jnp.bfloat16)
        .reshape(passage_length, HEAD_SIZE)
    )
    chosen = (own_index[:, None] == jnp.arange(passage_length, dtype=jnp.int32)[None, :]) & (
        recompute_live[:, None]
    )
    replaced = jnp.any(chosen, axis=0)[:, None]
    fresh_pair = jnp.concatenate([fresh_keys[prompt_rows:], fresh_values[prompt_rows:]], axis=1)
    placed = lax.dot_general(
        chosen.astype(jnp.bfloat16),
        fresh_pair,
        (((0,), (0,)), ((), ())),
        preferred_element_type=jnp.float32,
    ).astype(jnp.bfloat16)
    passage_keys = jnp.where(replaced, placed[:, :HEAD_SIZE], shifted_keys)
    passage_values = jnp.where(replaced, placed[:, HEAD_SIZE:], value_cache[0])

    nx, nz = SEQ_SHAPE
    all_queries = relay_gather(
        queries.reshape(2, prompt_rows * local_heads, HEAD_SIZE), nx, nz
    )
    q_blocks = all_queries.reshape(n_seq * 2, prompt_rows * local_heads, HEAD_SIZE)
    packed = passage_attention(nx, nz, meta, q_blocks, passage_keys, passage_values, lim)
    block_rows = packed.shape[1]

    back = relay_reduce(packed.reshape(n_seq, 2, block_rows, HEAD_SIZE), nx, nz)
    n_parts = back.shape[0]
    rows128 = prompt_rows * local_heads
    stats_back = back[:, :, rows128 : rows128 + 4].astype(jnp.float32)
    part_max = (stats_back[:, :, 0] + stats_back[:, :, 1]).reshape(n_parts, query_rows, local_heads)
    part_tot = (stats_back[:, :, 2] + stats_back[:, :, 3]).reshape(n_parts, query_rows, local_heads)
    part_acc = (
        back[:, :, :rows128].reshape(n_parts, query_rows, local_heads, HEAD_SIZE).astype(jnp.float32)
    )

    pq = queries[:prompt_rows].astype(jnp.float32)
    pk = fresh_keys[:prompt_rows].astype(jnp.float32)
    pv = fresh_values[:prompt_rows].astype(jnp.float32)
    ps = jnp.einsum("qhd,kd->qhk", pq, pk) * scale
    jj = jnp.arange(prompt_rows, dtype=jnp.int32)
    pvis = (jj[None, :] <= jj[:, None]) & prompt_live[None, :]
    ps = jnp.where(pvis[:, None, :], ps, NEGATIVE_FLOOR)
    pmax = jnp.max(ps, axis=-1)
    pw = jnp.where(pvis[:, None, :], jnp.exp(ps - pmax[..., None]), 0.0)
    ptot = jnp.sum(pw, axis=-1)
    pacc = jnp.einsum("qhk,kd->qhd", pw.astype(jnp.bfloat16).astype(jnp.float32), pv)
    loc_max = jnp.concatenate(
        [pmax, jnp.full((recompute_rows, local_heads), NEGATIVE_FLOOR, jnp.float32)]
    )
    loc_tot = jnp.concatenate([ptot, jnp.zeros((recompute_rows, local_heads), jnp.float32)])
    loc_acc = jnp.concatenate(
        [pacc, jnp.zeros((recompute_rows, local_heads, HEAD_SIZE), jnp.float32)]
    )

    highest = jnp.maximum(jnp.max(part_max, axis=0), loc_max)
    part_scale = jnp.exp(part_max - highest[None])
    loc_scale = jnp.exp(loc_max - highest)
    accumulated = jnp.sum(part_acc * part_scale[..., None], axis=0) + loc_acc * loc_scale[..., None]
    totals = jnp.sum(part_tot * part_scale, axis=0) + loc_tot * loc_scale
    safe_totals = jnp.where(totals > 0, totals, 1.0)
    attention = jnp.where(
        own_live[:, None, None], accumulated / safe_totals[..., None], 0.0
    ).astype(jnp.bfloat16).reshape(query_rows, local_heads * HEAD_SIZE)
    projected = jnp.dot(attention, w_out, preferred_element_type=jnp.float32)
    shares = mp_scatter(projected.astype(jnp.bfloat16), n_mp)
    combined = jnp.sum(shares.astype(jnp.float32), axis=0).astype(jnp.bfloat16)
    return (combined[:prompt_rows], combined[prompt_rows:])


def solution(mesh):
    global SEQ_SHAPE
    sizes = dict(zip(mesh.axis_names, mesh.devices.shape))
    seq_devices = mesh.devices.reshape(sizes["seq"], sizes["mp"])[:, 0]
    xs = sorted({d.coords[0] for d in seq_devices})
    SEQ_SHAPE = (len(xs), sizes["seq"] // len(xs))
    return jax.shard_map(
        local,
        mesh=mesh,
        in_specs=(
            P("seq", "mp"),
            P("seq", "mp"),
            P("seq", None, "mp"),
            P("seq", None, "mp"),
            P(),
            P(None, "mp"),
            P(None, "mp"),
            P(None, "mp"),
            P("mp", None),
            P(),
            P(),
            P(),
            P(),
            P(),
        ),
        out_specs=(P("seq", "mp"), P("seq", "mp")),
        check_vma=False,
    )
```

```python
import functools
import math

import jax
import jax.numpy as jnp
from jax import lax
from jax.experimental import pallas as pl
from jax.experimental.pallas import tpu as pltpu
from jax.sharding import PartitionSpec as P

HEAD_SIZE = 128
NEGATIVE_FLOOR = -1e30


def apply_rotation(vectors, positions):
    half_width = vectors.shape[-1] // 2
    exponent = jnp.arange(half_width).astype(jnp.float32) * (2.0 / vectors.shape[-1])
    frequency = jnp.exp(-exponent * math.log(500000.0))
    angles = positions.astype(jnp.float32)[:, None] * frequency[None, :]
    cosines = jnp.cos(angles)[:, None, :]
    sines = jnp.sin(angles)[:, None, :]
    leading = vectors[..., :half_width]
    trailing = vectors[..., half_width:]
    return jnp.concatenate(
        [leading * cosines - trailing * sines, trailing * cosines + leading * sines], axis=-1
    )


def normalize(rows_in, norm_gain):
    values = rows_in.astype(jnp.float32)
    inverse_rms = lax.rsqrt(jnp.mean(values * values, axis=-1, keepdims=True) + 1e-05)
    return (values * inverse_rms * norm_gain).astype(jnp.bfloat16)


MESH = pl.DeviceIdType.MESH


def passage_kernel(nx, nz, flags_ref, q_ref, k_ref, v_ref, lim_ref, out_ref):
    nb, rows, _ = q_ref.shape
    keys = k_ref.shape[0]
    token = lax.broadcasted_iota(jnp.int32, (rows, keys), 1)
    sub = lax.broadcasted_iota(jnp.int32, (16, rows), 0)

    def split(m_row, l_row):
        m_hi = m_row.astype(jnp.bfloat16).astype(jnp.float32)
        l_hi = l_row.astype(jnp.bfloat16).astype(jnp.float32)
        st = jnp.where(
            sub == 0,
            m_row,
            jnp.where(
                sub == 1,
                m_row - m_hi,
                jnp.where(sub == 2, l_row, jnp.where(sub == 3, l_row - l_hi, 0.0)),
            ),
        )
        return st.astype(jnp.bfloat16)

    out_ref[:, 0:rows] = jnp.zeros((nb, rows, HEAD_SIZE), out_ref.dtype)
    floor = jnp.full((16, rows), NEGATIVE_FLOOR, jnp.float32)
    empty = split(floor, jnp.zeros((16, rows), jnp.float32))
    out_ref[:, rows:] = jnp.broadcast_to(empty[None], (nb, 16, rows))

    def attend(b, masked):
        d = b // 2
        stored = ((d % nz) * nx + d // nz) * 2 + b % 2
        scores = lax.dot_general(
            q_ref[stored], k_ref[...], (((1,), (1,)), ((), ())), preferred_element_type=jnp.float32
        ) * (1.0 / math.sqrt(HEAD_SIZE))
        if masked:
            scores = jnp.where(token <= lim_ref[...], scores, NEGATIVE_FLOOR)
        maxima = jnp.max(scores, axis=1, keepdims=True)
        weights = jnp.exp(scores - maxima)
        totals = jnp.sum(weights, axis=1, keepdims=True)
        out_ref[b, 0:rows] = jnp.dot(
            weights.astype(jnp.bfloat16), v_ref[...], preferred_element_type=jnp.float32
        ).astype(out_ref.dtype)
        m_row = jnp.transpose(jnp.broadcast_to(maxima, (rows, rows)))[0:16]
        l_row = jnp.transpose(jnp.broadcast_to(totals, (rows, rows)))[0:16]
        out_ref[b, rows:] = split(m_row, l_row)

    def body(b, carry):
        flag = flags_ref[4 + b % 2, b // 2]

        @pl.when(flag == 1)
        def _():
            attend(b, False)

        @pl.when(flag == 2)
        def _():
            attend(b, True)

        return carry

    lax.fori_loop(0, nb, body, 0)


def passage_attention(nx, nz, flags, q_blocks, keys, values, lim):
    nb, rows, _ = q_blocks.shape
    vmem = pl.BlockSpec(memory_space=pltpu.VMEM)
    return pl.pallas_call(
        functools.partial(passage_kernel, nx, nz),
        in_specs=[pl.BlockSpec(memory_space=pltpu.SMEM), vmem, vmem, vmem, vmem],
        out_specs=vmem,
        out_shape=jax.ShapeDtypeStruct((nb, rows + 16, HEAD_SIZE), jnp.bfloat16),
    )(flags, q_blocks, keys, values, lim)


def mp_gather_kernel(n, span, p_ref, r_ref, owner_ref, slot_ref, plen_ref, count_ref, index_ref,
                     y_ref, meta_ref, lim_ref, send_sem, recv_sem, local_sem):
    me = lax.axis_index("mp")
    row = lax.axis_index("seq")
    rows, width = p_ref.shape
    barrier = pltpu.get_barrier_semaphore()
    for k in range(1, n):
        peer = lax.rem(me + k, n)
        pl.semaphore_signal(barrier, inc=1, device_id=(row, peer), device_id_type=MESH)
    pl.semaphore_wait(barrier, n - 1)
    cols = pl.ds(pl.multiple_of(me * width, width), width)
    copies = []
    for k in range(1, n):
        peer = lax.rem(me + k, n)
        for part, src in enumerate((p_ref, r_ref)):
            c = pltpu.make_async_remote_copy(
                src_ref=src,
                dst_ref=y_ref.at[pl.ds(part * rows, rows), cols],
                send_sem=send_sem.at[part, k],
                recv_sem=recv_sem.at[part, k],
                device_id=(row, peer),
                device_id_type=MESH,
            )
            c.start()
            copies.append(c)
    own = [
        pltpu.make_async_copy(src, y_ref.at[pl.ds(part * rows, rows), cols], local_sem.at[part])
        for part, src in enumerate((p_ref, r_ref))
    ]
    for c in own:
        c.start()

    f32 = jnp.float32
    owner = owner_ref[...].astype(f32)
    slot = slot_ref[...].astype(f32)
    lane = lax.broadcasted_iota(jnp.int32, owner.shape, 1)
    mine = lane == row

    def pick(v):
        return jnp.sum(jnp.where(mine, v, 0.0), axis=1, keepdims=True)

    own_owner = pick(owner)
    own_slot = pick(slot)
    rank = jnp.sum(jnp.where((owner == own_owner) & (lane < row), 1.0, 0.0), axis=1, keepdims=True)
    held = jnp.sum(jnp.where(owner == own_slot, 1.0, 0.0), axis=1, keepdims=True)
    length = pick(plen_ref[...].astype(f32))
    count = pick(count_ref[...].astype(f32))
    index = index_ref[pl.ds(row, 1), :].astype(f32)
    lanef = lane.astype(f32)
    quantities = [
        held * span + lanef,
        rank * span + index,
        jnp.where(lanef < length, 1.0, 0.0),
        jnp.where(lanef < count, 1.0, 0.0),
        jnp.where(slot == own_owner, 1.0, 0.0),
        jnp.where(mine, 2.0, jnp.where((owner == own_owner) & (lane > row), 1.0, 0.0)),
        index,
        rank * span + 0.0 * lanef,
    ]
    for q, value in enumerate(quantities):
        meta_ref[q : q + 1, :] = value.astype(jnp.int32)
    heads = lim_ref.shape[0] // index.shape[1]
    wide = jnp.broadcast_to(index, (lim_ref.shape[0], index.shape[1]))
    which = lax.broadcasted_iota(jnp.int32, wide.shape, 0) // heads
    pick_lane = lax.broadcasted_iota(jnp.int32, wide.shape, 1)
    lim_ref[...] = jnp.sum(jnp.where(which == pick_lane, wide, 0.0), axis=1, keepdims=True).astype(jnp.int32)

    for c in copies:
        c.wait()
    for c in own:
        c.wait()


def mp_gather(prompt_part, recompute_part, owner, slot, plen, count, index, n, span, heads):
    vmem = pl.BlockSpec(memory_space=pltpu.VMEM)
    rows, width = prompt_part.shape
    small = [v.reshape(1, -1) for v in (owner, slot, plen, count)]
    return pl.pallas_call(
        functools.partial(mp_gather_kernel, n, span),
        in_specs=[vmem] * 7,
        out_specs=[vmem, vmem, vmem],
        out_shape=[
            jax.ShapeDtypeStruct((2 * rows, width * n), prompt_part.dtype),
            jax.ShapeDtypeStruct((8, owner.shape[0]), jnp.int32),
            jax.ShapeDtypeStruct((index.shape[1] * heads, 1), jnp.int32),
        ],
        scratch_shapes=[
            pltpu.SemaphoreType.DMA((2, n)),
            pltpu.SemaphoreType.DMA((2, n)),
            pltpu.SemaphoreType.DMA((2,)),
        ],
        compiler_params=pltpu.CompilerParams(collective_id=0, has_side_effects=True),
    )(prompt_part, recompute_part, *small, index)


def mp_scatter_kernel(n, a_ref, w_ref, y_ref, buf, send_sem, recv_sem):
    me = lax.axis_index("mp")
    row = lax.axis_index("seq")
    width = y_ref.shape[2]
    barrier = pltpu.get_barrier_semaphore()
    for k in range(1, n):
        peer = lax.rem(me + k, n)
        pl.semaphore_signal(barrier, inc=1, device_id=(row, peer), device_id_type=MESH)
    pl.semaphore_wait(barrier, n - 1)

    def block(d):
        cols = pl.ds(pl.multiple_of(d * width, width), width)
        return jnp.dot(a_ref[...], w_ref[:, cols], preferred_element_type=jnp.float32).astype(
            y_ref.dtype
        )

    copies = []
    for k in range(1, n):
        peer = lax.rem(me + k, n)
        buf[k] = block(peer)
        c = pltpu.make_async_remote_copy(
            src_ref=buf.at[k],
            dst_ref=y_ref.at[me],
            send_sem=send_sem.at[k],
            recv_sem=recv_sem.at[k],
            device_id=(row, peer),
            device_id_type=MESH,
        )
        c.start()
        copies.append(c)
    y_ref[me] = block(me)
    for c in copies:
        c.wait()


def mp_scatter(attention, w_out, n):
    vmem = pl.BlockSpec(memory_space=pltpu.VMEM)
    rows = attention.shape[0]
    width = w_out.shape[1] // n
    return pl.pallas_call(
        functools.partial(mp_scatter_kernel, n),
        in_specs=[vmem, vmem],
        out_specs=vmem,
        out_shape=jax.ShapeDtypeStruct((n, rows, width), jnp.bfloat16),
        scratch_shapes=[
            pltpu.VMEM((n, rows, width), jnp.bfloat16),
            pltpu.SemaphoreType.DMA((n,)),
            pltpu.SemaphoreType.DMA((n,)),
        ],
        compiler_params=pltpu.CompilerParams(collective_id=1, has_side_effects=True),
    )(attention, w_out)


def relay_gather_kernel(nx, nz, x_ref, y_ref, *sems):
    (sx_send, sx_recv, zp_send, zp_recv, zm_send, zm_recv, own_sem,
     bp_send, bp_recv, bm_send, bm_recv, xp_send, xp_recv, xm_send, xm_recv,
     fp_send, fp_recv, fm_send, fm_recv) = sems
    me = lax.axis_index("seq")
    mp = lax.axis_index("mp")
    x = me // nz
    z = me % nz
    up = lax.rem(z + 1, nz)
    down = lax.rem(z + nz - 1, nz)
    right = lax.rem(x + 1, nx)
    left = lax.rem(x + nx - 1, nx)
    barrier = pltpu.get_barrier_semaphore()
    peers = [(lax.rem(x + k, nx) * nz + z, mp) for k in range(1, nx)]
    peers += [(x * nz + up, mp), (x * nz + down, mp)]
    for p in peers:
        pl.semaphore_signal(barrier, inc=1, device_id=p, device_id_type=MESH)
    pl.semaphore_wait(barrier, len(peers))

    def copy(src, dst, send_sem, recv_sem, device):
        c = pltpu.make_async_remote_copy(
            src_ref=src,
            dst_ref=dst,
            send_sem=send_sem,
            recv_sem=recv_sem,
            device_id=device,
            device_id_type=MESH,
        )
        c.start()
        return c

    sent = []
    slot = z * nx + x
    first = [
        copy(x_ref.at[0], y_ref.at[slot, 0], sx_send.at[k], sx_recv.at[k], peers[k - 1])
        for k in range(1, nx)
    ]
    own = pltpu.make_async_copy(x_ref, y_ref.at[slot], own_sem)
    own.start()

    def x_out(column):
        a = copy(
            y_ref.at[column * nx + x, 1], y_ref.at[column * nx + x, 1],
            xp_send.at[column], xp_recv.at[column], (right * nz + z, mp),
        )
        b = copy(
            y_ref.at[column * nx + x, 1], y_ref.at[column * nx + x, 1],
            xm_send.at[column], xm_recv.at[column], (left * nz + z, mp),
        )
        return [a, b]

    own.wait()
    steps = nz // 2
    half = nx // 2
    zlast = {}
    blast = {}
    xcopies = {}
    for c in first:
        c.wait()
    for t in range(1, steps + 1):
        for sign, send_sem, recv_sem, target, count in (
            (1, bp_send, bp_recv, up, steps),
            (-1, bm_send, bm_recv, down, nz - 1 - steps),
        ):
            if t > count:
                continue
            if t > 1:
                blast[sign].wait_recv()
            column = lax.rem(z - sign * (t - 1) + nz, nz)
            if t > 1:
                xcopies[(sign, t - 1)] = x_out(column)
            elif sign == 1:
                xcopies[(0, 0)] = x_out(column)
            blast[sign] = copy(
                y_ref.at[column * nx + x, 1], y_ref.at[column * nx + x, 1],
                send_sem.at[t], recv_sem.at[t], (x * nz + target, mp),
            )
            sent.append(blast[sign])
        for i in range(nx):
            for sign, send_sem, recv_sem, target in (
                (1, zp_send, zp_recv, up),
                (-1, zm_send, zm_recv, down),
            ):
                if t == steps and (i < half) != (sign == 1):
                    continue
                if t > 1:
                    zlast[(sign, i)].wait_recv()
                column = lax.rem(z - sign * (t - 1) + nz, nz)
                zlast[(sign, i)] = copy(
                    y_ref.at[column * nx + i, 0], y_ref.at[column * nx + i, 0],
                    send_sem.at[t, i], recv_sem.at[t, i], (x * nz + target, mp),
                )
                sent.append(zlast[(sign, i)])
    for sign, count in ((1, steps), (-1, nz - 1 - steps)):
        blast[sign].wait_recv()
        column = lax.rem(z - sign * count + nz, nz)
        xcopies[(sign, count)] = x_out(column)
    order = [(0, 0)] + [(s, t) for t in range(1, steps + 1) for s in (1, -1) if (s, t) in xcopies]
    forwards = []
    for key in order:
        sign, t = key
        column = lax.rem(z - sign * t + nz, nz)
        from_left, from_right = xcopies[key]
        from_left.wait_recv()
        from_right.wait_recv()
        sent += xcopies[key]
    for zc in range(nz):
        if zc < nz // 2:
            forwards.append(
                copy(
                    y_ref.at[zc * nx + left, 1], y_ref.at[zc * nx + left, 1],
                    fp_send.at[zc], fp_recv.at[zc], (right * nz + z, mp),
                )
            )
        else:
            forwards.append(
                copy(
                    y_ref.at[zc * nx + right, 1], y_ref.at[zc * nx + right, 1],
                    fm_send.at[zc], fm_recv.at[zc], (left * nz + z, mp),
                )
            )
    for c in zlast.values():
        c.wait_recv()
    for c in forwards:
        c.wait_recv()
    for c in sent:
        c.wait_send()
    for c in forwards:
        c.wait_send()


def relay_gather(x, nx, nz):
    assert nx == 4 and nz % 2 == 0
    vmem = pl.BlockSpec(memory_space=pltpu.VMEM)
    steps = nz // 2
    dma = pltpu.SemaphoreType.DMA
    return pl.pallas_call(
        functools.partial(relay_gather_kernel, nx, nz),
        in_specs=[vmem],
        out_specs=vmem,
        out_shape=jax.ShapeDtypeStruct((nx * nz,) + x.shape, x.dtype),
        scratch_shapes=[
            dma((nx,)), dma((nx,)),
            dma((steps + 1, nx)), dma((steps + 1, nx)), dma((steps + 1, nx)), dma((steps + 1, nx)),
            dma(()),
            dma((steps + 1,)), dma((steps + 1,)), dma((steps + 1,)), dma((steps + 1,)),
            dma((nz,)), dma((nz,)), dma((nz,)), dma((nz,)),
            dma((nz,)), dma((nz,)), dma((nz,)), dma((nz,)),
        ],
        compiler_params=pltpu.CompilerParams(collective_id=2, has_side_effects=True),
    )(x)


def merge_piece(a, b, rows):
    af = a.astype(jnp.float32)
    bf = b.astype(jnp.float32)
    m1 = af[rows : rows + 1] + af[rows + 1 : rows + 2]
    l1 = af[rows + 2 : rows + 3] + af[rows + 3 : rows + 4]
    m2 = bf[rows : rows + 1] + bf[rows + 1 : rows + 2]
    l2 = bf[rows + 2 : rows + 3] + bf[rows + 3 : rows + 4]
    top = jnp.maximum(m1, m2)
    s1 = jnp.exp(m1 - top)
    s2 = jnp.exp(m2 - top)
    total = l1 * s1 + l2 * s2
    c1 = jnp.transpose(jnp.broadcast_to(s1, (rows, rows)))
    c2 = jnp.transpose(jnp.broadcast_to(s2, (rows, rows)))
    acc = af[0:rows] * c1 + bf[0:rows] * c2
    sub = lax.broadcasted_iota(jnp.int32, (16, rows), 0)
    top_hi = top.astype(jnp.bfloat16).astype(jnp.float32)
    tot_hi = total.astype(jnp.bfloat16).astype(jnp.float32)
    st = jnp.where(
        sub == 0,
        top,
        jnp.where(
            sub == 1, top - top_hi, jnp.where(sub == 2, total, jnp.where(sub == 3, total - tot_hi, 0.0))
        ),
    )
    return acc.astype(jnp.bfloat16), st.astype(jnp.bfloat16)


def relay_reduce_kernel(
    nx, nz, x_ref, y_ref, rp, rm, bp, bm, col, sp_send, sp_recv, sm_send, sm_recv, sx_send, sx_recv
):
    me = lax.axis_index("seq")
    mp = lax.axis_index("mp")
    x = me // nz
    z = me % nz
    up = lax.rem(z + 1, nz)
    down = lax.rem(z + nz - 1, nz)
    rows = x_ref.shape[2] - 16
    barrier = pltpu.get_barrier_semaphore()
    peers = [(lax.rem(x + k, nx) * nz + z, mp) for k in range(1, nx)]
    peers += [(x * nz + up, mp), (x * nz + down, mp)]
    for p in peers:
        pl.semaphore_signal(barrier, inc=1, device_id=p, device_id_type=MESH)
    pl.semaphore_wait(barrier, len(peers))

    def merge_into(dst, first, second):
        for h in range(2):
            acc, st = merge_piece(first[h], second[h], rows)
            dst[h, 0:rows] = acc
            dst[h, rows:] = st

    steps = nz // 2
    half = nx // 2
    last = {}
    sent = []
    dirs = ((1, rp, bp, sp_send, sp_recv, up), (-1, rm, bm, sm_send, sm_recv, down))
    for t in range(1, steps + 1):
        for i in range(nx):
            for sign, recv_buf, send_buf, send_sem, recv_sem, target in dirs:
                if t == 1 and (i < half) != (sign == 1):
                    continue
                column = lax.rem(z + sign * (steps + 1 - t) + nz, nz)
                own = x_ref.at[i * nz + column]
                if (sign, i) in last:
                    last[(sign, i)].wait_recv()
                    merge_into(send_buf.at[t, i], own, recv_buf.at[t - 1, i])
                    src = send_buf.at[t, i]
                else:
                    src = own
                c = pltpu.make_async_remote_copy(
                    src_ref=src,
                    dst_ref=recv_buf.at[t, i],
                    send_sem=send_sem.at[t, i],
                    recv_sem=recv_sem.at[t, i],
                    device_id=(x * nz + target, mp),
                    device_id_type=MESH,
                )
                c.start()
                last[(sign, i)] = c
                sent.append(c)

    mine = []
    for i in range(nx):
        last[(1, i)].wait_recv()
        last[(-1, i)].wait_recv()
        merge_into(col.at[i], x_ref.at[i * nz + z], rp.at[steps, i])
        merge_into(col.at[i], col.at[i], rm.at[steps, i])
    for k in range(1, nx):
        target = lax.rem(x + k, nx)
        c = pltpu.make_async_remote_copy(
            src_ref=col.at[target],
            dst_ref=y_ref.at[x],
            send_sem=sx_send.at[k],
            recv_sem=sx_recv.at[k],
            device_id=(target * nz + z, mp),
            device_id_type=MESH,
        )
        c.start()
        mine.append(c)
    y_ref[x] = col[x]
    for c in sent:
        c.wait_send()
    for c in mine:
        c.wait()


def relay_reduce(parts, nx, nz):
    vmem = pl.BlockSpec(memory_space=pltpu.VMEM)
    steps = nz // 2
    piece = parts.shape[1:]
    return pl.pallas_call(
        functools.partial(relay_reduce_kernel, nx, nz),
        in_specs=[vmem],
        out_specs=vmem,
        out_shape=jax.ShapeDtypeStruct((nx,) + piece, parts.dtype),
        scratch_shapes=[
            pltpu.VMEM((steps + 1, nx) + piece, parts.dtype),
            pltpu.VMEM((steps + 1, nx) + piece, parts.dtype),
            pltpu.VMEM((steps + 1, nx) + piece, parts.dtype),
            pltpu.VMEM((steps + 1, nx) + piece, parts.dtype),
            pltpu.VMEM((nx,) + piece, parts.dtype),
            pltpu.SemaphoreType.DMA((steps + 1, nx)),
            pltpu.SemaphoreType.DMA((steps + 1, nx)),
            pltpu.SemaphoreType.DMA((steps + 1, nx)),
            pltpu.SemaphoreType.DMA((steps + 1, nx)),
            pltpu.SemaphoreType.DMA((nx,)),
            pltpu.SemaphoreType.DMA((nx,)),
        ],
        compiler_params=pltpu.CompilerParams(collective_id=3, has_side_effects=True),
    )(parts)


def local(
    prompt_hidden,
    recompute_hidden,
    key_cache,
    value_cache,
    norm_gain,
    w_query,
    key_weight,
    value_weight,
    w_out,
    passage_owner,
    prompt_slot,
    prompt_length,
    recompute_count,
    recompute_index,
):
    prompt_rows = prompt_hidden.shape[0]
    recompute_rows = recompute_hidden.shape[0]
    query_rows = prompt_rows + recompute_rows
    passage_length = key_cache.shape[1]
    local_heads = w_query.shape[1] // HEAD_SIZE
    n_seq = passage_owner.shape[0]
    me = lax.axis_index("seq")
    scale = 1.0 / math.sqrt(HEAD_SIZE)

    n_mp = w_out.shape[1] // prompt_hidden.shape[1]
    full_rows, meta, lim = mp_gather(
        prompt_hidden, recompute_hidden, passage_owner, prompt_slot, prompt_length,
        recompute_count, recompute_index, n_mp, passage_length, local_heads,
    )
    own_pos = jnp.concatenate([meta[0], meta[1]])
    own_live = jnp.concatenate([meta[2], meta[3]]) > 0
    own_index = meta[6]
    own_shift = meta[7, 0]
    prompt_live = meta[2] > 0
    recompute_live = meta[3] > 0
    normalized_hidden = normalize(full_rows, norm_gain)
    queries = (
        apply_rotation(
            jnp.dot(normalized_hidden, w_query, preferred_element_type=jnp.float32).reshape(
                query_rows, local_heads, HEAD_SIZE
            ),
            own_pos,
        )
        .astype(jnp.bfloat16)
    )
    fresh_keys = (
        apply_rotation(
            jnp.dot(normalized_hidden, key_weight, preferred_element_type=jnp.float32).reshape(
                query_rows, 1, HEAD_SIZE
            ),
            own_pos,
        )
        .astype(jnp.bfloat16)
        .reshape(query_rows, HEAD_SIZE)
    )
    fresh_values = jnp.dot(
        normalized_hidden, value_weight, preferred_element_type=jnp.float32
    ).astype(jnp.bfloat16)

    position_shift = jnp.full((passage_length,), own_shift, jnp.int32)
    shifted_keys = (
        apply_rotation(
            key_cache[0].astype(jnp.float32).reshape(passage_length, 1, HEAD_SIZE),
            position_shift,
        )
        .astype(jnp.bfloat16)
        .reshape(passage_length, HEAD_SIZE)
    )
    chosen = (own_index[:, None] == jnp.arange(passage_length, dtype=jnp.int32)[None, :]) & (
        recompute_live[:, None]
    )
    replaced = jnp.any(chosen, axis=0)[:, None]
    fresh_pair = jnp.concatenate([fresh_keys[prompt_rows:], fresh_values[prompt_rows:]], axis=1)
    placed = lax.dot_general(
        chosen.astype(jnp.bfloat16),
        fresh_pair,
        (((0,), (0,)), ((), ())),
        preferred_element_type=jnp.float32,
    ).astype(jnp.bfloat16)
    passage_keys = jnp.where(replaced, placed[:, :HEAD_SIZE], shifted_keys)
    passage_values = jnp.where(replaced, placed[:, HEAD_SIZE:], value_cache[0])

    nx, nz = SEQ_SHAPE
    all_queries = relay_gather(
        queries.reshape(2, prompt_rows * local_heads, HEAD_SIZE), nx, nz
    )
    q_blocks = all_queries.reshape(n_seq * 2, prompt_rows * local_heads, HEAD_SIZE)
    packed = passage_attention(nx, nz, meta, q_blocks, passage_keys, passage_values, lim)
    block_rows = packed.shape[1]

    back = relay_reduce(packed.reshape(n_seq, 2, block_rows, HEAD_SIZE), nx, nz)
    n_parts = back.shape[0]
    rows128 = prompt_rows * local_heads
    stats_back = back[:, :, rows128 : rows128 + 4].astype(jnp.float32)
    part_max = (stats_back[:, :, 0] + stats_back[:, :, 1]).reshape(n_parts, query_rows, local_heads)
    part_tot = (stats_back[:, :, 2] + stats_back[:, :, 3]).reshape(n_parts, query_rows, local_heads)
    part_acc = (
        back[:, :, :rows128].reshape(n_parts, query_rows, local_heads, HEAD_SIZE).astype(jnp.float32)
    )

    pq = queries[:prompt_rows].astype(jnp.float32)
    pk = fresh_keys[:prompt_rows].astype(jnp.float32)
    pv = fresh_values[:prompt_rows].astype(jnp.float32)
    ps = jnp.einsum("qhd,kd->qhk", pq, pk) * scale
    jj = jnp.arange(prompt_rows, dtype=jnp.int32)
    pvis = (jj[None, :] <= jj[:, None]) & prompt_live[None, :]
    ps = jnp.where(pvis[:, None, :], ps, NEGATIVE_FLOOR)
    pmax = jnp.max(ps, axis=-1)
    pw = jnp.where(pvis[:, None, :], jnp.exp(ps - pmax[..., None]), 0.0)
    ptot = jnp.sum(pw, axis=-1)
    pacc = jnp.einsum("qhk,kd->qhd", pw.astype(jnp.bfloat16).astype(jnp.float32), pv)
    loc_max = jnp.concatenate(
        [pmax, jnp.full((recompute_rows, local_heads), NEGATIVE_FLOOR, jnp.float32)]
    )
    loc_tot = jnp.concatenate([ptot, jnp.zeros((recompute_rows, local_heads), jnp.float32)])
    loc_acc = jnp.concatenate(
        [pacc, jnp.zeros((recompute_rows, local_heads, HEAD_SIZE), jnp.float32)]
    )

    highest = jnp.maximum(jnp.max(part_max, axis=0), loc_max)
    part_scale = jnp.exp(part_max - highest[None])
    loc_scale = jnp.exp(loc_max - highest)
    accumulated = jnp.sum(part_acc * part_scale[..., None], axis=0) + loc_acc * loc_scale[..., None]
    totals = jnp.sum(part_tot * part_scale, axis=0) + loc_tot * loc_scale
    safe_totals = jnp.where(totals > 0, totals, 1.0)
    attention = jnp.where(
        own_live[:, None, None], accumulated / safe_totals[..., None], 0.0
    ).astype(jnp.bfloat16).reshape(query_rows, local_heads * HEAD_SIZE)
    shares = mp_scatter(attention, w_out, n_mp)
    combined = jnp.sum(shares.astype(jnp.float32), axis=0).astype(jnp.bfloat16)
    return (combined[:prompt_rows], combined[prompt_rows:])


def solution(mesh):
    global SEQ_SHAPE
    sizes = dict(zip(mesh.axis_names, mesh.devices.shape))
    seq_devices = mesh.devices.reshape(sizes["seq"], sizes["mp"])[:, 0]
    xs = sorted({d.coords[0] for d in seq_devices})
    SEQ_SHAPE = (len(xs), sizes["seq"] // len(xs))
    return jax.shard_map(
        local,
        mesh=mesh,
        in_specs=(
            P("seq", "mp"),
            P("seq", "mp"),
            P("seq", None, "mp"),
            P("seq", None, "mp"),
            P(),
            P(None, "mp"),
            P(None, "mp"),
            P(None, "mp"),
            P("mp", None),
            P(),
            P(),
            P(),
            P(),
            P(),
        ),
        out_specs=(P("seq", "mp"), P("seq", "mp")),
        check_vma=False,
    )
```

```python
import functools
import math

import jax
import jax.numpy as jnp
from jax import lax
from jax.experimental import pallas as pl
from jax.experimental.pallas import tpu as pltpu
from jax.sharding import PartitionSpec as P

HEAD_SIZE = 128
NEGATIVE_FLOOR = -1e30


def apply_rotation(vectors, positions):
    half_width = vectors.shape[-1] // 2
    exponent = jnp.arange(half_width).astype(jnp.float32) * (2.0 / vectors.shape[-1])
    frequency = jnp.exp(-exponent * math.log(500000.0))
    angles = positions.astype(jnp.float32)[:, None] * frequency[None, :]
    cosines = jnp.cos(angles)[:, None, :]
    sines = jnp.sin(angles)[:, None, :]
    leading = vectors[..., :half_width]
    trailing = vectors[..., half_width:]
    return jnp.concatenate(
        [leading * cosines - trailing * sines, trailing * cosines + leading * sines], axis=-1
    )


def normalize(rows_in, norm_gain):
    values = rows_in.astype(jnp.float32)
    inverse_rms = lax.rsqrt(jnp.mean(values * values, axis=-1, keepdims=True) + 1e-05)
    return (values * inverse_rms * norm_gain).astype(jnp.bfloat16)


MESH = pl.DeviceIdType.MESH


def passage_kernel(nx, nz, flags_ref, q_ref, k_ref, v_ref, lim_ref, out_ref):
    nb, rows, _ = q_ref.shape
    keys = k_ref.shape[0]
    token = lax.broadcasted_iota(jnp.int32, (rows, keys), 1)
    sub = lax.broadcasted_iota(jnp.int32, (16, rows), 0)

    def split(m_row, l_row):
        m_hi = m_row.astype(jnp.bfloat16).astype(jnp.float32)
        l_hi = l_row.astype(jnp.bfloat16).astype(jnp.float32)
        st = jnp.where(
            sub == 0,
            m_row,
            jnp.where(
                sub == 1,
                m_row - m_hi,
                jnp.where(sub == 2, l_row, jnp.where(sub == 3, l_row - l_hi, 0.0)),
            ),
        )
        return st.astype(jnp.bfloat16)

    out_ref[:, 0:rows] = jnp.zeros((nb, rows, HEAD_SIZE), out_ref.dtype)
    floor = jnp.full((16, rows), NEGATIVE_FLOOR, jnp.float32)
    empty = split(floor, jnp.zeros((16, rows), jnp.float32))
    out_ref[:, rows:] = jnp.broadcast_to(empty[None], (nb, 16, rows))

    def attend(b, masked):
        d = b // 2
        stored = ((d % nz) * nx + d // nz) * 2 + b % 2
        scores = lax.dot_general(
            q_ref[stored], k_ref[...], (((1,), (1,)), ((), ())), preferred_element_type=jnp.float32
        ) * (1.0 / math.sqrt(HEAD_SIZE))
        if masked:
            scores = jnp.where(token <= lim_ref[...], scores, NEGATIVE_FLOOR)
        maxima = jnp.max(scores, axis=1, keepdims=True)
        weights = jnp.exp(scores - maxima)
        totals = jnp.sum(weights, axis=1, keepdims=True)
        out_ref[b, 0:rows] = jnp.dot(
            weights.astype(jnp.bfloat16), v_ref[...], preferred_element_type=jnp.float32
        ).astype(out_ref.dtype)
        m_row = jnp.transpose(jnp.broadcast_to(maxima, (rows, rows)))[0:16]
        l_row = jnp.transpose(jnp.broadcast_to(totals, (rows, rows)))[0:16]
        out_ref[b, rows:] = split(m_row, l_row)

    def body(b, carry):
        flag = flags_ref[4 + b % 2, b // 2]

        @pl.when(flag == 1)
        def _():
            attend(b, False)

        @pl.when(flag == 2)
        def _():
            attend(b, True)

        return carry

    lax.fori_loop(0, nb, body, 0)


def passage_attention(nx, nz, flags, q_blocks, keys, values, lim):
    nb, rows, _ = q_blocks.shape
    vmem = pl.BlockSpec(memory_space=pltpu.VMEM)
    return pl.pallas_call(
        functools.partial(passage_kernel, nx, nz),
        in_specs=[pl.BlockSpec(memory_space=pltpu.SMEM), vmem, vmem, vmem, vmem],
        out_specs=vmem,
        out_shape=jax.ShapeDtypeStruct((nb, rows + 16, HEAD_SIZE), jnp.bfloat16),
    )(flags, q_blocks, keys, values, lim)


def mp_gather_kernel(n, span, p_ref, r_ref, owner_ref, slot_ref, plen_ref, count_ref, index_ref,
                     y_ref, meta_ref, lim_ref, send_sem, recv_sem, local_sem):
    me = lax.axis_index("mp")
    row = lax.axis_index("seq")
    rows, width = p_ref.shape
    barrier = pltpu.get_barrier_semaphore()
    for k in range(1, n):
        peer = lax.rem(me + k, n)
        pl.semaphore_signal(barrier, inc=1, device_id=(row, peer), device_id_type=MESH)
    pl.semaphore_wait(barrier, n - 1)
    cols = pl.ds(pl.multiple_of(me * width, width), width)
    copies = []
    for k in range(1, n):
        peer = lax.rem(me + k, n)
        for part, src in enumerate((p_ref, r_ref)):
            c = pltpu.make_async_remote_copy(
                src_ref=src,
                dst_ref=y_ref.at[pl.ds(part * rows, rows), cols],
                send_sem=send_sem.at[part, k],
                recv_sem=recv_sem.at[part, k],
                device_id=(row, peer),
                device_id_type=MESH,
            )
            c.start()
            copies.append(c)
    own = [
        pltpu.make_async_copy(src, y_ref.at[pl.ds(part * rows, rows), cols], local_sem.at[part])
        for part, src in enumerate((p_ref, r_ref))
    ]
    for c in own:
        c.start()

    f32 = jnp.float32
    owner = owner_ref[...].astype(f32)
    slot = slot_ref[...].astype(f32)
    lane = lax.broadcasted_iota(jnp.int32, owner.shape, 1)
    mine = lane == row

    def pick(v):
        return jnp.sum(jnp.where(mine, v, 0.0), axis=1, keepdims=True)

    own_owner = pick(owner)
    own_slot = pick(slot)
    rank = jnp.sum(jnp.where((owner == own_owner) & (lane < row), 1.0, 0.0), axis=1, keepdims=True)
    held = jnp.sum(jnp.where(owner == own_slot, 1.0, 0.0), axis=1, keepdims=True)
    length = pick(plen_ref[...].astype(f32))
    count = pick(count_ref[...].astype(f32))
    index = index_ref[pl.ds(row, 1), :].astype(f32)
    lanef = lane.astype(f32)
    quantities = [
        held * span + lanef,
        rank * span + index,
        jnp.where(lanef < length, 1.0, 0.0),
        jnp.where(lanef < count, 1.0, 0.0),
        jnp.where(slot == own_owner, 1.0, 0.0),
        jnp.where(mine, 2.0, jnp.where((owner == own_owner) & (lane > row), 1.0, 0.0)),
        index,
        rank * span + 0.0 * lanef,
    ]
    for q, value in enumerate(quantities):
        meta_ref[q : q + 1, :] = value.astype(jnp.int32)
    heads = lim_ref.shape[0] // index.shape[1]
    wide = jnp.broadcast_to(index, (lim_ref.shape[0], index.shape[1]))
    which = lax.broadcasted_iota(jnp.int32, wide.shape, 0) // heads
    pick_lane = lax.broadcasted_iota(jnp.int32, wide.shape, 1)
    lim_ref[...] = jnp.sum(jnp.where(which == pick_lane, wide, 0.0), axis=1, keepdims=True).astype(jnp.int32)

    for c in copies:
        c.wait()
    for c in own:
        c.wait()


def mp_gather(prompt_part, recompute_part, owner, slot, plen, count, index, n, span, heads):
    vmem = pl.BlockSpec(memory_space=pltpu.VMEM)
    rows, width = prompt_part.shape
    small = [v.reshape(1, -1) for v in (owner, slot, plen, count)]
    return pl.pallas_call(
        functools.partial(mp_gather_kernel, n, span),
        in_specs=[vmem] * 7,
        out_specs=[vmem, vmem, vmem],
        out_shape=[
            jax.ShapeDtypeStruct((2 * rows, width * n), prompt_part.dtype),
            jax.ShapeDtypeStruct((8, owner.shape[0]), jnp.int32),
            jax.ShapeDtypeStruct((index.shape[1] * heads, 1), jnp.int32),
        ],
        scratch_shapes=[
            pltpu.SemaphoreType.DMA((2, n)),
            pltpu.SemaphoreType.DMA((2, n)),
            pltpu.SemaphoreType.DMA((2,)),
        ],
        compiler_params=pltpu.CompilerParams(collective_id=0, has_side_effects=True),
    )(prompt_part, recompute_part, *small, index)


def mp_scatter_kernel(n, a_ref, w_ref, y_ref, buf, send_sem, recv_sem):
    me = lax.axis_index("mp")
    row = lax.axis_index("seq")
    width = y_ref.shape[2]
    barrier = pltpu.get_barrier_semaphore()
    for k in range(1, n):
        peer = lax.rem(me + k, n)
        pl.semaphore_signal(barrier, inc=1, device_id=(row, peer), device_id_type=MESH)
    pl.semaphore_wait(barrier, n - 1)

    def block(d):
        cols = pl.ds(pl.multiple_of(d * width, width), width)
        return jnp.dot(a_ref[...], w_ref[:, cols], preferred_element_type=jnp.float32).astype(
            y_ref.dtype
        )

    copies = []
    for k in range(1, n):
        peer = lax.rem(me + k, n)
        buf[k] = block(peer)
        c = pltpu.make_async_remote_copy(
            src_ref=buf.at[k],
            dst_ref=y_ref.at[me],
            send_sem=send_sem.at[k],
            recv_sem=recv_sem.at[k],
            device_id=(row, peer),
            device_id_type=MESH,
        )
        c.start()
        copies.append(c)
    y_ref[me] = block(me)
    for c in copies:
        c.wait()


def mp_scatter(attention, w_out, n):
    vmem = pl.BlockSpec(memory_space=pltpu.VMEM)
    rows = attention.shape[0]
    width = w_out.shape[1] // n
    return pl.pallas_call(
        functools.partial(mp_scatter_kernel, n),
        in_specs=[vmem, vmem],
        out_specs=vmem,
        out_shape=jax.ShapeDtypeStruct((n, rows, width), jnp.bfloat16),
        scratch_shapes=[
            pltpu.VMEM((n, rows, width), jnp.bfloat16),
            pltpu.SemaphoreType.DMA((n,)),
            pltpu.SemaphoreType.DMA((n,)),
        ],
        compiler_params=pltpu.CompilerParams(collective_id=1, has_side_effects=True),
    )(attention, w_out)


def relay_gather_kernel(nx, nz, x_ref, kc_ref, vc_ref, fresh_ref, meta_ref, rot_ref,
                        y_ref, pk_ref, pv_ref, *sems):
    (sx_send, sx_recv, zp_send, zp_recv, zm_send, zm_recv, own_sem,
     bp_send, bp_recv, bm_send, bm_recv, xp_send, xp_recv, xm_send, xm_recv,
     fp_send, fp_recv, fm_send, fm_recv) = sems
    me = lax.axis_index("seq")
    mp = lax.axis_index("mp")
    x = me // nz
    z = me % nz
    up = lax.rem(z + 1, nz)
    down = lax.rem(z + nz - 1, nz)
    right = lax.rem(x + 1, nx)
    left = lax.rem(x + nx - 1, nx)
    barrier = pltpu.get_barrier_semaphore()
    peers = [(lax.rem(x + k, nx) * nz + z, mp) for k in range(1, nx)]
    peers += [(x * nz + up, mp), (x * nz + down, mp)]
    for p in peers:
        pl.semaphore_signal(barrier, inc=1, device_id=p, device_id_type=MESH)
    pl.semaphore_wait(barrier, len(peers))

    def copy(src, dst, send_sem, recv_sem, device):
        c = pltpu.make_async_remote_copy(
            src_ref=src,
            dst_ref=dst,
            send_sem=send_sem,
            recv_sem=recv_sem,
            device_id=device,
            device_id_type=MESH,
        )
        c.start()
        return c

    sent = []
    slot = z * nx + x
    first = [
        copy(x_ref.at[0], y_ref.at[slot, 0], sx_send.at[k], sx_recv.at[k], peers[k - 1])
        for k in range(1, nx)
    ]
    own = pltpu.make_async_copy(x_ref, y_ref.at[slot], own_sem)
    own.start()

    width = kc_ref.shape[1]
    cached = kc_ref[...].astype(jnp.float32)
    turned = pltpu.roll(cached, width // 2, 1)
    shifted = (cached * rot_ref[0:1, :] + turned * rot_ref[1:2, :]).astype(pk_ref.dtype)
    token = lax.broadcasted_iota(jnp.int32, (kc_ref.shape[0], meta_ref.shape[1]), 0)
    chosen = (token == meta_ref[6:7, :]) & (meta_ref[3:4, :] > 0)
    placed = jnp.dot(
        chosen.astype(jnp.bfloat16), fresh_ref[...], preferred_element_type=jnp.float32
    ).astype(pk_ref.dtype)
    replaced = jnp.max(jnp.where(chosen, 1.0, 0.0), axis=1, keepdims=True) > 0.0
    pk_ref[...] = jnp.where(replaced, placed[:, :width], shifted)
    pv_ref[...] = jnp.where(replaced, placed[:, width:], vc_ref[...])

    def x_out(column):
        a = copy(
            y_ref.at[column * nx + x, 1], y_ref.at[column * nx + x, 1],
            xp_send.at[column], xp_recv.at[column], (right * nz + z, mp),
        )
        b = copy(
            y_ref.at[column * nx + x, 1], y_ref.at[column * nx + x, 1],
            xm_send.at[column], xm_recv.at[column], (left * nz + z, mp),
        )
        return [a, b]

    own.wait()
    steps = nz // 2
    half = nx // 2
    zlast = {}
    blast = {}
    xcopies = {}
    for c in first:
        c.wait()
    for t in range(1, steps + 1):
        for sign, send_sem, recv_sem, target, count in (
            (1, bp_send, bp_recv, up, steps),
            (-1, bm_send, bm_recv, down, nz - 1 - steps),
        ):
            if t > count:
                continue
            if t > 1:
                blast[sign].wait_recv()
            column = lax.rem(z - sign * (t - 1) + nz, nz)
            if t > 1:
                xcopies[(sign, t - 1)] = x_out(column)
            elif sign == 1:
                xcopies[(0, 0)] = x_out(column)
            blast[sign] = copy(
                y_ref.at[column * nx + x, 1], y_ref.at[column * nx + x, 1],
                send_sem.at[t], recv_sem.at[t], (x * nz + target, mp),
            )
            sent.append(blast[sign])
        for i in range(nx):
            for sign, send_sem, recv_sem, target in (
                (1, zp_send, zp_recv, up),
                (-1, zm_send, zm_recv, down),
            ):
                if t == steps and (i < half) != (sign == 1):
                    continue
                if t > 1:
                    zlast[(sign, i)].wait_recv()
                column = lax.rem(z - sign * (t - 1) + nz, nz)
                zlast[(sign, i)] = copy(
                    y_ref.at[column * nx + i, 0], y_ref.at[column * nx + i, 0],
                    send_sem.at[t, i], recv_sem.at[t, i], (x * nz + target, mp),
                )
                sent.append(zlast[(sign, i)])
    for sign, count in ((1, steps), (-1, nz - 1 - steps)):
        blast[sign].wait_recv()
        column = lax.rem(z - sign * count + nz, nz)
        xcopies[(sign, count)] = x_out(column)
    order = [(0, 0)] + [(s, t) for t in range(1, steps + 1) for s in (1, -1) if (s, t) in xcopies]
    forwards = []
    for key in order:
        sign, t = key
        column = lax.rem(z - sign * t + nz, nz)
        from_left, from_right = xcopies[key]
        from_left.wait_recv()
        from_right.wait_recv()
        sent += xcopies[key]
    for zc in range(nz):
        if zc < nz // 2:
            forwards.append(
                copy(
                    y_ref.at[zc * nx + left, 1], y_ref.at[zc * nx + left, 1],
                    fp_send.at[zc], fp_recv.at[zc], (right * nz + z, mp),
                )
            )
        else:
            forwards.append(
                copy(
                    y_ref.at[zc * nx + right, 1], y_ref.at[zc * nx + right, 1],
                    fm_send.at[zc], fm_recv.at[zc], (left * nz + z, mp),
                )
            )
    for c in zlast.values():
        c.wait_recv()
    for c in forwards:
        c.wait_recv()
    for c in sent:
        c.wait_send()
    for c in forwards:
        c.wait_send()


def relay_gather(x, kc, vc, fresh, meta, rot, nx, nz):
    assert nx == 4 and nz % 2 == 0
    vmem = pl.BlockSpec(memory_space=pltpu.VMEM)
    steps = nz // 2
    dma = pltpu.SemaphoreType.DMA
    return pl.pallas_call(
        functools.partial(relay_gather_kernel, nx, nz),
        in_specs=[vmem] * 6,
        out_specs=[vmem, vmem, vmem],
        out_shape=[
            jax.ShapeDtypeStruct((nx * nz,) + x.shape, x.dtype),
            jax.ShapeDtypeStruct(kc.shape, kc.dtype),
            jax.ShapeDtypeStruct(vc.shape, vc.dtype),
        ],
        scratch_shapes=[
            dma((nx,)), dma((nx,)),
            dma((steps + 1, nx)), dma((steps + 1, nx)), dma((steps + 1, nx)), dma((steps + 1, nx)),
            dma(()),
            dma((steps + 1,)), dma((steps + 1,)), dma((steps + 1,)), dma((steps + 1,)),
            dma((nz,)), dma((nz,)), dma((nz,)), dma((nz,)),
            dma((nz,)), dma((nz,)), dma((nz,)), dma((nz,)),
        ],
        compiler_params=pltpu.CompilerParams(collective_id=2, has_side_effects=True),
    )(x, kc, vc, fresh, meta, rot)


def merge_piece(a, b, rows):
    af = a.astype(jnp.float32)
    bf = b.astype(jnp.float32)
    m1 = af[rows : rows + 1] + af[rows + 1 : rows + 2]
    l1 = af[rows + 2 : rows + 3] + af[rows + 3 : rows + 4]
    m2 = bf[rows : rows + 1] + bf[rows + 1 : rows + 2]
    l2 = bf[rows + 2 : rows + 3] + bf[rows + 3 : rows + 4]
    top = jnp.maximum(m1, m2)
    s1 = jnp.exp(m1 - top)
    s2 = jnp.exp(m2 - top)
    total = l1 * s1 + l2 * s2
    c1 = jnp.transpose(jnp.broadcast_to(s1, (rows, rows)))
    c2 = jnp.transpose(jnp.broadcast_to(s2, (rows, rows)))
    acc = af[0:rows] * c1 + bf[0:rows] * c2
    sub = lax.broadcasted_iota(jnp.int32, (16, rows), 0)
    top_hi = top.astype(jnp.bfloat16).astype(jnp.float32)
    tot_hi = total.astype(jnp.bfloat16).astype(jnp.float32)
    st = jnp.where(
        sub == 0,
        top,
        jnp.where(
            sub == 1, top - top_hi, jnp.where(sub == 2, total, jnp.where(sub == 3, total - tot_hi, 0.0))
        ),
    )
    return acc.astype(jnp.bfloat16), st.astype(jnp.bfloat16)


def relay_reduce_kernel(
    nx, nz, x_ref, y_ref, rp, rm, bp, bm, col, sp_send, sp_recv, sm_send, sm_recv, sx_send, sx_recv
):
    me = lax.axis_index("seq")
    mp = lax.axis_index("mp")
    x = me // nz
    z = me % nz
    up = lax.rem(z + 1, nz)
    down = lax.rem(z + nz - 1, nz)
    rows = x_ref.shape[2] - 16
    barrier = pltpu.get_barrier_semaphore()
    peers = [(lax.rem(x + k, nx) * nz + z, mp) for k in range(1, nx)]
    peers += [(x * nz + up, mp), (x * nz + down, mp)]
    for p in peers:
        pl.semaphore_signal(barrier, inc=1, device_id=p, device_id_type=MESH)
    pl.semaphore_wait(barrier, len(peers))

    def merge_into(dst, first, second):
        for h in range(2):
            acc, st = merge_piece(first[h], second[h], rows)
            dst[h, 0:rows] = acc
            dst[h, rows:] = st

    steps = nz // 2
    half = nx // 2
    last = {}
    sent = []
    dirs = ((1, rp, bp, sp_send, sp_recv, up), (-1, rm, bm, sm_send, sm_recv, down))
    for t in range(1, steps + 1):
        for i in range(nx):
            for sign, recv_buf, send_buf, send_sem, recv_sem, target in dirs:
                if t == 1 and (i < half) != (sign == 1):
                    continue
                column = lax.rem(z + sign * (steps + 1 - t) + nz, nz)
                own = x_ref.at[i * nz + column]
                if (sign, i) in last:
                    last[(sign, i)].wait_recv()
                    merge_into(send_buf.at[t, i], own, recv_buf.at[t - 1, i])
                    src = send_buf.at[t, i]
                else:
                    src = own
                c = pltpu.make_async_remote_copy(
                    src_ref=src,
                    dst_ref=recv_buf.at[t, i],
                    send_sem=send_sem.at[t, i],
                    recv_sem=recv_sem.at[t, i],
                    device_id=(x * nz + target, mp),
                    device_id_type=MESH,
                )
                c.start()
                last[(sign, i)] = c
                sent.append(c)

    mine = []
    for i in range(nx):
        last[(1, i)].wait_recv()
        last[(-1, i)].wait_recv()
        merge_into(col.at[i], x_ref.at[i * nz + z], rp.at[steps, i])
        merge_into(col.at[i], col.at[i], rm.at[steps, i])
    for k in range(1, nx):
        target = lax.rem(x + k, nx)
        c = pltpu.make_async_remote_copy(
            src_ref=col.at[target],
            dst_ref=y_ref.at[x],
            send_sem=sx_send.at[k],
            recv_sem=sx_recv.at[k],
            device_id=(target * nz + z, mp),
            device_id_type=MESH,
        )
        c.start()
        mine.append(c)
    y_ref[x] = col[x]
    for c in sent:
        c.wait_send()
    for c in mine:
        c.wait()


def relay_reduce(parts, nx, nz):
    vmem = pl.BlockSpec(memory_space=pltpu.VMEM)
    steps = nz // 2
    piece = parts.shape[1:]
    return pl.pallas_call(
        functools.partial(relay_reduce_kernel, nx, nz),
        in_specs=[vmem],
        out_specs=vmem,
        out_shape=jax.ShapeDtypeStruct((nx,) + piece, parts.dtype),
        scratch_shapes=[
            pltpu.VMEM((steps + 1, nx) + piece, parts.dtype),
            pltpu.VMEM((steps + 1, nx) + piece, parts.dtype),
            pltpu.VMEM((steps + 1, nx) + piece, parts.dtype),
            pltpu.VMEM((steps + 1, nx) + piece, parts.dtype),
            pltpu.VMEM((nx,) + piece, parts.dtype),
            pltpu.SemaphoreType.DMA((steps + 1, nx)),
            pltpu.SemaphoreType.DMA((steps + 1, nx)),
            pltpu.SemaphoreType.DMA((steps + 1, nx)),
            pltpu.SemaphoreType.DMA((steps + 1, nx)),
            pltpu.SemaphoreType.DMA((nx,)),
            pltpu.SemaphoreType.DMA((nx,)),
        ],
        compiler_params=pltpu.CompilerParams(collective_id=3, has_side_effects=True),
    )(parts)


def local(
    prompt_hidden,
    recompute_hidden,
    key_cache,
    value_cache,
    norm_gain,
    w_query,
    key_weight,
    value_weight,
    w_out,
    passage_owner,
    prompt_slot,
    prompt_length,
    recompute_count,
    recompute_index,
):
    prompt_rows = prompt_hidden.shape[0]
    recompute_rows = recompute_hidden.shape[0]
    query_rows = prompt_rows + recompute_rows
    passage_length = key_cache.shape[1]
    local_heads = w_query.shape[1] // HEAD_SIZE
    n_seq = passage_owner.shape[0]
    me = lax.axis_index("seq")
    scale = 1.0 / math.sqrt(HEAD_SIZE)

    n_mp = w_out.shape[1] // prompt_hidden.shape[1]
    full_rows, meta, lim = mp_gather(
        prompt_hidden, recompute_hidden, passage_owner, prompt_slot, prompt_length,
        recompute_count, recompute_index, n_mp, passage_length, local_heads,
    )
    own_pos = jnp.concatenate([meta[0], meta[1]])
    own_live = jnp.concatenate([meta[2], meta[3]]) > 0
    own_index = meta[6]
    own_shift = meta[7, 0]
    prompt_live = meta[2] > 0
    recompute_live = meta[3] > 0
    normalized_hidden = normalize(full_rows, norm_gain)
    queries = (
        apply_rotation(
            jnp.dot(normalized_hidden, w_query, preferred_element_type=jnp.float32).reshape(
                query_rows, local_heads, HEAD_SIZE
            ),
            own_pos,
        )
        .astype(jnp.bfloat16)
    )
    fresh_keys = (
        apply_rotation(
            jnp.dot(normalized_hidden, key_weight, preferred_element_type=jnp.float32).reshape(
                query_rows, 1, HEAD_SIZE
            ),
            own_pos,
        )
        .astype(jnp.bfloat16)
        .reshape(query_rows, HEAD_SIZE)
    )
    fresh_values = jnp.dot(
        normalized_hidden, value_weight, preferred_element_type=jnp.float32
    ).astype(jnp.bfloat16)

    half_width = HEAD_SIZE // 2
    exponent = jnp.arange(half_width).astype(jnp.float32) * (2.0 / HEAD_SIZE)
    frequency = jnp.exp(-exponent * math.log(500000.0))
    angle = own_shift.astype(jnp.float32) * frequency
    rot = jnp.stack(
        [
            jnp.concatenate([jnp.cos(angle), jnp.cos(angle)]),
            jnp.concatenate([-jnp.sin(angle), jnp.sin(angle)]),
        ]
    )
    fresh_pair = jnp.concatenate([fresh_keys[prompt_rows:], fresh_values[prompt_rows:]], axis=1)

    nx, nz = SEQ_SHAPE
    all_queries, passage_keys, passage_values = relay_gather(
        queries.reshape(2, prompt_rows * local_heads, HEAD_SIZE),
        key_cache[0],
        value_cache[0],
        fresh_pair,
        meta,
        rot,
        nx,
        nz,
    )
    q_blocks = all_queries.reshape(n_seq * 2, prompt_rows * local_heads, HEAD_SIZE)
    packed = passage_attention(nx, nz, meta, q_blocks, passage_keys, passage_values, lim)
    block_rows = packed.shape[1]

    back = relay_reduce(packed.reshape(n_seq, 2, block_rows, HEAD_SIZE), nx, nz)
    n_parts = back.shape[0]
    rows128 = prompt_rows * local_heads
    stats_back = back[:, :, rows128 : rows128 + 4].astype(jnp.float32)
    part_max = (stats_back[:, :, 0] + stats_back[:, :, 1]).reshape(n_parts, query_rows, local_heads)
    part_tot = (stats_back[:, :, 2] + stats_back[:, :, 3]).reshape(n_parts, query_rows, local_heads)
    part_acc = (
        back[:, :, :rows128].reshape(n_parts, query_rows, local_heads, HEAD_SIZE).astype(jnp.float32)
    )

    pq = queries[:prompt_rows].astype(jnp.float32)
    pk = fresh_keys[:prompt_rows].astype(jnp.float32)
    pv = fresh_values[:prompt_rows].astype(jnp.float32)
    ps = jnp.einsum("qhd,kd->qhk", pq, pk) * scale
    jj = jnp.arange(prompt_rows, dtype=jnp.int32)
    pvis = (jj[None, :] <= jj[:, None]) & prompt_live[None, :]
    ps = jnp.where(pvis[:, None, :], ps, NEGATIVE_FLOOR)
    pmax = jnp.max(ps, axis=-1)
    pw = jnp.where(pvis[:, None, :], jnp.exp(ps - pmax[..., None]), 0.0)
    ptot = jnp.sum(pw, axis=-1)
    pacc = jnp.einsum("qhk,kd->qhd", pw.astype(jnp.bfloat16).astype(jnp.float32), pv)
    loc_max = jnp.concatenate(
        [pmax, jnp.full((recompute_rows, local_heads), NEGATIVE_FLOOR, jnp.float32)]
    )
    loc_tot = jnp.concatenate([ptot, jnp.zeros((recompute_rows, local_heads), jnp.float32)])
    loc_acc = jnp.concatenate(
        [pacc, jnp.zeros((recompute_rows, local_heads, HEAD_SIZE), jnp.float32)]
    )

    highest = jnp.maximum(jnp.max(part_max, axis=0), loc_max)
    part_scale = jnp.exp(part_max - highest[None])
    loc_scale = jnp.exp(loc_max - highest)
    accumulated = jnp.sum(part_acc * part_scale[..., None], axis=0) + loc_acc * loc_scale[..., None]
    totals = jnp.sum(part_tot * part_scale, axis=0) + loc_tot * loc_scale
    safe_totals = jnp.where(totals > 0, totals, 1.0)
    attention = jnp.where(
        own_live[:, None, None], accumulated / safe_totals[..., None], 0.0
    ).astype(jnp.bfloat16).reshape(query_rows, local_heads * HEAD_SIZE)
    shares = mp_scatter(attention, w_out, n_mp)
    combined = jnp.sum(shares.astype(jnp.float32), axis=0).astype(jnp.bfloat16)
    return (combined[:prompt_rows], combined[prompt_rows:])


def solution(mesh):
    global SEQ_SHAPE
    sizes = dict(zip(mesh.axis_names, mesh.devices.shape))
    seq_devices = mesh.devices.reshape(sizes["seq"], sizes["mp"])[:, 0]
    xs = sorted({d.coords[0] for d in seq_devices})
    SEQ_SHAPE = (len(xs), sizes["seq"] // len(xs))
    return jax.shard_map(
        local,
        mesh=mesh,
        in_specs=(
            P("seq", "mp"),
            P("seq", "mp"),
            P("seq", None, "mp"),
            P("seq", None, "mp"),
            P(),
            P(None, "mp"),
            P(None, "mp"),
            P(None, "mp"),
            P("mp", None),
            P(),
            P(),
            P(),
            P(),
            P(),
        ),
        out_specs=(P("seq", "mp"), P("seq", "mp")),
        check_vma=False,
    )
```

```python
import functools
import math

import jax
import jax.numpy as jnp
from jax import lax
from jax.experimental import pallas as pl
from jax.experimental.pallas import tpu as pltpu
from jax.sharding import PartitionSpec as P

HEAD_SIZE = 128
NEGATIVE_FLOOR = -1e30


def apply_rotation(vectors, positions):
    half_width = vectors.shape[-1] // 2
    exponent = jnp.arange(half_width).astype(jnp.float32) * (2.0 / vectors.shape[-1])
    frequency = jnp.exp(-exponent * math.log(500000.0))
    angles = positions.astype(jnp.float32)[:, None] * frequency[None, :]
    cosines = jnp.cos(angles)[:, None, :]
    sines = jnp.sin(angles)[:, None, :]
    leading = vectors[..., :half_width]
    trailing = vectors[..., half_width:]
    return jnp.concatenate(
        [leading * cosines - trailing * sines, trailing * cosines + leading * sines], axis=-1
    )


def normalize(rows_in, norm_gain):
    values = rows_in.astype(jnp.float32)
    inverse_rms = lax.rsqrt(jnp.mean(values * values, axis=-1, keepdims=True) + 1e-05)
    return (values * inverse_rms * norm_gain).astype(jnp.bfloat16)


MESH = pl.DeviceIdType.MESH


def passage_kernel(nx, nz, flags_ref, q_ref, k_ref, v_ref, lim_ref, out_ref):
    nb, rows, _ = q_ref.shape
    keys = k_ref.shape[0]
    token = lax.broadcasted_iota(jnp.int32, (rows, keys), 1)
    sub = lax.broadcasted_iota(jnp.int32, (16, rows), 0)

    def split(m_row, l_row):
        m_hi = m_row.astype(jnp.bfloat16).astype(jnp.float32)
        l_hi = l_row.astype(jnp.bfloat16).astype(jnp.float32)
        st = jnp.where(
            sub == 0,
            m_row,
            jnp.where(
                sub == 1,
                m_row - m_hi,
                jnp.where(sub == 2, l_row, jnp.where(sub == 3, l_row - l_hi, 0.0)),
            ),
        )
        return st.astype(jnp.bfloat16)

    out_ref[:, 0:rows] = jnp.zeros((nb, rows, HEAD_SIZE), out_ref.dtype)
    floor = jnp.full((16, rows), NEGATIVE_FLOOR, jnp.float32)
    empty = split(floor, jnp.zeros((16, rows), jnp.float32))
    out_ref[:, rows:] = jnp.broadcast_to(empty[None], (nb, 16, rows))

    def attend(b, masked):
        d = b // 2
        stored = ((d % nz) * nx + d // nz) * 2 + b % 2
        scores = lax.dot_general(
            q_ref[stored], k_ref[...], (((1,), (1,)), ((), ())), preferred_element_type=jnp.float32
        ) * (1.0 / math.sqrt(HEAD_SIZE))
        if masked:
            scores = jnp.where(token <= lim_ref[...], scores, NEGATIVE_FLOOR)
        maxima = jnp.max(scores, axis=1, keepdims=True)
        weights = jnp.exp(scores - maxima)
        totals = jnp.sum(weights, axis=1, keepdims=True)
        out_ref[b, 0:rows] = jnp.dot(
            weights.astype(jnp.bfloat16), v_ref[...], preferred_element_type=jnp.float32
        ).astype(out_ref.dtype)
        m_row = jnp.transpose(jnp.broadcast_to(maxima, (rows, rows)))[0:16]
        l_row = jnp.transpose(jnp.broadcast_to(totals, (rows, rows)))[0:16]
        out_ref[b, rows:] = split(m_row, l_row)

    def body(b, carry):
        flag = flags_ref[4 + b % 2, b // 2]

        @pl.when(flag == 1)
        def _():
            attend(b, False)

        @pl.when(flag == 2)
        def _():
            attend(b, True)

        return carry

    lax.fori_loop(0, nb, body, 0)


def passage_attention(nx, nz, flags, q_blocks, keys, values, lim):
    nb, rows, _ = q_blocks.shape
    vmem = pl.BlockSpec(memory_space=pltpu.VMEM)
    return pl.pallas_call(
        functools.partial(passage_kernel, nx, nz),
        in_specs=[pl.BlockSpec(memory_space=pltpu.SMEM), vmem, vmem, vmem, vmem],
        out_specs=vmem,
        out_shape=jax.ShapeDtypeStruct((nb, rows + 16, HEAD_SIZE), jnp.bfloat16),
    )(flags, q_blocks, keys, values, lim)


def mp_gather_kernel(n, span, p_ref, r_ref, owner_ref, slot_ref, plen_ref, count_ref, index_ref,
                     y_ref, meta_ref, lim_ref, send_sem, recv_sem, local_sem):
    me = lax.axis_index("mp")
    row = lax.axis_index("seq")
    rows, width = p_ref.shape
    barrier = pltpu.get_barrier_semaphore()
    for k in range(1, n):
        peer = lax.rem(me + k, n)
        pl.semaphore_signal(barrier, inc=1, device_id=(row, peer), device_id_type=MESH)
    pl.semaphore_wait(barrier, n - 1)
    cols = pl.ds(pl.multiple_of(me * width, width), width)
    copies = []
    for k in range(1, n):
        peer = lax.rem(me + k, n)
        for part, src in enumerate((p_ref, r_ref)):
            c = pltpu.make_async_remote_copy(
                src_ref=src,
                dst_ref=y_ref.at[pl.ds(part * rows, rows), cols],
                send_sem=send_sem.at[part, k],
                recv_sem=recv_sem.at[part, k],
                device_id=(row, peer),
                device_id_type=MESH,
            )
            c.start()
            copies.append(c)
    own = [
        pltpu.make_async_copy(src, y_ref.at[pl.ds(part * rows, rows), cols], local_sem.at[part])
        for part, src in enumerate((p_ref, r_ref))
    ]
    for c in own:
        c.start()

    f32 = jnp.float32
    owner = owner_ref[...].astype(f32)
    slot = slot_ref[...].astype(f32)
    lane = lax.broadcasted_iota(jnp.int32, owner.shape, 1)
    mine = lane == row

    def pick(v):
        return jnp.sum(jnp.where(mine, v, 0.0), axis=1, keepdims=True)

    own_owner = pick(owner)
    own_slot = pick(slot)
    rank = jnp.sum(jnp.where((owner == own_owner) & (lane < row), 1.0, 0.0), axis=1, keepdims=True)
    held = jnp.sum(jnp.where(owner == own_slot, 1.0, 0.0), axis=1, keepdims=True)
    length = pick(plen_ref[...].astype(f32))
    count = pick(count_ref[...].astype(f32))
    index = index_ref[pl.ds(row, 1), :].astype(f32)
    lanef = lane.astype(f32)
    quantities = [
        held * span + lanef,
        rank * span + index,
        jnp.where(lanef < length, 1.0, 0.0),
        jnp.where(lanef < count, 1.0, 0.0),
        jnp.where(slot == own_owner, 1.0, 0.0),
        jnp.where(mine, 2.0, jnp.where((owner == own_owner) & (lane > row), 1.0, 0.0)),
        index,
        rank * span + 0.0 * lanef,
    ]
    for q, value in enumerate(quantities):
        meta_ref[q : q + 1, :] = value.astype(jnp.int32)
    heads = lim_ref.shape[0] // index.shape[1]
    wide = jnp.broadcast_to(index, (lim_ref.shape[0], index.shape[1]))
    which = lax.broadcasted_iota(jnp.int32, wide.shape, 0) // heads
    pick_lane = lax.broadcasted_iota(jnp.int32, wide.shape, 1)
    lim_ref[...] = jnp.sum(jnp.where(which == pick_lane, wide, 0.0), axis=1, keepdims=True).astype(jnp.int32)

    for c in copies:
        c.wait()
    for c in own:
        c.wait()


def mp_gather(prompt_part, recompute_part, owner, slot, plen, count, index, n, span, heads):
    vmem = pl.BlockSpec(memory_space=pltpu.VMEM)
    rows, width = prompt_part.shape
    small = [v.reshape(1, -1) for v in (owner, slot, plen, count)]
    return pl.pallas_call(
        functools.partial(mp_gather_kernel, n, span),
        in_specs=[vmem] * 7,
        out_specs=[vmem, vmem, vmem],
        out_shape=[
            jax.ShapeDtypeStruct((2 * rows, width * n), prompt_part.dtype),
            jax.ShapeDtypeStruct((8, owner.shape[0]), jnp.int32),
            jax.ShapeDtypeStruct((index.shape[1] * heads, 1), jnp.int32),
        ],
        scratch_shapes=[
            pltpu.SemaphoreType.DMA((2, n)),
            pltpu.SemaphoreType.DMA((2, n)),
            pltpu.SemaphoreType.DMA((2,)),
        ],
        compiler_params=pltpu.CompilerParams(collective_id=0, has_side_effects=True),
    )(prompt_part, recompute_part, *small, index)


def mp_scatter_kernel(n, a_ref, w_ref, p_ref, r_ref, y_ref, buf, send_sem, recv_sem):
    me = lax.axis_index("mp")
    row = lax.axis_index("seq")
    width = y_ref.shape[2]
    barrier = pltpu.get_barrier_semaphore()
    for k in range(1, n):
        peer = lax.rem(me + k, n)
        pl.semaphore_signal(barrier, inc=1, device_id=(row, peer), device_id_type=MESH)
    pl.semaphore_wait(barrier, n - 1)

    def block(d):
        cols = pl.ds(pl.multiple_of(d * width, width), width)
        return jnp.dot(a_ref[...], w_ref[:, cols], preferred_element_type=jnp.float32).astype(
            y_ref.dtype
        )

    copies = []
    for k in range(1, n):
        peer = lax.rem(me + k, n)
        buf[k] = block(peer)
        c = pltpu.make_async_remote_copy(
            src_ref=buf.at[k],
            dst_ref=y_ref.at[me],
            send_sem=send_sem.at[k],
            recv_sem=recv_sem.at[k],
            device_id=(row, peer),
            device_id_type=MESH,
        )
        c.start()
        copies.append(c)
    y_ref[me] = block(me)
    for c in copies:
        c.wait()
    total = y_ref[0].astype(jnp.float32)
    for k in range(1, n):
        total = total + y_ref[k].astype(jnp.float32)
    rows = p_ref.shape[0]
    p_ref[...] = total[:rows].astype(p_ref.dtype)
    r_ref[...] = total[rows:].astype(r_ref.dtype)


def mp_scatter(attention, w_out, n, split):
    vmem = pl.BlockSpec(memory_space=pltpu.VMEM)
    rows = attention.shape[0]
    width = w_out.shape[1] // n
    return pl.pallas_call(
        functools.partial(mp_scatter_kernel, n),
        in_specs=[vmem, vmem],
        out_specs=[vmem, vmem],
        out_shape=[
            jax.ShapeDtypeStruct((split, width), jnp.bfloat16),
            jax.ShapeDtypeStruct((rows - split, width), jnp.bfloat16),
        ],
        scratch_shapes=[
            pltpu.VMEM((n, rows, width), jnp.bfloat16),
            pltpu.VMEM((n, rows, width), jnp.bfloat16),
            pltpu.SemaphoreType.DMA((n,)),
            pltpu.SemaphoreType.DMA((n,)),
        ],
        compiler_params=pltpu.CompilerParams(collective_id=1, has_side_effects=True),
    )(attention, w_out)


def relay_gather_kernel(nx, nz, x_ref, kc_ref, vc_ref, fresh_ref, meta_ref, rot_ref,
                        y_ref, pk_ref, pv_ref, *sems):
    (sx_send, sx_recv, zp_send, zp_recv, zm_send, zm_recv, own_sem,
     bp_send, bp_recv, bm_send, bm_recv, xp_send, xp_recv, xm_send, xm_recv,
     fp_send, fp_recv, fm_send, fm_recv) = sems
    me = lax.axis_index("seq")
    mp = lax.axis_index("mp")
    x = me // nz
    z = me % nz
    up = lax.rem(z + 1, nz)
    down = lax.rem(z + nz - 1, nz)
    right = lax.rem(x + 1, nx)
    left = lax.rem(x + nx - 1, nx)
    barrier = pltpu.get_barrier_semaphore()
    peers = [(lax.rem(x + k, nx) * nz + z, mp) for k in range(1, nx)]
    peers += [(x * nz + up, mp), (x * nz + down, mp)]
    for p in peers:
        pl.semaphore_signal(barrier, inc=1, device_id=p, device_id_type=MESH)
    pl.semaphore_wait(barrier, len(peers))

    def copy(src, dst, send_sem, recv_sem, device):
        c = pltpu.make_async_remote_copy(
            src_ref=src,
            dst_ref=dst,
            send_sem=send_sem,
            recv_sem=recv_sem,
            device_id=device,
            device_id_type=MESH,
        )
        c.start()
        return c

    sent = []
    slot = z * nx + x
    first = [
        copy(x_ref.at[0], y_ref.at[slot, 0], sx_send.at[k], sx_recv.at[k], peers[k - 1])
        for k in range(1, nx)
    ]
    own = pltpu.make_async_copy(x_ref, y_ref.at[slot], own_sem)
    own.start()

    width = kc_ref.shape[1]
    cached = kc_ref[...].astype(jnp.float32)
    turned = pltpu.roll(cached, width // 2, 1)
    shifted = (cached * rot_ref[0:1, :] + turned * rot_ref[1:2, :]).astype(pk_ref.dtype)
    token = lax.broadcasted_iota(jnp.int32, (kc_ref.shape[0], meta_ref.shape[1]), 0)
    chosen = (token == meta_ref[6:7, :]) & (meta_ref[3:4, :] > 0)
    placed = jnp.dot(
        chosen.astype(jnp.bfloat16), fresh_ref[...], preferred_element_type=jnp.float32
    ).astype(pk_ref.dtype)
    replaced = jnp.max(jnp.where(chosen, 1.0, 0.0), axis=1, keepdims=True) > 0.0
    pk_ref[...] = jnp.where(replaced, placed[:, :width], shifted)
    pv_ref[...] = jnp.where(replaced, placed[:, width:], vc_ref[...])

    def x_out(column):
        a = copy(
            y_ref.at[column * nx + x, 1], y_ref.at[column * nx + x, 1],
            xp_send.at[column], xp_recv.at[column], (right * nz + z, mp),
        )
        b = copy(
            y_ref.at[column * nx + x, 1], y_ref.at[column * nx + x, 1],
            xm_send.at[column], xm_recv.at[column], (left * nz + z, mp),
        )
        return [a, b]

    own.wait()
    steps = nz // 2
    half = nx // 2
    zlast = {}
    blast = {}
    xcopies = {}
    for c in first:
        c.wait()
    for t in range(1, steps + 1):
        for sign, send_sem, recv_sem, target, count in (
            (1, bp_send, bp_recv, up, steps),
            (-1, bm_send, bm_recv, down, nz - 1 - steps),
        ):
            if t > count:
                continue
            if t > 1:
                blast[sign].wait_recv()
            column = lax.rem(z - sign * (t - 1) + nz, nz)
            if t > 1:
                xcopies[(sign, t - 1)] = x_out(column)
            elif sign == 1:
                xcopies[(0, 0)] = x_out(column)
            blast[sign] = copy(
                y_ref.at[column * nx + x, 1], y_ref.at[column * nx + x, 1],
                send_sem.at[t], recv_sem.at[t], (x * nz + target, mp),
            )
            sent.append(blast[sign])
        for i in range(nx):
            for sign, send_sem, recv_sem, target in (
                (1, zp_send, zp_recv, up),
                (-1, zm_send, zm_recv, down),
            ):
                if t == steps and (i < half) != (sign == 1):
                    continue
                if t > 1:
                    zlast[(sign, i)].wait_recv()
                column = lax.rem(z - sign * (t - 1) + nz, nz)
                zlast[(sign, i)] = copy(
                    y_ref.at[column * nx + i, 0], y_ref.at[column * nx + i, 0],
                    send_sem.at[t, i], recv_sem.at[t, i], (x * nz + target, mp),
                )
                sent.append(zlast[(sign, i)])
    for sign, count in ((1, steps), (-1, nz - 1 - steps)):
        blast[sign].wait_recv()
        column = lax.rem(z - sign * count + nz, nz)
        xcopies[(sign, count)] = x_out(column)
    order = [(0, 0)] + [(s, t) for t in range(1, steps + 1) for s in (1, -1) if (s, t) in xcopies]
    forwards = []
    for key in order:
        sign, t = key
        column = lax.rem(z - sign * t + nz, nz)
        from_left, from_right = xcopies[key]
        from_left.wait_recv()
        from_right.wait_recv()
        sent += xcopies[key]
    for zc in range(nz):
        if zc < nz // 2:
            forwards.append(
                copy(
                    y_ref.at[zc * nx + left, 1], y_ref.at[zc * nx + left, 1],
                    fp_send.at[zc], fp_recv.at[zc], (right * nz + z, mp),
                )
            )
        else:
            forwards.append(
                copy(
                    y_ref.at[zc * nx + right, 1], y_ref.at[zc * nx + right, 1],
                    fm_send.at[zc], fm_recv.at[zc], (left * nz + z, mp),
                )
            )
    for c in zlast.values():
        c.wait_recv()
    for c in forwards:
        c.wait_recv()
    for c in sent:
        c.wait_send()
    for c in forwards:
        c.wait_send()


def relay_gather(x, kc, vc, fresh, meta, rot, nx, nz):
    assert nx == 4 and nz % 2 == 0
    vmem = pl.BlockSpec(memory_space=pltpu.VMEM)
    steps = nz // 2
    dma = pltpu.SemaphoreType.DMA
    return pl.pallas_call(
        functools.partial(relay_gather_kernel, nx, nz),
        in_specs=[vmem] * 6,
        out_specs=[vmem, vmem, vmem],
        out_shape=[
            jax.ShapeDtypeStruct((nx * nz,) + x.shape, x.dtype),
            jax.ShapeDtypeStruct(kc.shape, kc.dtype),
            jax.ShapeDtypeStruct(vc.shape, vc.dtype),
        ],
        scratch_shapes=[
            dma((nx,)), dma((nx,)),
            dma((steps + 1, nx)), dma((steps + 1, nx)), dma((steps + 1, nx)), dma((steps + 1, nx)),
            dma(()),
            dma((steps + 1,)), dma((steps + 1,)), dma((steps + 1,)), dma((steps + 1,)),
            dma((nz,)), dma((nz,)), dma((nz,)), dma((nz,)),
            dma((nz,)), dma((nz,)), dma((nz,)), dma((nz,)),
        ],
        compiler_params=pltpu.CompilerParams(collective_id=2, has_side_effects=True),
    )(x, kc, vc, fresh, meta, rot)


def merge_piece(a, b, rows):
    af = a.astype(jnp.float32)
    bf = b.astype(jnp.float32)
    m1 = af[rows : rows + 1] + af[rows + 1 : rows + 2]
    l1 = af[rows + 2 : rows + 3] + af[rows + 3 : rows + 4]
    m2 = bf[rows : rows + 1] + bf[rows + 1 : rows + 2]
    l2 = bf[rows + 2 : rows + 3] + bf[rows + 3 : rows + 4]
    top = jnp.maximum(m1, m2)
    s1 = jnp.exp(m1 - top)
    s2 = jnp.exp(m2 - top)
    total = l1 * s1 + l2 * s2
    c1 = jnp.transpose(jnp.broadcast_to(s1, (rows, rows)))
    c2 = jnp.transpose(jnp.broadcast_to(s2, (rows, rows)))
    acc = af[0:rows] * c1 + bf[0:rows] * c2
    sub = lax.broadcasted_iota(jnp.int32, (16, rows), 0)
    top_hi = top.astype(jnp.bfloat16).astype(jnp.float32)
    tot_hi = total.astype(jnp.bfloat16).astype(jnp.float32)
    st = jnp.where(
        sub == 0,
        top,
        jnp.where(
            sub == 1, top - top_hi, jnp.where(sub == 2, total, jnp.where(sub == 3, total - tot_hi, 0.0))
        ),
    )
    return acc.astype(jnp.bfloat16), st.astype(jnp.bfloat16)


def relay_reduce_kernel(
    nx, nz, x_ref, y_ref, rp, rm, bp, bm, col, sp_send, sp_recv, sm_send, sm_recv, sx_send, sx_recv
):
    me = lax.axis_index("seq")
    mp = lax.axis_index("mp")
    x = me // nz
    z = me % nz
    up = lax.rem(z + 1, nz)
    down = lax.rem(z + nz - 1, nz)
    rows = x_ref.shape[2] - 16
    barrier = pltpu.get_barrier_semaphore()
    peers = [(lax.rem(x + k, nx) * nz + z, mp) for k in range(1, nx)]
    peers += [(x * nz + up, mp), (x * nz + down, mp)]
    for p in peers:
        pl.semaphore_signal(barrier, inc=1, device_id=p, device_id_type=MESH)
    pl.semaphore_wait(barrier, len(peers))

    def merge_into(dst, first, second):
        for h in range(2):
            acc, st = merge_piece(first[h], second[h], rows)
            dst[h, 0:rows] = acc
            dst[h, rows:] = st

    steps = nz // 2
    half = nx // 2
    last = {}
    sent = []
    dirs = ((1, rp, bp, sp_send, sp_recv, up), (-1, rm, bm, sm_send, sm_recv, down))
    for t in range(1, steps + 1):
        for i in range(nx):
            for sign, recv_buf, send_buf, send_sem, recv_sem, target in dirs:
                if t == 1 and (i < half) != (sign == 1):
                    continue
                column = lax.rem(z + sign * (steps + 1 - t) + nz, nz)
                own = x_ref.at[i * nz + column]
                if (sign, i) in last:
                    last[(sign, i)].wait_recv()
                    merge_into(send_buf.at[t, i], own, recv_buf.at[t - 1, i])
                    src = send_buf.at[t, i]
                else:
                    src = own
                c = pltpu.make_async_remote_copy(
                    src_ref=src,
                    dst_ref=recv_buf.at[t, i],
                    send_sem=send_sem.at[t, i],
                    recv_sem=recv_sem.at[t, i],
                    device_id=(x * nz + target, mp),
                    device_id_type=MESH,
                )
                c.start()
                last[(sign, i)] = c
                sent.append(c)

    mine = []
    for i in range(nx):
        last[(1, i)].wait_recv()
        last[(-1, i)].wait_recv()
        merge_into(col.at[i], x_ref.at[i * nz + z], rp.at[steps, i])
        merge_into(col.at[i], col.at[i], rm.at[steps, i])
    for k in range(1, nx):
        target = lax.rem(x + k, nx)
        c = pltpu.make_async_remote_copy(
            src_ref=col.at[target],
            dst_ref=y_ref.at[x],
            send_sem=sx_send.at[k],
            recv_sem=sx_recv.at[k],
            device_id=(target * nz + z, mp),
            device_id_type=MESH,
        )
        c.start()
        mine.append(c)
    y_ref[x] = col[x]
    for c in sent:
        c.wait_send()
    for c in mine:
        c.wait()


def relay_reduce(parts, nx, nz):
    vmem = pl.BlockSpec(memory_space=pltpu.VMEM)
    steps = nz // 2
    piece = parts.shape[1:]
    return pl.pallas_call(
        functools.partial(relay_reduce_kernel, nx, nz),
        in_specs=[vmem],
        out_specs=vmem,
        out_shape=jax.ShapeDtypeStruct((nx,) + piece, parts.dtype),
        scratch_shapes=[
            pltpu.VMEM((steps + 1, nx) + piece, parts.dtype),
            pltpu.VMEM((steps + 1, nx) + piece, parts.dtype),
            pltpu.VMEM((steps + 1, nx) + piece, parts.dtype),
            pltpu.VMEM((steps + 1, nx) + piece, parts.dtype),
            pltpu.VMEM((nx,) + piece, parts.dtype),
            pltpu.SemaphoreType.DMA((steps + 1, nx)),
            pltpu.SemaphoreType.DMA((steps + 1, nx)),
            pltpu.SemaphoreType.DMA((steps + 1, nx)),
            pltpu.SemaphoreType.DMA((steps + 1, nx)),
            pltpu.SemaphoreType.DMA((nx,)),
            pltpu.SemaphoreType.DMA((nx,)),
        ],
        compiler_params=pltpu.CompilerParams(collective_id=3, has_side_effects=True),
    )(parts)


def local(
    prompt_hidden,
    recompute_hidden,
    key_cache,
    value_cache,
    norm_gain,
    w_query,
    key_weight,
    value_weight,
    w_out,
    passage_owner,
    prompt_slot,
    prompt_length,
    recompute_count,
    recompute_index,
):
    prompt_rows = prompt_hidden.shape[0]
    recompute_rows = recompute_hidden.shape[0]
    query_rows = prompt_rows + recompute_rows
    passage_length = key_cache.shape[1]
    local_heads = w_query.shape[1] // HEAD_SIZE
    n_seq = passage_owner.shape[0]
    me = lax.axis_index("seq")
    scale = 1.0 / math.sqrt(HEAD_SIZE)

    n_mp = w_out.shape[1] // prompt_hidden.shape[1]
    full_rows, meta, lim = mp_gather(
        prompt_hidden, recompute_hidden, passage_owner, prompt_slot, prompt_length,
        recompute_count, recompute_index, n_mp, passage_length, local_heads,
    )
    own_pos = jnp.concatenate([meta[0], meta[1]])
    own_live = jnp.concatenate([meta[2], meta[3]]) > 0
    own_index = meta[6]
    own_shift = meta[7, 0]
    prompt_live = meta[2] > 0
    recompute_live = meta[3] > 0
    normalized_hidden = normalize(full_rows, norm_gain)
    queries = (
        apply_rotation(
            jnp.dot(normalized_hidden, w_query, preferred_element_type=jnp.float32).reshape(
                query_rows, local_heads, HEAD_SIZE
            ),
            own_pos,
        )
        .astype(jnp.bfloat16)
    )
    fresh_keys = (
        apply_rotation(
            jnp.dot(normalized_hidden, key_weight, preferred_element_type=jnp.float32).reshape(
                query_rows, 1, HEAD_SIZE
            ),
            own_pos,
        )
        .astype(jnp.bfloat16)
        .reshape(query_rows, HEAD_SIZE)
    )
    fresh_values = jnp.dot(
        normalized_hidden, value_weight, preferred_element_type=jnp.float32
    ).astype(jnp.bfloat16)

    half_width = HEAD_SIZE // 2
    exponent = jnp.arange(half_width).astype(jnp.float32) * (2.0 / HEAD_SIZE)
    frequency = jnp.exp(-exponent * math.log(500000.0))
    angle = own_shift.astype(jnp.float32) * frequency
    rot = jnp.stack(
        [
            jnp.concatenate([jnp.cos(angle), jnp.cos(angle)]),
            jnp.concatenate([-jnp.sin(angle), jnp.sin(angle)]),
        ]
    )
    fresh_pair = jnp.concatenate([fresh_keys[prompt_rows:], fresh_values[prompt_rows:]], axis=1)

    nx, nz = SEQ_SHAPE
    all_queries, passage_keys, passage_values = relay_gather(
        queries.reshape(2, prompt_rows * local_heads, HEAD_SIZE),
        key_cache[0],
        value_cache[0],
        fresh_pair,
        meta,
        rot,
        nx,
        nz,
    )
    q_blocks = all_queries.reshape(n_seq * 2, prompt_rows * local_heads, HEAD_SIZE)
    packed = passage_attention(nx, nz, meta, q_blocks, passage_keys, passage_values, lim)
    block_rows = packed.shape[1]

    back = relay_reduce(packed.reshape(n_seq, 2, block_rows, HEAD_SIZE), nx, nz)
    n_parts = back.shape[0]
    rows128 = prompt_rows * local_heads
    stats_back = back[:, :, rows128 : rows128 + 4].astype(jnp.float32)
    part_max = (stats_back[:, :, 0] + stats_back[:, :, 1]).reshape(n_parts, query_rows, local_heads)
    part_tot = (stats_back[:, :, 2] + stats_back[:, :, 3]).reshape(n_parts, query_rows, local_heads)
    part_acc = (
        back[:, :, :rows128].reshape(n_parts, query_rows, local_heads, HEAD_SIZE).astype(jnp.float32)
    )

    pq = queries[:prompt_rows].astype(jnp.float32)
    pk = fresh_keys[:prompt_rows].astype(jnp.float32)
    pv = fresh_values[:prompt_rows].astype(jnp.float32)
    ps = jnp.einsum("qhd,kd->qhk", pq, pk) * scale
    jj = jnp.arange(prompt_rows, dtype=jnp.int32)
    pvis = (jj[None, :] <= jj[:, None]) & prompt_live[None, :]
    ps = jnp.where(pvis[:, None, :], ps, NEGATIVE_FLOOR)
    pmax = jnp.max(ps, axis=-1)
    pw = jnp.where(pvis[:, None, :], jnp.exp(ps - pmax[..., None]), 0.0)
    ptot = jnp.sum(pw, axis=-1)
    pacc = jnp.einsum("qhk,kd->qhd", pw.astype(jnp.bfloat16).astype(jnp.float32), pv)
    loc_max = jnp.concatenate(
        [pmax, jnp.full((recompute_rows, local_heads), NEGATIVE_FLOOR, jnp.float32)]
    )
    loc_tot = jnp.concatenate([ptot, jnp.zeros((recompute_rows, local_heads), jnp.float32)])
    loc_acc = jnp.concatenate(
        [pacc, jnp.zeros((recompute_rows, local_heads, HEAD_SIZE), jnp.float32)]
    )

    highest = jnp.maximum(jnp.max(part_max, axis=0), loc_max)
    part_scale = jnp.exp(part_max - highest[None])
    loc_scale = jnp.exp(loc_max - highest)
    accumulated = jnp.sum(part_acc * part_scale[..., None], axis=0) + loc_acc * loc_scale[..., None]
    totals = jnp.sum(part_tot * part_scale, axis=0) + loc_tot * loc_scale
    safe_totals = jnp.where(totals > 0, totals, 1.0)
    attention = jnp.where(
        own_live[:, None, None], accumulated / safe_totals[..., None], 0.0
    ).astype(jnp.bfloat16).reshape(query_rows, local_heads * HEAD_SIZE)
    prompt_out, recompute_out = mp_scatter(attention, w_out, n_mp, prompt_rows)
    return (prompt_out, recompute_out)


def solution(mesh):
    global SEQ_SHAPE
    sizes = dict(zip(mesh.axis_names, mesh.devices.shape))
    seq_devices = mesh.devices.reshape(sizes["seq"], sizes["mp"])[:, 0]
    xs = sorted({d.coords[0] for d in seq_devices})
    SEQ_SHAPE = (len(xs), sizes["seq"] // len(xs))
    return jax.shard_map(
        local,
        mesh=mesh,
        in_specs=(
            P("seq", "mp"),
            P("seq", "mp"),
            P("seq", None, "mp"),
            P("seq", None, "mp"),
            P(),
            P(None, "mp"),
            P(None, "mp"),
            P(None, "mp"),
            P("mp", None),
            P(),
            P(),
            P(),
            P(),
            P(),
        ),
        out_specs=(P("seq", "mp"), P("seq", "mp")),
        check_vma=False,
    )
```

```python
import functools
import math

import jax
import jax.numpy as jnp
from jax import lax
from jax.experimental import pallas as pl
from jax.experimental.pallas import tpu as pltpu
from jax.sharding import PartitionSpec as P

HEAD_SIZE = 128
NEGATIVE_FLOOR = -1e30


def apply_rotation(vectors, positions):
    half_width = vectors.shape[-1] // 2
    exponent = jnp.arange(half_width).astype(jnp.float32) * (2.0 / vectors.shape[-1])
    frequency = jnp.exp(-exponent * math.log(500000.0))
    angles = positions.astype(jnp.float32)[:, None] * frequency[None, :]
    cosines = jnp.cos(angles)[:, None, :]
    sines = jnp.sin(angles)[:, None, :]
    leading = vectors[..., :half_width]
    trailing = vectors[..., half_width:]
    return jnp.concatenate(
        [leading * cosines - trailing * sines, trailing * cosines + leading * sines], axis=-1
    )


def normalize(rows_in, norm_gain):
    values = rows_in.astype(jnp.float32)
    inverse_rms = lax.rsqrt(jnp.mean(values * values, axis=-1, keepdims=True) + 1e-05)
    return (values * inverse_rms * norm_gain).astype(jnp.bfloat16)


MESH = pl.DeviceIdType.MESH


def passage_kernel(nx, nz, flags_ref, q_ref, k_ref, v_ref, lim_ref, out_ref):
    nb, rows, _ = q_ref.shape
    keys = k_ref.shape[0]
    token = lax.broadcasted_iota(jnp.int32, (rows, keys), 1)
    sub = lax.broadcasted_iota(jnp.int32, (16, rows), 0)

    def split(m_row, l_row):
        m_hi = m_row.astype(jnp.bfloat16).astype(jnp.float32)
        l_hi = l_row.astype(jnp.bfloat16).astype(jnp.float32)
        st = jnp.where(
            sub == 0,
            m_row,
            jnp.where(
                sub == 1,
                m_row - m_hi,
                jnp.where(sub == 2, l_row, jnp.where(sub == 3, l_row - l_hi, 0.0)),
            ),
        )
        return st.astype(jnp.bfloat16)

    out_ref[:, 0:rows] = jnp.zeros((nb, rows, HEAD_SIZE), out_ref.dtype)
    floor = jnp.full((16, rows), NEGATIVE_FLOOR, jnp.float32)
    empty = split(floor, jnp.zeros((16, rows), jnp.float32))
    out_ref[:, rows:] = jnp.broadcast_to(empty[None], (nb, 16, rows))

    def attend(b, masked):
        d = b // 2
        stored = ((d % nz) * nx + d // nz) * 2 + b % 2
        scores = lax.dot_general(
            q_ref[stored], k_ref[...], (((1,), (1,)), ((), ())), preferred_element_type=jnp.float32
        ) * (1.0 / math.sqrt(HEAD_SIZE))
        if masked:
            scores = jnp.where(token <= lim_ref[...], scores, NEGATIVE_FLOOR)
        maxima = jnp.max(scores, axis=1, keepdims=True)
        weights = jnp.exp(scores - maxima)
        totals = jnp.sum(weights, axis=1, keepdims=True)
        out_ref[b, 0:rows] = jnp.dot(
            weights.astype(jnp.bfloat16), v_ref[...], preferred_element_type=jnp.float32
        ).astype(out_ref.dtype)
        m_row = jnp.transpose(jnp.broadcast_to(maxima, (rows, rows)))[0:16]
        l_row = jnp.transpose(jnp.broadcast_to(totals, (rows, rows)))[0:16]
        out_ref[b, rows:] = split(m_row, l_row)

    def body(b, carry):
        flag = flags_ref[4 + b % 2, b // 2]

        @pl.when(flag == 1)
        def _():
            attend(b, False)

        @pl.when(flag == 2)
        def _():
            attend(b, True)

        return carry

    lax.fori_loop(0, nb, body, 0)


def passage_attention(nx, nz, flags, q_blocks, keys, values, lim):
    nb, rows, _ = q_blocks.shape
    vmem = pl.BlockSpec(memory_space=pltpu.VMEM)
    return pl.pallas_call(
        functools.partial(passage_kernel, nx, nz),
        in_specs=[pl.BlockSpec(memory_space=pltpu.SMEM), vmem, vmem, vmem, vmem],
        out_specs=vmem,
        out_shape=jax.ShapeDtypeStruct((nb, rows + 16, HEAD_SIZE), jnp.bfloat16),
    )(flags, q_blocks, keys, values, lim)


def mp_gather_kernel(n, span, p_ref, r_ref, owner_ref, slot_ref, plen_ref, count_ref, index_ref,
                     y_ref, meta_ref, lim_ref, send_sem, recv_sem, local_sem):
    me = lax.axis_index("mp")
    row = lax.axis_index("seq")
    rows, width = p_ref.shape
    barrier = pltpu.get_barrier_semaphore()
    for k in range(1, n):
        peer = lax.rem(me + k, n)
        pl.semaphore_signal(barrier, inc=1, device_id=(row, peer), device_id_type=MESH)
    pl.semaphore_wait(barrier, n - 1)
    cols = pl.ds(pl.multiple_of(me * width, width), width)
    copies = []
    for k in range(1, n):
        peer = lax.rem(me + k, n)
        for part, src in enumerate((p_ref, r_ref)):
            c = pltpu.make_async_remote_copy(
                src_ref=src,
                dst_ref=y_ref.at[pl.ds(part * rows, rows), cols],
                send_sem=send_sem.at[part, k],
                recv_sem=recv_sem.at[part, k],
                device_id=(row, peer),
                device_id_type=MESH,
            )
            c.start()
            copies.append(c)
    own = [
        pltpu.make_async_copy(src, y_ref.at[pl.ds(part * rows, rows), cols], local_sem.at[part])
        for part, src in enumerate((p_ref, r_ref))
    ]
    for c in own:
        c.start()

    f32 = jnp.float32
    owner = owner_ref[...].astype(f32)
    slot = slot_ref[...].astype(f32)
    lane = lax.broadcasted_iota(jnp.int32, owner.shape, 1)
    mine = lane == row

    def pick(v):
        return jnp.sum(jnp.where(mine, v, 0.0), axis=1, keepdims=True)

    own_owner = pick(owner)
    own_slot = pick(slot)
    rank = jnp.sum(jnp.where((owner == own_owner) & (lane < row), 1.0, 0.0), axis=1, keepdims=True)
    held = jnp.sum(jnp.where(owner == own_slot, 1.0, 0.0), axis=1, keepdims=True)
    length = pick(plen_ref[...].astype(f32))
    count = pick(count_ref[...].astype(f32))
    index = index_ref[pl.ds(row, 1), :].astype(f32)
    lanef = lane.astype(f32)
    quantities = [
        held * span + lanef,
        rank * span + index,
        jnp.where(lanef < length, 1.0, 0.0),
        jnp.where(lanef < count, 1.0, 0.0),
        jnp.where(slot == own_owner, 1.0, 0.0),
        jnp.where(mine, 2.0, jnp.where((owner == own_owner) & (lane > row), 1.0, 0.0)),
        index,
        rank * span + 0.0 * lanef,
    ]
    for q, value in enumerate(quantities):
        meta_ref[q : q + 1, :] = value.astype(jnp.int32)
    heads = lim_ref.shape[0] // index.shape[1]
    wide = jnp.broadcast_to(index, (lim_ref.shape[0], index.shape[1]))
    which = lax.broadcasted_iota(jnp.int32, wide.shape, 0) // heads
    pick_lane = lax.broadcasted_iota(jnp.int32, wide.shape, 1)
    lim_ref[...] = jnp.sum(jnp.where(which == pick_lane, wide, 0.0), axis=1, keepdims=True).astype(jnp.int32)

    for c in copies:
        c.wait()
    for c in own:
        c.wait()


def mp_gather(prompt_part, recompute_part, owner, slot, plen, count, index, n, span, heads):
    vmem = pl.BlockSpec(memory_space=pltpu.VMEM)
    rows, width = prompt_part.shape
    small = [v.reshape(1, -1) for v in (owner, slot, plen, count)]
    return pl.pallas_call(
        functools.partial(mp_gather_kernel, n, span),
        in_specs=[vmem] * 7,
        out_specs=[vmem, vmem, vmem],
        out_shape=[
            jax.ShapeDtypeStruct((2 * rows, width * n), prompt_part.dtype),
            jax.ShapeDtypeStruct((8, owner.shape[0]), jnp.int32),
            jax.ShapeDtypeStruct((index.shape[1] * heads, 1), jnp.int32),
        ],
        scratch_shapes=[
            pltpu.SemaphoreType.DMA((2, n)),
            pltpu.SemaphoreType.DMA((2, n)),
            pltpu.SemaphoreType.DMA((2,)),
        ],
        compiler_params=pltpu.CompilerParams(collective_id=0, has_side_effects=True),
    )(prompt_part, recompute_part, *small, index)


def mp_scatter_kernel(n, a_ref, w_ref, y_ref, buf, send_sem, recv_sem):
    me = lax.axis_index("mp")
    row = lax.axis_index("seq")
    width = y_ref.shape[2]
    barrier = pltpu.get_barrier_semaphore()
    for k in range(1, n):
        peer = lax.rem(me + k, n)
        pl.semaphore_signal(barrier, inc=1, device_id=(row, peer), device_id_type=MESH)
    pl.semaphore_wait(barrier, n - 1)

    def block(d):
        cols = pl.ds(pl.multiple_of(d * width, width), width)
        return jnp.dot(a_ref[...], w_ref[:, cols], preferred_element_type=jnp.float32).astype(
            y_ref.dtype
        )

    copies = []
    for k in range(1, n):
        peer = lax.rem(me + k, n)
        buf[k] = block(peer)
        c = pltpu.make_async_remote_copy(
            src_ref=buf.at[k],
            dst_ref=y_ref.at[me],
            send_sem=send_sem.at[k],
            recv_sem=recv_sem.at[k],
            device_id=(row, peer),
            device_id_type=MESH,
        )
        c.start()
        copies.append(c)
    y_ref[me] = block(me)
    for c in copies:
        c.wait()


def mp_scatter(attention, w_out, n):
    vmem = pl.BlockSpec(memory_space=pltpu.VMEM)
    rows = attention.shape[0]
    width = w_out.shape[1] // n
    return pl.pallas_call(
        functools.partial(mp_scatter_kernel, n),
        in_specs=[vmem, vmem],
        out_specs=vmem,
        out_shape=jax.ShapeDtypeStruct((n, rows, width), jnp.bfloat16),
        scratch_shapes=[
            pltpu.VMEM((n, rows, width), jnp.bfloat16),
            pltpu.SemaphoreType.DMA((n,)),
            pltpu.SemaphoreType.DMA((n,)),
        ],
        compiler_params=pltpu.CompilerParams(collective_id=1, has_side_effects=True),
    )(attention, w_out)


def relay_gather_kernel(nx, nz, x_ref, kc_ref, vc_ref, fresh_ref, meta_ref, rot_ref,
                        y_ref, pk_ref, pv_ref, *sems):
    (sx_send, sx_recv, zp_send, zp_recv, zm_send, zm_recv, own_sem,
     bp_send, bp_recv, bm_send, bm_recv, xp_send, xp_recv, xm_send, xm_recv,
     fp_send, fp_recv, fm_send, fm_recv) = sems
    me = lax.axis_index("seq")
    mp = lax.axis_index("mp")
    x = me // nz
    z = me % nz
    up = lax.rem(z + 1, nz)
    down = lax.rem(z + nz - 1, nz)
    right = lax.rem(x + 1, nx)
    left = lax.rem(x + nx - 1, nx)
    barrier = pltpu.get_barrier_semaphore()
    peers = [(lax.rem(x + k, nx) * nz + z, mp) for k in range(1, nx)]
    peers += [(x * nz + up, mp), (x * nz + down, mp)]
    for p in peers:
        pl.semaphore_signal(barrier, inc=1, device_id=p, device_id_type=MESH)
    pl.semaphore_wait(barrier, len(peers))

    def copy(src, dst, send_sem, recv_sem, device):
        c = pltpu.make_async_remote_copy(
            src_ref=src,
            dst_ref=dst,
            send_sem=send_sem,
            recv_sem=recv_sem,
            device_id=device,
            device_id_type=MESH,
        )
        c.start()
        return c

    sent = []
    slot = z * nx + x
    first = [
        copy(x_ref.at[0], y_ref.at[slot, 0], sx_send.at[k], sx_recv.at[k], peers[k - 1])
        for k in range(1, nx)
    ]
    own = pltpu.make_async_copy(x_ref, y_ref.at[slot], own_sem)
    own.start()

    width = kc_ref.shape[1]
    cached = kc_ref[...].astype(jnp.float32)
    turned = pltpu.roll(cached, width // 2, 1)
    shifted = (cached * rot_ref[0:1, :] + turned * rot_ref[1:2, :]).astype(pk_ref.dtype)
    token = lax.broadcasted_iota(jnp.int32, (kc_ref.shape[0], meta_ref.shape[1]), 0)
    chosen = (token == meta_ref[6:7, :]) & (meta_ref[3:4, :] > 0)
    placed = jnp.dot(
        chosen.astype(jnp.bfloat16), fresh_ref[...], preferred_element_type=jnp.float32
    ).astype(pk_ref.dtype)
    replaced = jnp.max(jnp.where(chosen, 1.0, 0.0), axis=1, keepdims=True) > 0.0
    pk_ref[...] = jnp.where(replaced, placed[:, :width], shifted)
    pv_ref[...] = jnp.where(replaced, placed[:, width:], vc_ref[...])

    def x_out(column):
        a = copy(
            y_ref.at[column * nx + x, 1], y_ref.at[column * nx + x, 1],
            xp_send.at[column], xp_recv.at[column], (right * nz + z, mp),
        )
        b = copy(
            y_ref.at[column * nx + x, 1], y_ref.at[column * nx + x, 1],
            xm_send.at[column], xm_recv.at[column], (left * nz + z, mp),
        )
        return [a, b]

    own.wait()
    steps = nz // 2
    half = nx // 2
    zlast = {}
    blast = {}
    xcopies = {}
    for c in first:
        c.wait()
    for t in range(1, steps + 1):
        for sign, send_sem, recv_sem, target, count in (
            (1, bp_send, bp_recv, up, steps),
            (-1, bm_send, bm_recv, down, nz - 1 - steps),
        ):
            if t > count:
                continue
            if t > 1:
                blast[sign].wait_recv()
            column = lax.rem(z - sign * (t - 1) + nz, nz)
            if t > 1:
                xcopies[(sign, t - 1)] = x_out(column)
            elif sign == 1:
                xcopies[(0, 0)] = x_out(column)
            blast[sign] = copy(
                y_ref.at[column * nx + x, 1], y_ref.at[column * nx + x, 1],
                send_sem.at[t], recv_sem.at[t], (x * nz + target, mp),
            )
            sent.append(blast[sign])
        for i in range(nx):
            for sign, send_sem, recv_sem, target in (
                (1, zp_send, zp_recv, up),
                (-1, zm_send, zm_recv, down),
            ):
                if t == steps and (i < half) != (sign == 1):
                    continue
                if t > 1:
                    zlast[(sign, i)].wait_recv()
                column = lax.rem(z - sign * (t - 1) + nz, nz)
                zlast[(sign, i)] = copy(
                    y_ref.at[column * nx + i, 0], y_ref.at[column * nx + i, 0],
                    send_sem.at[t, i], recv_sem.at[t, i], (x * nz + target, mp),
                )
                sent.append(zlast[(sign, i)])
    for sign, count in ((1, steps), (-1, nz - 1 - steps)):
        blast[sign].wait_recv()
        column = lax.rem(z - sign * count + nz, nz)
        xcopies[(sign, count)] = x_out(column)
    order = [(0, 0)] + [(s, t) for t in range(1, steps + 1) for s in (1, -1) if (s, t) in xcopies]
    forwards = []
    for key in order:
        sign, t = key
        column = lax.rem(z - sign * t + nz, nz)
        from_left, from_right = xcopies[key]
        from_left.wait_recv()
        from_right.wait_recv()
        sent += xcopies[key]
    for zc in range(nz):
        if zc < nz // 2:
            forwards.append(
                copy(
                    y_ref.at[zc * nx + left, 1], y_ref.at[zc * nx + left, 1],
                    fp_send.at[zc], fp_recv.at[zc], (right * nz + z, mp),
                )
            )
        else:
            forwards.append(
                copy(
                    y_ref.at[zc * nx + right, 1], y_ref.at[zc * nx + right, 1],
                    fm_send.at[zc], fm_recv.at[zc], (left * nz + z, mp),
                )
            )
    for c in zlast.values():
        c.wait_recv()
    for c in forwards:
        c.wait_recv()
    for c in sent:
        c.wait_send()
    for c in forwards:
        c.wait_send()


def relay_gather(x, kc, vc, fresh, meta, rot, nx, nz):
    assert nx == 4 and nz % 2 == 0
    vmem = pl.BlockSpec(memory_space=pltpu.VMEM)
    steps = nz // 2
    dma = pltpu.SemaphoreType.DMA
    return pl.pallas_call(
        functools.partial(relay_gather_kernel, nx, nz),
        in_specs=[vmem] * 6,
        out_specs=[vmem, vmem, vmem],
        out_shape=[
            jax.ShapeDtypeStruct((nx * nz,) + x.shape, x.dtype),
            jax.ShapeDtypeStruct(kc.shape, kc.dtype),
            jax.ShapeDtypeStruct(vc.shape, vc.dtype),
        ],
        scratch_shapes=[
            dma((nx,)), dma((nx,)),
            dma((steps + 1, nx)), dma((steps + 1, nx)), dma((steps + 1, nx)), dma((steps + 1, nx)),
            dma(()),
            dma((steps + 1,)), dma((steps + 1,)), dma((steps + 1,)), dma((steps + 1,)),
            dma((nz,)), dma((nz,)), dma((nz,)), dma((nz,)),
            dma((nz,)), dma((nz,)), dma((nz,)), dma((nz,)),
        ],
        compiler_params=pltpu.CompilerParams(collective_id=2, has_side_effects=True),
    )(x, kc, vc, fresh, meta, rot)


def merge_piece(a, b, rows):
    af = a.astype(jnp.float32)
    bf = b.astype(jnp.float32)
    m1 = af[rows : rows + 1] + af[rows + 1 : rows + 2]
    l1 = af[rows + 2 : rows + 3] + af[rows + 3 : rows + 4]
    m2 = bf[rows : rows + 1] + bf[rows + 1 : rows + 2]
    l2 = bf[rows + 2 : rows + 3] + bf[rows + 3 : rows + 4]
    top = jnp.maximum(m1, m2)
    s1 = jnp.exp(m1 - top)
    s2 = jnp.exp(m2 - top)
    total = l1 * s1 + l2 * s2
    c1 = jnp.transpose(jnp.broadcast_to(s1, (rows, rows)))
    c2 = jnp.transpose(jnp.broadcast_to(s2, (rows, rows)))
    acc = af[0:rows] * c1 + bf[0:rows] * c2
    sub = lax.broadcasted_iota(jnp.int32, (16, rows), 0)
    top_hi = top.astype(jnp.bfloat16).astype(jnp.float32)
    tot_hi = total.astype(jnp.bfloat16).astype(jnp.float32)
    st = jnp.where(
        sub == 0,
        top,
        jnp.where(
            sub == 1, top - top_hi, jnp.where(sub == 2, total, jnp.where(sub == 3, total - tot_hi, 0.0))
        ),
    )
    return acc.astype(jnp.bfloat16), st.astype(jnp.bfloat16)


def relay_reduce_kernel(
    nx, nz, x_ref, y_ref, rp, rm, bp, bm, col, sp_send, sp_recv, sm_send, sm_recv, sx_send, sx_recv
):
    me = lax.axis_index("seq")
    mp = lax.axis_index("mp")
    x = me // nz
    z = me % nz
    up = lax.rem(z + 1, nz)
    down = lax.rem(z + nz - 1, nz)
    rows = x_ref.shape[2] - 16
    barrier = pltpu.get_barrier_semaphore()
    peers = [(lax.rem(x + k, nx) * nz + z, mp) for k in range(1, nx)]
    peers += [(x * nz + up, mp), (x * nz + down, mp)]
    for p in peers:
        pl.semaphore_signal(barrier, inc=1, device_id=p, device_id_type=MESH)
    pl.semaphore_wait(barrier, len(peers))

    def merge_into(dst, first, second):
        for h in range(2):
            acc, st = merge_piece(first[h], second[h], rows)
            dst[h, 0:rows] = acc
            dst[h, rows:] = st

    steps = nz // 2
    half = nx // 2
    last = {}
    sent = []
    dirs = ((1, rp, bp, sp_send, sp_recv, up), (-1, rm, bm, sm_send, sm_recv, down))
    for t in range(1, steps + 1):
        for i in range(nx):
            for sign, recv_buf, send_buf, send_sem, recv_sem, target in dirs:
                if t == 1 and (i < half) != (sign == 1):
                    continue
                column = lax.rem(z + sign * (steps + 1 - t) + nz, nz)
                own = x_ref.at[i * nz + column]
                if (sign, i) in last:
                    last[(sign, i)].wait_recv()
                    merge_into(send_buf.at[t, i], own, recv_buf.at[t - 1, i])
                    src = send_buf.at[t, i]
                else:
                    src = own
                c = pltpu.make_async_remote_copy(
                    src_ref=src,
                    dst_ref=recv_buf.at[t, i],
                    send_sem=send_sem.at[t, i],
                    recv_sem=recv_sem.at[t, i],
                    device_id=(x * nz + target, mp),
                    device_id_type=MESH,
                )
                c.start()
                last[(sign, i)] = c
                sent.append(c)

    mine = []
    for i in range(nx):
        last[(1, i)].wait_recv()
        last[(-1, i)].wait_recv()
    for k in list(range(1, nx)) + [0]:
        target = lax.rem(x + k, nx)
        merge_into(col.at[target], x_ref.at[target * nz + z], rp.at[steps, target])
        merge_into(col.at[target], col.at[target], rm.at[steps, target])
        if k == 0:
            continue
        c = pltpu.make_async_remote_copy(
            src_ref=col.at[target],
            dst_ref=y_ref.at[x],
            send_sem=sx_send.at[k],
            recv_sem=sx_recv.at[k],
            device_id=(target * nz + z, mp),
            device_id_type=MESH,
        )
        c.start()
        mine.append(c)
    y_ref[x] = col[x]
    for c in sent:
        c.wait_send()
    for c in mine:
        c.wait()


def relay_reduce(parts, nx, nz):
    vmem = pl.BlockSpec(memory_space=pltpu.VMEM)
    steps = nz // 2
    piece = parts.shape[1:]
    return pl.pallas_call(
        functools.partial(relay_reduce_kernel, nx, nz),
        in_specs=[vmem],
        out_specs=vmem,
        out_shape=jax.ShapeDtypeStruct((nx,) + piece, parts.dtype),
        scratch_shapes=[
            pltpu.VMEM((steps + 1, nx) + piece, parts.dtype),
            pltpu.VMEM((steps + 1, nx) + piece, parts.dtype),
            pltpu.VMEM((steps + 1, nx) + piece, parts.dtype),
            pltpu.VMEM((steps + 1, nx) + piece, parts.dtype),
            pltpu.VMEM((nx,) + piece, parts.dtype),
            pltpu.SemaphoreType.DMA((steps + 1, nx)),
            pltpu.SemaphoreType.DMA((steps + 1, nx)),
            pltpu.SemaphoreType.DMA((steps + 1, nx)),
            pltpu.SemaphoreType.DMA((steps + 1, nx)),
            pltpu.SemaphoreType.DMA((nx,)),
            pltpu.SemaphoreType.DMA((nx,)),
        ],
        compiler_params=pltpu.CompilerParams(collective_id=3, has_side_effects=True),
    )(parts)


def local(
    prompt_hidden,
    recompute_hidden,
    key_cache,
    value_cache,
    norm_gain,
    w_query,
    key_weight,
    value_weight,
    w_out,
    passage_owner,
    prompt_slot,
    prompt_length,
    recompute_count,
    recompute_index,
):
    prompt_rows = prompt_hidden.shape[0]
    recompute_rows = recompute_hidden.shape[0]
    query_rows = prompt_rows + recompute_rows
    passage_length = key_cache.shape[1]
    local_heads = w_query.shape[1] // HEAD_SIZE
    n_seq = passage_owner.shape[0]
    me = lax.axis_index("seq")
    scale = 1.0 / math.sqrt(HEAD_SIZE)

    n_mp = w_out.shape[1] // prompt_hidden.shape[1]
    full_rows, meta, lim = mp_gather(
        prompt_hidden, recompute_hidden, passage_owner, prompt_slot, prompt_length,
        recompute_count, recompute_index, n_mp, passage_length, local_heads,
    )
    own_pos = jnp.concatenate([meta[0], meta[1]])
    own_live = jnp.concatenate([meta[2], meta[3]]) > 0
    own_index = meta[6]
    own_shift = meta[7, 0]
    prompt_live = meta[2] > 0
    recompute_live = meta[3] > 0
    normalized_hidden = normalize(full_rows, norm_gain)
    queries = (
        apply_rotation(
            jnp.dot(normalized_hidden, w_query, preferred_element_type=jnp.float32).reshape(
                query_rows, local_heads, HEAD_SIZE
            ),
            own_pos,
        )
        .astype(jnp.bfloat16)
    )
    fresh_keys = (
        apply_rotation(
            jnp.dot(normalized_hidden, key_weight, preferred_element_type=jnp.float32).reshape(
                query_rows, 1, HEAD_SIZE
            ),
            own_pos,
        )
        .astype(jnp.bfloat16)
        .reshape(query_rows, HEAD_SIZE)
    )
    fresh_values = jnp.dot(
        normalized_hidden, value_weight, preferred_element_type=jnp.float32
    ).astype(jnp.bfloat16)

    half_width = HEAD_SIZE // 2
    exponent = jnp.arange(half_width).astype(jnp.float32) * (2.0 / HEAD_SIZE)
    frequency = jnp.exp(-exponent * math.log(500000.0))
    angle = own_shift.astype(jnp.float32) * frequency
    rot = jnp.stack(
        [
            jnp.concatenate([jnp.cos(angle), jnp.cos(angle)]),
            jnp.concatenate([-jnp.sin(angle), jnp.sin(angle)]),
        ]
    )
    fresh_pair = jnp.concatenate([fresh_keys[prompt_rows:], fresh_values[prompt_rows:]], axis=1)

    nx, nz = SEQ_SHAPE
    all_queries, passage_keys, passage_values = relay_gather(
        queries.reshape(2, prompt_rows * local_heads, HEAD_SIZE),
        key_cache[0],
        value_cache[0],
        fresh_pair,
        meta,
        rot,
        nx,
        nz,
    )
    q_blocks = all_queries.reshape(n_seq * 2, prompt_rows * local_heads, HEAD_SIZE)
    packed = passage_attention(nx, nz, meta, q_blocks, passage_keys, passage_values, lim)
    block_rows = packed.shape[1]

    back = relay_reduce(packed.reshape(n_seq, 2, block_rows, HEAD_SIZE), nx, nz)
    n_parts = back.shape[0]
    rows128 = prompt_rows * local_heads
    stats_back = back[:, :, rows128 : rows128 + 4].astype(jnp.float32)
    part_max = (stats_back[:, :, 0] + stats_back[:, :, 1]).reshape(n_parts, query_rows, local_heads)
    part_tot = (stats_back[:, :, 2] + stats_back[:, :, 3]).reshape(n_parts, query_rows, local_heads)
    part_acc = (
        back[:, :, :rows128].reshape(n_parts, query_rows, local_heads, HEAD_SIZE).astype(jnp.float32)
    )

    pq = queries[:prompt_rows].astype(jnp.float32)
    pk = fresh_keys[:prompt_rows].astype(jnp.float32)
    pv = fresh_values[:prompt_rows].astype(jnp.float32)
    ps = jnp.einsum("qhd,kd->qhk", pq, pk) * scale
    jj = jnp.arange(prompt_rows, dtype=jnp.int32)
    pvis = (jj[None, :] <= jj[:, None]) & prompt_live[None, :]
    ps = jnp.where(pvis[:, None, :], ps, NEGATIVE_FLOOR)
    pmax = jnp.max(ps, axis=-1)
    pw = jnp.where(pvis[:, None, :], jnp.exp(ps - pmax[..., None]), 0.0)
    ptot = jnp.sum(pw, axis=-1)
    pacc = jnp.einsum("qhk,kd->qhd", pw.astype(jnp.bfloat16).astype(jnp.float32), pv)
    loc_max = jnp.concatenate(
        [pmax, jnp.full((recompute_rows, local_heads), NEGATIVE_FLOOR, jnp.float32)]
    )
    loc_tot = jnp.concatenate([ptot, jnp.zeros((recompute_rows, local_heads), jnp.float32)])
    loc_acc = jnp.concatenate(
        [pacc, jnp.zeros((recompute_rows, local_heads, HEAD_SIZE), jnp.float32)]
    )

    highest = jnp.maximum(jnp.max(part_max, axis=0), loc_max)
    part_scale = jnp.exp(part_max - highest[None])
    loc_scale = jnp.exp(loc_max - highest)
    accumulated = jnp.sum(part_acc * part_scale[..., None], axis=0) + loc_acc * loc_scale[..., None]
    totals = jnp.sum(part_tot * part_scale, axis=0) + loc_tot * loc_scale
    safe_totals = jnp.where(totals > 0, totals, 1.0)
    attention = jnp.where(
        own_live[:, None, None], accumulated / safe_totals[..., None], 0.0
    ).astype(jnp.bfloat16).reshape(query_rows, local_heads * HEAD_SIZE)
    shares = mp_scatter(attention, w_out, n_mp)
    combined = jnp.sum(shares.astype(jnp.float32), axis=0).astype(jnp.bfloat16)
    return (combined[:prompt_rows], combined[prompt_rows:])


def solution(mesh):
    global SEQ_SHAPE
    sizes = dict(zip(mesh.axis_names, mesh.devices.shape))
    seq_devices = mesh.devices.reshape(sizes["seq"], sizes["mp"])[:, 0]
    xs = sorted({d.coords[0] for d in seq_devices})
    SEQ_SHAPE = (len(xs), sizes["seq"] // len(xs))
    return jax.shard_map(
        local,
        mesh=mesh,
        in_specs=(
            P("seq", "mp"),
            P("seq", "mp"),
            P("seq", None, "mp"),
            P("seq", None, "mp"),
            P(),
            P(None, "mp"),
            P(None, "mp"),
            P(None, "mp"),
            P("mp", None),
            P(),
            P(),
            P(),
            P(),
            P(),
        ),
        out_specs=(P("seq", "mp"), P("seq", "mp")),
        check_vma=False,
    )
```

```python
import functools
import math

import jax
import jax.numpy as jnp
from jax import lax
from jax.experimental import pallas as pl
from jax.experimental.pallas import tpu as pltpu
from jax.sharding import PartitionSpec as P

HEAD_SIZE = 128
NEGATIVE_FLOOR = -1e30


def apply_rotation(vectors, positions):
    half_width = vectors.shape[-1] // 2
    exponent = jnp.arange(half_width).astype(jnp.float32) * (2.0 / vectors.shape[-1])
    frequency = jnp.exp(-exponent * math.log(500000.0))
    angles = positions.astype(jnp.float32)[:, None] * frequency[None, :]
    cosines = jnp.cos(angles)[:, None, :]
    sines = jnp.sin(angles)[:, None, :]
    leading = vectors[..., :half_width]
    trailing = vectors[..., half_width:]
    return jnp.concatenate(
        [leading * cosines - trailing * sines, trailing * cosines + leading * sines], axis=-1
    )


def normalize(rows_in, norm_gain):
    values = rows_in.astype(jnp.float32)
    inverse_rms = lax.rsqrt(jnp.mean(values * values, axis=-1, keepdims=True) + 1e-05)
    return (values * inverse_rms * norm_gain).astype(jnp.bfloat16)


MESH = pl.DeviceIdType.MESH


def passage_kernel(nx, nz, flags_ref, q_ref, k_ref, v_ref, lim_ref, out_ref):
    nb, rows, _ = q_ref.shape
    keys = k_ref.shape[0]
    token = lax.broadcasted_iota(jnp.int32, (rows, keys), 1)
    sub = lax.broadcasted_iota(jnp.int32, (16, rows), 0)

    def split(m_row, l_row):
        m_hi = m_row.astype(jnp.bfloat16).astype(jnp.float32)
        l_hi = l_row.astype(jnp.bfloat16).astype(jnp.float32)
        st = jnp.where(
            sub == 0,
            m_row,
            jnp.where(
                sub == 1,
                m_row - m_hi,
                jnp.where(sub == 2, l_row, jnp.where(sub == 3, l_row - l_hi, 0.0)),
            ),
        )
        return st.astype(jnp.bfloat16)

    out_ref[:, 0:rows] = jnp.zeros((nb, rows, HEAD_SIZE), out_ref.dtype)
    floor = jnp.full((16, rows), NEGATIVE_FLOOR, jnp.float32)
    empty = split(floor, jnp.zeros((16, rows), jnp.float32))
    out_ref[:, rows:] = jnp.broadcast_to(empty[None], (nb, 16, rows))

    def attend(b, masked):
        d = b // 2
        stored = ((d % nz) * nx + d // nz) * 2 + b % 2
        scale = 1.0 / math.sqrt(HEAD_SIZE)
        raw = lax.dot_general(
            q_ref[stored], k_ref[...], (((1,), (1,)), ((), ())), preferred_element_type=jnp.float32
        )
        if masked:
            raw = jnp.where(token <= lim_ref[...], raw, NEGATIVE_FLOOR)
        raw_max = jnp.max(raw, axis=1, keepdims=True)
        weights = jnp.exp((raw - raw_max) * scale)
        totals = jnp.sum(weights, axis=1, keepdims=True)
        out_ref[b, 0:rows] = jnp.dot(
            weights.astype(jnp.bfloat16), v_ref[...], preferred_element_type=jnp.float32
        ).astype(out_ref.dtype)
        lane = lax.broadcasted_iota(jnp.int32, (rows, rows), 1)
        both = jnp.transpose(jnp.where(lane < rows // 2, raw_max * scale, totals))
        out_ref[b, rows:] = split(both[0:16], both[rows // 2 : rows // 2 + 16])

    def body(b, carry):
        flag = flags_ref[4 + b % 2, b // 2]

        @pl.when(flag == 1)
        def _():
            attend(b, False)

        @pl.when(flag == 2)
        def _():
            attend(b, True)

        return carry

    lax.fori_loop(0, nb, body, 0)


def passage_attention(nx, nz, flags, q_blocks, keys, values, lim):
    nb, rows, _ = q_blocks.shape
    vmem = pl.BlockSpec(memory_space=pltpu.VMEM)
    return pl.pallas_call(
        functools.partial(passage_kernel, nx, nz),
        in_specs=[pl.BlockSpec(memory_space=pltpu.SMEM), vmem, vmem, vmem, vmem],
        out_specs=vmem,
        out_shape=jax.ShapeDtypeStruct((nb, rows + 16, HEAD_SIZE), jnp.bfloat16),
    )(flags, q_blocks, keys, values, lim)


def mp_gather_kernel(n, span, p_ref, r_ref, owner_ref, slot_ref, plen_ref, count_ref, index_ref,
                     y_ref, meta_ref, lim_ref, send_sem, recv_sem, local_sem):
    me = lax.axis_index("mp")
    row = lax.axis_index("seq")
    rows, width = p_ref.shape
    barrier = pltpu.get_barrier_semaphore()
    for k in range(1, n):
        peer = lax.rem(me + k, n)
        pl.semaphore_signal(barrier, inc=1, device_id=(row, peer), device_id_type=MESH)
    pl.semaphore_wait(barrier, n - 1)
    cols = pl.ds(pl.multiple_of(me * width, width), width)
    copies = []
    for k in range(1, n):
        peer = lax.rem(me + k, n)
        for part, src in enumerate((p_ref, r_ref)):
            c = pltpu.make_async_remote_copy(
                src_ref=src,
                dst_ref=y_ref.at[pl.ds(part * rows, rows), cols],
                send_sem=send_sem.at[part, k],
                recv_sem=recv_sem.at[part, k],
                device_id=(row, peer),
                device_id_type=MESH,
            )
            c.start()
            copies.append(c)
    own = [
        pltpu.make_async_copy(src, y_ref.at[pl.ds(part * rows, rows), cols], local_sem.at[part])
        for part, src in enumerate((p_ref, r_ref))
    ]
    for c in own:
        c.start()

    f32 = jnp.float32
    owner = owner_ref[...].astype(f32)
    slot = slot_ref[...].astype(f32)
    lane = lax.broadcasted_iota(jnp.int32, owner.shape, 1)
    mine = lane == row

    def pick(v):
        return jnp.sum(jnp.where(mine, v, 0.0), axis=1, keepdims=True)

    own_owner = pick(owner)
    own_slot = pick(slot)
    rank = jnp.sum(jnp.where((owner == own_owner) & (lane < row), 1.0, 0.0), axis=1, keepdims=True)
    held = jnp.sum(jnp.where(owner == own_slot, 1.0, 0.0), axis=1, keepdims=True)
    length = pick(plen_ref[...].astype(f32))
    count = pick(count_ref[...].astype(f32))
    index = index_ref[pl.ds(row, 1), :].astype(f32)
    lanef = lane.astype(f32)
    quantities = [
        held * span + lanef,
        rank * span + index,
        jnp.where(lanef < length, 1.0, 0.0),
        jnp.where(lanef < count, 1.0, 0.0),
        jnp.where(slot == own_owner, 1.0, 0.0),
        jnp.where(mine, 2.0, jnp.where((owner == own_owner) & (lane > row), 1.0, 0.0)),
        index,
        rank * span + 0.0 * lanef,
    ]
    for q, value in enumerate(quantities):
        meta_ref[q : q + 1, :] = value.astype(jnp.int32)
    heads = lim_ref.shape[0] // index.shape[1]
    wide = jnp.broadcast_to(index, (lim_ref.shape[0], index.shape[1]))
    which = lax.broadcasted_iota(jnp.int32, wide.shape, 0) // heads
    pick_lane = lax.broadcasted_iota(jnp.int32, wide.shape, 1)
    lim_ref[...] = jnp.sum(jnp.where(which == pick_lane, wide, 0.0), axis=1, keepdims=True).astype(jnp.int32)

    for c in copies:
        c.wait()
    for c in own:
        c.wait()


def mp_gather(prompt_part, recompute_part, owner, slot, plen, count, index, n, span, heads):
    vmem = pl.BlockSpec(memory_space=pltpu.VMEM)
    rows, width = prompt_part.shape
    small = [v.reshape(1, -1) for v in (owner, slot, plen, count)]
    return pl.pallas_call(
        functools.partial(mp_gather_kernel, n, span),
        in_specs=[vmem] * 7,
        out_specs=[vmem, vmem, vmem],
        out_shape=[
            jax.ShapeDtypeStruct((2 * rows, width * n), prompt_part.dtype),
            jax.ShapeDtypeStruct((8, owner.shape[0]), jnp.int32),
            jax.ShapeDtypeStruct((index.shape[1] * heads, 1), jnp.int32),
        ],
        scratch_shapes=[
            pltpu.SemaphoreType.DMA((2, n)),
            pltpu.SemaphoreType.DMA((2, n)),
            pltpu.SemaphoreType.DMA((2,)),
        ],
        compiler_params=pltpu.CompilerParams(collective_id=0, has_side_effects=True),
    )(prompt_part, recompute_part, *small, index)


def mp_scatter_kernel(n, a_ref, w_ref, y_ref, buf, send_sem, recv_sem):
    me = lax.axis_index("mp")
    row = lax.axis_index("seq")
    width = y_ref.shape[2]
    barrier = pltpu.get_barrier_semaphore()
    for k in range(1, n):
        peer = lax.rem(me + k, n)
        pl.semaphore_signal(barrier, inc=1, device_id=(row, peer), device_id_type=MESH)
    pl.semaphore_wait(barrier, n - 1)

    def block(d):
        cols = pl.ds(pl.multiple_of(d * width, width), width)
        return jnp.dot(a_ref[...], w_ref[:, cols], preferred_element_type=jnp.float32).astype(
            y_ref.dtype
        )

    copies = []
    for k in range(1, n):
        peer = lax.rem(me + k, n)
        buf[k] = block(peer)
        c = pltpu.make_async_remote_copy(
            src_ref=buf.at[k],
            dst_ref=y_ref.at[me],
            send_sem=send_sem.at[k],
            recv_sem=recv_sem.at[k],
            device_id=(row, peer),
            device_id_type=MESH,
        )
        c.start()
        copies.append(c)
    y_ref[me] = block(me)
    for c in copies:
        c.wait()


def mp_scatter(attention, w_out, n):
    vmem = pl.BlockSpec(memory_space=pltpu.VMEM)
    rows = attention.shape[0]
    width = w_out.shape[1] // n
    return pl.pallas_call(
        functools.partial(mp_scatter_kernel, n),
        in_specs=[vmem, vmem],
        out_specs=vmem,
        out_shape=jax.ShapeDtypeStruct((n, rows, width), jnp.bfloat16),
        scratch_shapes=[
            pltpu.VMEM((n, rows, width), jnp.bfloat16),
            pltpu.SemaphoreType.DMA((n,)),
            pltpu.SemaphoreType.DMA((n,)),
        ],
        compiler_params=pltpu.CompilerParams(collective_id=1, has_side_effects=True),
    )(attention, w_out)


def relay_gather_kernel(nx, nz, x_ref, kc_ref, vc_ref, fresh_ref, meta_ref, rot_ref,
                        y_ref, pk_ref, pv_ref, *sems):
    (sx_send, sx_recv, zp_send, zp_recv, zm_send, zm_recv, own_sem,
     bp_send, bp_recv, bm_send, bm_recv, xp_send, xp_recv, xm_send, xm_recv,
     fp_send, fp_recv, fm_send, fm_recv) = sems
    me = lax.axis_index("seq")
    mp = lax.axis_index("mp")
    x = me // nz
    z = me % nz
    up = lax.rem(z + 1, nz)
    down = lax.rem(z + nz - 1, nz)
    right = lax.rem(x + 1, nx)
    left = lax.rem(x + nx - 1, nx)
    barrier = pltpu.get_barrier_semaphore()
    peers = [(lax.rem(x + k, nx) * nz + z, mp) for k in range(1, nx)]
    peers += [(x * nz + up, mp), (x * nz + down, mp)]
    for p in peers:
        pl.semaphore_signal(barrier, inc=1, device_id=p, device_id_type=MESH)
    pl.semaphore_wait(barrier, len(peers))

    def copy(src, dst, send_sem, recv_sem, device):
        c = pltpu.make_async_remote_copy(
            src_ref=src,
            dst_ref=dst,
            send_sem=send_sem,
            recv_sem=recv_sem,
            device_id=device,
            device_id_type=MESH,
        )
        c.start()
        return c

    sent = []
    slot = z * nx + x
    first = [
        copy(x_ref.at[0], y_ref.at[slot, 0], sx_send.at[k], sx_recv.at[k], peers[k - 1])
        for k in range(1, nx)
    ]
    own = pltpu.make_async_copy(x_ref, y_ref.at[slot], own_sem)
    own.start()

    width = kc_ref.shape[1]
    cached = kc_ref[...].astype(jnp.float32)
    turned = pltpu.roll(cached, width // 2, 1)
    shifted = (cached * rot_ref[0:1, :] + turned * rot_ref[1:2, :]).astype(pk_ref.dtype)
    token = lax.broadcasted_iota(jnp.int32, (kc_ref.shape[0], meta_ref.shape[1]), 0)
    chosen = (token == meta_ref[6:7, :]) & (meta_ref[3:4, :] > 0)
    placed = jnp.dot(
        chosen.astype(jnp.bfloat16), fresh_ref[...], preferred_element_type=jnp.float32
    ).astype(pk_ref.dtype)
    replaced = jnp.max(jnp.where(chosen, 1.0, 0.0), axis=1, keepdims=True) > 0.0
    pk_ref[...] = jnp.where(replaced, placed[:, :width], shifted)
    pv_ref[...] = jnp.where(replaced, placed[:, width:], vc_ref[...])

    def x_out(column):
        a = copy(
            y_ref.at[column * nx + x, 1], y_ref.at[column * nx + x, 1],
            xp_send.at[column], xp_recv.at[column], (right * nz + z, mp),
        )
        b = copy(
            y_ref.at[column * nx + x, 1], y_ref.at[column * nx + x, 1],
            xm_send.at[column], xm_recv.at[column], (left * nz + z, mp),
        )
        return [a, b]

    own.wait()
    steps = nz // 2
    half = nx // 2
    zlast = {}
    blast = {}
    xcopies = {}
    for c in first:
        c.wait()
    for t in range(1, steps + 1):
        for sign, send_sem, recv_sem, target, count in (
            (1, bp_send, bp_recv, up, steps),
            (-1, bm_send, bm_recv, down, nz - 1 - steps),
        ):
            if t > count:
                continue
            if t > 1:
                blast[sign].wait_recv()
            column = lax.rem(z - sign * (t - 1) + nz, nz)
            if t > 1:
                xcopies[(sign, t - 1)] = x_out(column)
            elif sign == 1:
                xcopies[(0, 0)] = x_out(column)
            blast[sign] = copy(
                y_ref.at[column * nx + x, 1], y_ref.at[column * nx + x, 1],
                send_sem.at[t], recv_sem.at[t], (x * nz + target, mp),
            )
            sent.append(blast[sign])
        for i in range(nx):
            for sign, send_sem, recv_sem, target in (
                (1, zp_send, zp_recv, up),
                (-1, zm_send, zm_recv, down),
            ):
                if t == steps and (i < half) != (sign == 1):
                    continue
                if t > 1:
                    zlast[(sign, i)].wait_recv()
                column = lax.rem(z - sign * (t - 1) + nz, nz)
                zlast[(sign, i)] = copy(
                    y_ref.at[column * nx + i, 0], y_ref.at[column * nx + i, 0],
                    send_sem.at[t, i], recv_sem.at[t, i], (x * nz + target, mp),
                )
                sent.append(zlast[(sign, i)])
    for sign, count in ((1, steps), (-1, nz - 1 - steps)):
        blast[sign].wait_recv()
        column = lax.rem(z - sign * count + nz, nz)
        xcopies[(sign, count)] = x_out(column)
    order = [(0, 0)] + [(s, t) for t in range(1, steps + 1) for s in (1, -1) if (s, t) in xcopies]
    forwards = []
    for key in order:
        sign, t = key
        column = lax.rem(z - sign * t + nz, nz)
        from_left, from_right = xcopies[key]
        from_left.wait_recv()
        from_right.wait_recv()
        sent += xcopies[key]
    for zc in range(nz):
        if zc < nz // 2:
            forwards.append(
                copy(
                    y_ref.at[zc * nx + left, 1], y_ref.at[zc * nx + left, 1],
                    fp_send.at[zc], fp_recv.at[zc], (right * nz + z, mp),
                )
            )
        else:
            forwards.append(
                copy(
                    y_ref.at[zc * nx + right, 1], y_ref.at[zc * nx + right, 1],
                    fm_send.at[zc], fm_recv.at[zc], (left * nz + z, mp),
                )
            )
    for c in zlast.values():
        c.wait_recv()
    for c in forwards:
        c.wait_recv()
    for c in sent:
        c.wait_send()
    for c in forwards:
        c.wait_send()


def relay_gather(x, kc, vc, fresh, meta, rot, nx, nz):
    assert nx == 4 and nz % 2 == 0
    vmem = pl.BlockSpec(memory_space=pltpu.VMEM)
    steps = nz // 2
    dma = pltpu.SemaphoreType.DMA
    return pl.pallas_call(
        functools.partial(relay_gather_kernel, nx, nz),
        in_specs=[vmem] * 6,
        out_specs=[vmem, vmem, vmem],
        out_shape=[
            jax.ShapeDtypeStruct((nx * nz,) + x.shape, x.dtype),
            jax.ShapeDtypeStruct(kc.shape, kc.dtype),
            jax.ShapeDtypeStruct(vc.shape, vc.dtype),
        ],
        scratch_shapes=[
            dma((nx,)), dma((nx,)),
            dma((steps + 1, nx)), dma((steps + 1, nx)), dma((steps + 1, nx)), dma((steps + 1, nx)),
            dma(()),
            dma((steps + 1,)), dma((steps + 1,)), dma((steps + 1,)), dma((steps + 1,)),
            dma((nz,)), dma((nz,)), dma((nz,)), dma((nz,)),
            dma((nz,)), dma((nz,)), dma((nz,)), dma((nz,)),
        ],
        compiler_params=pltpu.CompilerParams(collective_id=2, has_side_effects=True),
    )(x, kc, vc, fresh, meta, rot)


def merge_piece(a, b, rows):
    af = a.astype(jnp.float32)
    bf = b.astype(jnp.float32)
    m1 = af[rows : rows + 1] + af[rows + 1 : rows + 2]
    l1 = af[rows + 2 : rows + 3] + af[rows + 3 : rows + 4]
    m2 = bf[rows : rows + 1] + bf[rows + 1 : rows + 2]
    l2 = bf[rows + 2 : rows + 3] + bf[rows + 3 : rows + 4]
    top = jnp.maximum(m1, m2)
    s1 = jnp.exp(m1 - top)
    s2 = jnp.exp(m2 - top)
    total = l1 * s1 + l2 * s2
    c1 = jnp.transpose(jnp.broadcast_to(s1, (rows, rows)))
    c2 = jnp.transpose(jnp.broadcast_to(s2, (rows, rows)))
    acc = af[0:rows] * c1 + bf[0:rows] * c2
    sub = lax.broadcasted_iota(jnp.int32, (16, rows), 0)
    top_hi = top.astype(jnp.bfloat16).astype(jnp.float32)
    tot_hi = total.astype(jnp.bfloat16).astype(jnp.float32)
    st = jnp.where(
        sub == 0,
        top,
        jnp.where(
            sub == 1, top - top_hi, jnp.where(sub == 2, total, jnp.where(sub == 3, total - tot_hi, 0.0))
        ),
    )
    return acc.astype(jnp.bfloat16), st.astype(jnp.bfloat16)


def relay_reduce_kernel(
    nx, nz, x_ref, y_ref, rp, rm, bp, bm, col, sp_send, sp_recv, sm_send, sm_recv, sx_send, sx_recv
):
    me = lax.axis_index("seq")
    mp = lax.axis_index("mp")
    x = me // nz
    z = me % nz
    up = lax.rem(z + 1, nz)
    down = lax.rem(z + nz - 1, nz)
    rows = x_ref.shape[2] - 16
    barrier = pltpu.get_barrier_semaphore()
    peers = [(lax.rem(x + k, nx) * nz + z, mp) for k in range(1, nx)]
    peers += [(x * nz + up, mp), (x * nz + down, mp)]
    for p in peers:
        pl.semaphore_signal(barrier, inc=1, device_id=p, device_id_type=MESH)
    pl.semaphore_wait(barrier, len(peers))

    def merge_into(dst, first, second):
        for h in range(2):
            acc, st = merge_piece(first[h], second[h], rows)
            dst[h, 0:rows] = acc
            dst[h, rows:] = st

    steps = nz // 2
    half = nx // 2
    last = {}
    sent = []
    dirs = ((1, rp, bp, sp_send, sp_recv, up), (-1, rm, bm, sm_send, sm_recv, down))
    for t in range(1, steps + 1):
        for i in range(nx):
            for sign, recv_buf, send_buf, send_sem, recv_sem, target in dirs:
                if t == 1 and (i < half) != (sign == 1):
                    continue
                column = lax.rem(z + sign * (steps + 1 - t) + nz, nz)
                own = x_ref.at[i * nz + column]
                if (sign, i) in last:
                    last[(sign, i)].wait_recv()
                    merge_into(send_buf.at[t, i], own, recv_buf.at[t - 1, i])
                    src = send_buf.at[t, i]
                else:
                    src = own
                c = pltpu.make_async_remote_copy(
                    src_ref=src,
                    dst_ref=recv_buf.at[t, i],
                    send_sem=send_sem.at[t, i],
                    recv_sem=recv_sem.at[t, i],
                    device_id=(x * nz + target, mp),
                    device_id_type=MESH,
                )
                c.start()
                last[(sign, i)] = c
                sent.append(c)

    mine = []
    for i in range(nx):
        last[(1, i)].wait_recv()
        last[(-1, i)].wait_recv()
    for k in list(range(1, nx)) + [0]:
        target = lax.rem(x + k, nx)
        merge_into(col.at[target], x_ref.at[target * nz + z], rp.at[steps, target])
        merge_into(col.at[target], col.at[target], rm.at[steps, target])
        if k == 0:
            continue
        c = pltpu.make_async_remote_copy(
            src_ref=col.at[target],
            dst_ref=y_ref.at[x],
            send_sem=sx_send.at[k],
            recv_sem=sx_recv.at[k],
            device_id=(target * nz + z, mp),
            device_id_type=MESH,
        )
        c.start()
        mine.append(c)
    y_ref[x] = col[x]
    for c in sent:
        c.wait_send()
    for c in mine:
        c.wait()


def relay_reduce(parts, nx, nz):
    vmem = pl.BlockSpec(memory_space=pltpu.VMEM)
    steps = nz // 2
    piece = parts.shape[1:]
    return pl.pallas_call(
        functools.partial(relay_reduce_kernel, nx, nz),
        in_specs=[vmem],
        out_specs=vmem,
        out_shape=jax.ShapeDtypeStruct((nx,) + piece, parts.dtype),
        scratch_shapes=[
            pltpu.VMEM((steps + 1, nx) + piece, parts.dtype),
            pltpu.VMEM((steps + 1, nx) + piece, parts.dtype),
            pltpu.VMEM((steps + 1, nx) + piece, parts.dtype),
            pltpu.VMEM((steps + 1, nx) + piece, parts.dtype),
            pltpu.VMEM((nx,) + piece, parts.dtype),
            pltpu.SemaphoreType.DMA((steps + 1, nx)),
            pltpu.SemaphoreType.DMA((steps + 1, nx)),
            pltpu.SemaphoreType.DMA((steps + 1, nx)),
            pltpu.SemaphoreType.DMA((steps + 1, nx)),
            pltpu.SemaphoreType.DMA((nx,)),
            pltpu.SemaphoreType.DMA((nx,)),
        ],
        compiler_params=pltpu.CompilerParams(collective_id=3, has_side_effects=True),
    )(parts)


def local(
    prompt_hidden,
    recompute_hidden,
    key_cache,
    value_cache,
    norm_gain,
    w_query,
    key_weight,
    value_weight,
    w_out,
    passage_owner,
    prompt_slot,
    prompt_length,
    recompute_count,
    recompute_index,
):
    prompt_rows = prompt_hidden.shape[0]
    recompute_rows = recompute_hidden.shape[0]
    query_rows = prompt_rows + recompute_rows
    passage_length = key_cache.shape[1]
    local_heads = w_query.shape[1] // HEAD_SIZE
    n_seq = passage_owner.shape[0]
    me = lax.axis_index("seq")
    scale = 1.0 / math.sqrt(HEAD_SIZE)

    n_mp = w_out.shape[1] // prompt_hidden.shape[1]
    full_rows, meta, lim = mp_gather(
        prompt_hidden, recompute_hidden, passage_owner, prompt_slot, prompt_length,
        recompute_count, recompute_index, n_mp, passage_length, local_heads,
    )
    own_pos = jnp.concatenate([meta[0], meta[1]])
    own_live = jnp.concatenate([meta[2], meta[3]]) > 0
    own_index = meta[6]
    own_shift = meta[7, 0]
    prompt_live = meta[2] > 0
    recompute_live = meta[3] > 0
    normalized_hidden = normalize(full_rows, norm_gain)
    queries = (
        apply_rotation(
            jnp.dot(normalized_hidden, w_query, preferred_element_type=jnp.float32).reshape(
                query_rows, local_heads, HEAD_SIZE
            ),
            own_pos,
        )
        .astype(jnp.bfloat16)
    )
    fresh_keys = (
        apply_rotation(
            jnp.dot(normalized_hidden, key_weight, preferred_element_type=jnp.float32).reshape(
                query_rows, 1, HEAD_SIZE
            ),
            own_pos,
        )
        .astype(jnp.bfloat16)
        .reshape(query_rows, HEAD_SIZE)
    )
    fresh_values = jnp.dot(
        normalized_hidden, value_weight, preferred_element_type=jnp.float32
    ).astype(jnp.bfloat16)

    half_width = HEAD_SIZE // 2
    exponent = jnp.arange(half_width).astype(jnp.float32) * (2.0 / HEAD_SIZE)
    frequency = jnp.exp(-exponent * math.log(500000.0))
    angle = own_shift.astype(jnp.float32) * frequency
    rot = jnp.stack(
        [
            jnp.concatenate([jnp.cos(angle), jnp.cos(angle)]),
            jnp.concatenate([-jnp.sin(angle), jnp.sin(angle)]),
        ]
    )
    fresh_pair = jnp.concatenate([fresh_keys[prompt_rows:], fresh_values[prompt_rows:]], axis=1)

    nx, nz = SEQ_SHAPE
    all_queries, passage_keys, passage_values = relay_gather(
        queries.reshape(2, prompt_rows * local_heads, HEAD_SIZE),
        key_cache[0],
        value_cache[0],
        fresh_pair,
        meta,
        rot,
        nx,
        nz,
    )
    q_blocks = all_queries.reshape(n_seq * 2, prompt_rows * local_heads, HEAD_SIZE)
    packed = passage_attention(nx, nz, meta, q_blocks, passage_keys, passage_values, lim)
    block_rows = packed.shape[1]

    back = relay_reduce(packed.reshape(n_seq, 2, block_rows, HEAD_SIZE), nx, nz)
    n_parts = back.shape[0]
    rows128 = prompt_rows * local_heads
    stats_back = back[:, :, rows128 : rows128 + 4].astype(jnp.float32)
    part_max = (stats_back[:, :, 0] + stats_back[:, :, 1]).reshape(n_parts, query_rows, local_heads)
    part_tot = (stats_back[:, :, 2] + stats_back[:, :, 3]).reshape(n_parts, query_rows, local_heads)
    part_acc = (
        back[:, :, :rows128].reshape(n_parts, query_rows, local_heads, HEAD_SIZE).astype(jnp.float32)
    )

    pq = queries[:prompt_rows].astype(jnp.float32)
    pk = fresh_keys[:prompt_rows].astype(jnp.float32)
    pv = fresh_values[:prompt_rows].astype(jnp.float32)
    ps = jnp.einsum("qhd,kd->qhk", pq, pk) * scale
    jj = jnp.arange(prompt_rows, dtype=jnp.int32)
    pvis = (jj[None, :] <= jj[:, None]) & prompt_live[None, :]
    ps = jnp.where(pvis[:, None, :], ps, NEGATIVE_FLOOR)
    pmax = jnp.max(ps, axis=-1)
    pw = jnp.where(pvis[:, None, :], jnp.exp(ps - pmax[..., None]), 0.0)
    ptot = jnp.sum(pw, axis=-1)
    pacc = jnp.einsum("qhk,kd->qhd", pw.astype(jnp.bfloat16).astype(jnp.float32), pv)
    loc_max = jnp.concatenate(
        [pmax, jnp.full((recompute_rows, local_heads), NEGATIVE_FLOOR, jnp.float32)]
    )
    loc_tot = jnp.concatenate([ptot, jnp.zeros((recompute_rows, local_heads), jnp.float32)])
    loc_acc = jnp.concatenate(
        [pacc, jnp.zeros((recompute_rows, local_heads, HEAD_SIZE), jnp.float32)]
    )

    highest = jnp.maximum(jnp.max(part_max, axis=0), loc_max)
    part_scale = jnp.exp(part_max - highest[None])
    loc_scale = jnp.exp(loc_max - highest)
    accumulated = jnp.sum(part_acc * part_scale[..., None], axis=0) + loc_acc * loc_scale[..., None]
    totals = jnp.sum(part_tot * part_scale, axis=0) + loc_tot * loc_scale
    safe_totals = jnp.where(totals > 0, totals, 1.0)
    attention = jnp.where(
        own_live[:, None, None], accumulated / safe_totals[..., None], 0.0
    ).astype(jnp.bfloat16).reshape(query_rows, local_heads * HEAD_SIZE)
    shares = mp_scatter(attention, w_out, n_mp)
    combined = jnp.sum(shares.astype(jnp.float32), axis=0).astype(jnp.bfloat16)
    return (combined[:prompt_rows], combined[prompt_rows:])


def solution(mesh):
    global SEQ_SHAPE
    sizes = dict(zip(mesh.axis_names, mesh.devices.shape))
    seq_devices = mesh.devices.reshape(sizes["seq"], sizes["mp"])[:, 0]
    xs = sorted({d.coords[0] for d in seq_devices})
    SEQ_SHAPE = (len(xs), sizes["seq"] // len(xs))
    return jax.shard_map(
        local,
        mesh=mesh,
        in_specs=(
            P("seq", "mp"),
            P("seq", "mp"),
            P("seq", None, "mp"),
            P("seq", None, "mp"),
            P(),
            P(None, "mp"),
            P(None, "mp"),
            P(None, "mp"),
            P("mp", None),
            P(),
            P(),
            P(),
            P(),
            P(),
        ),
        out_specs=(P("seq", "mp"), P("seq", "mp")),
        check_vma=False,
    )
```

```python
import functools
import math

import jax
import jax.numpy as jnp
from jax import lax
from jax.experimental import pallas as pl
from jax.experimental.pallas import tpu as pltpu
from jax.sharding import PartitionSpec as P

HEAD_SIZE = 128
NEGATIVE_FLOOR = -1e30


def apply_rotation(vectors, positions):
    half_width = vectors.shape[-1] // 2
    exponent = jnp.arange(half_width).astype(jnp.float32) * (2.0 / vectors.shape[-1])
    frequency = jnp.exp(-exponent * math.log(500000.0))
    angles = positions.astype(jnp.float32)[:, None] * frequency[None, :]
    cosines = jnp.cos(angles)[:, None, :]
    sines = jnp.sin(angles)[:, None, :]
    leading = vectors[..., :half_width]
    trailing = vectors[..., half_width:]
    return jnp.concatenate(
        [leading * cosines - trailing * sines, trailing * cosines + leading * sines], axis=-1
    )


def normalize(rows_in, norm_gain):
    values = rows_in.astype(jnp.float32)
    inverse_rms = lax.rsqrt(jnp.mean(values * values, axis=-1, keepdims=True) + 1e-05)
    return (values * inverse_rms * norm_gain).astype(jnp.bfloat16)


MESH = pl.DeviceIdType.MESH


def passage_kernel(nx, nz, flags_ref, q_ref, k_ref, v_ref, lim_ref, out_ref):
    nb, rows, _ = q_ref.shape
    keys = k_ref.shape[0]
    token = lax.broadcasted_iota(jnp.int32, (rows, keys), 1)
    sub = lax.broadcasted_iota(jnp.int32, (16, rows), 0)

    def split(m_row, l_row):
        m_hi = m_row.astype(jnp.bfloat16).astype(jnp.float32)
        l_hi = l_row.astype(jnp.bfloat16).astype(jnp.float32)
        st = jnp.where(
            sub == 0,
            m_row,
            jnp.where(
                sub == 1,
                m_row - m_hi,
                jnp.where(sub == 2, l_row, jnp.where(sub == 3, l_row - l_hi, 0.0)),
            ),
        )
        return st.astype(jnp.bfloat16)

    out_ref[:, 0:rows] = jnp.zeros((nb, rows, HEAD_SIZE), out_ref.dtype)
    floor = jnp.full((16, rows), NEGATIVE_FLOOR, jnp.float32)
    empty = split(floor, jnp.zeros((16, rows), jnp.float32))
    out_ref[:, rows:] = jnp.broadcast_to(empty[None], (nb, 16, rows))

    def attend(b, masked):
        d = b // 2
        stored = ((d % nz) * nx + d // nz) * 2 + b % 2
        scale = 1.0 / math.sqrt(HEAD_SIZE)
        raw = lax.dot_general(
            q_ref[stored], k_ref[...], (((1,), (1,)), ((), ())), preferred_element_type=jnp.float32
        )
        if masked:
            raw = jnp.where(token <= lim_ref[...], raw, NEGATIVE_FLOOR)
        raw_max = jnp.max(raw, axis=1, keepdims=True)
        weights = jnp.exp((raw - raw_max) * scale)
        totals = jnp.sum(weights, axis=1, keepdims=True)
        out_ref[b, 0:rows] = jnp.dot(
            weights.astype(jnp.bfloat16), v_ref[...], preferred_element_type=jnp.float32
        ).astype(out_ref.dtype)
        lane = lax.broadcasted_iota(jnp.int32, (rows, rows), 1)
        both = jnp.transpose(jnp.where(lane < rows // 2, raw_max * scale, totals))
        out_ref[b, rows:] = split(both[0:16], both[rows // 2 : rows // 2 + 16])

    def body(b, carry):
        flag = flags_ref[4 + b % 2, b // 2]

        @pl.when(flag == 1)
        def _():
            attend(b, False)

        @pl.when(flag == 2)
        def _():
            attend(b, True)

        return carry

    lax.fori_loop(0, nb, body, 0)


def passage_attention(nx, nz, flags, q_blocks, keys, values, lim):
    nb, rows, _ = q_blocks.shape
    vmem = pl.BlockSpec(memory_space=pltpu.VMEM)
    return pl.pallas_call(
        functools.partial(passage_kernel, nx, nz),
        in_specs=[pl.BlockSpec(memory_space=pltpu.SMEM), vmem, vmem, vmem, vmem],
        out_specs=vmem,
        out_shape=jax.ShapeDtypeStruct((nb, rows + 16, HEAD_SIZE), jnp.bfloat16),
    )(flags, q_blocks, keys, values, lim)


def mp_gather_kernel(n, span, p_ref, r_ref, owner_ref, slot_ref, plen_ref, count_ref, index_ref,
                     y_ref, meta_ref, lim_ref, send_sem, recv_sem, local_sem):
    me = lax.axis_index("mp")
    row = lax.axis_index("seq")
    rows, width = p_ref.shape
    barrier = pltpu.get_barrier_semaphore()
    for k in range(1, n):
        peer = lax.rem(me + k, n)
        pl.semaphore_signal(barrier, inc=1, device_id=(row, peer), device_id_type=MESH)
    pl.semaphore_wait(barrier, n - 1)
    cols = pl.ds(pl.multiple_of(me * width, width), width)
    copies = []
    for k in range(1, n):
        peer = lax.rem(me + k, n)
        for part, src in enumerate((p_ref, r_ref)):
            c = pltpu.make_async_remote_copy(
                src_ref=src,
                dst_ref=y_ref.at[pl.ds(part * rows, rows), cols],
                send_sem=send_sem.at[part, k],
                recv_sem=recv_sem.at[part, k],
                device_id=(row, peer),
                device_id_type=MESH,
            )
            c.start()
            copies.append(c)
    own = [
        pltpu.make_async_copy(src, y_ref.at[pl.ds(part * rows, rows), cols], local_sem.at[part])
        for part, src in enumerate((p_ref, r_ref))
    ]
    for c in own:
        c.start()

    f32 = jnp.float32
    owner = owner_ref[...].astype(f32)
    slot = slot_ref[...].astype(f32)
    lane = lax.broadcasted_iota(jnp.int32, owner.shape, 1)
    mine = lane == row

    def pick(v):
        return jnp.sum(jnp.where(mine, v, 0.0), axis=1, keepdims=True)

    own_owner = pick(owner)
    own_slot = pick(slot)
    rank = jnp.sum(jnp.where((owner == own_owner) & (lane < row), 1.0, 0.0), axis=1, keepdims=True)
    held = jnp.sum(jnp.where(owner == own_slot, 1.0, 0.0), axis=1, keepdims=True)
    length = pick(plen_ref[...].astype(f32))
    count = pick(count_ref[...].astype(f32))
    index = index_ref[pl.ds(row, 1), :].astype(f32)
    lanef = lane.astype(f32)
    quantities = [
        held * span + lanef,
        rank * span + index,
        jnp.where(lanef < length, 1.0, 0.0),
        jnp.where(lanef < count, 1.0, 0.0),
        jnp.where(slot == own_owner, 1.0, 0.0),
        jnp.where(mine, 2.0, jnp.where((owner == own_owner) & (lane > row), 1.0, 0.0)),
        index,
        rank * span + 0.0 * lanef,
    ]
    for q, value in enumerate(quantities):
        meta_ref[q : q + 1, :] = value.astype(jnp.int32)
    heads = lim_ref.shape[0] // index.shape[1]
    wide = jnp.broadcast_to(index, (lim_ref.shape[0], index.shape[1]))
    which = lax.broadcasted_iota(jnp.int32, wide.shape, 0) // heads
    pick_lane = lax.broadcasted_iota(jnp.int32, wide.shape, 1)
    lim_ref[...] = jnp.sum(jnp.where(which == pick_lane, wide, 0.0), axis=1, keepdims=True).astype(jnp.int32)

    for c in copies:
        c.wait()
    for c in own:
        c.wait()


def mp_gather(prompt_part, recompute_part, owner, slot, plen, count, index, n, span, heads):
    vmem = pl.BlockSpec(memory_space=pltpu.VMEM)
    rows, width = prompt_part.shape
    small = [v.reshape(1, -1) for v in (owner, slot, plen, count)]
    return pl.pallas_call(
        functools.partial(mp_gather_kernel, n, span),
        in_specs=[vmem] * 7,
        out_specs=[vmem, vmem, vmem],
        out_shape=[
            jax.ShapeDtypeStruct((2 * rows, width * n), prompt_part.dtype),
            jax.ShapeDtypeStruct((8, owner.shape[0]), jnp.int32),
            jax.ShapeDtypeStruct((index.shape[1] * heads, 1), jnp.int32),
        ],
        scratch_shapes=[
            pltpu.SemaphoreType.DMA((2, n)),
            pltpu.SemaphoreType.DMA((2, n)),
            pltpu.SemaphoreType.DMA((2,)),
        ],
        compiler_params=pltpu.CompilerParams(collective_id=0, has_side_effects=True),
    )(prompt_part, recompute_part, *small, index)


def mp_scatter_kernel(n, a_ref, w_ref, y_ref, buf, send_sem, recv_sem):
    me = lax.axis_index("mp")
    row = lax.axis_index("seq")
    width = y_ref.shape[2]
    barrier = pltpu.get_barrier_semaphore()
    for k in range(1, n):
        peer = lax.rem(me + k, n)
        pl.semaphore_signal(barrier, inc=1, device_id=(row, peer), device_id_type=MESH)
    pl.semaphore_wait(barrier, n - 1)

    def block(d):
        cols = pl.ds(pl.multiple_of(d * width, width), width)
        return jnp.dot(a_ref[...], w_ref[:, cols], preferred_element_type=jnp.float32).astype(
            y_ref.dtype
        )

    copies = []
    for k in range(1, n):
        peer = lax.rem(me + k, n)
        buf[k] = block(peer)
        c = pltpu.make_async_remote_copy(
            src_ref=buf.at[k],
            dst_ref=y_ref.at[me],
            send_sem=send_sem.at[k],
            recv_sem=recv_sem.at[k],
            device_id=(row, peer),
            device_id_type=MESH,
        )
        c.start()
        copies.append(c)
    y_ref[me] = block(me)
    for c in copies:
        c.wait()


def mp_scatter(attention, w_out, n):
    vmem = pl.BlockSpec(memory_space=pltpu.VMEM)
    rows = attention.shape[0]
    width = w_out.shape[1] // n
    return pl.pallas_call(
        functools.partial(mp_scatter_kernel, n),
        in_specs=[vmem, vmem],
        out_specs=vmem,
        out_shape=jax.ShapeDtypeStruct((n, rows, width), jnp.bfloat16),
        scratch_shapes=[
            pltpu.VMEM((n, rows, width), jnp.bfloat16),
            pltpu.SemaphoreType.DMA((n,)),
            pltpu.SemaphoreType.DMA((n,)),
        ],
        compiler_params=pltpu.CompilerParams(collective_id=1, has_side_effects=True),
    )(attention, w_out)


def relay_gather_kernel(nx, nz, x_ref, kc_ref, vc_ref, fresh_ref, meta_ref, rot_ref,
                        y_ref, pk_ref, pv_ref, *sems):
    (sx_send, sx_recv, zp_send, zp_recv, zm_send, zm_recv, own_sem,
     bp_send, bp_recv, bm_send, bm_recv, xp_send, xp_recv, xm_send, xm_recv,
     fp_send, fp_recv, fm_send, fm_recv) = sems
    me = lax.axis_index("seq")
    mp = lax.axis_index("mp")
    x = me // nz
    z = me % nz
    up = lax.rem(z + 1, nz)
    down = lax.rem(z + nz - 1, nz)
    right = lax.rem(x + 1, nx)
    left = lax.rem(x + nx - 1, nx)
    barrier = pltpu.get_barrier_semaphore()
    peers = [(lax.rem(x + k, nx) * nz + z, mp) for k in range(1, nx)]
    peers += [(x * nz + up, mp), (x * nz + down, mp)]
    for p in peers:
        pl.semaphore_signal(barrier, inc=1, device_id=p, device_id_type=MESH)
    pl.semaphore_wait(barrier, len(peers))

    def copy(src, dst, send_sem, recv_sem, device):
        c = pltpu.make_async_remote_copy(
            src_ref=src,
            dst_ref=dst,
            send_sem=send_sem,
            recv_sem=recv_sem,
            device_id=device,
            device_id_type=MESH,
        )
        c.start()
        return c

    sent = []
    slot = z * nx + x
    first = [
        copy(x_ref.at[0], y_ref.at[slot, 0], sx_send.at[k], sx_recv.at[k], peers[k - 1])
        for k in range(1, nx)
    ]
    own = pltpu.make_async_copy(x_ref, y_ref.at[slot], own_sem)
    own.start()

    def x_out(column):
        a = copy(
            y_ref.at[column * nx + x, 1], y_ref.at[column * nx + x, 1],
            xp_send.at[column], xp_recv.at[column], (right * nz + z, mp),
        )
        b = copy(
            y_ref.at[column * nx + x, 1], y_ref.at[column * nx + x, 1],
            xm_send.at[column], xm_recv.at[column], (left * nz + z, mp),
        )
        return [a, b]

    own.wait()
    steps = nz // 2
    half = nx // 2
    zlast = {}
    blast = {}
    xcopies = {}
    for c in first:
        c.wait()
    for t in range(1, steps + 1):
        for sign, send_sem, recv_sem, target, count in (
            (1, bp_send, bp_recv, up, steps),
            (-1, bm_send, bm_recv, down, nz - 1 - steps),
        ):
            if t > count:
                continue
            if t > 1:
                blast[sign].wait_recv()
            column = lax.rem(z - sign * (t - 1) + nz, nz)
            if t > 1:
                xcopies[(sign, t - 1)] = x_out(column)
            elif sign == 1:
                xcopies[(0, 0)] = x_out(column)
            blast[sign] = copy(
                y_ref.at[column * nx + x, 1], y_ref.at[column * nx + x, 1],
                send_sem.at[t], recv_sem.at[t], (x * nz + target, mp),
            )
            sent.append(blast[sign])
        for i in range(nx):
            for sign, send_sem, recv_sem, target in (
                (1, zp_send, zp_recv, up),
                (-1, zm_send, zm_recv, down),
            ):
                if t == steps and (i < half) != (sign == 1):
                    continue
                if t > 1:
                    zlast[(sign, i)].wait_recv()
                column = lax.rem(z - sign * (t - 1) + nz, nz)
                zlast[(sign, i)] = copy(
                    y_ref.at[column * nx + i, 0], y_ref.at[column * nx + i, 0],
                    send_sem.at[t, i], recv_sem.at[t, i], (x * nz + target, mp),
                )
                sent.append(zlast[(sign, i)])
    for sign, count in ((1, steps), (-1, nz - 1 - steps)):
        blast[sign].wait_recv()
        column = lax.rem(z - sign * count + nz, nz)
        xcopies[(sign, count)] = x_out(column)
    order = [(0, 0)] + [(s, t) for t in range(1, steps + 1) for s in (1, -1) if (s, t) in xcopies]
    forwards = []
    for key in order:
        sign, t = key
        column = lax.rem(z - sign * t + nz, nz)
        from_left, from_right = xcopies[key]
        from_left.wait_recv()
        from_right.wait_recv()
        sent += xcopies[key]
    for zc in range(nz):
        if zc < nz // 2:
            forwards.append(
                copy(
                    y_ref.at[zc * nx + left, 1], y_ref.at[zc * nx + left, 1],
                    fp_send.at[zc], fp_recv.at[zc], (right * nz + z, mp),
                )
            )
        else:
            forwards.append(
                copy(
                    y_ref.at[zc * nx + right, 1], y_ref.at[zc * nx + right, 1],
                    fm_send.at[zc], fm_recv.at[zc], (left * nz + z, mp),
                )
            )
    width = kc_ref.shape[1]
    cached = kc_ref[...].astype(jnp.float32)
    turned = pltpu.roll(cached, width // 2, 1)
    shifted = (cached * rot_ref[0:1, :] + turned * rot_ref[1:2, :]).astype(pk_ref.dtype)
    token = lax.broadcasted_iota(jnp.int32, (kc_ref.shape[0], meta_ref.shape[1]), 0)
    chosen = (token == meta_ref[6:7, :]) & (meta_ref[3:4, :] > 0)
    placed = jnp.dot(
        chosen.astype(jnp.bfloat16), fresh_ref[...], preferred_element_type=jnp.float32
    ).astype(pk_ref.dtype)
    replaced = jnp.max(jnp.where(chosen, 1.0, 0.0), axis=1, keepdims=True) > 0.0
    pk_ref[...] = jnp.where(replaced, placed[:, :width], shifted)
    pv_ref[...] = jnp.where(replaced, placed[:, width:], vc_ref[...])

    for c in zlast.values():
        c.wait_recv()
    for c in forwards:
        c.wait_recv()
    for c in sent:
        c.wait_send()
    for c in forwards:
        c.wait_send()


def relay_gather(x, kc, vc, fresh, meta, rot, nx, nz):
    assert nx == 4 and nz % 2 == 0
    vmem = pl.BlockSpec(memory_space=pltpu.VMEM)
    steps = nz // 2
    dma = pltpu.SemaphoreType.DMA
    return pl.pallas_call(
        functools.partial(relay_gather_kernel, nx, nz),
        in_specs=[vmem] * 6,
        out_specs=[vmem, vmem, vmem],
        out_shape=[
            jax.ShapeDtypeStruct((nx * nz,) + x.shape, x.dtype),
            jax.ShapeDtypeStruct(kc.shape, kc.dtype),
            jax.ShapeDtypeStruct(vc.shape, vc.dtype),
        ],
        scratch_shapes=[
            dma((nx,)), dma((nx,)),
            dma((steps + 1, nx)), dma((steps + 1, nx)), dma((steps + 1, nx)), dma((steps + 1, nx)),
            dma(()),
            dma((steps + 1,)), dma((steps + 1,)), dma((steps + 1,)), dma((steps + 1,)),
            dma((nz,)), dma((nz,)), dma((nz,)), dma((nz,)),
            dma((nz,)), dma((nz,)), dma((nz,)), dma((nz,)),
        ],
        compiler_params=pltpu.CompilerParams(collective_id=2, has_side_effects=True),
    )(x, kc, vc, fresh, meta, rot)


def merge_piece(a, b, rows):
    af = a.astype(jnp.float32)
    bf = b.astype(jnp.float32)
    m1 = af[rows : rows + 1] + af[rows + 1 : rows + 2]
    l1 = af[rows + 2 : rows + 3] + af[rows + 3 : rows + 4]
    m2 = bf[rows : rows + 1] + bf[rows + 1 : rows + 2]
    l2 = bf[rows + 2 : rows + 3] + bf[rows + 3 : rows + 4]
    top = jnp.maximum(m1, m2)
    s1 = jnp.exp(m1 - top)
    s2 = jnp.exp(m2 - top)
    total = l1 * s1 + l2 * s2
    c1 = jnp.transpose(jnp.broadcast_to(s1, (rows, rows)))
    c2 = jnp.transpose(jnp.broadcast_to(s2, (rows, rows)))
    acc = af[0:rows] * c1 + bf[0:rows] * c2
    sub = lax.broadcasted_iota(jnp.int32, (16, rows), 0)
    top_hi = top.astype(jnp.bfloat16).astype(jnp.float32)
    tot_hi = total.astype(jnp.bfloat16).astype(jnp.float32)
    st = jnp.where(
        sub == 0,
        top,
        jnp.where(
            sub == 1, top - top_hi, jnp.where(sub == 2, total, jnp.where(sub == 3, total - tot_hi, 0.0))
        ),
    )
    return acc.astype(jnp.bfloat16), st.astype(jnp.bfloat16)


def relay_reduce_kernel(
    nx, nz, x_ref, y_ref, rp, rm, bp, bm, col, sp_send, sp_recv, sm_send, sm_recv, sx_send, sx_recv
):
    me = lax.axis_index("seq")
    mp = lax.axis_index("mp")
    x = me // nz
    z = me % nz
    up = lax.rem(z + 1, nz)
    down = lax.rem(z + nz - 1, nz)
    rows = x_ref.shape[2] - 16
    barrier = pltpu.get_barrier_semaphore()
    peers = [(lax.rem(x + k, nx) * nz + z, mp) for k in range(1, nx)]
    peers += [(x * nz + up, mp), (x * nz + down, mp)]
    for p in peers:
        pl.semaphore_signal(barrier, inc=1, device_id=p, device_id_type=MESH)
    pl.semaphore_wait(barrier, len(peers))

    def merge_into(dst, first, second):
        for h in range(2):
            acc, st = merge_piece(first[h], second[h], rows)
            dst[h, 0:rows] = acc
            dst[h, rows:] = st

    steps = nz // 2
    half = nx // 2
    last = {}
    sent = []
    dirs = ((1, rp, bp, sp_send, sp_recv, up), (-1, rm, bm, sm_send, sm_recv, down))
    for t in range(1, steps + 1):
        for i in range(nx):
            for sign, recv_buf, send_buf, send_sem, recv_sem, target in dirs:
                if t == 1 and (i < half) != (sign == 1):
                    continue
                column = lax.rem(z + sign * (steps + 1 - t) + nz, nz)
                own = x_ref.at[i * nz + column]
                if (sign, i) in last:
                    last[(sign, i)].wait_recv()
                    merge_into(send_buf.at[t, i], own, recv_buf.at[t - 1, i])
                    src = send_buf.at[t, i]
                else:
                    src = own
                c = pltpu.make_async_remote_copy(
                    src_ref=src,
                    dst_ref=recv_buf.at[t, i],
                    send_sem=send_sem.at[t, i],
                    recv_sem=recv_sem.at[t, i],
                    device_id=(x * nz + target, mp),
                    device_id_type=MESH,
                )
                c.start()
                last[(sign, i)] = c
                sent.append(c)

    mine = []
    for i in range(nx):
        last[(1, i)].wait_recv()
        last[(-1, i)].wait_recv()
    for k in list(range(1, nx)) + [0]:
        target = lax.rem(x + k, nx)
        merge_into(col.at[target], x_ref.at[target * nz + z], rp.at[steps, target])
        merge_into(col.at[target], col.at[target], rm.at[steps, target])
        if k == 0:
            continue
        c = pltpu.make_async_remote_copy(
            src_ref=col.at[target],
            dst_ref=y_ref.at[x],
            send_sem=sx_send.at[k],
            recv_sem=sx_recv.at[k],
            device_id=(target * nz + z, mp),
            device_id_type=MESH,
        )
        c.start()
        mine.append(c)
    y_ref[x] = col[x]
    for c in sent:
        c.wait_send()
    for c in mine:
        c.wait()


def relay_reduce(parts, nx, nz):
    vmem = pl.BlockSpec(memory_space=pltpu.VMEM)
    steps = nz // 2
    piece = parts.shape[1:]
    return pl.pallas_call(
        functools.partial(relay_reduce_kernel, nx, nz),
        in_specs=[vmem],
        out_specs=vmem,
        out_shape=jax.ShapeDtypeStruct((nx,) + piece, parts.dtype),
        scratch_shapes=[
            pltpu.VMEM((steps + 1, nx) + piece, parts.dtype),
            pltpu.VMEM((steps + 1, nx) + piece, parts.dtype),
            pltpu.VMEM((steps + 1, nx) + piece, parts.dtype),
            pltpu.VMEM((steps + 1, nx) + piece, parts.dtype),
            pltpu.VMEM((nx,) + piece, parts.dtype),
            pltpu.SemaphoreType.DMA((steps + 1, nx)),
            pltpu.SemaphoreType.DMA((steps + 1, nx)),
            pltpu.SemaphoreType.DMA((steps + 1, nx)),
            pltpu.SemaphoreType.DMA((steps + 1, nx)),
            pltpu.SemaphoreType.DMA((nx,)),
            pltpu.SemaphoreType.DMA((nx,)),
        ],
        compiler_params=pltpu.CompilerParams(collective_id=3, has_side_effects=True),
    )(parts)


def local(
    prompt_hidden,
    recompute_hidden,
    key_cache,
    value_cache,
    norm_gain,
    w_query,
    key_weight,
    value_weight,
    w_out,
    passage_owner,
    prompt_slot,
    prompt_length,
    recompute_count,
    recompute_index,
):
    prompt_rows = prompt_hidden.shape[0]
    recompute_rows = recompute_hidden.shape[0]
    query_rows = prompt_rows + recompute_rows
    passage_length = key_cache.shape[1]
    local_heads = w_query.shape[1] // HEAD_SIZE
    n_seq = passage_owner.shape[0]
    me = lax.axis_index("seq")
    scale = 1.0 / math.sqrt(HEAD_SIZE)

    n_mp = w_out.shape[1] // prompt_hidden.shape[1]
    full_rows, meta, lim = mp_gather(
        prompt_hidden, recompute_hidden, passage_owner, prompt_slot, prompt_length,
        recompute_count, recompute_index, n_mp, passage_length, local_heads,
    )
    own_pos = jnp.concatenate([meta[0], meta[1]])
    own_live = jnp.concatenate([meta[2], meta[3]]) > 0
    own_index = meta[6]
    own_shift = meta[7, 0]
    prompt_live = meta[2] > 0
    recompute_live = meta[3] > 0
    normalized_hidden = normalize(full_rows, norm_gain)
    queries = (
        apply_rotation(
            jnp.dot(normalized_hidden, w_query, preferred_element_type=jnp.float32).reshape(
                query_rows, local_heads, HEAD_SIZE
            ),
            own_pos,
        )
        .astype(jnp.bfloat16)
    )
    fresh_keys = (
        apply_rotation(
            jnp.dot(normalized_hidden, key_weight, preferred_element_type=jnp.float32).reshape(
                query_rows, 1, HEAD_SIZE
            ),
            own_pos,
        )
        .astype(jnp.bfloat16)
        .reshape(query_rows, HEAD_SIZE)
    )
    fresh_values = jnp.dot(
        normalized_hidden, value_weight, preferred_element_type=jnp.float32
    ).astype(jnp.bfloat16)

    half_width = HEAD_SIZE // 2
    exponent = jnp.arange(half_width).astype(jnp.float32) * (2.0 / HEAD_SIZE)
    frequency = jnp.exp(-exponent * math.log(500000.0))
    angle = own_shift.astype(jnp.float32) * frequency
    rot = jnp.stack(
        [
            jnp.concatenate([jnp.cos(angle), jnp.cos(angle)]),
            jnp.concatenate([-jnp.sin(angle), jnp.sin(angle)]),
        ]
    )
    fresh_pair = jnp.concatenate([fresh_keys[prompt_rows:], fresh_values[prompt_rows:]], axis=1)

    nx, nz = SEQ_SHAPE
    all_queries, passage_keys, passage_values = relay_gather(
        queries.reshape(2, prompt_rows * local_heads, HEAD_SIZE),
        key_cache[0],
        value_cache[0],
        fresh_pair,
        meta,
        rot,
        nx,
        nz,
    )
    q_blocks = all_queries.reshape(n_seq * 2, prompt_rows * local_heads, HEAD_SIZE)
    packed = passage_attention(nx, nz, meta, q_blocks, passage_keys, passage_values, lim)
    block_rows = packed.shape[1]

    back = relay_reduce(packed.reshape(n_seq, 2, block_rows, HEAD_SIZE), nx, nz)
    n_parts = back.shape[0]
    rows128 = prompt_rows * local_heads
    stats_back = back[:, :, rows128 : rows128 + 4].astype(jnp.float32)
    part_max = (stats_back[:, :, 0] + stats_back[:, :, 1]).reshape(n_parts, query_rows, local_heads)
    part_tot = (stats_back[:, :, 2] + stats_back[:, :, 3]).reshape(n_parts, query_rows, local_heads)
    part_acc = (
        back[:, :, :rows128].reshape(n_parts, query_rows, local_heads, HEAD_SIZE).astype(jnp.float32)
    )

    pq = queries[:prompt_rows].astype(jnp.float32)
    pk = fresh_keys[:prompt_rows].astype(jnp.float32)
    pv = fresh_values[:prompt_rows].astype(jnp.float32)
    ps = jnp.einsum("qhd,kd->qhk", pq, pk) * scale
    jj = jnp.arange(prompt_rows, dtype=jnp.int32)
    pvis = (jj[None, :] <= jj[:, None]) & prompt_live[None, :]
    ps = jnp.where(pvis[:, None, :], ps, NEGATIVE_FLOOR)
    pmax = jnp.max(ps, axis=-1)
    pw = jnp.where(pvis[:, None, :], jnp.exp(ps - pmax[..., None]), 0.0)
    ptot = jnp.sum(pw, axis=-1)
    pacc = jnp.einsum("qhk,kd->qhd", pw.astype(jnp.bfloat16).astype(jnp.float32), pv)
    loc_max = jnp.concatenate(
        [pmax, jnp.full((recompute_rows, local_heads), NEGATIVE_FLOOR, jnp.float32)]
    )
    loc_tot = jnp.concatenate([ptot, jnp.zeros((recompute_rows, local_heads), jnp.float32)])
    loc_acc = jnp.concatenate(
        [pacc, jnp.zeros((recompute_rows, local_heads, HEAD_SIZE), jnp.float32)]
    )

    highest = jnp.maximum(jnp.max(part_max, axis=0), loc_max)
    part_scale = jnp.exp(part_max - highest[None])
    loc_scale = jnp.exp(loc_max - highest)
    accumulated = jnp.sum(part_acc * part_scale[..., None], axis=0) + loc_acc * loc_scale[..., None]
    totals = jnp.sum(part_tot * part_scale, axis=0) + loc_tot * loc_scale
    safe_totals = jnp.where(totals > 0, totals, 1.0)
    attention = jnp.where(
        own_live[:, None, None], accumulated / safe_totals[..., None], 0.0
    ).astype(jnp.bfloat16).reshape(query_rows, local_heads * HEAD_SIZE)
    shares = mp_scatter(attention, w_out, n_mp)
    combined = jnp.sum(shares.astype(jnp.float32), axis=0).astype(jnp.bfloat16)
    return (combined[:prompt_rows], combined[prompt_rows:])


def solution(mesh):
    global SEQ_SHAPE
    sizes = dict(zip(mesh.axis_names, mesh.devices.shape))
    seq_devices = mesh.devices.reshape(sizes["seq"], sizes["mp"])[:, 0]
    xs = sorted({d.coords[0] for d in seq_devices})
    SEQ_SHAPE = (len(xs), sizes["seq"] // len(xs))
    return jax.shard_map(
        local,
        mesh=mesh,
        in_specs=(
            P("seq", "mp"),
            P("seq", "mp"),
            P("seq", None, "mp"),
            P("seq", None, "mp"),
            P(),
            P(None, "mp"),
            P(None, "mp"),
            P(None, "mp"),
            P("mp", None),
            P(),
            P(),
            P(),
            P(),
            P(),
        ),
        out_specs=(P("seq", "mp"), P("seq", "mp")),
        check_vma=False,
    )
```

```python
import functools
import math

import jax
import jax.numpy as jnp
from jax import lax
from jax.experimental import pallas as pl
from jax.experimental.pallas import tpu as pltpu
from jax.sharding import PartitionSpec as P

HEAD_SIZE = 128
NEGATIVE_FLOOR = -1e30


def apply_rotation(vectors, positions):
    half_width = vectors.shape[-1] // 2
    exponent = jnp.arange(half_width).astype(jnp.float32) * (2.0 / vectors.shape[-1])
    frequency = jnp.exp(-exponent * math.log(500000.0))
    angles = positions.astype(jnp.float32)[:, None] * frequency[None, :]
    cosines = jnp.cos(angles)[:, None, :]
    sines = jnp.sin(angles)[:, None, :]
    leading = vectors[..., :half_width]
    trailing = vectors[..., half_width:]
    return jnp.concatenate(
        [leading * cosines - trailing * sines, trailing * cosines + leading * sines], axis=-1
    )


def normalize(rows_in, norm_gain):
    values = rows_in.astype(jnp.float32)
    inverse_rms = lax.rsqrt(jnp.mean(values * values, axis=-1, keepdims=True) + 1e-05)
    return (values * inverse_rms * norm_gain).astype(jnp.bfloat16)


MESH = pl.DeviceIdType.MESH


def passage_kernel(nx, nz, flags_ref, q_ref, k_ref, v_ref, lim_ref, out_ref):
    nb, rows, _ = q_ref.shape
    keys = k_ref.shape[0]
    token = lax.broadcasted_iota(jnp.int32, (rows, keys), 1)
    sub = lax.broadcasted_iota(jnp.int32, (16, rows), 0)

    def split(m_row, l_row):
        m_hi = m_row.astype(jnp.bfloat16).astype(jnp.float32)
        l_hi = l_row.astype(jnp.bfloat16).astype(jnp.float32)
        st = jnp.where(
            sub == 0,
            m_row,
            jnp.where(
                sub == 1,
                m_row - m_hi,
                jnp.where(sub == 2, l_row, jnp.where(sub == 3, l_row - l_hi, 0.0)),
            ),
        )
        return st.astype(jnp.bfloat16)

    out_ref[:, 0:rows] = jnp.zeros((nb, rows, HEAD_SIZE), out_ref.dtype)
    floor = jnp.full((16, rows), NEGATIVE_FLOOR, jnp.float32)
    empty = split(floor, jnp.zeros((16, rows), jnp.float32))
    out_ref[:, rows:] = jnp.broadcast_to(empty[None], (nb, 16, rows))

    def attend(b, masked):
        d = b // 2
        stored = ((d % nz) * nx + d // nz) * 2 + b % 2
        scores = lax.dot_general(
            q_ref[stored], k_ref[...], (((1,), (1,)), ((), ())), preferred_element_type=jnp.float32
        ) * (1.0 / math.sqrt(HEAD_SIZE))
        if masked:
            scores = jnp.where(token <= lim_ref[...], scores, NEGATIVE_FLOOR)
        maxima = jnp.max(scores, axis=1, keepdims=True)
        weights = jnp.exp(scores - maxima)
        totals = jnp.sum(weights, axis=1, keepdims=True)
        out_ref[b, 0:rows] = jnp.dot(
            weights.astype(jnp.bfloat16), v_ref[...], preferred_element_type=jnp.float32
        ).astype(out_ref.dtype)
        m_row = jnp.transpose(jnp.broadcast_to(maxima, (rows, rows)))[0:16]
        l_row = jnp.transpose(jnp.broadcast_to(totals, (rows, rows)))[0:16]
        out_ref[b, rows:] = split(m_row, l_row)

    def body(b, carry):
        flag = flags_ref[4 + b % 2, b // 2]

        @pl.when(flag == 1)
        def _():
            attend(b, False)

        @pl.when(flag == 2)
        def _():
            attend(b, True)

        return carry

    lax.fori_loop(0, nb, body, 0)


def passage_attention(nx, nz, flags, q_blocks, keys, values, lim):
    nb, rows, _ = q_blocks.shape
    vmem = pl.BlockSpec(memory_space=pltpu.VMEM)
    return pl.pallas_call(
        functools.partial(passage_kernel, nx, nz),
        in_specs=[pl.BlockSpec(memory_space=pltpu.SMEM), vmem, vmem, vmem, vmem],
        out_specs=vmem,
        out_shape=jax.ShapeDtypeStruct((nb, rows + 16, HEAD_SIZE), jnp.bfloat16),
    )(flags, q_blocks, keys, values, lim)


def mp_gather_kernel(n, span, p_ref, r_ref, owner_ref, slot_ref, plen_ref, count_ref, index_ref,
                     y_ref, meta_ref, lim_ref, send_sem, recv_sem, local_sem):
    me = lax.axis_index("mp")
    row = lax.axis_index("seq")
    rows, width = p_ref.shape
    barrier = pltpu.get_barrier_semaphore()
    for k in range(1, n):
        peer = lax.rem(me + k, n)
        pl.semaphore_signal(barrier, inc=1, device_id=(row, peer), device_id_type=MESH)
    pl.semaphore_wait(barrier, n - 1)
    cols = pl.ds(pl.multiple_of(me * width, width), width)
    copies = []
    for k in range(1, n):
        peer = lax.rem(me + k, n)
        for part, src in enumerate((p_ref, r_ref)):
            c = pltpu.make_async_remote_copy(
                src_ref=src,
                dst_ref=y_ref.at[pl.ds(part * rows, rows), cols],
                send_sem=send_sem.at[part, k],
                recv_sem=recv_sem.at[part, k],
                device_id=(row, peer),
                device_id_type=MESH,
            )
            c.start()
            copies.append(c)
    own = [
        pltpu.make_async_copy(src, y_ref.at[pl.ds(part * rows, rows), cols], local_sem.at[part])
        for part, src in enumerate((p_ref, r_ref))
    ]
    for c in own:
        c.start()

    f32 = jnp.float32
    owner = owner_ref[...].astype(f32)
    slot = slot_ref[...].astype(f32)
    lane = lax.broadcasted_iota(jnp.int32, owner.shape, 1)
    mine = lane == row

    def pick(v):
        return jnp.sum(jnp.where(mine, v, 0.0), axis=1, keepdims=True)

    own_owner = pick(owner)
    own_slot = pick(slot)
    rank = jnp.sum(jnp.where((owner == own_owner) & (lane < row), 1.0, 0.0), axis=1, keepdims=True)
    held = jnp.sum(jnp.where(owner == own_slot, 1.0, 0.0), axis=1, keepdims=True)
    length = pick(plen_ref[...].astype(f32))
    count = pick(count_ref[...].astype(f32))
    index = index_ref[pl.ds(row, 1), :].astype(f32)
    lanef = lane.astype(f32)
    quantities = [
        held * span + lanef,
        rank * span + index,
        jnp.where(lanef < length, 1.0, 0.0),
        jnp.where(lanef < count, 1.0, 0.0),
        jnp.where(slot == own_owner, 1.0, 0.0),
        jnp.where(mine, 2.0, jnp.where((owner == own_owner) & (lane > row), 1.0, 0.0)),
        index,
        rank * span + 0.0 * lanef,
    ]
    for q, value in enumerate(quantities):
        meta_ref[q : q + 1, :] = value.astype(jnp.int32)
    heads = lim_ref.shape[0] // index.shape[1]
    wide = jnp.broadcast_to(index, (lim_ref.shape[0], index.shape[1]))
    which = lax.broadcasted_iota(jnp.int32, wide.shape, 0) // heads
    pick_lane = lax.broadcasted_iota(jnp.int32, wide.shape, 1)
    lim_ref[...] = jnp.sum(jnp.where(which == pick_lane, wide, 0.0), axis=1, keepdims=True).astype(jnp.int32)

    for c in copies:
        c.wait()
    for c in own:
        c.wait()


def mp_gather(prompt_part, recompute_part, owner, slot, plen, count, index, n, span, heads):
    vmem = pl.BlockSpec(memory_space=pltpu.VMEM)
    rows, width = prompt_part.shape
    small = [v.reshape(1, -1) for v in (owner, slot, plen, count)]
    return pl.pallas_call(
        functools.partial(mp_gather_kernel, n, span),
        in_specs=[vmem] * 7,
        out_specs=[vmem, vmem, vmem],
        out_shape=[
            jax.ShapeDtypeStruct((2 * rows, width * n), prompt_part.dtype),
            jax.ShapeDtypeStruct((8, owner.shape[0]), jnp.int32),
            jax.ShapeDtypeStruct((index.shape[1] * heads, 1), jnp.int32),
        ],
        scratch_shapes=[
            pltpu.SemaphoreType.DMA((2, n)),
            pltpu.SemaphoreType.DMA((2, n)),
            pltpu.SemaphoreType.DMA((2,)),
        ],
        compiler_params=pltpu.CompilerParams(collective_id=0, has_side_effects=True),
    )(prompt_part, recompute_part, *small, index)


def mp_scatter_kernel(n, a_ref, w_ref, y_ref, buf, send_sem, recv_sem):
    me = lax.axis_index("mp")
    row = lax.axis_index("seq")
    width = y_ref.shape[2]
    barrier = pltpu.get_barrier_semaphore()
    for k in range(1, n):
        peer = lax.rem(me + k, n)
        pl.semaphore_signal(barrier, inc=1, device_id=(row, peer), device_id_type=MESH)
    pl.semaphore_wait(barrier, n - 1)

    def block(d):
        cols = pl.ds(pl.multiple_of(d * width, width), width)
        return jnp.dot(a_ref[...], w_ref[:, cols], preferred_element_type=jnp.float32).astype(
            y_ref.dtype
        )

    copies = []
    for k in range(1, n):
        peer = lax.rem(me + k, n)
        buf[k] = block(peer)
        c = pltpu.make_async_remote_copy(
            src_ref=buf.at[k],
            dst_ref=y_ref.at[me],
            send_sem=send_sem.at[k],
            recv_sem=recv_sem.at[k],
            device_id=(row, peer),
            device_id_type=MESH,
        )
        c.start()
        copies.append(c)
    y_ref[me] = block(me)
    for c in copies:
        c.wait()


def mp_scatter(attention, w_out, n):
    vmem = pl.BlockSpec(memory_space=pltpu.VMEM)
    rows = attention.shape[0]
    width = w_out.shape[1] // n
    return pl.pallas_call(
        functools.partial(mp_scatter_kernel, n),
        in_specs=[vmem, vmem],
        out_specs=vmem,
        out_shape=jax.ShapeDtypeStruct((n, rows, width), jnp.bfloat16),
        scratch_shapes=[
            pltpu.VMEM((n, rows, width), jnp.bfloat16),
            pltpu.SemaphoreType.DMA((n,)),
            pltpu.SemaphoreType.DMA((n,)),
        ],
        compiler_params=pltpu.CompilerParams(collective_id=1, has_side_effects=True),
    )(attention, w_out)


def relay_gather_kernel(nx, nz, x_ref, kc_ref, vc_ref, fresh_ref, meta_ref, rot_ref,
                        y_ref, pk_ref, pv_ref, *sems):
    (sx_send, sx_recv, zp_send, zp_recv, zm_send, zm_recv, own_sem,
     bp_send, bp_recv, bm_send, bm_recv, xp_send, xp_recv, xm_send, xm_recv,
     fp_send, fp_recv, fm_send, fm_recv) = sems
    me = lax.axis_index("seq")
    mp = lax.axis_index("mp")
    x = me // nz
    z = me % nz
    up = lax.rem(z + 1, nz)
    down = lax.rem(z + nz - 1, nz)
    right = lax.rem(x + 1, nx)
    left = lax.rem(x + nx - 1, nx)
    barrier = pltpu.get_barrier_semaphore()
    peers = [(lax.rem(x + k, nx) * nz + z, mp) for k in range(1, nx)]
    peers += [(x * nz + up, mp), (x * nz + down, mp)]
    for p in peers:
        pl.semaphore_signal(barrier, inc=1, device_id=p, device_id_type=MESH)
    pl.semaphore_wait(barrier, len(peers))

    def copy(src, dst, send_sem, recv_sem, device):
        c = pltpu.make_async_remote_copy(
            src_ref=src,
            dst_ref=dst,
            send_sem=send_sem,
            recv_sem=recv_sem,
            device_id=device,
            device_id_type=MESH,
        )
        c.start()
        return c

    sent = []
    slot = z * nx + x
    first = [
        copy(x_ref.at[0], y_ref.at[slot, 0], sx_send.at[k], sx_recv.at[k], peers[k - 1])
        for k in range(1, nx)
    ]
    own = pltpu.make_async_copy(x_ref, y_ref.at[slot], own_sem)
    own.start()

    width = kc_ref.shape[1]
    cached = kc_ref[...].astype(jnp.float32)
    turned = pltpu.roll(cached, width // 2, 1)
    shifted = (cached * rot_ref[0:1, :] + turned * rot_ref[1:2, :]).astype(pk_ref.dtype)
    token = lax.broadcasted_iota(jnp.int32, (kc_ref.shape[0], meta_ref.shape[1]), 0)
    chosen = (token == meta_ref[6:7, :]) & (meta_ref[3:4, :] > 0)
    placed = jnp.dot(
        chosen.astype(jnp.bfloat16), fresh_ref[...], preferred_element_type=jnp.float32
    ).astype(pk_ref.dtype)
    replaced = jnp.max(jnp.where(chosen, 1.0, 0.0), axis=1, keepdims=True) > 0.0
    pk_ref[...] = jnp.where(replaced, placed[:, :width], shifted)
    pv_ref[...] = jnp.where(replaced, placed[:, width:], vc_ref[...])

    def x_out(column):
        a = copy(
            y_ref.at[column * nx + x, 1], y_ref.at[column * nx + x, 1],
            xp_send.at[column], xp_recv.at[column], (right * nz + z, mp),
        )
        b = copy(
            y_ref.at[column * nx + x, 1], y_ref.at[column * nx + x, 1],
            xm_send.at[column], xm_recv.at[column], (left * nz + z, mp),
        )
        return [a, b]

    own.wait()
    steps = nz // 2
    half = nx // 2
    zlast = {}
    blast = {}
    xcopies = {}
    for c in first:
        c.wait()
    for t in range(1, steps + 1):
        for sign, send_sem, recv_sem, target, count in (
            (1, bp_send, bp_recv, up, steps),
            (-1, bm_send, bm_recv, down, nz - 1 - steps),
        ):
            if t > count:
                continue
            if t > 1:
                blast[sign].wait_recv()
            column = lax.rem(z - sign * (t - 1) + nz, nz)
            if t > 1:
                xcopies[(sign, t - 1)] = x_out(column)
            elif sign == 1:
                xcopies[(0, 0)] = x_out(column)
            blast[sign] = copy(
                y_ref.at[column * nx + x, 1], y_ref.at[column * nx + x, 1],
                send_sem.at[t], recv_sem.at[t], (x * nz + target, mp),
            )
            sent.append(blast[sign])
        for i in range(nx):
            for sign, send_sem, recv_sem, target in (
                (1, zp_send, zp_recv, up),
                (-1, zm_send, zm_recv, down),
            ):
                if t == steps and (i < half) != (sign == 1):
                    continue
                if t > 1:
                    zlast[(sign, i)].wait_recv()
                column = lax.rem(z - sign * (t - 1) + nz, nz)
                zlast[(sign, i)] = copy(
                    y_ref.at[column * nx + i, 0], y_ref.at[column * nx + i, 0],
                    send_sem.at[t, i], recv_sem.at[t, i], (x * nz + target, mp),
                )
                sent.append(zlast[(sign, i)])
    for sign, count in ((1, steps), (-1, nz - 1 - steps)):
        blast[sign].wait_recv()
        column = lax.rem(z - sign * count + nz, nz)
        xcopies[(sign, count)] = x_out(column)
    order = [(0, 0)] + [(s, t) for t in range(1, steps + 1) for s in (1, -1) if (s, t) in xcopies]
    forwards = []
    for key in order:
        sign, t = key
        column = lax.rem(z - sign * t + nz, nz)
        from_left, from_right = xcopies[key]
        from_left.wait_recv()
        from_right.wait_recv()
        sent += xcopies[key]
    for zc in range(nz):
        if zc < nz // 2:
            forwards.append(
                copy(
                    y_ref.at[zc * nx + left, 1], y_ref.at[zc * nx + left, 1],
                    fp_send.at[zc], fp_recv.at[zc], (right * nz + z, mp),
                )
            )
        else:
            forwards.append(
                copy(
                    y_ref.at[zc * nx + right, 1], y_ref.at[zc * nx + right, 1],
                    fm_send.at[zc], fm_recv.at[zc], (left * nz + z, mp),
                )
            )
    for c in zlast.values():
        c.wait_recv()
    for c in forwards:
        c.wait_recv()
    for c in sent:
        c.wait_send()
    for c in forwards:
        c.wait_send()


def relay_gather(x, kc, vc, fresh, meta, rot, nx, nz):
    assert nx == 4 and nz % 2 == 0
    vmem = pl.BlockSpec(memory_space=pltpu.VMEM)
    steps = nz // 2
    dma = pltpu.SemaphoreType.DMA
    return pl.pallas_call(
        functools.partial(relay_gather_kernel, nx, nz),
        in_specs=[vmem] * 6,
        out_specs=[vmem, vmem, vmem],
        out_shape=[
            jax.ShapeDtypeStruct((nx * nz,) + x.shape, x.dtype),
            jax.ShapeDtypeStruct(kc.shape, kc.dtype),
            jax.ShapeDtypeStruct(vc.shape, vc.dtype),
        ],
        scratch_shapes=[
            dma((nx,)), dma((nx,)),
            dma((steps + 1, nx)), dma((steps + 1, nx)), dma((steps + 1, nx)), dma((steps + 1, nx)),
            dma(()),
            dma((steps + 1,)), dma((steps + 1,)), dma((steps + 1,)), dma((steps + 1,)),
            dma((nz,)), dma((nz,)), dma((nz,)), dma((nz,)),
            dma((nz,)), dma((nz,)), dma((nz,)), dma((nz,)),
        ],
        compiler_params=pltpu.CompilerParams(collective_id=2, has_side_effects=True),
    )(x, kc, vc, fresh, meta, rot)


def merge_piece(a, b, rows):
    af = a.astype(jnp.float32)
    bf = b.astype(jnp.float32)
    m1 = af[rows : rows + 1] + af[rows + 1 : rows + 2]
    l1 = af[rows + 2 : rows + 3] + af[rows + 3 : rows + 4]
    m2 = bf[rows : rows + 1] + bf[rows + 1 : rows + 2]
    l2 = bf[rows + 2 : rows + 3] + bf[rows + 3 : rows + 4]
    top = jnp.maximum(m1, m2)
    s1 = jnp.exp(m1 - top)
    s2 = jnp.exp(m2 - top)
    total = l1 * s1 + l2 * s2
    upper = lax.broadcasted_iota(jnp.int32, (rows, rows), 0) < rows // 2
    both = jnp.transpose(jnp.where(upper, s1, s2))
    c1 = both[:, 0:1]
    c2 = both[:, rows // 2 : rows // 2 + 1]
    acc = af[0:rows] * c1 + bf[0:rows] * c2
    sub = lax.broadcasted_iota(jnp.int32, (16, rows), 0)
    top_hi = top.astype(jnp.bfloat16).astype(jnp.float32)
    tot_hi = total.astype(jnp.bfloat16).astype(jnp.float32)
    st = jnp.where(
        sub == 0,
        top,
        jnp.where(
            sub == 1, top - top_hi, jnp.where(sub == 2, total, jnp.where(sub == 3, total - tot_hi, 0.0))
        ),
    )
    return acc.astype(jnp.bfloat16), st.astype(jnp.bfloat16)


def relay_reduce_kernel(
    nx, nz, x_ref, y_ref, rp, rm, bp, bm, col, sp_send, sp_recv, sm_send, sm_recv, sx_send, sx_recv
):
    me = lax.axis_index("seq")
    mp = lax.axis_index("mp")
    x = me // nz
    z = me % nz
    up = lax.rem(z + 1, nz)
    down = lax.rem(z + nz - 1, nz)
    rows = x_ref.shape[2] - 16
    barrier = pltpu.get_barrier_semaphore()
    peers = [(lax.rem(x + k, nx) * nz + z, mp) for k in range(1, nx)]
    peers += [(x * nz + up, mp), (x * nz + down, mp)]
    for p in peers:
        pl.semaphore_signal(barrier, inc=1, device_id=p, device_id_type=MESH)
    pl.semaphore_wait(barrier, len(peers))

    def merge_into(dst, first, second):
        for h in range(2):
            acc, st = merge_piece(first[h], second[h], rows)
            dst[h, 0:rows] = acc
            dst[h, rows:] = st

    steps = nz // 2
    half = nx // 2
    last = {}
    sent = []
    dirs = ((1, rp, bp, sp_send, sp_recv, up), (-1, rm, bm, sm_send, sm_recv, down))
    for t in range(1, steps + 1):
        for i in range(nx):
            for sign, recv_buf, send_buf, send_sem, recv_sem, target in dirs:
                if t == 1 and (i < half) != (sign == 1):
                    continue
                column = lax.rem(z + sign * (steps + 1 - t) + nz, nz)
                own = x_ref.at[i * nz + column]
                if (sign, i) in last:
                    last[(sign, i)].wait_recv()
                    merge_into(send_buf.at[t, i], own, recv_buf.at[t - 1, i])
                    src = send_buf.at[t, i]
                else:
                    src = own
                c = pltpu.make_async_remote_copy(
                    src_ref=src,
                    dst_ref=recv_buf.at[t, i],
                    send_sem=send_sem.at[t, i],
                    recv_sem=recv_sem.at[t, i],
                    device_id=(x * nz + target, mp),
                    device_id_type=MESH,
                )
                c.start()
                last[(sign, i)] = c
                sent.append(c)

    mine = []
    for i in range(nx):
        last[(1, i)].wait_recv()
        last[(-1, i)].wait_recv()
        merge_into(col.at[i], x_ref.at[i * nz + z], rp.at[steps, i])
        merge_into(col.at[i], col.at[i], rm.at[steps, i])
    for k in range(1, nx):
        target = lax.rem(x + k, nx)
        c = pltpu.make_async_remote_copy(
            src_ref=col.at[target],
            dst_ref=y_ref.at[x],
            send_sem=sx_send.at[k],
            recv_sem=sx_recv.at[k],
            device_id=(target * nz + z, mp),
            device_id_type=MESH,
        )
        c.start()
        mine.append(c)
    y_ref[x] = col[x]
    for c in sent:
        c.wait_send()
    for c in mine:
        c.wait()


def relay_reduce(parts, nx, nz):
    vmem = pl.BlockSpec(memory_space=pltpu.VMEM)
    steps = nz // 2
    piece = parts.shape[1:]
    return pl.pallas_call(
        functools.partial(relay_reduce_kernel, nx, nz),
        in_specs=[vmem],
        out_specs=vmem,
        out_shape=jax.ShapeDtypeStruct((nx,) + piece, parts.dtype),
        scratch_shapes=[
            pltpu.VMEM((steps + 1, nx) + piece, parts.dtype),
            pltpu.VMEM((steps + 1, nx) + piece, parts.dtype),
            pltpu.VMEM((steps + 1, nx) + piece, parts.dtype),
            pltpu.VMEM((steps + 1, nx) + piece, parts.dtype),
            pltpu.VMEM((nx,) + piece, parts.dtype),
            pltpu.SemaphoreType.DMA((steps + 1, nx)),
            pltpu.SemaphoreType.DMA((steps + 1, nx)),
            pltpu.SemaphoreType.DMA((steps + 1, nx)),
            pltpu.SemaphoreType.DMA((steps + 1, nx)),
            pltpu.SemaphoreType.DMA((nx,)),
            pltpu.SemaphoreType.DMA((nx,)),
        ],
        compiler_params=pltpu.CompilerParams(collective_id=3, has_side_effects=True),
    )(parts)


def local(
    prompt_hidden,
    recompute_hidden,
    key_cache,
    value_cache,
    norm_gain,
    w_query,
    key_weight,
    value_weight,
    w_out,
    passage_owner,
    prompt_slot,
    prompt_length,
    recompute_count,
    recompute_index,
):
    prompt_rows = prompt_hidden.shape[0]
    recompute_rows = recompute_hidden.shape[0]
    query_rows = prompt_rows + recompute_rows
    passage_length = key_cache.shape[1]
    local_heads = w_query.shape[1] // HEAD_SIZE
    n_seq = passage_owner.shape[0]
    me = lax.axis_index("seq")
    scale = 1.0 / math.sqrt(HEAD_SIZE)

    n_mp = w_out.shape[1] // prompt_hidden.shape[1]
    full_rows, meta, lim = mp_gather(
        prompt_hidden, recompute_hidden, passage_owner, prompt_slot, prompt_length,
        recompute_count, recompute_index, n_mp, passage_length, local_heads,
    )
    own_pos = jnp.concatenate([meta[0], meta[1]])
    own_live = jnp.concatenate([meta[2], meta[3]]) > 0
    own_index = meta[6]
    own_shift = meta[7, 0]
    prompt_live = meta[2] > 0
    recompute_live = meta[3] > 0
    normalized_hidden = normalize(full_rows, norm_gain)
    queries = (
        apply_rotation(
            jnp.dot(normalized_hidden, w_query, preferred_element_type=jnp.float32).reshape(
                query_rows, local_heads, HEAD_SIZE
            ),
            own_pos,
        )
        .astype(jnp.bfloat16)
    )
    fresh_keys = (
        apply_rotation(
            jnp.dot(normalized_hidden, key_weight, preferred_element_type=jnp.float32).reshape(
                query_rows, 1, HEAD_SIZE
            ),
            own_pos,
        )
        .astype(jnp.bfloat16)
        .reshape(query_rows, HEAD_SIZE)
    )
    fresh_values = jnp.dot(
        normalized_hidden, value_weight, preferred_element_type=jnp.float32
    ).astype(jnp.bfloat16)

    half_width = HEAD_SIZE // 2
    exponent = jnp.arange(half_width).astype(jnp.float32) * (2.0 / HEAD_SIZE)
    frequency = jnp.exp(-exponent * math.log(500000.0))
    angle = own_shift.astype(jnp.float32) * frequency
    rot = jnp.stack(
        [
            jnp.concatenate([jnp.cos(angle), jnp.cos(angle)]),
            jnp.concatenate([-jnp.sin(angle), jnp.sin(angle)]),
        ]
    )
    fresh_pair = jnp.concatenate([fresh_keys[prompt_rows:], fresh_values[prompt_rows:]], axis=1)

    nx, nz = SEQ_SHAPE
    all_queries, passage_keys, passage_values = relay_gather(
        queries.reshape(2, prompt_rows * local_heads, HEAD_SIZE),
        key_cache[0],
        value_cache[0],
        fresh_pair,
        meta,
        rot,
        nx,
        nz,
    )
    q_blocks = all_queries.reshape(n_seq * 2, prompt_rows * local_heads, HEAD_SIZE)
    packed = passage_attention(nx, nz, meta, q_blocks, passage_keys, passage_values, lim)
    block_rows = packed.shape[1]

    back = relay_reduce(packed.reshape(n_seq, 2, block_rows, HEAD_SIZE), nx, nz)
    n_parts = back.shape[0]
    rows128 = prompt_rows * local_heads
    stats_back = back[:, :, rows128 : rows128 + 4].astype(jnp.float32)
    part_max = (stats_back[:, :, 0] + stats_back[:, :, 1]).reshape(n_parts, query_rows, local_heads)
    part_tot = (stats_back[:, :, 2] + stats_back[:, :, 3]).reshape(n_parts, query_rows, local_heads)
    part_acc = (
        back[:, :, :rows128].reshape(n_parts, query_rows, local_heads, HEAD_SIZE).astype(jnp.float32)
    )

    pq = queries[:prompt_rows].astype(jnp.float32)
    pk = fresh_keys[:prompt_rows].astype(jnp.float32)
    pv = fresh_values[:prompt_rows].astype(jnp.float32)
    ps = jnp.einsum("qhd,kd->qhk", pq, pk) * scale
    jj = jnp.arange(prompt_rows, dtype=jnp.int32)
    pvis = (jj[None, :] <= jj[:, None]) & prompt_live[None, :]
    ps = jnp.where(pvis[:, None, :], ps, NEGATIVE_FLOOR)
    pmax = jnp.max(ps, axis=-1)
    pw = jnp.where(pvis[:, None, :], jnp.exp(ps - pmax[..., None]), 0.0)
    ptot = jnp.sum(pw, axis=-1)
    pacc = jnp.einsum("qhk,kd->qhd", pw.astype(jnp.bfloat16).astype(jnp.float32), pv)
    loc_max = jnp.concatenate(
        [pmax, jnp.full((recompute_rows, local_heads), NEGATIVE_FLOOR, jnp.float32)]
    )
    loc_tot = jnp.concatenate([ptot, jnp.zeros((recompute_rows, local_heads), jnp.float32)])
    loc_acc = jnp.concatenate(
        [pacc, jnp.zeros((recompute_rows, local_heads, HEAD_SIZE), jnp.float32)]
    )

    highest = jnp.maximum(jnp.max(part_max, axis=0), loc_max)
    part_scale = jnp.exp(part_max - highest[None])
    loc_scale = jnp.exp(loc_max - highest)
    accumulated = jnp.sum(part_acc * part_scale[..., None], axis=0) + loc_acc * loc_scale[..., None]
    totals = jnp.sum(part_tot * part_scale, axis=0) + loc_tot * loc_scale
    safe_totals = jnp.where(totals > 0, totals, 1.0)
    attention = jnp.where(
        own_live[:, None, None], accumulated / safe_totals[..., None], 0.0
    ).astype(jnp.bfloat16).reshape(query_rows, local_heads * HEAD_SIZE)
    shares = mp_scatter(attention, w_out, n_mp)
    combined = jnp.sum(shares.astype(jnp.float32), axis=0).astype(jnp.bfloat16)
    return (combined[:prompt_rows], combined[prompt_rows:])


def solution(mesh):
    global SEQ_SHAPE
    sizes = dict(zip(mesh.axis_names, mesh.devices.shape))
    seq_devices = mesh.devices.reshape(sizes["seq"], sizes["mp"])[:, 0]
    xs = sorted({d.coords[0] for d in seq_devices})
    SEQ_SHAPE = (len(xs), sizes["seq"] // len(xs))
    return jax.shard_map(
        local,
        mesh=mesh,
        in_specs=(
            P("seq", "mp"),
            P("seq", "mp"),
            P("seq", None, "mp"),
            P("seq", None, "mp"),
            P(),
            P(None, "mp"),
            P(None, "mp"),
            P(None, "mp"),
            P("mp", None),
            P(),
            P(),
            P(),
            P(),
            P(),
        ),
        out_specs=(P("seq", "mp"), P("seq", "mp")),
        check_vma=False,
    )
```

```python
import functools
import math

import jax
import jax.numpy as jnp
from jax import lax
from jax.experimental import pallas as pl
from jax.experimental.pallas import tpu as pltpu
from jax.sharding import PartitionSpec as P

HEAD_SIZE = 128
NEGATIVE_FLOOR = -1e30


def apply_rotation(vectors, positions):
    half_width = vectors.shape[-1] // 2
    exponent = jnp.arange(half_width).astype(jnp.float32) * (2.0 / vectors.shape[-1])
    frequency = jnp.exp(-exponent * math.log(500000.0))
    angles = positions.astype(jnp.float32)[:, None] * frequency[None, :]
    cosines = jnp.cos(angles)[:, None, :]
    sines = jnp.sin(angles)[:, None, :]
    leading = vectors[..., :half_width]
    trailing = vectors[..., half_width:]
    return jnp.concatenate(
        [leading * cosines - trailing * sines, trailing * cosines + leading * sines], axis=-1
    )


def normalize(rows_in, norm_gain):
    values = rows_in.astype(jnp.float32)
    inverse_rms = lax.rsqrt(jnp.mean(values * values, axis=-1, keepdims=True) + 1e-05)
    return (values * inverse_rms * norm_gain).astype(jnp.bfloat16)


MESH = pl.DeviceIdType.MESH


def passage_kernel(nx, nz, flags_ref, q_ref, k_ref, v_ref, lim_ref, out_ref):
    nb, rows, _ = q_ref.shape
    keys = k_ref.shape[0]
    token = lax.broadcasted_iota(jnp.int32, (rows, keys), 1)
    sub = lax.broadcasted_iota(jnp.int32, (16, rows), 0)

    def split(m_row, l_row):
        m_hi = m_row.astype(jnp.bfloat16).astype(jnp.float32)
        l_hi = l_row.astype(jnp.bfloat16).astype(jnp.float32)
        st = jnp.where(
            sub == 0,
            m_row,
            jnp.where(
                sub == 1,
                m_row - m_hi,
                jnp.where(sub == 2, l_row, jnp.where(sub == 3, l_row - l_hi, 0.0)),
            ),
        )
        return st.astype(jnp.bfloat16)

    out_ref[:, 0:rows] = jnp.zeros((nb, rows, HEAD_SIZE), out_ref.dtype)
    floor = jnp.full((16, rows), NEGATIVE_FLOOR, jnp.float32)
    empty = split(floor, jnp.zeros((16, rows), jnp.float32))
    out_ref[:, rows:] = jnp.broadcast_to(empty[None], (nb, 16, rows))

    def attend(b, masked):
        d = b // 2
        stored = ((d % nz) * nx + d // nz) * 2 + b % 2
        scores = lax.dot_general(
            q_ref[stored], k_ref[...], (((1,), (1,)), ((), ())), preferred_element_type=jnp.float32
        ) * (1.0 / math.sqrt(HEAD_SIZE))
        if masked:
            scores = jnp.where(token <= lim_ref[...], scores, NEGATIVE_FLOOR)
        maxima = jnp.max(scores, axis=1, keepdims=True)
        weights = jnp.exp(scores - maxima)
        totals = jnp.sum(weights, axis=1, keepdims=True)
        out_ref[b, 0:rows] = jnp.dot(
            weights.astype(jnp.bfloat16), v_ref[...], preferred_element_type=jnp.float32
        ).astype(out_ref.dtype)
        m_row = jnp.transpose(jnp.broadcast_to(maxima, (rows, rows)))[0:16]
        l_row = jnp.transpose(jnp.broadcast_to(totals, (rows, rows)))[0:16]
        out_ref[b, rows:] = split(m_row, l_row)

    def body(b, carry):
        flag = flags_ref[4 + b % 2, b // 2]

        @pl.when(flag == 1)
        def _():
            attend(b, False)

        @pl.when(flag == 2)
        def _():
            attend(b, True)

        return carry

    lax.fori_loop(0, nb, body, 0)


def passage_attention(nx, nz, flags, q_blocks, keys, values, lim):
    nb, rows, _ = q_blocks.shape
    vmem = pl.BlockSpec(memory_space=pltpu.VMEM)
    return pl.pallas_call(
        functools.partial(passage_kernel, nx, nz),
        in_specs=[pl.BlockSpec(memory_space=pltpu.SMEM), vmem, vmem, vmem, vmem],
        out_specs=vmem,
        out_shape=jax.ShapeDtypeStruct((nb, rows + 16, HEAD_SIZE), jnp.bfloat16),
    )(flags, q_blocks, keys, values, lim)


def mp_gather_kernel(n, span, p_ref, r_ref, owner_ref, slot_ref, plen_ref, count_ref, index_ref,
                     y_ref, meta_ref, lim_ref, send_sem, recv_sem, local_sem):
    me = lax.axis_index("mp")
    row = lax.axis_index("seq")
    rows, width = p_ref.shape
    barrier = pltpu.get_barrier_semaphore()
    for k in range(1, n):
        peer = lax.rem(me + k, n)
        pl.semaphore_signal(barrier, inc=1, device_id=(row, peer), device_id_type=MESH)
    pl.semaphore_wait(barrier, n - 1)
    cols = pl.ds(pl.multiple_of(me * width, width), width)
    copies = []
    for k in range(1, n):
        peer = lax.rem(me + k, n)
        for part, src in enumerate((p_ref, r_ref)):
            c = pltpu.make_async_remote_copy(
                src_ref=src,
                dst_ref=y_ref.at[pl.ds(part * rows, rows), cols],
                send_sem=send_sem.at[part, k],
                recv_sem=recv_sem.at[part, k],
                device_id=(row, peer),
                device_id_type=MESH,
            )
            c.start()
            copies.append(c)
    own = [
        pltpu.make_async_copy(src, y_ref.at[pl.ds(part * rows, rows), cols], local_sem.at[part])
        for part, src in enumerate((p_ref, r_ref))
    ]
    for c in own:
        c.start()

    f32 = jnp.float32
    owner = owner_ref[...].astype(f32)
    slot = slot_ref[...].astype(f32)
    lane = lax.broadcasted_iota(jnp.int32, owner.shape, 1)
    mine = lane == row

    def pick(v):
        return jnp.sum(jnp.where(mine, v, 0.0), axis=1, keepdims=True)

    own_owner = pick(owner)
    own_slot = pick(slot)
    rank = jnp.sum(jnp.where((owner == own_owner) & (lane < row), 1.0, 0.0), axis=1, keepdims=True)
    held = jnp.sum(jnp.where(owner == own_slot, 1.0, 0.0), axis=1, keepdims=True)
    length = pick(plen_ref[...].astype(f32))
    count = pick(count_ref[...].astype(f32))
    index = index_ref[pl.ds(row, 1), :].astype(f32)
    lanef = lane.astype(f32)
    quantities = [
        held * span + lanef,
        rank * span + index,
        jnp.where(lanef < length, 1.0, 0.0),
        jnp.where(lanef < count, 1.0, 0.0),
        jnp.where(slot == own_owner, 1.0, 0.0),
        jnp.where(mine, 2.0, jnp.where((owner == own_owner) & (lane > row), 1.0, 0.0)),
        index,
        rank * span + 0.0 * lanef,
    ]
    for q, value in enumerate(quantities):
        meta_ref[q : q + 1, :] = value.astype(jnp.int32)
    heads = lim_ref.shape[0] // index.shape[1]
    wide = jnp.broadcast_to(index, (lim_ref.shape[0], index.shape[1]))
    which = lax.broadcasted_iota(jnp.int32, wide.shape, 0) // heads
    pick_lane = lax.broadcasted_iota(jnp.int32, wide.shape, 1)
    lim_ref[...] = jnp.sum(jnp.where(which == pick_lane, wide, 0.0), axis=1, keepdims=True).astype(jnp.int32)

    for c in copies:
        c.wait()
    for c in own:
        c.wait()


def mp_gather(prompt_part, recompute_part, owner, slot, plen, count, index, n, span, heads):
    vmem = pl.BlockSpec(memory_space=pltpu.VMEM)
    rows, width = prompt_part.shape
    small = [v.reshape(1, -1) for v in (owner, slot, plen, count)]
    return pl.pallas_call(
        functools.partial(mp_gather_kernel, n, span),
        in_specs=[vmem] * 7,
        out_specs=[vmem, vmem, vmem],
        out_shape=[
            jax.ShapeDtypeStruct((2 * rows, width * n), prompt_part.dtype),
            jax.ShapeDtypeStruct((8, owner.shape[0]), jnp.int32),
            jax.ShapeDtypeStruct((index.shape[1] * heads, 1), jnp.int32),
        ],
        scratch_shapes=[
            pltpu.SemaphoreType.DMA((2, n)),
            pltpu.SemaphoreType.DMA((2, n)),
            pltpu.SemaphoreType.DMA((2,)),
        ],
        compiler_params=pltpu.CompilerParams(collective_id=0, has_side_effects=True),
    )(prompt_part, recompute_part, *small, index)


def mp_scatter_kernel(n, a_ref, w_ref, y_ref, buf, send_sem, recv_sem):
    me = lax.axis_index("mp")
    row = lax.axis_index("seq")
    width = y_ref.shape[2]
    barrier = pltpu.get_barrier_semaphore()
    for k in range(1, n):
        peer = lax.rem(me + k, n)
        pl.semaphore_signal(barrier, inc=1, device_id=(row, peer), device_id_type=MESH)
    pl.semaphore_wait(barrier, n - 1)

    def block(d):
        cols = pl.ds(pl.multiple_of(d * width, width), width)
        return jnp.dot(a_ref[...], w_ref[:, cols], preferred_element_type=jnp.float32).astype(
            y_ref.dtype
        )

    copies = []
    for k in range(1, n):
        peer = lax.rem(me + k, n)
        buf[k] = block(peer)
        c = pltpu.make_async_remote_copy(
            src_ref=buf.at[k],
            dst_ref=y_ref.at[me],
            send_sem=send_sem.at[k],
            recv_sem=recv_sem.at[k],
            device_id=(row, peer),
            device_id_type=MESH,
        )
        c.start()
        copies.append(c)
    y_ref[me] = block(me)
    for c in copies:
        c.wait()


def mp_scatter(attention, w_out, n):
    vmem = pl.BlockSpec(memory_space=pltpu.VMEM)
    rows = attention.shape[0]
    width = w_out.shape[1] // n
    return pl.pallas_call(
        functools.partial(mp_scatter_kernel, n),
        in_specs=[vmem, vmem],
        out_specs=vmem,
        out_shape=jax.ShapeDtypeStruct((n, rows, width), jnp.bfloat16),
        scratch_shapes=[
            pltpu.VMEM((n, rows, width), jnp.bfloat16),
            pltpu.SemaphoreType.DMA((n,)),
            pltpu.SemaphoreType.DMA((n,)),
        ],
        compiler_params=pltpu.CompilerParams(collective_id=1, has_side_effects=True),
    )(attention, w_out)


def relay_gather_kernel(nx, nz, x_ref, kc_ref, vc_ref, fresh_ref, meta_ref, rot_ref,
                        y_ref, pk_ref, pv_ref, *sems):
    (sx_send, sx_recv, zp_send, zp_recv, zm_send, zm_recv, own_sem,
     bp_send, bp_recv, bm_send, bm_recv, xp_send, xp_recv, xm_send, xm_recv,
     fp_send, fp_recv, fm_send, fm_recv) = sems
    me = lax.axis_index("seq")
    mp = lax.axis_index("mp")
    x = me // nz
    z = me % nz
    up = lax.rem(z + 1, nz)
    down = lax.rem(z + nz - 1, nz)
    right = lax.rem(x + 1, nx)
    left = lax.rem(x + nx - 1, nx)
    barrier = pltpu.get_barrier_semaphore()
    peers = [(lax.rem(x + k, nx) * nz + z, mp) for k in range(1, nx)]
    peers += [(x * nz + up, mp), (x * nz + down, mp)]
    for p in peers:
        pl.semaphore_signal(barrier, inc=1, device_id=p, device_id_type=MESH)
    pl.semaphore_wait(barrier, len(peers))

    def copy(src, dst, send_sem, recv_sem, device):
        c = pltpu.make_async_remote_copy(
            src_ref=src,
            dst_ref=dst,
            send_sem=send_sem,
            recv_sem=recv_sem,
            device_id=device,
            device_id_type=MESH,
        )
        c.start()
        return c

    sent = []
    slot = z * nx + x
    first = [
        copy(x_ref.at[0], y_ref.at[slot, 0], sx_send.at[k], sx_recv.at[k], peers[k - 1])
        for k in range(1, nx)
    ]
    own = pltpu.make_async_copy(x_ref, y_ref.at[slot], own_sem)
    own.start()

    width = kc_ref.shape[1]
    cached = kc_ref[...].astype(jnp.float32)
    turned = pltpu.roll(cached, width // 2, 1)
    shifted = (cached * rot_ref[0:1, :] + turned * rot_ref[1:2, :]).astype(pk_ref.dtype)
    token = lax.broadcasted_iota(jnp.int32, (kc_ref.shape[0], meta_ref.shape[1]), 0)
    chosen = (token == meta_ref[6:7, :]) & (meta_ref[3:4, :] > 0)
    placed = jnp.dot(
        chosen.astype(jnp.bfloat16), fresh_ref[...], preferred_element_type=jnp.float32
    ).astype(pk_ref.dtype)
    replaced = jnp.max(jnp.where(chosen, 1.0, 0.0), axis=1, keepdims=True) > 0.0
    pk_ref[...] = jnp.where(replaced, placed[:, :width], shifted)
    pv_ref[...] = jnp.where(replaced, placed[:, width:], vc_ref[...])

    def x_out(column):
        a = copy(
            y_ref.at[column * nx + x, 1], y_ref.at[column * nx + x, 1],
            xp_send.at[column], xp_recv.at[column], (right * nz + z, mp),
        )
        b = copy(
            y_ref.at[column * nx + x, 1], y_ref.at[column * nx + x, 1],
            xm_send.at[column], xm_recv.at[column], (left * nz + z, mp),
        )
        return [a, b]

    own.wait()
    steps = nz // 2
    half = nx // 2
    zlast = {}
    blast = {}
    xcopies = {}
    for c in first:
        c.wait()
    for t in range(1, steps + 1):
        for sign, send_sem, recv_sem, target, count in (
            (1, bp_send, bp_recv, up, steps),
            (-1, bm_send, bm_recv, down, nz - 1 - steps),
        ):
            if t > count:
                continue
            if t > 1:
                blast[sign].wait_recv()
            column = lax.rem(z - sign * (t - 1) + nz, nz)
            if t > 1:
                xcopies[(sign, t - 1)] = x_out(column)
            elif sign == 1:
                xcopies[(0, 0)] = x_out(column)
            blast[sign] = copy(
                y_ref.at[column * nx + x, 1], y_ref.at[column * nx + x, 1],
                send_sem.at[t], recv_sem.at[t], (x * nz + target, mp),
            )
            sent.append(blast[sign])
        for i in range(nx):
            for sign, send_sem, recv_sem, target in (
                (1, zp_send, zp_recv, up),
                (-1, zm_send, zm_recv, down),
            ):
                if t == steps and (i < half) != (sign == 1):
                    continue
                if t > 1:
                    zlast[(sign, i)].wait_recv()
                column = lax.rem(z - sign * (t - 1) + nz, nz)
                zlast[(sign, i)] = copy(
                    y_ref.at[column * nx + i, 0], y_ref.at[column * nx + i, 0],
                    send_sem.at[t, i], recv_sem.at[t, i], (x * nz + target, mp),
                )
                sent.append(zlast[(sign, i)])
    for sign, count in ((1, steps), (-1, nz - 1 - steps)):
        blast[sign].wait_recv()
        column = lax.rem(z - sign * count + nz, nz)
        xcopies[(sign, count)] = x_out(column)
    order = [(0, 0)] + [(s, t) for t in range(1, steps + 1) for s in (1, -1) if (s, t) in xcopies]
    forwards = []
    for key in order:
        sign, t = key
        column = lax.rem(z - sign * t + nz, nz)
        from_left, from_right = xcopies[key]
        from_left.wait_recv()
        from_right.wait_recv()
        sent += xcopies[key]
    for zc in range(nz):
        if zc < nz // 2:
            forwards.append(
                copy(
                    y_ref.at[zc * nx + left, 1], y_ref.at[zc * nx + left, 1],
                    fp_send.at[zc], fp_recv.at[zc], (right * nz + z, mp),
                )
            )
        else:
            forwards.append(
                copy(
                    y_ref.at[zc * nx + right, 1], y_ref.at[zc * nx + right, 1],
                    fm_send.at[zc], fm_recv.at[zc], (left * nz + z, mp),
                )
            )
    for c in zlast.values():
        c.wait_recv()
    for c in forwards:
        c.wait_recv()
    for c in sent:
        c.wait_send()
    for c in forwards:
        c.wait_send()


def relay_gather(x, kc, vc, fresh, meta, rot, nx, nz):
    assert nx == 4 and nz % 2 == 0
    vmem = pl.BlockSpec(memory_space=pltpu.VMEM)
    steps = nz // 2
    dma = pltpu.SemaphoreType.DMA
    return pl.pallas_call(
        functools.partial(relay_gather_kernel, nx, nz),
        in_specs=[vmem] * 6,
        out_specs=[vmem, vmem, vmem],
        out_shape=[
            jax.ShapeDtypeStruct((nx * nz,) + x.shape, x.dtype),
            jax.ShapeDtypeStruct(kc.shape, kc.dtype),
            jax.ShapeDtypeStruct(vc.shape, vc.dtype),
        ],
        scratch_shapes=[
            dma((nx,)), dma((nx,)),
            dma((steps + 1, nx)), dma((steps + 1, nx)), dma((steps + 1, nx)), dma((steps + 1, nx)),
            dma(()),
            dma((steps + 1,)), dma((steps + 1,)), dma((steps + 1,)), dma((steps + 1,)),
            dma((nz,)), dma((nz,)), dma((nz,)), dma((nz,)),
            dma((nz,)), dma((nz,)), dma((nz,)), dma((nz,)),
        ],
        compiler_params=pltpu.CompilerParams(collective_id=2, has_side_effects=True),
    )(x, kc, vc, fresh, meta, rot)


def merge_piece(a, b, rows):
    af = a.astype(jnp.float32)
    bf = b.astype(jnp.float32)
    m1 = af[rows : rows + 1] + af[rows + 1 : rows + 2]
    l1 = af[rows + 2 : rows + 3] + af[rows + 3 : rows + 4]
    m2 = bf[rows : rows + 1] + bf[rows + 1 : rows + 2]
    l2 = bf[rows + 2 : rows + 3] + bf[rows + 3 : rows + 4]
    top = jnp.maximum(m1, m2)
    s1 = jnp.exp(m1 - top)
    s2 = jnp.exp(m2 - top)
    total = l1 * s1 + l2 * s2
    upper = lax.broadcasted_iota(jnp.int32, (rows, rows), 0) < rows // 2
    both = jnp.transpose(jnp.where(upper, s1, s2))
    c1 = both[:, 0:1]
    c2 = both[:, rows // 2 : rows // 2 + 1]
    acc = af[0:rows] * c1 + bf[0:rows] * c2
    sub = lax.broadcasted_iota(jnp.int32, (16, rows), 0)
    top_hi = top.astype(jnp.bfloat16).astype(jnp.float32)
    tot_hi = total.astype(jnp.bfloat16).astype(jnp.float32)
    st = jnp.where(
        sub == 0,
        top,
        jnp.where(
            sub == 1, top - top_hi, jnp.where(sub == 2, total, jnp.where(sub == 3, total - tot_hi, 0.0))
        ),
    )
    return acc.astype(jnp.bfloat16), st.astype(jnp.bfloat16)


def merge_three(a, b, c, rows):
    parts = [p.astype(jnp.float32) for p in (a, b, c)]
    maxima = [p[rows : rows + 1] + p[rows + 1 : rows + 2] for p in parts]
    totals = [p[rows + 2 : rows + 3] + p[rows + 3 : rows + 4] for p in parts]
    top = jnp.maximum(jnp.maximum(maxima[0], maxima[1]), maxima[2])
    scales = [jnp.exp(m - top) for m in maxima]
    total = totals[0] * scales[0] + totals[1] * scales[1] + totals[2] * scales[2]
    third = rows // 3
    sub_all = lax.broadcasted_iota(jnp.int32, (rows, rows), 0)
    cols = jnp.transpose(
        jnp.where(sub_all < third, scales[0], jnp.where(sub_all < 2 * third, scales[1], scales[2]))
    )
    acc = (
        parts[0][0:rows] * cols[:, 0:1]
        + parts[1][0:rows] * cols[:, third : third + 1]
        + parts[2][0:rows] * cols[:, 2 * third : 2 * third + 1]
    )
    sub = lax.broadcasted_iota(jnp.int32, (16, rows), 0)
    top_hi = top.astype(jnp.bfloat16).astype(jnp.float32)
    tot_hi = total.astype(jnp.bfloat16).astype(jnp.float32)
    st = jnp.where(
        sub == 0,
        top,
        jnp.where(
            sub == 1, top - top_hi, jnp.where(sub == 2, total, jnp.where(sub == 3, total - tot_hi, 0.0))
        ),
    )
    return acc.astype(jnp.bfloat16), st.astype(jnp.bfloat16)


def relay_reduce_kernel(
    nx, nz, x_ref, y_ref, rp, rm, bp, bm, col, sp_send, sp_recv, sm_send, sm_recv, sx_send, sx_recv
):
    me = lax.axis_index("seq")
    mp = lax.axis_index("mp")
    x = me // nz
    z = me % nz
    up = lax.rem(z + 1, nz)
    down = lax.rem(z + nz - 1, nz)
    rows = x_ref.shape[2] - 16
    barrier = pltpu.get_barrier_semaphore()
    peers = [(lax.rem(x + k, nx) * nz + z, mp) for k in range(1, nx)]
    peers += [(x * nz + up, mp), (x * nz + down, mp)]
    for p in peers:
        pl.semaphore_signal(barrier, inc=1, device_id=p, device_id_type=MESH)
    pl.semaphore_wait(barrier, len(peers))

    def merge_into(dst, first, second):
        for h in range(2):
            acc, st = merge_piece(first[h], second[h], rows)
            dst[h, 0:rows] = acc
            dst[h, rows:] = st

    steps = nz // 2
    half = nx // 2
    last = {}
    sent = []
    dirs = ((1, rp, bp, sp_send, sp_recv, up), (-1, rm, bm, sm_send, sm_recv, down))
    for t in range(1, steps + 1):
        for i in range(nx):
            for sign, recv_buf, send_buf, send_sem, recv_sem, target in dirs:
                if t == 1 and (i < half) != (sign == 1):
                    continue
                column = lax.rem(z + sign * (steps + 1 - t) + nz, nz)
                own = x_ref.at[i * nz + column]
                if (sign, i) in last:
                    last[(sign, i)].wait_recv()
                    merge_into(send_buf.at[t, i], own, recv_buf.at[t - 1, i])
                    src = send_buf.at[t, i]
                else:
                    src = own
                c = pltpu.make_async_remote_copy(
                    src_ref=src,
                    dst_ref=recv_buf.at[t, i],
                    send_sem=send_sem.at[t, i],
                    recv_sem=recv_sem.at[t, i],
                    device_id=(x * nz + target, mp),
                    device_id_type=MESH,
                )
                c.start()
                last[(sign, i)] = c
                sent.append(c)

    mine = []
    for i in range(nx):
        last[(1, i)].wait_recv()
        last[(-1, i)].wait_recv()
        for h in range(2):
            acc, st = merge_three(
                x_ref.at[i * nz + z][h], rp.at[steps, i][h], rm.at[steps, i][h], rows
            )
            col[i, h, 0:rows] = acc
            col[i, h, rows:] = st
    for k in range(1, nx):
        target = lax.rem(x + k, nx)
        c = pltpu.make_async_remote_copy(
            src_ref=col.at[target],
            dst_ref=y_ref.at[x],
            send_sem=sx_send.at[k],
            recv_sem=sx_recv.at[k],
            device_id=(target * nz + z, mp),
            device_id_type=MESH,
        )
        c.start()
        mine.append(c)
    y_ref[x] = col[x]
    for c in sent:
        c.wait_send()
    for c in mine:
        c.wait()


def relay_reduce(parts, nx, nz):
    vmem = pl.BlockSpec(memory_space=pltpu.VMEM)
    steps = nz // 2
    piece = parts.shape[1:]
    return pl.pallas_call(
        functools.partial(relay_reduce_kernel, nx, nz),
        in_specs=[vmem],
        out_specs=vmem,
        out_shape=jax.ShapeDtypeStruct((nx,) + piece, parts.dtype),
        scratch_shapes=[
            pltpu.VMEM((steps + 1, nx) + piece, parts.dtype),
            pltpu.VMEM((steps + 1, nx) + piece, parts.dtype),
            pltpu.VMEM((steps + 1, nx) + piece, parts.dtype),
            pltpu.VMEM((steps + 1, nx) + piece, parts.dtype),
            pltpu.VMEM((nx,) + piece, parts.dtype),
            pltpu.SemaphoreType.DMA((steps + 1, nx)),
            pltpu.SemaphoreType.DMA((steps + 1, nx)),
            pltpu.SemaphoreType.DMA((steps + 1, nx)),
            pltpu.SemaphoreType.DMA((steps + 1, nx)),
            pltpu.SemaphoreType.DMA((nx,)),
            pltpu.SemaphoreType.DMA((nx,)),
        ],
        compiler_params=pltpu.CompilerParams(collective_id=3, has_side_effects=True),
    )(parts)


def local(
    prompt_hidden,
    recompute_hidden,
    key_cache,
    value_cache,
    norm_gain,
    w_query,
    key_weight,
    value_weight,
    w_out,
    passage_owner,
    prompt_slot,
    prompt_length,
    recompute_count,
    recompute_index,
):
    prompt_rows = prompt_hidden.shape[0]
    recompute_rows = recompute_hidden.shape[0]
    query_rows = prompt_rows + recompute_rows
    passage_length = key_cache.shape[1]
    local_heads = w_query.shape[1] // HEAD_SIZE
    n_seq = passage_owner.shape[0]
    me = lax.axis_index("seq")
    scale = 1.0 / math.sqrt(HEAD_SIZE)

    n_mp = w_out.shape[1] // prompt_hidden.shape[1]
    full_rows, meta, lim = mp_gather(
        prompt_hidden, recompute_hidden, passage_owner, prompt_slot, prompt_length,
        recompute_count, recompute_index, n_mp, passage_length, local_heads,
    )
    own_pos = jnp.concatenate([meta[0], meta[1]])
    own_live = jnp.concatenate([meta[2], meta[3]]) > 0
    own_index = meta[6]
    own_shift = meta[7, 0]
    prompt_live = meta[2] > 0
    recompute_live = meta[3] > 0
    normalized_hidden = normalize(full_rows, norm_gain)
    queries = (
        apply_rotation(
            jnp.dot(normalized_hidden, w_query, preferred_element_type=jnp.float32).reshape(
                query_rows, local_heads, HEAD_SIZE
            ),
            own_pos,
        )
        .astype(jnp.bfloat16)
    )
    fresh_keys = (
        apply_rotation(
            jnp.dot(normalized_hidden, key_weight, preferred_element_type=jnp.float32).reshape(
                query_rows, 1, HEAD_SIZE
            ),
            own_pos,
        )
        .astype(jnp.bfloat16)
        .reshape(query_rows, HEAD_SIZE)
    )
    fresh_values = jnp.dot(
        normalized_hidden, value_weight, preferred_element_type=jnp.float32
    ).astype(jnp.bfloat16)

    half_width = HEAD_SIZE // 2
    exponent = jnp.arange(half_width).astype(jnp.float32) * (2.0 / HEAD_SIZE)
    frequency = jnp.exp(-exponent * math.log(500000.0))
    angle = own_shift.astype(jnp.float32) * frequency
    rot = jnp.stack(
        [
            jnp.concatenate([jnp.cos(angle), jnp.cos(angle)]),
            jnp.concatenate([-jnp.sin(angle), jnp.sin(angle)]),
        ]
    )
    fresh_pair = jnp.concatenate([fresh_keys[prompt_rows:], fresh_values[prompt_rows:]], axis=1)

    nx, nz = SEQ_SHAPE
    all_queries, passage_keys, passage_values = relay_gather(
        queries.reshape(2, prompt_rows * local_heads, HEAD_SIZE),
        key_cache[0],
        value_cache[0],
        fresh_pair,
        meta,
        rot,
        nx,
        nz,
    )
    q_blocks = all_queries.reshape(n_seq * 2, prompt_rows * local_heads, HEAD_SIZE)
    packed = passage_attention(nx, nz, meta, q_blocks, passage_keys, passage_values, lim)
    block_rows = packed.shape[1]

    back = relay_reduce(packed.reshape(n_seq, 2, block_rows, HEAD_SIZE), nx, nz)
    n_parts = back.shape[0]
    rows128 = prompt_rows * local_heads
    stats_back = back[:, :, rows128 : rows128 + 4].astype(jnp.float32)
    part_max = (stats_back[:, :, 0] + stats_back[:, :, 1]).reshape(n_parts, query_rows, local_heads)
    part_tot = (stats_back[:, :, 2] + stats_back[:, :, 3]).reshape(n_parts, query_rows, local_heads)
    part_acc = (
        back[:, :, :rows128].reshape(n_parts, query_rows, local_heads, HEAD_SIZE).astype(jnp.float32)
    )

    pq = queries[:prompt_rows].astype(jnp.float32)
    pk = fresh_keys[:prompt_rows].astype(jnp.float32)
    pv = fresh_values[:prompt_rows].astype(jnp.float32)
    ps = jnp.einsum("qhd,kd->qhk", pq, pk) * scale
    jj = jnp.arange(prompt_rows, dtype=jnp.int32)
    pvis = (jj[None, :] <= jj[:, None]) & prompt_live[None, :]
    ps = jnp.where(pvis[:, None, :], ps, NEGATIVE_FLOOR)
    pmax = jnp.max(ps, axis=-1)
    pw = jnp.where(pvis[:, None, :], jnp.exp(ps - pmax[..., None]), 0.0)
    ptot = jnp.sum(pw, axis=-1)
    pacc = jnp.einsum("qhk,kd->qhd", pw.astype(jnp.bfloat16).astype(jnp.float32), pv)
    loc_max = jnp.concatenate(
        [pmax, jnp.full((recompute_rows, local_heads), NEGATIVE_FLOOR, jnp.float32)]
    )
    loc_tot = jnp.concatenate([ptot, jnp.zeros((recompute_rows, local_heads), jnp.float32)])
    loc_acc = jnp.concatenate(
        [pacc, jnp.zeros((recompute_rows, local_heads, HEAD_SIZE), jnp.float32)]
    )

    highest = jnp.maximum(jnp.max(part_max, axis=0), loc_max)
    part_scale = jnp.exp(part_max - highest[None])
    loc_scale = jnp.exp(loc_max - highest)
    accumulated = jnp.sum(part_acc * part_scale[..., None], axis=0) + loc_acc * loc_scale[..., None]
    totals = jnp.sum(part_tot * part_scale, axis=0) + loc_tot * loc_scale
    safe_totals = jnp.where(totals > 0, totals, 1.0)
    attention = jnp.where(
        own_live[:, None, None], accumulated / safe_totals[..., None], 0.0
    ).astype(jnp.bfloat16).reshape(query_rows, local_heads * HEAD_SIZE)
    shares = mp_scatter(attention, w_out, n_mp)
    combined = jnp.sum(shares.astype(jnp.float32), axis=0).astype(jnp.bfloat16)
    return (combined[:prompt_rows], combined[prompt_rows:])


def solution(mesh):
    global SEQ_SHAPE
    sizes = dict(zip(mesh.axis_names, mesh.devices.shape))
    seq_devices = mesh.devices.reshape(sizes["seq"], sizes["mp"])[:, 0]
    xs = sorted({d.coords[0] for d in seq_devices})
    SEQ_SHAPE = (len(xs), sizes["seq"] // len(xs))
    return jax.shard_map(
        local,
        mesh=mesh,
        in_specs=(
            P("seq", "mp"),
            P("seq", "mp"),
            P("seq", None, "mp"),
            P("seq", None, "mp"),
            P(),
            P(None, "mp"),
            P(None, "mp"),
            P(None, "mp"),
            P("mp", None),
            P(),
            P(),
            P(),
            P(),
            P(),
        ),
        out_specs=(P("seq", "mp"), P("seq", "mp")),
        check_vma=False,
    )
```

```python
import functools
import math

import jax
import jax.numpy as jnp
from jax import lax
from jax.experimental import pallas as pl
from jax.experimental.pallas import tpu as pltpu
from jax.sharding import PartitionSpec as P

HEAD_SIZE = 128
NEGATIVE_FLOOR = -1e30


def apply_rotation(vectors, positions):
    half_width = vectors.shape[-1] // 2
    exponent = jnp.arange(half_width).astype(jnp.float32) * (2.0 / vectors.shape[-1])
    frequency = jnp.exp(-exponent * math.log(500000.0))
    angles = positions.astype(jnp.float32)[:, None] * frequency[None, :]
    cosines = jnp.cos(angles)[:, None, :]
    sines = jnp.sin(angles)[:, None, :]
    leading = vectors[..., :half_width]
    trailing = vectors[..., half_width:]
    return jnp.concatenate(
        [leading * cosines - trailing * sines, trailing * cosines + leading * sines], axis=-1
    )


def normalize(rows_in, norm_gain):
    values = rows_in.astype(jnp.float32)
    inverse_rms = lax.rsqrt(jnp.mean(values * values, axis=-1, keepdims=True) + 1e-05)
    return (values * inverse_rms * norm_gain).astype(jnp.bfloat16)


MESH = pl.DeviceIdType.MESH


def passage_kernel(nx, nz, flags_ref, q_ref, k_ref, v_ref, lim_ref, out_ref):
    nb, rows, _ = q_ref.shape
    keys = k_ref.shape[0]
    token = lax.broadcasted_iota(jnp.int32, (rows, keys), 1)
    sub = lax.broadcasted_iota(jnp.int32, (16, rows), 0)

    def split(m_row, l_row):
        m_hi = m_row.astype(jnp.bfloat16).astype(jnp.float32)
        l_hi = l_row.astype(jnp.bfloat16).astype(jnp.float32)
        st = jnp.where(
            sub == 0,
            m_row,
            jnp.where(
                sub == 1,
                m_row - m_hi,
                jnp.where(sub == 2, l_row, jnp.where(sub == 3, l_row - l_hi, 0.0)),
            ),
        )
        return st.astype(jnp.bfloat16)

    out_ref[:, 0:rows] = jnp.zeros((nb, rows, HEAD_SIZE), out_ref.dtype)
    floor = jnp.full((16, rows), NEGATIVE_FLOOR, jnp.float32)
    empty = split(floor, jnp.zeros((16, rows), jnp.float32))
    out_ref[:, rows:] = jnp.broadcast_to(empty[None], (nb, 16, rows))

    def attend(b, masked):
        d = b // 2
        stored = ((d % nz) * nx + d // nz) * 2 + b % 2
        scores = lax.dot_general(
            q_ref[stored], k_ref[...], (((1,), (1,)), ((), ())), preferred_element_type=jnp.float32
        ) * (1.0 / math.sqrt(HEAD_SIZE))
        if masked:
            scores = jnp.where(token <= lim_ref[...], scores, NEGATIVE_FLOOR)
        maxima = jnp.max(scores, axis=1, keepdims=True)
        weights = jnp.exp(scores - maxima)
        totals = jnp.sum(weights, axis=1, keepdims=True)
        out_ref[b, 0:rows] = jnp.dot(
            weights.astype(jnp.bfloat16), v_ref[...], preferred_element_type=jnp.float32
        ).astype(out_ref.dtype)
        lane = lax.broadcasted_iota(jnp.int32, (rows, rows), 1)
        both = jnp.transpose(jnp.where(lane < rows // 2, maxima, totals))
        out_ref[b, rows:] = split(both[0:16], both[rows // 2 : rows // 2 + 16])

    def body(b, carry):
        flag = flags_ref[4 + b % 2, b // 2]

        @pl.when(flag == 1)
        def _():
            attend(b, False)

        @pl.when(flag == 2)
        def _():
            attend(b, True)

        return carry

    lax.fori_loop(0, nb, body, 0)


def passage_attention(nx, nz, flags, q_blocks, keys, values, lim):
    nb, rows, _ = q_blocks.shape
    vmem = pl.BlockSpec(memory_space=pltpu.VMEM)
    return pl.pallas_call(
        functools.partial(passage_kernel, nx, nz),
        in_specs=[pl.BlockSpec(memory_space=pltpu.SMEM), vmem, vmem, vmem, vmem],
        out_specs=vmem,
        out_shape=jax.ShapeDtypeStruct((nb, rows + 16, HEAD_SIZE), jnp.bfloat16),
    )(flags, q_blocks, keys, values, lim)


def mp_gather_kernel(n, span, p_ref, r_ref, owner_ref, slot_ref, plen_ref, count_ref, index_ref,
                     y_ref, meta_ref, lim_ref, send_sem, recv_sem, local_sem):
    me = lax.axis_index("mp")
    row = lax.axis_index("seq")
    rows, width = p_ref.shape
    barrier = pltpu.get_barrier_semaphore()
    for k in range(1, n):
        peer = lax.rem(me + k, n)
        pl.semaphore_signal(barrier, inc=1, device_id=(row, peer), device_id_type=MESH)
    pl.semaphore_wait(barrier, n - 1)
    cols = pl.ds(pl.multiple_of(me * width, width), width)
    copies = []
    for k in range(1, n):
        peer = lax.rem(me + k, n)
        for part, src in enumerate((p_ref, r_ref)):
            c = pltpu.make_async_remote_copy(
                src_ref=src,
                dst_ref=y_ref.at[pl.ds(part * rows, rows), cols],
                send_sem=send_sem.at[part, k],
                recv_sem=recv_sem.at[part, k],
                device_id=(row, peer),
                device_id_type=MESH,
            )
            c.start()
            copies.append(c)
    own = [
        pltpu.make_async_copy(src, y_ref.at[pl.ds(part * rows, rows), cols], local_sem.at[part])
        for part, src in enumerate((p_ref, r_ref))
    ]
    for c in own:
        c.start()

    f32 = jnp.float32
    owner = owner_ref[...].astype(f32)
    slot = slot_ref[...].astype(f32)
    lane = lax.broadcasted_iota(jnp.int32, owner.shape, 1)
    mine = lane == row

    def pick(v):
        return jnp.sum(jnp.where(mine, v, 0.0), axis=1, keepdims=True)

    own_owner = pick(owner)
    own_slot = pick(slot)
    rank = jnp.sum(jnp.where((owner == own_owner) & (lane < row), 1.0, 0.0), axis=1, keepdims=True)
    held = jnp.sum(jnp.where(owner == own_slot, 1.0, 0.0), axis=1, keepdims=True)
    length = pick(plen_ref[...].astype(f32))
    count = pick(count_ref[...].astype(f32))
    index = index_ref[pl.ds(row, 1), :].astype(f32)
    lanef = lane.astype(f32)
    quantities = [
        held * span + lanef,
        rank * span + index,
        jnp.where(lanef < length, 1.0, 0.0),
        jnp.where(lanef < count, 1.0, 0.0),
        jnp.where(slot == own_owner, 1.0, 0.0),
        jnp.where(mine, 2.0, jnp.where((owner == own_owner) & (lane > row), 1.0, 0.0)),
        index,
        rank * span + 0.0 * lanef,
    ]
    for q, value in enumerate(quantities):
        meta_ref[q : q + 1, :] = value.astype(jnp.int32)
    heads = lim_ref.shape[0] // index.shape[1]
    wide = jnp.broadcast_to(index, (lim_ref.shape[0], index.shape[1]))
    which = lax.broadcasted_iota(jnp.int32, wide.shape, 0) // heads
    pick_lane = lax.broadcasted_iota(jnp.int32, wide.shape, 1)
    lim_ref[...] = jnp.sum(jnp.where(which == pick_lane, wide, 0.0), axis=1, keepdims=True).astype(jnp.int32)

    for c in copies:
        c.wait()
    for c in own:
        c.wait()


def mp_gather(prompt_part, recompute_part, owner, slot, plen, count, index, n, span, heads):
    vmem = pl.BlockSpec(memory_space=pltpu.VMEM)
    rows, width = prompt_part.shape
    small = [v.reshape(1, -1) for v in (owner, slot, plen, count)]
    return pl.pallas_call(
        functools.partial(mp_gather_kernel, n, span),
        in_specs=[vmem] * 7,
        out_specs=[vmem, vmem, vmem],
        out_shape=[
            jax.ShapeDtypeStruct((2 * rows, width * n), prompt_part.dtype),
            jax.ShapeDtypeStruct((8, owner.shape[0]), jnp.int32),
            jax.ShapeDtypeStruct((index.shape[1] * heads, 1), jnp.int32),
        ],
        scratch_shapes=[
            pltpu.SemaphoreType.DMA((2, n)),
            pltpu.SemaphoreType.DMA((2, n)),
            pltpu.SemaphoreType.DMA((2,)),
        ],
        compiler_params=pltpu.CompilerParams(collective_id=0, has_side_effects=True),
    )(prompt_part, recompute_part, *small, index)


def mp_scatter_kernel(n, a_ref, w_ref, y_ref, buf, send_sem, recv_sem):
    me = lax.axis_index("mp")
    row = lax.axis_index("seq")
    width = y_ref.shape[2]
    barrier = pltpu.get_barrier_semaphore()
    for k in range(1, n):
        peer = lax.rem(me + k, n)
        pl.semaphore_signal(barrier, inc=1, device_id=(row, peer), device_id_type=MESH)
    pl.semaphore_wait(barrier, n - 1)

    def block(d):
        cols = pl.ds(pl.multiple_of(d * width, width), width)
        return jnp.dot(a_ref[...], w_ref[:, cols], preferred_element_type=jnp.float32).astype(
            y_ref.dtype
        )

    copies = []
    for k in range(1, n):
        peer = lax.rem(me + k, n)
        buf[k] = block(peer)
        c = pltpu.make_async_remote_copy(
            src_ref=buf.at[k],
            dst_ref=y_ref.at[me],
            send_sem=send_sem.at[k],
            recv_sem=recv_sem.at[k],
            device_id=(row, peer),
            device_id_type=MESH,
        )
        c.start()
        copies.append(c)
    y_ref[me] = block(me)
    for c in copies:
        c.wait()


def mp_scatter(attention, w_out, n):
    vmem = pl.BlockSpec(memory_space=pltpu.VMEM)
    rows = attention.shape[0]
    width = w_out.shape[1] // n
    return pl.pallas_call(
        functools.partial(mp_scatter_kernel, n),
        in_specs=[vmem, vmem],
        out_specs=vmem,
        out_shape=jax.ShapeDtypeStruct((n, rows, width), jnp.bfloat16),
        scratch_shapes=[
            pltpu.VMEM((n, rows, width), jnp.bfloat16),
            pltpu.SemaphoreType.DMA((n,)),
            pltpu.SemaphoreType.DMA((n,)),
        ],
        compiler_params=pltpu.CompilerParams(collective_id=1, has_side_effects=True),
    )(attention, w_out)


def relay_gather_kernel(nx, nz, x_ref, kc_ref, vc_ref, fresh_ref, meta_ref, rot_ref,
                        y_ref, pk_ref, pv_ref, *sems):
    (sx_send, sx_recv, zp_send, zp_recv, zm_send, zm_recv, own_sem,
     bp_send, bp_recv, bm_send, bm_recv, xp_send, xp_recv, xm_send, xm_recv,
     fp_send, fp_recv, fm_send, fm_recv) = sems
    me = lax.axis_index("seq")
    mp = lax.axis_index("mp")
    x = me // nz
    z = me % nz
    up = lax.rem(z + 1, nz)
    down = lax.rem(z + nz - 1, nz)
    right = lax.rem(x + 1, nx)
    left = lax.rem(x + nx - 1, nx)
    barrier = pltpu.get_barrier_semaphore()
    peers = [(lax.rem(x + k, nx) * nz + z, mp) for k in range(1, nx)]
    peers += [(x * nz + up, mp), (x * nz + down, mp)]
    for p in peers:
        pl.semaphore_signal(barrier, inc=1, device_id=p, device_id_type=MESH)
    pl.semaphore_wait(barrier, len(peers))

    def copy(src, dst, send_sem, recv_sem, device):
        c = pltpu.make_async_remote_copy(
            src_ref=src,
            dst_ref=dst,
            send_sem=send_sem,
            recv_sem=recv_sem,
            device_id=device,
            device_id_type=MESH,
        )
        c.start()
        return c

    sent = []
    slot = z * nx + x
    first = [
        copy(x_ref.at[0], y_ref.at[slot, 0], sx_send.at[k], sx_recv.at[k], peers[k - 1])
        for k in range(1, nx)
    ]
    own = pltpu.make_async_copy(x_ref, y_ref.at[slot], own_sem)
    own.start()

    width = kc_ref.shape[1]
    cached = kc_ref[...].astype(jnp.float32)
    turned = pltpu.roll(cached, width // 2, 1)
    shifted = (cached * rot_ref[0:1, :] + turned * rot_ref[1:2, :]).astype(pk_ref.dtype)
    token = lax.broadcasted_iota(jnp.int32, (kc_ref.shape[0], meta_ref.shape[1]), 0)
    chosen = (token == meta_ref[6:7, :]) & (meta_ref[3:4, :] > 0)
    placed = jnp.dot(
        chosen.astype(jnp.bfloat16), fresh_ref[...], preferred_element_type=jnp.float32
    ).astype(pk_ref.dtype)
    replaced = jnp.max(jnp.where(chosen, 1.0, 0.0), axis=1, keepdims=True) > 0.0
    pk_ref[...] = jnp.where(replaced, placed[:, :width], shifted)
    pv_ref[...] = jnp.where(replaced, placed[:, width:], vc_ref[...])

    def x_out(column):
        a = copy(
            y_ref.at[column * nx + x, 1], y_ref.at[column * nx + x, 1],
            xp_send.at[column], xp_recv.at[column], (right * nz + z, mp),
        )
        b = copy(
            y_ref.at[column * nx + x, 1], y_ref.at[column * nx + x, 1],
            xm_send.at[column], xm_recv.at[column], (left * nz + z, mp),
        )
        return [a, b]

    own.wait()
    steps = nz // 2
    half = nx // 2
    zlast = {}
    blast = {}
    xcopies = {}
    for c in first:
        c.wait()
    for t in range(1, steps + 1):
        for sign, send_sem, recv_sem, target, count in (
            (1, bp_send, bp_recv, up, steps),
            (-1, bm_send, bm_recv, down, nz - 1 - steps),
        ):
            if t > count:
                continue
            if t > 1:
                blast[sign].wait_recv()
            column = lax.rem(z - sign * (t - 1) + nz, nz)
            if t > 1:
                xcopies[(sign, t - 1)] = x_out(column)
            elif sign == 1:
                xcopies[(0, 0)] = x_out(column)
            blast[sign] = copy(
                y_ref.at[column * nx + x, 1], y_ref.at[column * nx + x, 1],
                send_sem.at[t], recv_sem.at[t], (x * nz + target, mp),
            )
            sent.append(blast[sign])
        for i in range(nx):
            for sign, send_sem, recv_sem, target in (
                (1, zp_send, zp_recv, up),
                (-1, zm_send, zm_recv, down),
            ):
                if t == steps and (i < half) != (sign == 1):
                    continue
                if t > 1:
                    zlast[(sign, i)].wait_recv()
                column = lax.rem(z - sign * (t - 1) + nz, nz)
                zlast[(sign, i)] = copy(
                    y_ref.at[column * nx + i, 0], y_ref.at[column * nx + i, 0],
                    send_sem.at[t, i], recv_sem.at[t, i], (x * nz + target, mp),
                )
                sent.append(zlast[(sign, i)])
    for sign, count in ((1, steps), (-1, nz - 1 - steps)):
        blast[sign].wait_recv()
        column = lax.rem(z - sign * count + nz, nz)
        xcopies[(sign, count)] = x_out(column)
    order = [(0, 0)] + [(s, t) for t in range(1, steps + 1) for s in (1, -1) if (s, t) in xcopies]
    forwards = []
    for key in order:
        sign, t = key
        column = lax.rem(z - sign * t + nz, nz)
        from_left, from_right = xcopies[key]
        from_left.wait_recv()
        from_right.wait_recv()
        sent += xcopies[key]
    for zc in range(nz):
        if zc < nz // 2:
            forwards.append(
                copy(
                    y_ref.at[zc * nx + left, 1], y_ref.at[zc * nx + left, 1],
                    fp_send.at[zc], fp_recv.at[zc], (right * nz + z, mp),
                )
            )
        else:
            forwards.append(
                copy(
                    y_ref.at[zc * nx + right, 1], y_ref.at[zc * nx + right, 1],
                    fm_send.at[zc], fm_recv.at[zc], (left * nz + z, mp),
                )
            )
    for c in zlast.values():
        c.wait_recv()
    for c in forwards:
        c.wait_recv()
    for c in sent:
        c.wait_send()
    for c in forwards:
        c.wait_send()


def relay_gather(x, kc, vc, fresh, meta, rot, nx, nz):
    assert nx == 4 and nz % 2 == 0
    vmem = pl.BlockSpec(memory_space=pltpu.VMEM)
    steps = nz // 2
    dma = pltpu.SemaphoreType.DMA
    return pl.pallas_call(
        functools.partial(relay_gather_kernel, nx, nz),
        in_specs=[vmem] * 6,
        out_specs=[vmem, vmem, vmem],
        out_shape=[
            jax.ShapeDtypeStruct((nx * nz,) + x.shape, x.dtype),
            jax.ShapeDtypeStruct(kc.shape, kc.dtype),
            jax.ShapeDtypeStruct(vc.shape, vc.dtype),
        ],
        scratch_shapes=[
            dma((nx,)), dma((nx,)),
            dma((steps + 1, nx)), dma((steps + 1, nx)), dma((steps + 1, nx)), dma((steps + 1, nx)),
            dma(()),
            dma((steps + 1,)), dma((steps + 1,)), dma((steps + 1,)), dma((steps + 1,)),
            dma((nz,)), dma((nz,)), dma((nz,)), dma((nz,)),
            dma((nz,)), dma((nz,)), dma((nz,)), dma((nz,)),
        ],
        compiler_params=pltpu.CompilerParams(collective_id=2, has_side_effects=True),
    )(x, kc, vc, fresh, meta, rot)


def merge_piece(a, b, rows):
    af = a.astype(jnp.float32)
    bf = b.astype(jnp.float32)
    m1 = af[rows : rows + 1] + af[rows + 1 : rows + 2]
    l1 = af[rows + 2 : rows + 3] + af[rows + 3 : rows + 4]
    m2 = bf[rows : rows + 1] + bf[rows + 1 : rows + 2]
    l2 = bf[rows + 2 : rows + 3] + bf[rows + 3 : rows + 4]
    top = jnp.maximum(m1, m2)
    s1 = jnp.exp(m1 - top)
    s2 = jnp.exp(m2 - top)
    total = l1 * s1 + l2 * s2
    upper = lax.broadcasted_iota(jnp.int32, (rows, rows), 0) < rows // 2
    both = jnp.transpose(jnp.where(upper, s1, s2))
    c1 = both[:, 0:1]
    c2 = both[:, rows // 2 : rows // 2 + 1]
    acc = af[0:rows] * c1 + bf[0:rows] * c2
    sub = lax.broadcasted_iota(jnp.int32, (16, rows), 0)
    top_hi = top.astype(jnp.bfloat16).astype(jnp.float32)
    tot_hi = total.astype(jnp.bfloat16).astype(jnp.float32)
    st = jnp.where(
        sub == 0,
        top,
        jnp.where(
            sub == 1, top - top_hi, jnp.where(sub == 2, total, jnp.where(sub == 3, total - tot_hi, 0.0))
        ),
    )
    return acc.astype(jnp.bfloat16), st.astype(jnp.bfloat16)


def relay_reduce_kernel(
    nx, nz, x_ref, y_ref, rp, rm, bp, bm, col, sp_send, sp_recv, sm_send, sm_recv, sx_send, sx_recv
):
    me = lax.axis_index("seq")
    mp = lax.axis_index("mp")
    x = me // nz
    z = me % nz
    up = lax.rem(z + 1, nz)
    down = lax.rem(z + nz - 1, nz)
    rows = x_ref.shape[2] - 16
    barrier = pltpu.get_barrier_semaphore()
    peers = [(lax.rem(x + k, nx) * nz + z, mp) for k in range(1, nx)]
    peers += [(x * nz + up, mp), (x * nz + down, mp)]
    for p in peers:
        pl.semaphore_signal(barrier, inc=1, device_id=p, device_id_type=MESH)
    pl.semaphore_wait(barrier, len(peers))

    def merge_into(dst, first, second):
        for h in range(2):
            acc, st = merge_piece(first[h], second[h], rows)
            dst[h, 0:rows] = acc
            dst[h, rows:] = st

    steps = nz // 2
    half = nx // 2
    last = {}
    sent = []
    dirs = ((1, rp, bp, sp_send, sp_recv, up), (-1, rm, bm, sm_send, sm_recv, down))
    for t in range(1, steps + 1):
        for i in range(nx):
            for sign, recv_buf, send_buf, send_sem, recv_sem, target in dirs:
                if t == 1 and (i < half) != (sign == 1):
                    continue
                column = lax.rem(z + sign * (steps + 1 - t) + nz, nz)
                own = x_ref.at[i * nz + column]
                if (sign, i) in last:
                    last[(sign, i)].wait_recv()
                    merge_into(send_buf.at[t, i], own, recv_buf.at[t - 1, i])
                    src = send_buf.at[t, i]
                else:
                    src = own
                c = pltpu.make_async_remote_copy(
                    src_ref=src,
                    dst_ref=recv_buf.at[t, i],
                    send_sem=send_sem.at[t, i],
                    recv_sem=recv_sem.at[t, i],
                    device_id=(x * nz + target, mp),
                    device_id_type=MESH,
                )
                c.start()
                last[(sign, i)] = c
                sent.append(c)

    mine = []
    for i in range(nx):
        last[(1, i)].wait_recv()
        last[(-1, i)].wait_recv()
        merge_into(col.at[i], x_ref.at[i * nz + z], rp.at[steps, i])
        merge_into(col.at[i], col.at[i], rm.at[steps, i])
    for k in range(1, nx):
        target = lax.rem(x + k, nx)
        c = pltpu.make_async_remote_copy(
            src_ref=col.at[target],
            dst_ref=y_ref.at[x],
            send_sem=sx_send.at[k],
            recv_sem=sx_recv.at[k],
            device_id=(target * nz + z, mp),
            device_id_type=MESH,
        )
        c.start()
        mine.append(c)
    y_ref[x] = col[x]
    for c in sent:
        c.wait_send()
    for c in mine:
        c.wait()


def relay_reduce(parts, nx, nz):
    vmem = pl.BlockSpec(memory_space=pltpu.VMEM)
    steps = nz // 2
    piece = parts.shape[1:]
    return pl.pallas_call(
        functools.partial(relay_reduce_kernel, nx, nz),
        in_specs=[vmem],
        out_specs=vmem,
        out_shape=jax.ShapeDtypeStruct((nx,) + piece, parts.dtype),
        scratch_shapes=[
            pltpu.VMEM((steps + 1, nx) + piece, parts.dtype),
            pltpu.VMEM((steps + 1, nx) + piece, parts.dtype),
            pltpu.VMEM((steps + 1, nx) + piece, parts.dtype),
            pltpu.VMEM((steps + 1, nx) + piece, parts.dtype),
            pltpu.VMEM((nx,) + piece, parts.dtype),
            pltpu.SemaphoreType.DMA((steps + 1, nx)),
            pltpu.SemaphoreType.DMA((steps + 1, nx)),
            pltpu.SemaphoreType.DMA((steps + 1, nx)),
            pltpu.SemaphoreType.DMA((steps + 1, nx)),
            pltpu.SemaphoreType.DMA((nx,)),
            pltpu.SemaphoreType.DMA((nx,)),
        ],
        compiler_params=pltpu.CompilerParams(collective_id=3, has_side_effects=True),
    )(parts)


def local(
    prompt_hidden,
    recompute_hidden,
    key_cache,
    value_cache,
    norm_gain,
    w_query,
    key_weight,
    value_weight,
    w_out,
    passage_owner,
    prompt_slot,
    prompt_length,
    recompute_count,
    recompute_index,
):
    prompt_rows = prompt_hidden.shape[0]
    recompute_rows = recompute_hidden.shape[0]
    query_rows = prompt_rows + recompute_rows
    passage_length = key_cache.shape[1]
    local_heads = w_query.shape[1] // HEAD_SIZE
    n_seq = passage_owner.shape[0]
    me = lax.axis_index("seq")
    scale = 1.0 / math.sqrt(HEAD_SIZE)

    n_mp = w_out.shape[1] // prompt_hidden.shape[1]
    full_rows, meta, lim = mp_gather(
        prompt_hidden, recompute_hidden, passage_owner, prompt_slot, prompt_length,
        recompute_count, recompute_index, n_mp, passage_length, local_heads,
    )
    own_pos = jnp.concatenate([meta[0], meta[1]])
    own_live = jnp.concatenate([meta[2], meta[3]]) > 0
    own_index = meta[6]
    own_shift = meta[7, 0]
    prompt_live = meta[2] > 0
    recompute_live = meta[3] > 0
    normalized_hidden = normalize(full_rows, norm_gain)
    queries = (
        apply_rotation(
            jnp.dot(normalized_hidden, w_query, preferred_element_type=jnp.float32).reshape(
                query_rows, local_heads, HEAD_SIZE
            ),
            own_pos,
        )
        .astype(jnp.bfloat16)
    )
    fresh_keys = (
        apply_rotation(
            jnp.dot(normalized_hidden, key_weight, preferred_element_type=jnp.float32).reshape(
                query_rows, 1, HEAD_SIZE
            ),
            own_pos,
        )
        .astype(jnp.bfloat16)
        .reshape(query_rows, HEAD_SIZE)
    )
    fresh_values = jnp.dot(
        normalized_hidden, value_weight, preferred_element_type=jnp.float32
    ).astype(jnp.bfloat16)

    half_width = HEAD_SIZE // 2
    exponent = jnp.arange(half_width).astype(jnp.float32) * (2.0 / HEAD_SIZE)
    frequency = jnp.exp(-exponent * math.log(500000.0))
    angle = own_shift.astype(jnp.float32) * frequency
    rot = jnp.stack(
        [
            jnp.concatenate([jnp.cos(angle), jnp.cos(angle)]),
            jnp.concatenate([-jnp.sin(angle), jnp.sin(angle)]),
        ]
    )
    fresh_pair = jnp.concatenate([fresh_keys[prompt_rows:], fresh_values[prompt_rows:]], axis=1)

    nx, nz = SEQ_SHAPE
    all_queries, passage_keys, passage_values = relay_gather(
        queries.reshape(2, prompt_rows * local_heads, HEAD_SIZE),
        key_cache[0],
        value_cache[0],
        fresh_pair,
        meta,
        rot,
        nx,
        nz,
    )
    q_blocks = all_queries.reshape(n_seq * 2, prompt_rows * local_heads, HEAD_SIZE)
    packed = passage_attention(nx, nz, meta, q_blocks, passage_keys, passage_values, lim)
    block_rows = packed.shape[1]

    back = relay_reduce(packed.reshape(n_seq, 2, block_rows, HEAD_SIZE), nx, nz)
    n_parts = back.shape[0]
    rows128 = prompt_rows * local_heads
    stats_back = back[:, :, rows128 : rows128 + 4].astype(jnp.float32)
    part_max = (stats_back[:, :, 0] + stats_back[:, :, 1]).reshape(n_parts, query_rows, local_heads)
    part_tot = (stats_back[:, :, 2] + stats_back[:, :, 3]).reshape(n_parts, query_rows, local_heads)
    part_acc = (
        back[:, :, :rows128].reshape(n_parts, query_rows, local_heads, HEAD_SIZE).astype(jnp.float32)
    )

    pq = queries[:prompt_rows].astype(jnp.float32)
    pk = fresh_keys[:prompt_rows].astype(jnp.float32)
    pv = fresh_values[:prompt_rows].astype(jnp.float32)
    ps = jnp.einsum("qhd,kd->qhk", pq, pk) * scale
    jj = jnp.arange(prompt_rows, dtype=jnp.int32)
    pvis = (jj[None, :] <= jj[:, None]) & prompt_live[None, :]
    ps = jnp.where(pvis[:, None, :], ps, NEGATIVE_FLOOR)
    pmax = jnp.max(ps, axis=-1)
    pw = jnp.where(pvis[:, None, :], jnp.exp(ps - pmax[..., None]), 0.0)
    ptot = jnp.sum(pw, axis=-1)
    pacc = jnp.einsum("qhk,kd->qhd", pw.astype(jnp.bfloat16).astype(jnp.float32), pv)
    loc_max = jnp.concatenate(
        [pmax, jnp.full((recompute_rows, local_heads), NEGATIVE_FLOOR, jnp.float32)]
    )
    loc_tot = jnp.concatenate([ptot, jnp.zeros((recompute_rows, local_heads), jnp.float32)])
    loc_acc = jnp.concatenate(
        [pacc, jnp.zeros((recompute_rows, local_heads, HEAD_SIZE), jnp.float32)]
    )

    highest = jnp.maximum(jnp.max(part_max, axis=0), loc_max)
    part_scale = jnp.exp(part_max - highest[None])
    loc_scale = jnp.exp(loc_max - highest)
    accumulated = jnp.sum(part_acc * part_scale[..., None], axis=0) + loc_acc * loc_scale[..., None]
    totals = jnp.sum(part_tot * part_scale, axis=0) + loc_tot * loc_scale
    safe_totals = jnp.where(totals > 0, totals, 1.0)
    attention = jnp.where(
        own_live[:, None, None], accumulated / safe_totals[..., None], 0.0
    ).astype(jnp.bfloat16).reshape(query_rows, local_heads * HEAD_SIZE)
    shares = mp_scatter(attention, w_out, n_mp)
    combined = jnp.sum(shares.astype(jnp.float32), axis=0).astype(jnp.bfloat16)
    return (combined[:prompt_rows], combined[prompt_rows:])


def solution(mesh):
    global SEQ_SHAPE
    sizes = dict(zip(mesh.axis_names, mesh.devices.shape))
    seq_devices = mesh.devices.reshape(sizes["seq"], sizes["mp"])[:, 0]
    xs = sorted({d.coords[0] for d in seq_devices})
    SEQ_SHAPE = (len(xs), sizes["seq"] // len(xs))
    return jax.shard_map(
        local,
        mesh=mesh,
        in_specs=(
            P("seq", "mp"),
            P("seq", "mp"),
            P("seq", None, "mp"),
            P("seq", None, "mp"),
            P(),
            P(None, "mp"),
            P(None, "mp"),
            P(None, "mp"),
            P("mp", None),
            P(),
            P(),
            P(),
            P(),
            P(),
        ),
        out_specs=(P("seq", "mp"), P("seq", "mp")),
        check_vma=False,
    )
```
